32 devices in a mesh: shard: 2 (over x), ctx: 4 (over y, core), tensor: 4 (over z).
Axes of the slice: x: 2, y: 2, z: 4, core: 2. Of those that a mesh axis runs over, the one named last changes fastest.
Arguments:
- block_input: bfloat16 [4096, 1536], P(('shard', 'ctx'), 'tensor'), may hold values from -6 to 6
- gain_input: bfloat16 [1536], P('tensor'), may hold values from 0.5 to 1.5
- proj_main: bfloat16 [1536, 2, 3072], P(('shard', 'ctx'), None, 'tensor'), may hold values from -0.15625 to 0.15625
- proj_state: bfloat16 [1536, 256], P(('shard', 'ctx')), may hold values from -0.15625 to 0.15625
- proj_step: bfloat16 [1536, 48], P(('shard', 'ctx'), 'tensor'), may hold values from -0.15625 to 0.15625
- conv_main: bfloat16 [4, 3072], P(None, 'tensor'), may hold values from -3 to 3
- conv_state: bfloat16 [4, 256], replicated, may hold values from -3 to 3
- step_bias: float32 [48], P('tensor'), may hold values from -4 to -1
- decay_log: float32 [48], P('tensor'), may hold values from -8 to -1
- skip_gain: float32 [48], P('tensor'), may hold values from 0.5 to 1.5
- gain_gate: bfloat16 [3072], P('tensor'), may hold values from 0.5 to 1.5
- proj_out: bfloat16 [1536, 3072], P(('shard', 'ctx'), 'tensor'), may hold values from -0.109375 to 0.109375
- gain_mix: bfloat16 [1536], P('tensor'), may hold values from 0.5 to 1.5
- router_weight: bfloat16 [1536, 16], P(('shard', 'ctx')), may hold values from -0.078125 to 0.078125
- shared_gates: bfloat16 [1536, 2, 1024], P(('shard', 'ctx'), None, 'tensor'), may hold values from -0.15625 to 0.15625
- shared_down: bfloat16 [1536, 1024], P(('shard', 'ctx'), 'tensor'), may hold values from -0.1875 to 0.1875
- expert_gates: bfloat16 [16, 1536, 2, 512], P(('shard', 'ctx'), None, None, 'tensor'), may hold values from -0.15625 to 0.15625
- expert_down: bfloat16 [16, 512, 1536], P(('shard', 'ctx'), 'tensor'), may hold values from -0.5 to 0.5
- segments: int32 [2, 2048], P('shard', 'ctx'), may hold values from 0 to 2, never falling along the last dimension, each value on 1 to 1024 neighbouring positions
- routes: int32 [4096, 6], P(('shard', 'ctx')), may hold values from 0 to 15, all different within a row; in each aligned block of 512 rows (0 to 511, 512 to 1023, ...) at most 384 rows name the same one
- cotangent: bfloat16 [4096, 1536], P(('shard', 'ctx'), 'tensor'), may hold values from -6 to 6
Outputs:
- output: bfloat16 [4096, 1536], P(('shard', 'ctx'), 'tensor')
- grad_input: float32 [4096, 1536], P(('shard', 'ctx'), 'tensor')
- grad_gain_input: float32 [1536], P('tensor')
- grad_proj_main: float32 [1536, 2, 3072], P(('shard', 'ctx'), None, 'tensor')
- grad_proj_state: float32 [1536, 256], P(('shard', 'ctx'))
- grad_proj_step: float32 [1536, 48], P(('shard', 'ctx'), 'tensor')
- grad_conv_main: float32 [4, 3072], P(None, 'tensor')
- grad_conv_state: float32 [4, 256], replicated
- grad_step_bias: float32 [48], P('tensor')
- grad_decay_log: float32 [48], P('tensor')
- grad_skip_gain: float32 [48], P('tensor')
- grad_gain_gate: float32 [3072], P('tensor')
- grad_proj_out: float32 [1536, 3072], P(('shard', 'ctx'), 'tensor')
- grad_gain_mix: float32 [1536], P('tensor')
- grad_router_weight: float32 [1536, 16], P(('shard', 'ctx'))
- grad_shared_gates: float32 [1536, 2, 1024], P(('shard', 'ctx'), None, 'tensor')
- grad_shared_down: float32 [1536, 1024], P(('shard', 'ctx'), 'tensor')
- grad_expert_gates: float32 [16, 1536, 2, 512], P(('shard', 'ctx'), None, None, 'tensor')
- grad_expert_down: float32 [16, 512, 1536], P(('shard', 'ctx'), 'tensor')
The draws below stay inside these ranges and needn't reach their ends.
Inputs may be any that keep to these rules, and one draw needn't show every extreme that they name: `routes`: each row names 6 different experts; among the rows of one device (512 tokens, aligned blocks) no expert is named more than 384 times. `segments`: along each group the document numbers never fall; each document has at most 1024 tokens.
All inputs are finite; a program needn't handle non-finite values.
Results may differ from the reference program's by a relative error of at most 0.015.
Values may be sent and summed in bfloat16 or wider, within the bound.
A program may use at most 448 MiB of HBM per device.

```python
import math
import jax
import jax.numpy as jnp
import numpy as np
from jax import lax

D = 1536
HEADS = 48
HDIM = 64
NSTATE = 128
CONV = 4
DI = 3072
FS = 1024
FE = 512
TOPK = 6
EXPERTS = 16
TOK_DEV = 512
SEQ = 2048
DOCS = 3
GROUPS = 2
TOKENS = 4096
CAP = 384
N_SHARD = 2
N_CTX = 4


def block_levels(stream_key, shape, cuts, smallest, high):
    def one(dim, shards_of):
        draws = jax.random.uniform(jax.random.fold_in(jax.random.fold_in(stream_key, 6), dim), (shards_of,), jnp.float32, smallest / len(cuts), high / len(cuts))
        return jnp.repeat(jnp.exp(draws), shape[dim] // shards_of).reshape((-1,) + (1,) * (len(shape) - dim - 1))

    level = one(*cuts[0])
    for cut in cuts[1:]:
        level = level * one(*cut)
    return level


def split_up(amount, total, limit, slope):
    loads = [(1 << 20) // math.isqrt(standing ** slope) + 1 for standing in range(2, amount + 1)]
    surplus, given = total - limit - (amount - 1), [1] * (amount - 1)
    while surplus > 0:
        candidates = [i for i in range(amount - 1) if given[i] < limit]
        whole, remaining = sum([loads[i] for i in candidates]), surplus
        for i in candidates:
            extra = min(limit - given[i], max(1, remaining * loads[i] // whole), surplus)
            given[i] = given[i] + extra
            surplus = surplus - extra
    return np.array([limit] + given)


def ragged(stream_key, count, total, most, skew):
    if count == 2:
        one = jax.random.randint(stream_key, (), max(1, total - most), min(most, total - 1) + 1)
        return jnp.stack([one, total - one])
    lengths = jnp.asarray(split_up(count, total, most, skew), jnp.int32)
    twos = (count - 1) // 2
    donor, taker = lengths[1:1 + 2 * twos:2], lengths[2:2 + 2 * twos:2]
    slack = jnp.minimum(donor - 1, most - taker)
    passed = jax.random.randint(jax.random.fold_in(stream_key, 1), (twos,), 0, 1 << 20) % (slack + 1)
    lengths = lengths.at[1:1 + 2 * twos:2].set(donor - passed).at[2:2 + 2 * twos:2].set(taker + passed)
    return lengths[jax.random.permutation(jax.random.fold_in(stream_key, 2), count)]


def assign_block(key, own, number, rows, number_of, top, limit, lean):
    order = jax.random.permutation(key, number_of)
    crowded, usual = load_shares(number_of, rows * top, limit, lean, True), load_shares(number_of, rows * top, limit, lean, False)
    places = jnp.arange(number_of)

    def named(sizes, turn):
        used = int((sizes > 0).sum())
        fixed = max(1, used // 4)
        passed = fixed + (places - fixed + turn * (used - fixed)) % max(1, number_of - fixed)
        return jnp.zeros((number_of,), jnp.int32).at[order[jnp.where(places < fixed, places, passed)]].set(jnp.asarray(sizes, jnp.int32))

    sizes = jnp.where(number % 4 == 0, named(crowded, number // 4), named(usual, number - number // 4 - 1))
    mixed = jax.random.permutation(jax.random.fold_in(own, 3), number_of)
    donor, sink = mixed[0:number_of // 2 * 2:2], mixed[1:number_of // 2 * 2:2]
    slack = jnp.minimum(sizes[donor] - 1, limit - sizes[sink]) // 2
    slack = jnp.where((donor == order[0]) | (sink == order[0]) | (sizes[sink] == 0), 0, jnp.maximum(slack, 0))
    passed = jax.random.randint(jax.random.fold_in(own, 4), (number_of // 2,), 0, 1 << 20) % (slack + 1)
    sizes = sizes.at[donor].add(-passed).at[sink].add(passed)
    items = jnp.searchsorted(jnp.cumsum(sizes), jnp.arange(rows * top), side="right").astype(jnp.int32)
    listing = items.reshape(top, rows).T
    listing = listing[jax.random.permutation(jax.random.fold_in(own, 1), rows)]
    turn = jax.random.randint(jax.random.fold_in(own, 2), (rows, 1), 0, top)
    return jnp.take_along_axis(listing, (jnp.arange(top)[None, :] + turn) % top, axis=1)


def load_shares(amount, total, limit, skew, full):
    portions = [(1 << 20) // math.isqrt(standing ** skew) + 1 for standing in range(1, amount + 1)]
    largest = limit if full else min(limit, max(-(-total // amount), total * portions[0] // sum(portions)))
    least = 1 if total - largest >= amount - 1 else 0
    holding, spare = [largest] + [least] * (amount - 1), total - largest - least * (amount - 1)
    while spare > 0:
        free = [i for i in range(1, amount) if holding[i] < largest] or [i for i in range(1, amount) if holding[i] < limit]
        mass, remaining = sum([portions[i] for i in free]), spare
        for i in free:
            addition = min(limit - holding[i], max(1, remaining * portions[i] // mass), spare)
            holding[i] = holding[i] + addition
            spare = spare - addition
    return np.array(holding)


def scatter_about(stream_key, shape, deviation, reach, cuts=(), kind=jnp.bfloat16):
    values = jax.random.normal(stream_key, shape, jnp.float32) * deviation
    if len(cuts) > 0:
        values = block_levels(stream_key, shape, cuts, -0.22, 0.18) * values
    return jnp.clip(values, min=-reach, max=reach).astype(kind)


def setup_inputs(seed: int = 0) -> dict:
    seeds = jax.random.split(jax.random.key(seed), 22)
    block_input = scatter_about(seeds[0], (TOKENS, D), 1.0, 6.0, ((0, 8), (1, 4)))
    gain_input = jnp.clip(1.0 + 0.1 * jax.random.normal(seeds[1], (D,), jnp.float32), 0.5, 1.5).astype(jnp.bfloat16)
    proj_main = scatter_about(seeds[2], (D, 2, DI), D ** -0.5, 0.15625, ((0, 8), (2, 4)))
    proj_state = scatter_about(seeds[3], (D, 2 * NSTATE), D ** -0.5, 0.15625, ((0, 8),))
    proj_step = scatter_about(seeds[4], (D, HEADS), D ** -0.5, 0.15625, ((0, 8), (1, 4)))
    conv_main = scatter_about(seeds[5], (CONV, DI), CONV ** -0.5, 3.0, ((1, 4),))
    conv_state = scatter_about(seeds[6], (CONV, 2 * NSTATE), CONV ** -0.5, 3.0)
    step_bias = jnp.clip(-4.0 + 3.0 * jax.random.uniform(seeds[7], (HEADS,), jnp.float32) ** block_levels(seeds[7], (HEADS,), ((0, 4),), -0.2, 0.2), -4.0, -1.0)
    decay_log = jnp.clip(-8.0 + 7.0 * jax.random.uniform(seeds[8], (HEADS,), jnp.float32) ** block_levels(seeds[8], (HEADS,), ((0, 4),), -0.2, 0.2), -8.0, -1.0)
    skip_gain = jnp.clip(0.5 + 1.0 * jax.random.uniform(seeds[9], (HEADS,), jnp.float32) ** block_levels(seeds[9], (HEADS,), ((0, 4),), -0.2, 0.2), 0.5, 1.5)
    gain_gate = jnp.clip(1.0 + 0.1 * jax.random.normal(seeds[10], (DI,), jnp.float32), 0.5, 1.5).astype(jnp.bfloat16)
    proj_out = scatter_about(seeds[11], (D, DI), DI ** -0.5, 0.109375, ((0, 8), (1, 4)))
    gain_mix = jnp.clip(1.0 + 0.1 * jax.random.normal(seeds[12], (D,), jnp.float32), 0.5, 1.5).astype(jnp.bfloat16)
    router_weight = scatter_about(seeds[13], (D, EXPERTS), (4 * D) ** -0.5, 0.078125, ((0, 8),))
    shared_gates = scatter_about(seeds[14], (D, 2, FS), D ** -0.5, 0.15625, ((0, 8), (2, 4)))
    shared_down = scatter_about(seeds[15], (D, FS), FS ** -0.5, 0.1875, ((0, 8), (1, 4)))
    expert_gates = scatter_about(seeds[16], (EXPERTS, D, 2, FE), D ** -0.5, 0.15625, ((0, 8), (3, 4)))
    expert_down = scatter_about(seeds[17], (EXPERTS, FE, D), (FE // 4) ** -0.5, 0.5, ((0, 8), (1, 4)))
    segments = jax.vmap(lambda own: jnp.searchsorted(jnp.cumsum(ragged(own, DOCS, SEQ, SEQ // 2, 0)), jnp.arange(SEQ), side="right"))(jax.random.split(seeds[18], GROUPS)).reshape((GROUPS, SEQ)).astype(jnp.int32)
    routes_keys = jax.random.split(jax.random.fold_in(seeds[19], 1), TOKENS // TOK_DEV)
    routes_turns = jax.random.permutation(jax.random.fold_in(seeds[19], 3), TOKENS // TOK_DEV)
    routes = jax.vmap(lambda own, number: assign_block(jax.random.fold_in(seeds[19], 2), own, number, TOK_DEV, EXPERTS, TOPK, CAP, 1))(routes_keys, routes_turns).reshape((TOKENS, TOPK))
    cotangent = scatter_about(seeds[20], (TOKENS, D), 1.0, 6.0, ((0, 8), (1, 4)))
    return {"block_input": block_input, "gain_input": gain_input, "proj_main": proj_main, "proj_state": proj_state, "proj_step": proj_step, "conv_main": conv_main, "conv_state": conv_state, "step_bias": step_bias, "decay_log": decay_log, "skip_gain": skip_gain, "gain_gate": gain_gate, "proj_out": proj_out, "gain_mix": gain_mix, "router_weight": router_weight, "shared_gates": shared_gates, "shared_down": shared_down, "expert_gates": expert_gates, "expert_down": expert_down, "segments": segments, "routes": routes, "cotangent": cotangent}


epsilon = 1e-05
highest = lax.Precision.HIGHEST

@jax.custom_vjp
def low(v):
    return lax.optimization_barrier(v.astype(jnp.bfloat16)).astype(jnp.float32)

@jax.custom_vjp
def low_back(v):
    return v

def low_keep(v):
    return (low(v), None)

def low_pass(kept, grad):
    return (grad,)

def back_keep(v):
    return (v, None)

def back_low(kept, grad):
    return (low(grad),)
low.defvjp(low_keep, low_pass)
low_back.defvjp(back_keep, back_low)

def high_dot(left, right):
    return jnp.dot(left, right, preferred_element_type=jnp.float32, precision=highest)

def rms_scale(values):
    return lax.rsqrt(lax.optimization_barrier(jnp.mean(values * values, axis=-1, keepdims=True)) + epsilon)

def conv_group(rows, weights, seg_row):
    count = rows.shape[0]
    padded = jnp.concatenate([jnp.zeros((CONV - 1, rows.shape[1]), jnp.float32), rows], axis=0)
    seg_pad = jnp.concatenate([jnp.full((CONV - 1,), -1, jnp.int32), seg_row.astype(jnp.int32)], axis=0)
    total = jnp.zeros_like(rows)
    for offset in range(CONV):
        same = (seg_pad[offset:offset + count] == seg_row.astype(jnp.int32))[:, None]
        total = total + jnp.where(same, padded[offset:offset + count] * weights[offset], 0.0)
    return jax.nn.silu(total)

def group_scan(pieces):
    signal, step_size, log_decay, keys_state, query_state, seg_row = pieces
    positions = jnp.arange(SEQ)
    allowed = (positions[:, None] >= positions[None, :]) & (seg_row[:, None] == seg_row[None, :])
    scores = jnp.where(allowed, high_dot(query_state, keys_state.T), 0.0)
    scaled = signal * step_size[:, :, None]

    def one_head(columns):
        decay_col, scaled_col = columns
        running = jnp.cumsum(decay_col)
        spread = jnp.where(allowed, running[:, None] - running[None, :], 0.0)
        return high_dot(jnp.exp(spread) * scores, scaled_col)
    heads_out = lax.map(jax.checkpoint(one_head), (log_decay.T, scaled.transpose(1, 0, 2)))
    return heads_out.transpose(1, 0, 2)

def expert_tables(routes):
    sources = N_SHARD * N_CTX
    flat = routes.reshape(sources, TOK_DEV * TOPK).astype(jnp.int32)
    hits = (flat[:, :, None] == jnp.arange(EXPERTS, dtype=jnp.int32)[None, None, :]).astype(jnp.int32)
    ranks = lax.optimization_barrier(jnp.sum((jnp.cumsum(hits, axis=1) - 1) * hits, axis=2))
    slots = (jnp.arange(sources, dtype=jnp.int32)[:, None] * CAP + ranks).reshape(TOKENS, TOPK).astype(jnp.int32)
    owners = jnp.repeat(jnp.arange(TOKENS, dtype=jnp.int32), TOPK)
    flat_routes = routes.reshape(-1).astype(jnp.int32)
    flat_slots = slots.reshape(-1)
    rows = jnp.zeros((EXPERTS, sources * CAP), jnp.int32).at[flat_routes, flat_slots].set(owners)
    live = jnp.zeros((EXPERTS, sources * CAP), jnp.float32).at[flat_routes, flat_slots].set(1.0)
    return (slots, rows, live)

def forward(block_input, gain_input, proj_main, proj_state, proj_step, conv_main, conv_state, step_bias, decay_log, skip_gain, gain_gate, proj_out, gain_mix, router_weight, shared_gates, shared_down, expert_gates, expert_down, segments, routes, slots, rows, live):
    mixed_one = low(block_input * rms_scale(block_input) * gain_input)
    main_value = low_back(high_dot(mixed_one, proj_main.reshape(D, 2 * DI))).reshape(TOKENS, 2, DI)
    state_value = low_back(high_dot(mixed_one, proj_state))
    step_raw = low_back(high_dot(mixed_one, proj_step))
    gate_z = main_value[:, 0]
    conv_rows = jnp.concatenate([main_value[:, 1], state_value], axis=1)
    conv_weights = jnp.concatenate([conv_main, conv_state], axis=1)
    convolved = jax.vmap(conv_group, (0, None, 0))(conv_rows.reshape(GROUPS, SEQ, -1), conv_weights, segments)
    activated = low(convolved.reshape(TOKENS, -1))
    signal = activated[:, :DI]
    keys_state = activated[:, DI:DI + NSTATE]
    query_state = activated[:, DI + NSTATE:]
    step_size = jax.nn.softplus(step_raw + step_bias)
    log_decay = step_size * -jnp.exp(decay_log)
    heads_out = lax.map(group_scan, (signal.reshape(GROUPS, SEQ, HEADS, HDIM), step_size.reshape(GROUPS, SEQ, HEADS), log_decay.reshape(GROUPS, SEQ, HEADS), keys_state.reshape(GROUPS, SEQ, NSTATE), query_state.reshape(GROUPS, SEQ, NSTATE), segments))
    mixer = (heads_out.reshape(TOKENS, HEADS, HDIM) + skip_gain[None, :, None] * signal.reshape(TOKENS, HEADS, HDIM)).reshape(TOKENS, DI)
    gated = mixer * jax.nn.silu(gate_z)
    gated_out = low(gated * rms_scale(gated) * gain_gate)
    mixer_out = low_back(high_dot(gated_out, proj_out.T))
    residual = low(block_input + mixer_out)
    mixed_two = low(residual * rms_scale(residual) * gain_mix)
    logits = low_back(high_dot(mixed_two, router_weight))
    gates = jax.nn.softmax(jnp.take_along_axis(logits, routes, axis=1), axis=1)
    shared_value = low_back(high_dot(mixed_two, shared_gates.reshape(D, 2 * FS))).reshape(TOKENS, 2, FS)
    shared_hidden = low(jax.nn.silu(shared_value[:, 0]) * shared_value[:, 1])
    shared_out = low_back(high_dot(shared_hidden, shared_down.T))

    def one_expert(pieces):
        gate_weights, down_weights, row_ids, live_rows = pieces
        inputs = mixed_two[row_ids] * live_rows[:, None]
        value = low_back(high_dot(inputs, gate_weights.reshape(D, 2 * FE))).reshape(-1, 2, FE)
        hidden = low(jax.nn.silu(value[:, 0]) * value[:, 1])
        return low_back(high_dot(hidden, down_weights))
    expert_out = lax.map(jax.checkpoint(one_expert), (expert_gates, expert_down, rows, live))
    picked = expert_out[routes, slots]
    routed = lax.optimization_barrier(jnp.sum(gates[:, :, None] * picked, axis=1))
    return residual + routed + shared_out

def reference(block_input, gain_input, proj_main, proj_state, proj_step, conv_main, conv_state, step_bias, decay_log, skip_gain, gain_gate, proj_out, gain_mix, router_weight, shared_gates, shared_down, expert_gates, expert_down, segments, routes, cotangent):
    slots, rows, live = expert_tables(routes)
    floats = [value.astype(jnp.float32) for value in (block_input, gain_input, proj_main, proj_state, proj_step, conv_main, conv_state, step_bias, decay_log, skip_gain, gain_gate, proj_out, gain_mix, router_weight, shared_gates, shared_down, expert_gates, expert_down)]

    def bound(*values):
        return forward(*values, segments=segments, routes=routes, slots=slots, rows=rows, live=live)
    output, pull = jax.vjp(bound, *floats)
    grads = pull(cotangent.astype(jnp.float32))
    return (output.astype(jnp.bfloat16), grads[0], grads[1], grads[2], grads[3], grads[4], grads[5], grads[6], grads[7], grads[8], grads[9], grads[10], grads[11], grads[12], grads[13], grads[14], grads[15], grads[16], grads[17])
```

```python
from functools import partial

import jax
import jax.numpy as jnp
from jax import lax
from jax.experimental import pallas as pl
from jax.experimental.pallas import tpu as pltpu
from jax.sharding import PartitionSpec as P

CONV = 4
HALO = 16
LANES = 128
LANES = 128
LANES = 128


epsilon = 1e-05
highest = lax.Precision.HIGHEST
ROWS = ("shard", "ctx")
EVERY = ("shard", "ctx", "tensor")
f32 = jnp.float32
bf16 = jnp.bfloat16
BIG = pltpu.CompilerParams(vmem_limit_bytes=56 << 20)


def cost(micros):
    return pl.CostEstimate(flops=micros * 900_000_000, transcendentals=0, bytes_accessed=1 << 20)
BIG = pltpu.CompilerParams(vmem_limit_bytes=56 << 20)


def cost(micros):
    return pl.CostEstimate(flops=micros * 900_000_000, transcendentals=0, bytes_accessed=1 << 20)
BIG = pltpu.CompilerParams(vmem_limit_bytes=56 << 20)


def cost(micros):
    return pl.CostEstimate(flops=micros * 900_000_000, transcendentals=0, bytes_accessed=1 << 20)


def shifted(value, axis, steps):
    count = lax.axis_size(axis)
    leading, last = (max(0, -steps), min(count, count - steps))
    return lax.ppermute(value, axis, [(source, source + steps) for source in range(leading, last)])


def dot_rows(left, right, precision=None):
    return jnp.dot(left, right, preferred_element_type=f32, precision=precision)


def dot_inner(left, right):
    return lax.dot_general(left, right, (((0,), (0,)), ((), ())), preferred_element_type=f32)


def dot_outer(left, right):
    return lax.dot_general(left, right, (((1,), (1,)), ((), ())), preferred_element_type=f32)


def sigmoid(value):
    return 1.0 / (1.0 + jnp.exp(-value))


def gather_rows(value):
    return lax.all_gather(value, ROWS, axis=0, tiled=True)


def scatter_rows(value):
    return lax.psum_scatter(value, ROWS, scatter_dimension=0, tiled=True)


def exchange(blocks):
    return lax.all_to_all(blocks, "tensor", split_axis=0, concat_axis=0, tiled=True)


def spread(block):
    count = lax.axis_size("tensor")
    return exchange(jnp.broadcast_to(block[None], (count,) + block.shape))


def spread_small(block):
    count, index = lax.axis_size("tensor"), lax.axis_index("tensor")
    width = block.shape[1]
    full = jnp.zeros((block.shape[0], count * width), block.dtype)
    for away in range(count):
        moved = block if away == 0 else lax.ppermute(
            block, "tensor", [(i, (i + away) % count) for i in range(count)]
        )
        origin = lax.rem(index - away + count, count)
        full = lax.dynamic_update_slice_in_dim(full, moved, origin * width, 1)
    return full


def halves(value):
    high = value.astype(bf16)
    return high, (value - high.astype(f32)).astype(bf16)


def chain(through, state, reverse):
    count = lax.axis_size("ctx")
    width = state.shape[0] // through.shape[0]
    packed = (through, state.astype(bf16))
    passed, total = None, None
    for away in range(1, count):
        far_through, far_state = jax.tree.map(
            lambda part: shifted(part, "ctx", -away if reverse else away), packed
        )
        far_state = far_state.astype(f32)
        if total is None:
            total, passed = far_state, far_through
        else:
            total = total + jnp.repeat(passed, width)[:, None] * far_state
            passed = passed * far_through
    return total


def row_iota(shape):
    return lax.broadcasted_iota(jnp.int32, shape, 0)


def col_iota(shape):
    return lax.broadcasted_iota(jnp.int32, shape, 1)


def expander(lanes, width, per):
    low = row_iota((lanes, width)) * per
    at = col_iota((lanes, width))
    return ((at >= low) & (at < low + per)).astype(f32)


def head_fold(width, lanes, per):
    low = col_iota((width, lanes)) * per
    at = row_iota((width, lanes))
    return ((at >= low) & (at < low + per)).astype(f32)


def fold_heads(value, folds):
    high, low = halves(value)
    return dot_rows(high, folds) + dot_rows(low, folds)


def conv_pre(value_ref, column, taps_ref, taps_column, same_ref, tokens):
    rows = value_ref[:, pl.ds(column, LANES)]
    total = None
    for offset in range(CONV):
        first = HALO - CONV + 1 + offset
        term = rows[first : first + tokens] * (
            same_ref[offset] * taps_ref[offset : offset + 1, pl.ds(taps_column, LANES)]
        )
        total = term if total is None else total + term
    return rows, total


def enter_kernel(mixed_ref, w_ref, taps_ref, same_ref, bias_ref, decay_ref, end_ref,
                 value_ref, act_ref, scaled_ref, step_ref, run_ref, run_exp_ref,
                 state_ref, *, inner, nstate, per):
    tokens = act_ref.shape[0]
    width = w_ref.shape[1]
    tile = 384

    def matmul(i, _):
        columns = pl.ds(pl.multiple_of(i * tile, LANES), tile)
        value_ref[:, columns] = dot_rows(mixed_ref[...], w_ref[:, columns])
        return 0

    lax.fori_loop(0, width // tile, matmul, 0)

    def conv(i, _):
        at = pl.multiple_of(i * LANES, LANES)
        _, total = conv_pre(value_ref, inner + at, taps_ref, at, same_ref, tokens)
        act_ref[:, pl.ds(at, LANES)] = (total * sigmoid(total)).astype(bf16)
        return 0

    lax.fori_loop(0, (inner + 2 * nstate) // LANES, conv, 0)
    raw = value_ref[HALO:, 2 * inner + 2 * nstate :] + bias_ref[...]
    step = jnp.maximum(raw, 0.0) + jnp.log1p(jnp.exp(-jnp.abs(raw)))
    log_decay = step * -jnp.exp(decay_ref[...])
    tri = (row_iota((tokens, tokens)) >= col_iota((tokens, tokens))).astype(f32)
    running = dot_rows(tri, log_decay, highest)
    step_ref[...] = step
    run_ref[...] = running
    grow = expander(LANES, inner, per)
    run_exp_ref[...] = dot_rows(running, grow, highest)
    signal = act_ref[:, :inner].astype(f32)
    scaled_ref[...] = (signal * dot_rows(step, grow, highest)).astype(bf16)
    toward = step * jnp.exp(running[tokens - 1 :] - running) * end_ref[...]
    pushed = (signal * dot_rows(toward, grow, highest)).astype(bf16)
    state_ref[...] = dot_inner(pushed, act_ref[:, inner : inner + nstate])


def enter(mixed_ext, main_w, taps, same, bias, decay, at_end, inner, nstate, per):
    ext = mixed_ext.shape[0]
    tokens = ext - HALO
    shape = jax.ShapeDtypeStruct
    return pl.pallas_call(
        partial(enter_kernel, inner=inner, nstate=nstate, per=per),
        out_shape=[
            shape((ext, main_w.shape[1]), f32), shape((tokens, inner + 2 * nstate), bf16),
            shape((tokens, inner), bf16), shape((tokens, LANES), f32), shape((tokens, LANES), f32),
            shape((tokens, inner), f32), shape((inner, nstate), f32),
        ],
        compiler_params=BIG,
        cost_estimate=cost(8),
        name="enter",
    )(mixed_ext, main_w, taps, same, bias, decay, at_end)


def masked_scores(query, keys, seg_col_ref, seg_row_ref, start, stop):
    shape = (stop - start, stop)
    allowed = (row_iota(shape) + start >= col_iota(shape)) & (
        seg_col_ref[start:stop, :1] == seg_row_ref[:, :stop]
    )
    return jnp.where(allowed, dot_outer(query[start:stop], keys[:stop]), 0.0)


def intra_kernel(act_ref, scaled_ref, run_t_ref, run_exp_ref, seg_col_ref, seg_row_ref,
                 inner_ref, scores_ref, *, inner, nstate, per, block):
    tokens = act_ref.shape[0]
    keys = act_ref[:, inner : inner + nstate]
    query = act_ref[:, inner + nstate :]
    for start in range(0, tokens, block):
        stop = start + block
        scores_ref[start:stop, :stop] = masked_scores(
            query, keys, seg_col_ref, seg_row_ref, start, stop
        )

    def pair(i, _):
        columns = pl.ds(pl.multiple_of(i * LANES, LANES), LANES)
        scaled = scaled_ref[:, columns]
        lane = col_iota(scaled.shape)
        run = run_exp_ref[:, columns]
        for start in range(0, tokens, block):
            stop = start + block
            total = None
            for h in range(LANES // per):
                mine = (lane >= h * per) & (lane < (h + 1) * per)
                vals = jnp.where(mine, scaled, jnp.zeros_like(scaled))[:stop]
                row = run_t_ref[i * (LANES // per) + h, :, :stop]
                decay = jnp.exp(jnp.minimum(run[start:stop, h * per : h * per + 1] - row, 0.0))
                weight = (decay * scores_ref[start:stop, :stop]).astype(bf16)
                term = dot_rows(weight, vals)
                total = term if total is None else total + term
            inner_ref[start:stop, columns] = total
        return 0

    lax.fori_loop(0, inner // LANES, pair, 0)


def intra(act, scaled, run_t, run_exp, seg_col, seg_row, inner, nstate, per):
    tokens = act.shape[0]
    return pl.pallas_call(
        partial(intra_kernel, inner=inner, nstate=nstate, per=per, block=128),
        out_shape=jax.ShapeDtypeStruct((tokens, inner), f32),
        scratch_shapes=[pltpu.VMEM((tokens, tokens), f32)],
        compiler_params=BIG,
        cost_estimate=cost(10),
        name="intra",
    )(act, scaled, run_t, run_exp, seg_col, seg_row)


def leave_kernel(act_ref, inner_ref, z_ref, state_ref, run_exp_ref, link_ref, skip_ref, gain_ref,
                 w_ref, mixer_ref, part_ref, *, inner, nstate):
    depth = w_ref.shape[0]
    tokens = act_ref.shape[0]
    query = act_ref[:, inner + nstate :]
    carried = dot_outer(query, state_ref[...].astype(bf16)) * (
        jnp.exp(run_exp_ref[...]) * link_ref[...]
    )
    mixer = inner_ref[...] + carried + skip_ref[...] * act_ref[:, :inner].astype(f32)
    mixer_ref[...] = mixer
    z = z_ref[HALO:, :]
    gated = mixer * (z * sigmoid(z))
    high, low = halves(jnp.sum(gated * gated, axis=1, keepdims=True))
    lane = col_iota((tokens, LANES))
    part_ref[:, depth:] = jnp.where(lane == 0, high, jnp.where(lane == 1, low, jnp.zeros_like(low)))
    lifted = (gated * gain_ref[...]).astype(bf16)
    part_ref[:, :depth] = dot_outer(lifted, w_ref[...]).astype(bf16)


def leave(act, within, value, state, run_exp, link, skip, gain, mid_w, inner, nstate):
    tokens = act.shape[0]
    depth = mid_w.shape[0]
    full = lambda a: pl.BlockSpec(a.shape, lambda i: (0,) * a.ndim)
    columns = lambda a: pl.BlockSpec((a.shape[0], inner), lambda i: (0, 0))
    return pl.pallas_call(
        partial(leave_kernel, inner=inner, nstate=nstate),
        grid=(1,),
        in_specs=[full(act), full(within), columns(value), full(state), full(run_exp), full(link),
                  full(skip), full(gain), columns(mid_w)],
        out_specs=[pl.BlockSpec((tokens, inner), lambda i: (0, 0)),
                   pl.BlockSpec((tokens, depth + LANES), lambda i: (0, 0))],
        out_shape=[jax.ShapeDtypeStruct((tokens, inner), f32),
                   jax.ShapeDtypeStruct((tokens, depth + LANES), bf16)],
        compiler_params=BIG,
        cost_estimate=cost(8),
        name="leave",
    )(act, within, value, state, run_exp, link, skip, gain, mid_w)


def back_kernel(dout_ref, w_ref, mixer_ref, z_ref, act_ref, run_exp_ref, link_ref, gain_ref,
                stat_ref, heads_ref, zgrad_ref, gated_ref, direct_ref, sums_ref,
                *, inner, nstate, di_all):
    scale = stat_ref[:, 0:1]
    cross = stat_ref[:, 1:2]
    mixer = mixer_ref[...]
    z = z_ref[HALO:, :]
    sig = sigmoid(z)
    act = z * sig
    gated = mixer * act
    grad = dot_rows(dout_ref[...], w_ref[...])
    gated_ref[...] = (gated * scale * gain_ref[...]).astype(bf16)
    sums_ref[0:1, :] = jnp.sum(grad * gated * scale, axis=0, keepdims=True)
    gated_grad = scale * (grad * gain_ref[...]) - gated * (scale * scale * scale * cross / di_all)
    zgrad_ref[...] = (gated_grad * mixer * (sig * (1.0 + z * (1.0 - sig)))).astype(bf16)
    heads = gated_grad * act
    heads_ref[...] = heads
    sums_ref[1:2, :] = jnp.sum(heads * act_ref[:, :inner].astype(f32), axis=0, keepdims=True)
    sums_ref[2:, :] = jnp.zeros((6, inner), f32)
    carried = (heads * (jnp.exp(run_exp_ref[...]) * link_ref[...])).astype(bf16)
    direct_ref[...] = dot_inner(carried, act_ref[:, inner + nstate :])


def back(dout, mid_w, mixer, value, act, run_exp, link, gain, stats, inner, nstate, di_all):
    tokens = act.shape[0]
    full = lambda a: pl.BlockSpec(a.shape, lambda i: (0,) * a.ndim)
    columns = lambda a: pl.BlockSpec((a.shape[0], inner), lambda i: (0, 0))
    shape = jax.ShapeDtypeStruct
    outs = [shape((tokens, inner), f32), shape((tokens, inner), bf16), shape((tokens, inner), bf16),
            shape((inner, nstate), f32), shape((8, inner), f32)]
    return pl.pallas_call(
        partial(back_kernel, inner=inner, nstate=nstate, di_all=di_all),
        grid=(1,),
        in_specs=[pl.BlockSpec((tokens, mid_w.shape[0]), lambda i: (0, 0)), columns(mid_w),
                  full(mixer), columns(value), full(act), full(run_exp), full(link),
                  full(gain), full(stats)],
        out_specs=[full(o) for o in outs],
        out_shape=outs,
        compiler_params=BIG,
        cost_estimate=cost(8),
        name="back",
    )(dout, mid_w, mixer, value, act, run_exp, link, gain, stats)


def intra_back_kernel(heads_ref, act_ref, scaled_ref, run_t_ref, run_exp_ref, seg_col_ref,
                      seg_row_ref, dscaled_ref, dstate_ref, drun_ref, scores_ref, dscores_ref,
                      rows_ref, *, inner, nstate, per, block):
    tokens = act_ref.shape[0]
    keys = act_ref[:, inner : inner + nstate]
    query = act_ref[:, inner + nstate :]
    for start in range(0, tokens, block):
        stop = start + block
        scores_ref[start:stop, :stop] = masked_scores(
            query, keys, seg_col_ref, seg_row_ref, start, stop
        )
    dscores_ref[...] = jnp.zeros_like(dscores_ref)
    drun_ref[...] = jnp.zeros_like(drun_ref)

    def pair(i, _):
        columns = pl.ds(pl.multiple_of(i * LANES, LANES), LANES)
        scaled = scaled_ref[:, columns]
        heads = heads_ref[:, columns].astype(bf16)
        lane = col_iota(scaled.shape)
        run = run_exp_ref[:, columns]
        dscaled_ref[:, columns] = jnp.zeros((tokens, LANES), f32)
        for h in range(LANES // per):
            head = i * (LANES // per) + h
            mine = (lane >= h * per) & (lane < (h + 1) * per)
            vals = jnp.where(mine, scaled, jnp.zeros_like(scaled))
            grads = jnp.where(mine, heads, jnp.zeros_like(heads))
            pick = (col_iota((block, LANES)) == head).astype(bf16)
            for start in range(0, tokens, block):
                stop = start + block
                row = run_t_ref[head, :, :stop]
                decay = jnp.exp(jnp.minimum(run[start:stop, h * per : h * per + 1] - row, 0.0))
                weight = decay * scores_ref[start:stop, :stop]
                dweight = dot_outer(grads[start:stop], vals[:stop])
                dscores_ref[start:stop, :stop] += dweight * decay
                flow = (dweight * weight).astype(bf16)
                dscaled_ref[:stop, columns] += dot_inner(weight.astype(bf16), grads[start:stop])
                picks = jnp.broadcast_to(pick[:1], (stop, LANES))
                drun_ref[start:stop, :] += dot_rows(flow, picks)
                drun_ref[:stop, :] -= dot_inner(flow, pick)
        return 0

    lax.fori_loop(0, inner // LANES, pair, 0)
    dkeys = jnp.zeros((tokens, nstate), f32)
    dstate_ref[:, :nstate] = dkeys
    for start in range(0, tokens, block):
        stop = start + block
        shape = (block, stop)
        allowed = (row_iota(shape) + start >= col_iota(shape)) & (
            seg_col_ref[start:stop, :1] == seg_row_ref[:, :stop]
        )
        grad = jnp.where(allowed, dscores_ref[start:stop, :stop], 0.0).astype(bf16)
        dstate_ref[start:stop, nstate:] = dot_rows(grad, keys[:stop])
        dstate_ref[:stop, :nstate] += dot_inner(grad, query[start:stop])


def intra_back(heads, act, scaled, run_t, run_exp, seg_col, seg_row, inner, nstate, per):
    tokens = act.shape[0]
    shape = jax.ShapeDtypeStruct
    return pl.pallas_call(
        partial(intra_back_kernel, inner=inner, nstate=nstate, per=per, block=128),
        out_shape=[shape((tokens, inner), f32), shape((tokens, 2 * nstate), f32),
                   shape((tokens, LANES), f32)],
        scratch_shapes=[pltpu.VMEM((tokens, tokens), f32), pltpu.VMEM((tokens, tokens), f32),
                        pltpu.VMEM((8, LANES), f32)],
        compiler_params=BIG,
        cost_estimate=cost(20),
        name="intra_back",
    )(heads, act, scaled, run_t, run_exp, seg_col, seg_row)


def exit_kernel(heads_ref, act_ref, scaled_ref, step_ref, run_ref, run_exp_ref, link_ref,
                end_ref, value_ref, taps_ref, same_ref, bias_ref, decay_ref, skip_ref,
                mixer_ref, inner_ref, dscaled_ref, dstate_ref, drun_ref, in_ref, out_ref,
                through_ref, zgrad_ref,
                grad_ref, dtaps_ref, small_ref, pad_ref, *, inner, nstate, per):
    tokens = act_ref.shape[0]
    keys = act_ref[:, inner : inner + nstate]
    signal = act_ref[:, :inner].astype(f32)
    grow = expander(LANES, inner, per)
    folds = head_fold(inner, LANES, per).astype(bf16)
    step = step_ref[...]
    running = run_ref[...]
    state_grad = out_ref[...]
    heads = heads_ref[...]
    weight = jnp.exp(run_exp_ref[...]) * link_ref[...]
    carried = mixer_ref[...] - inner_ref[...] - skip_ref[...] * signal
    lifted = (heads * weight).astype(bf16)
    dquery = dot_rows(lifted, in_ref[...].astype(bf16)) + dstate_ref[:, nstate:]
    toward = jnp.exp(running[tokens - 1 :] - running) * end_ref[...]
    toward_exp = dot_rows(toward, grow, highest)
    step_exp = dot_rows(step, grow, highest)
    leaving = dot_outer(keys, state_grad.astype(bf16)) * toward_exp
    pushed = (signal * step_exp * toward_exp).astype(bf16)
    dkeys = dot_rows(pushed, state_grad.astype(bf16)) + dstate_ref[:, :nstate]
    dscaled = dscaled_ref[...] + leaving
    tri = (row_iota((tokens, tokens)) <= col_iota((tokens, tokens))).astype(f32)
    strict = (row_iota((tokens, tokens)) > col_iota((tokens, tokens))).astype(f32)
    kept = jnp.sum(in_ref[...] * state_grad, axis=1, keepdims=True)
    kept = jnp.sum(head_fold(inner, LANES, per) * kept, axis=0, keepdims=True) * through_ref[...]
    back_sum = drun_ref[...] + fold_heads(heads * carried, folds)
    front_sum = fold_heads(signal * step_exp * leaving, folds)
    dlog = dot_rows(tri, back_sum, highest) + dot_rows(strict, front_sum, highest) + kept
    rate = -jnp.exp(decay_ref[...])
    dstep = dlog * rate + fold_heads(dscaled * signal, folds)
    raw = value_ref[HALO:, 2 * inner + 2 * nstate :] + bias_ref[...]
    draw = dstep * sigmoid(raw)
    small_ref[0:1, :] = jnp.sum(draw, axis=0, keepdims=True)
    small_ref[1:2, :] = jnp.sum(dlog * step, axis=0, keepdims=True) * rate
    small_ref[2:, :] = jnp.zeros((6, LANES), f32)
    ext = tokens + HALO
    grad_ref[:HALO, :inner] = jnp.zeros((HALO, inner), bf16)
    grad_ref[HALO:, :inner] = zgrad_ref[...]
    grad_ref[:HALO, 2 * inner + 2 * nstate :] = jnp.zeros((HALO, LANES), bf16)
    used = col_iota((tokens, LANES)) < inner // per
    grad_ref[HALO:, 2 * inner + 2 * nstate :] = jnp.where(used, draw, 0.0).astype(bf16)
    pad_ref[:, :inner] = dscaled * step_exp + skip_ref[...] * heads
    pad_ref[:, inner : inner + nstate] = dkeys
    pad_ref[:, inner + nstate :] = dquery

    def conv(i, _):
        at = pl.multiple_of(i * LANES, LANES)
        rows, total = conv_pre(value_ref, inner + at, taps_ref, at, same_ref, tokens)
        sig = sigmoid(total)
        dpre = pad_ref[:, pl.ds(at, LANES)] * (sig * (1.0 + total * (1.0 - sig)))
        drows = None
        for offset in range(CONV):
            first = HALO - CONV + 1 + offset
            kept = dpre * same_ref[offset]
            dtaps_ref[offset : offset + 1, pl.ds(at, LANES)] = jnp.sum(
                kept * rows[first : first + tokens], axis=0, keepdims=True
            )
            term = kept * taps_ref[offset : offset + 1, pl.ds(at, LANES)]
            term = jnp.concatenate(
                [jnp.zeros((first, LANES), f32), term,
                 jnp.zeros((ext - first - tokens, LANES), f32)][: 3 if ext > first + tokens else 2],
                axis=0,
            )
            drows = term if drows is None else drows + term
        grad_ref[:, pl.ds(inner + at, LANES)] = drows.astype(bf16)
        return 0

    lax.fori_loop(0, (inner + 2 * nstate) // LANES, conv, 0)


def exits(args, inner, nstate, per):
    tokens = args[1].shape[0]
    wide = args[8].shape[1]
    shape = jax.ShapeDtypeStruct
    return pl.pallas_call(
        partial(exit_kernel, inner=inner, nstate=nstate, per=per),
        out_shape=[shape((tokens + HALO, wide), bf16), shape((CONV, inner + 2 * nstate), f32),
                   shape((8, LANES), f32)],
        scratch_shapes=[pltpu.VMEM((tokens, inner + 2 * nstate), f32)],
        compiler_params=BIG,
        cost_estimate=cost(15),
        name="exits",
    )(*args)


def experts_kernel(mix_ref, cot_ref, gate_ref, w_ref, out_in, dmix_in,
                   out_ref, dmix_ref, dgate_ref, dw_ref, down_ref, hidden_ref, dval_ref, *, tile):
    @pl.when(pl.program_id(0) == 0)
    def _():
        out_ref[...] = out_in[...]
        dmix_ref[...] = dmix_in[...]

    rows, depth = mix_ref.shape
    wide = w_ref.shape[3]
    hid = wide // 2
    chunks = depth // wide
    for p in range(2):
        for c in range(chunks):
            down_ref[p * hid : (p + 1) * hid, c * wide : (c + 1) * wide] = (
                w_ref[0, p, depth + c * hid : depth + (c + 1) * hid, :]
            )
    down = down_ref[...]

    def part(i, _):
        at = pl.ds(pl.multiple_of(i * tile, tile), tile)
        mix = mix_ref[at, :]
        dh_raw = dot_outer(cot_ref[at, :], down)
        dmix = None
        for p in range(2):
            gate = gate_ref[0, at, p : p + 1]
            value = dot_rows(mix, w_ref[0, p, :depth, :])
            first, second = value[:, :hid], value[:, hid:]
            sig = sigmoid(first)
            act = first * sig
            hidden = (act * second).astype(bf16).astype(f32)
            raw = dh_raw[:, p * hid : (p + 1) * hid]
            dgate_ref[0, at, p : p + 1] = jnp.sum(hidden * raw, axis=1, keepdims=True)
            dh = gate * raw
            dval_ref[p, at, :hid] = (dh * second * (sig * (1.0 + first * (1.0 - sig)))).astype(bf16)
            dval_ref[p, at, hid:] = (dh * act).astype(bf16)
            hidden_ref[at, p * hid : (p + 1) * hid] = (gate * hidden).astype(bf16)
            term = dot_outer(dval_ref[p, at, :], w_ref[0, p, :depth, :])
            dmix = term if dmix is None else dmix + term
        out_ref[at, :] += dot_rows(hidden_ref[at, :], down)
        dmix_ref[at, :] += dmix
        return 0

    lax.fori_loop(0, rows // tile, part, 0)
    for c in range(chunks):
        grad = dot_inner(hidden_ref[...], cot_ref[:, c * wide : (c + 1) * wide]).astype(bf16)
        for p in range(2):
            dw_ref[0, p, depth + c * hid : depth + (c + 1) * hid, :] = grad[p * hid : (p + 1) * hid]
    for p in range(2):
        dw_ref[0, p, :depth, :] = dot_inner(mix_ref[...], dval_ref[p]).astype(bf16)


def experts(mix, cot, gate, weights, out, dmix):
    pairs, _, deep, wide = weights.shape
    rows, depth = mix.shape
    whole = lambda shape: pl.BlockSpec(shape, lambda i: (0,) * len(shape))
    each = lambda shape: pl.BlockSpec((1,) + shape, lambda i: (i,) + (0,) * len(shape))
    return pl.pallas_call(
        partial(experts_kernel, tile=min(256, rows)),
        grid=(pairs,),
        in_specs=[
            whole((rows, depth)), pl.BlockSpec((rows, depth), lambda i: (0, 0)), each((rows, 2)),
            each((2, deep, wide)), whole((rows, depth)), whole((rows, depth)),
        ],
        out_specs=[
            whole((rows, depth)), whole((rows, depth)), each((rows, 2)), each((2, deep, wide)),
        ],
        out_shape=[
            jax.ShapeDtypeStruct((rows, depth), f32), jax.ShapeDtypeStruct((rows, depth), f32),
            jax.ShapeDtypeStruct((pairs, rows, 2), f32),
            jax.ShapeDtypeStruct(weights.shape, bf16),
        ],
        scratch_shapes=[
            pltpu.VMEM((wide, depth), bf16), pltpu.VMEM((rows, wide), bf16),
            pltpu.VMEM((2, rows, wide), bf16),
        ],
        compiler_params=BIG,
        cost_estimate=cost(6 * pairs),
        name="experts",
    )(mix, cot, gate, weights, out, dmix)


def pack_experts(gates, down):
    count, depth, wide = gates.shape
    hid = wide // 2
    down = down.reshape(count, hid, depth // wide, wide).transpose(0, 2, 1, 3)
    return jnp.concatenate([gates, down.reshape(count, -1, wide)], axis=1)


def unpack_experts(packed):
    count, deep, wide = packed.shape
    hid = wide // 2
    depth = deep * 2 // 3
    down = packed[:, depth:].reshape(count, depth // wide, hid, wide).transpose(0, 2, 1, 3)
    return packed[:, :depth], down.reshape(count, hid, depth)


def local(
    block_input, gain_input, proj_main, proj_state, proj_step, conv_main, conv_state, step_bias,
    decay_log, skip_gain, gain_gate, proj_out, gain_mix, router_weight, shared_gates, shared_down,
    expert_gates, expert_down, segments, routes, cotangent,
):
    tokens, quarter = block_input.shape
    heads = step_bias.shape[0]
    inner = conv_main.shape[1]
    nstate = conv_state.shape[1] // 2
    per = inner // heads
    tensors = lax.axis_size("tensor")
    zi = lax.axis_index("tensor")
    senders = lax.axis_size(ROWS)
    depth = quarter * tensors
    di_all = inner * tensors
    own = tokens // tensors
    column = zi * quarter
    row0 = zi * own
    wrows = proj_main.shape[0]
    hid = expert_gates.shape[3]
    local_experts = expert_gates.shape[0]
    experts_all = local_experts * senders
    shared_here = shared_down.shape[1]
    router_pad = -experts_all % LANES

    main_w = gather_rows(
        jnp.concatenate(
            [proj_main[:, 0], proj_main[:, 1], proj_state,
             jnp.pad(proj_step, ((0, 0), (0, LANES - heads)))], axis=1
        )
    )
    shared_pair = shared_gates.reshape(wrows, 2, 2, shared_here // 2).transpose(0, 2, 1, 3)
    mid_w = gather_rows(
        jnp.concatenate(
            [proj_out, shared_pair.reshape(wrows, -1), shared_down,
             jnp.pad(router_weight, ((0, 0), (0, router_pad)))], axis=1
        )
    )
    expert_w = gather_rows(
        pack_experts(expert_gates.reshape(local_experts, depth, 2 * hid), expert_down)[None]
    )
    at_down = inner + 2 * shared_here
    at_router = at_down + shared_here
    router_full = mid_w[:, at_router : at_router + experts_all]
    shared_w = pack_experts(
        jnp.stack([mid_w[:, inner : inner + shared_here], mid_w[:, inner + shared_here : at_down]]),
        mid_w[:, at_down:at_router].T.reshape(2, shared_here // 2, depth),
    )[None]

    seg_row = segments[0]
    last = jnp.concatenate(
        [block_input[tokens - CONV + 1 :],
         jnp.pad(seg_row[None, tokens - CONV + 1 :].astype(bf16), ((0, 0), (0, quarter - CONV + 1)))], axis=0
    )
    halo = shifted(last, "ctx", 1)
    halo_seg = halo[CONV - 1, : CONV - 1].astype(jnp.int32)
    extra = jnp.concatenate(
        [jnp.zeros((HALO - CONV + 1, quarter), bf16), halo[: CONV - 1], gain_input[None],
         gain_mix[None], jnp.zeros((14, quarter), bf16)], axis=0
    )
    wide = lambda got: got.transpose(1, 0, 2).reshape(got.shape[1], depth)
    got = spread(block_input)
    cotangent, got = lax.optimization_barrier((cotangent, got))
    got = wide(got)
    got_extra = spread_small(extra)
    cot_full = wide(spread(cotangent))
    gain_row = got_extra[HALO].astype(f32)
    gain_mid = got_extra[HALO + 1].astype(f32)
    x_ext = jnp.concatenate([got_extra[:HALO], got], axis=0).astype(f32)
    scale_ext = lax.rsqrt(jnp.mean(x_ext * x_ext, axis=-1, keepdims=True) + epsilon)
    normed_ext = x_ext * scale_ext
    mixed_ext = (normed_ext * gain_row).astype(bf16)

    segments_ext = jnp.concatenate([halo_seg, seg_row], axis=0)
    same = jnp.stack(
        [segments_ext[offset : offset + tokens] == seg_row for offset in range(CONV)]
    ).astype(f32)
    same = jnp.broadcast_to(same[:, :, None], (CONV, tokens, LANES))
    taps = jnp.concatenate([conv_main, conv_state], axis=1).astype(f32)
    lanes = lambda v: jnp.pad(v, (0, LANES - heads))[None]
    bias = lanes(step_bias)
    decay = lanes(decay_log)
    skip = jnp.repeat(skip_gain, per)[None]
    link = (seg_row == halo_seg[-1]).astype(f32)[:, None]
    at_end = (seg_row == seg_row[-1]).astype(f32)[:, None]
    seg_col = seg_row[:, None]
    seg_line = seg_row[None]
    value, act, scaled, step, running, run_exp, state_local = enter(
        mixed_ext, main_w, taps, same, bias, decay, at_end, inner, nstate, per
    )
    run_t = running[:, :heads].T[:, None, :]
    through_row = jnp.exp(running[-1]) * link[-1]
    through = through_row[:heads]
    state_in = chain(through, state_local, False)
    within = intra(act, scaled, run_t, run_exp, seg_col, seg_line, inner, nstate, per)
    gain_gate_f = gain_gate.astype(f32)[None, :]
    mixer, part = leave(
        act, within, value, state_in, run_exp, link, skip, gain_gate_f, mid_w, inner, nstate
    )
    part, cot_full = lax.optimization_barrier((part, cot_full))
    parts = jnp.sum(exchange(part.reshape(tensors, own, -1)).astype(f32), axis=0)
    scale_own = lax.rsqrt((parts[:, depth] + parts[:, depth + 1]) / di_all + epsilon)
    input_own = lax.dynamic_slice_in_dim(x_ext, row0 + HALO, own, 0)
    residual_own = (input_own + parts[:, :depth] * scale_own[:, None]).astype(bf16)
    scale_cols = jnp.pad(jnp.stack(halves(scale_own), axis=1), ((0, 0), (0, LANES - 2)))
    middle = spread(jnp.concatenate([residual_own, scale_cols], axis=1)).reshape(tokens, -1)
    residual = middle[:, :depth]
    gated_scale = middle[:, depth].astype(f32) + middle[:, depth + 1].astype(f32)

    res_f = residual.astype(f32)
    scale_two = lax.rsqrt(jnp.mean(res_f * res_f, axis=-1, keepdims=True) + epsilon)
    mixed_two = (res_f * scale_two * gain_mid).astype(bf16)
    logits = dot_rows(mixed_two, router_full)
    expert_ids = jnp.arange(experts_all, dtype=jnp.int32)
    chosen = jnp.any(routes[:, :, None] == expert_ids[None, None, :], axis=1)
    top = jnp.max(jnp.where(chosen, logits, -jnp.inf), axis=1, keepdims=True)
    weight = jnp.where(chosen, jnp.exp(jnp.where(chosen, logits - top, 0.0)), 0.0)
    gates = weight / jnp.sum(weight, axis=1, keepdims=True)
    zero = jnp.zeros((tokens, depth), f32)
    ones = jnp.ones((1, tokens, 2), f32)
    out_part, dmix_part, _, shared_grad = experts(mixed_two, cot_full, ones, shared_w, zero, zero)
    gate_pairs = gates.reshape(tokens, senders, local_experts).transpose(1, 0, 2)
    out_part, dmix_part, dgate, expert_grad = experts(
        mixed_two, cot_full, gate_pairs, expert_w, out_part, dmix_part
    )
    deep = expert_grad.shape[2]
    expert_rows = scatter_rows(expert_grad.reshape(-1, 2 * hid)).reshape(local_experts, deep, 2 * hid)

    dgate = dgate.transpose(1, 0, 2).reshape(tokens, experts_all)
    router_grad = lambda moved: (
        gates * (moved - jnp.sum(gates * moved, axis=1, keepdims=True))
    ).astype(bf16)
    dmix_part = (dmix_part + dot_outer(router_grad(dgate), router_full)).astype(bf16)
    marks = jnp.concatenate(halves(dgate), axis=1)
    mark_pad = -marks.shape[1] % LANES
    moved = exchange(
        jnp.concatenate([dmix_part, jnp.pad(marks, ((0, 0), (0, mark_pad)))], axis=1)
        .reshape(tensors, own, -1)
    )
    moved = jnp.sum(moved.astype(f32), axis=0)
    dmix = moved[:, :depth]
    dgate_own = moved[:, depth : depth + experts_all] + moved[:, depth + experts_all : depth + 2 * experts_all]
    res_own = residual_own.astype(f32)
    scale_mid = lax.rsqrt(jnp.mean(res_own * res_own, axis=-1, keepdims=True) + epsilon)
    normed_mid = res_own * scale_mid
    grad_gain_mix = jnp.sum(dmix * normed_mid, axis=0)
    lifted_mid = dmix * gain_mid
    cross_mid = jnp.mean(lifted_mid * normed_mid, axis=1, keepdims=True)
    cot_own = lax.dynamic_slice_in_dim(cot_full, row0, own, 0).astype(f32)
    dres_own = (cot_own + scale_mid * (lifted_mid - normed_mid * cross_mid)).astype(bf16)
    cross_own = jnp.sum(dres_own.astype(f32) * parts[:, :depth], axis=1, keepdims=True)
    notes = jnp.concatenate(halves(cross_own) + halves(dgate_own), axis=1)
    dres_all = spread(
        jnp.concatenate([dres_own, jnp.pad(notes, ((0, 0), (0, -notes.shape[1] % LANES)))], axis=1)
    ).reshape(tokens, -1)
    dmixer = dres_all[:, :depth]
    cross = dres_all[:, depth].astype(f32) + dres_all[:, depth + 1].astype(f32)
    first = depth + 2
    dgate_all = (dres_all[:, first : first + experts_all].astype(f32)
                 + dres_all[:, first + experts_all : first + 2 * experts_all].astype(f32))

    stats = jnp.stack([gated_scale, cross], axis=1)
    heads_grad, z_grad, gated_out, direct, sums = back(
        dres_all, mid_w, mixer, value, act, run_exp, link, gain_gate_f, stats, inner, nstate, di_all
    )
    state_grad = chain(through, direct, True)
    dscaled, dstate, drun = intra_back(
        heads_grad, act, scaled, run_t, run_exp, seg_col, seg_line, inner, nstate, per
    )
    value_grad, dtaps, small_sums = exits(
        (heads_grad, act, scaled, step, running, run_exp, link, at_end, value, taps, same, bias,
         decay, skip, mixer, within, dscaled, dstate, drun, state_in, state_grad,
         through_row[None], z_grad),
        inner, nstate, per,
    )
    first = 2 * inner
    last = first + 2 * nstate
    halo_back = shifted(value_grad[:HALO], "ctx", -1)
    mixed_grad = dot_outer(value_grad[HALO:], main_w)
    mixed_grad = mixed_grad.at[tokens - HALO :].add(dot_outer(halo_back, main_w))
    normed_one = normed_ext[HALO:]
    scale_one = scale_ext[HALO:]
    grad_gain_part = jnp.sum(mixed_grad * normed_one, axis=0)
    cross_part = jnp.concatenate(
        halves(jnp.sum(mixed_grad * gain_row * normed_one, axis=1, keepdims=True)), axis=1
    )
    cross_part = jnp.pad(cross_part, ((0, 0), (0, LANES - 2)))
    blocks = mixed_grad.astype(bf16).reshape(tokens, tensors, quarter).transpose(1, 0, 2)
    summed = jnp.sum(
        exchange(
            jnp.concatenate(
                [blocks, jnp.broadcast_to(cross_part[None], (tensors,) + cross_part.shape)], axis=2
            )
        ).astype(f32), axis=0,
    )
    normed_slice = lax.dynamic_slice_in_dim(normed_one, column, quarter, 1)
    cross_one = (summed[:, quarter] + summed[:, quarter + 1])[:, None]
    grad_input = (
        lax.dynamic_slice_in_dim(dmixer, column, quarter, 1).astype(f32)
        + scale_one * (summed[:, :quarter] * gain_input.astype(f32)[None, :]
                       - normed_slice * (cross_one / depth))
    )
    out_blocks = out_part.astype(bf16).reshape(tokens, tensors, quarter).transpose(1, 0, 2)
    block_sum = jnp.sum(exchange(out_blocks).astype(f32), axis=0)
    output = (
        lax.dynamic_slice_in_dim(residual, column, quarter, 1).astype(f32) + block_sum
    ).astype(bf16)

    state_all = jnp.sum(spread(value_grad[:, first:last]).astype(f32), axis=0).astype(bf16)
    grad_main = dot_inner(
        mixed_ext, jnp.concatenate([value_grad[:, :first], state_all, value_grad[:, last:]], axis=1)
    )
    grad_proj_out = dot_inner(dmixer, gated_out)
    grad_router = jnp.pad(dot_inner(mixed_two, router_grad(dgate_all)), ((0, 0), (0, router_pad)))
    shared_up, shared_dn = unpack_experts(shared_grad[0])
    mid_local = jnp.concatenate(
        [shared_up[0], shared_up[1], shared_dn.reshape(shared_here, depth).T,
         grad_proj_out.astype(bf16), grad_router.astype(bf16)], axis=1
    )
    mid_local, expert_rows = lax.optimization_barrier((mid_local, expert_rows))
    mid_grad = scatter_rows(mid_local)
    main_local, mid_grad = lax.optimization_barrier((grad_main.astype(bf16), mid_grad))
    mid_grad = mid_grad.astype(f32)
    main_grad = scatter_rows(main_local).astype(f32)
    gates_rows, down_rows = unpack_experts(expert_rows)
    shared_rows = mid_grad[:, : 2 * shared_here].reshape(wrows, 2, 2, shared_here // 2)
    gains, conv_state_grad = lax.psum(
        (jnp.stack([grad_gain_part, grad_gain_mix]), dtaps[:, inner:]), EVERY
    )
    small = lax.psum((dtaps[:, :inner], small_sums[:2], sums[:2]), ROWS)
    gains = lax.dynamic_slice_in_dim(gains, column, quarter, 1)
    return (
        output,
        grad_input,
        gains[0],
        jnp.stack([main_grad[:, :inner], main_grad[:, inner:first]], axis=1),
        main_grad[:, first:last],
        main_grad[:, last : last + heads],
        small[0],
        conv_state_grad,
        small[1][0, :heads],
        small[1][1, :heads],
        jnp.sum(small[2][1].reshape(heads, per), axis=1),
        small[2][0],
        mid_grad[:, 3 * shared_here : at_router],
        gains[1],
        mid_grad[:, at_router : at_router + experts_all],
        shared_rows.transpose(0, 2, 1, 3).reshape(wrows, 2, shared_here),
        mid_grad[:, 2 * shared_here : 3 * shared_here],
        gates_rows.reshape(expert_gates.shape).astype(f32),
        down_rows.astype(f32),
    )


def solution(mesh):
    return jax.shard_map(
        local,
        mesh=mesh,
        in_specs=(
            P(ROWS, "tensor"),
            P("tensor"),
            P(ROWS, None, "tensor"),
            P(ROWS, None),
            P(ROWS, "tensor"),
            P(None, "tensor"),
            P(),
            P("tensor"),
            P("tensor"),
            P("tensor"),
            P("tensor"),
            P(ROWS, "tensor"),
            P("tensor"),
            P(ROWS, None),
            P(ROWS, None, "tensor"),
            P(ROWS, "tensor"),
            P(ROWS, None, None, "tensor"),
            P(ROWS, "tensor", None),
            P("shard", "ctx"),
            P(ROWS, None),
            P(ROWS, "tensor"),
        ),
        out_specs=(
            P(ROWS, "tensor"),
            P(ROWS, "tensor"),
            P("tensor"),
            P(ROWS, None, "tensor"),
            P(ROWS, None),
            P(ROWS, "tensor"),
            P(None, "tensor"),
            P(),
            P("tensor"),
            P("tensor"),
            P("tensor"),
            P("tensor"),
            P(ROWS, "tensor"),
            P("tensor"),
            P(ROWS, None),
            P(ROWS, None, "tensor"),
            P(ROWS, "tensor"),
            P(ROWS, None, None, "tensor"),
            P(ROWS, "tensor", None),
        ),
        check_vma=False,
    )
```

```python
from functools import partial

import jax
import jax.numpy as jnp
from jax import lax
from jax.experimental import pallas as pl
from jax.experimental.pallas import tpu as pltpu
from jax.sharding import PartitionSpec as P

CONV = 4
HALO = 16
LANES = 128
LANES = 128
LANES = 128


epsilon = 1e-05
highest = lax.Precision.HIGHEST
CTX = ("cy", "core")
CHIPS = ("shard", "cy")
ROWS = ("shard", "cy", "core")
f32 = jnp.float32
MESH = pl.DeviceIdType.MESH
bf16 = jnp.bfloat16
BIG = pltpu.CompilerParams(vmem_limit_bytes=56 << 20)


def cost(micros):
    return pl.CostEstimate(flops=micros * 900_000_000, transcendentals=0, bytes_accessed=1 << 20)
BIG = pltpu.CompilerParams(vmem_limit_bytes=56 << 20)


def cost(micros):
    return pl.CostEstimate(flops=micros * 900_000_000, transcendentals=0, bytes_accessed=1 << 20)
BIG = pltpu.CompilerParams(vmem_limit_bytes=56 << 20)


def cost(micros):
    return pl.CostEstimate(flops=micros * 900_000_000, transcendentals=0, bytes_accessed=1 << 20)


def shifted(value, axis, steps):
    count = lax.axis_size(axis)
    leading, last = (max(0, -steps), min(count, count - steps))
    return lax.ppermute(value, axis, [(source, source + steps) for source in range(leading, last)])


def dot_rows(left, right, precision=None):
    return jnp.dot(left, right, preferred_element_type=f32, precision=precision)


def dot_inner(left, right):
    return lax.dot_general(left, right, (((0,), (0,)), ((), ())), preferred_element_type=f32)


def dot_outer(left, right):
    return lax.dot_general(left, right, (((1,), (1,)), ((), ())), preferred_element_type=f32)


def sigmoid(value):
    return 1.0 / (1.0 + jnp.exp(-value))


def gather_rows(value):
    return lax.all_gather(value, ROWS, axis=0, tiled=True)


def scatter_rows(value):
    return lax.psum_scatter(value, ROWS, scatter_dimension=0, tiled=True)


def scatter_chips(value):
    axes = CHIPS if lax.axis_size("core") == 2 else ROWS
    return lax.psum_scatter(value, axes, scatter_dimension=0, tiled=True)


def exchange(blocks):
    return lax.all_to_all(blocks, "tensor", split_axis=0, concat_axis=0, tiled=True)


def spread(block):
    count = lax.axis_size("tensor")
    return exchange(jnp.broadcast_to(block[None], (count,) + block.shape))


def spread_small(block):
    count, index = lax.axis_size("tensor"), lax.axis_index("tensor")
    width = block.shape[1]
    full = jnp.zeros((block.shape[0], count * width), block.dtype)
    for away in range(count):
        moved = block if away == 0 else lax.ppermute(
            block, "tensor", [(i, (i + away) % count) for i in range(count)]
        )
        origin = lax.rem(index - away + count, count)
        full = lax.dynamic_update_slice_in_dim(full, moved, origin * width, 1)
    return full


def halves(value):
    high = value.astype(bf16)
    return high, (value - high.astype(f32)).astype(bf16)


def far_states(packed, reverse):
    count = lax.axis_size(CTX)
    return jnp.stack([
        shifted(packed, CTX, -away if reverse else away) for away in range(1, count)
    ])


def row_iota(shape):
    return lax.broadcasted_iota(jnp.int32, shape, 0)


def col_iota(shape):
    return lax.broadcasted_iota(jnp.int32, shape, 1)


def expander(lanes, width, per):
    low = row_iota((lanes, width)) * per
    at = col_iota((lanes, width))
    return ((at >= low) & (at < low + per)).astype(f32)


def head_fold(width, lanes, per):
    low = col_iota((width, lanes)) * per
    at = row_iota((width, lanes))
    return ((at >= low) & (at < low + per)).astype(f32)


def pack_state(state, through):
    high, low = halves(through)
    row = row_iota((16, LANES))
    tail = jnp.where(row == 0, high.astype(f32), jnp.where(row == 1, low.astype(f32), 0.0))
    return jnp.concatenate([state, tail], axis=0).astype(bf16)


def join_states(far_ref, inner, per):
    spread_heads = head_fold(inner, LANES, per)
    total = None
    for k in reversed(range(far_ref.shape[0])):
        state = far_ref[k, :inner, :].astype(f32)
        if total is not None:
            through = far_ref[k, inner : inner + 16, :].astype(f32)
            through = through[0:1] + through[1:2]
            state = state + jnp.sum(spread_heads * through, axis=1, keepdims=True) * total
        total = state
    return total


def thirds(value):
    high = value.astype(bf16)
    rest = value - high.astype(f32)
    middle = rest.astype(bf16)
    return high, middle, (rest - middle.astype(f32)).astype(bf16)


def spread_lanes(value, grow):
    ones = grow.astype(bf16)
    return sum(dot_rows(part, ones) for part in thirds(value))


def left_sums(zero_one, value):
    return sum(dot_rows(zero_one, part) for part in thirds(value))


def fold_heads(value, folds):
    high, low = halves(value)
    return dot_rows(high, folds) + dot_rows(low, folds)


def conv_pre(value_ref, column, taps_ref, taps_column, same_ref, tokens):
    rows = value_ref[:, pl.ds(column, LANES)]
    total = None
    for offset in range(CONV):
        first = HALO - CONV + 1 + offset
        term = rows[first : first + tokens] * (
            same_ref[offset] * taps_ref[offset : offset + 1, pl.ds(taps_column, LANES)]
        )
        total = term if total is None else total + term
    return rows, total


def enter_kernel(mixed_ref, w_ref, taps_ref, same_ref, bias_ref, decay_ref, end_ref, link_ref,
                 value_ref, act_ref, scaled_ref, step_ref, run_ref, run_exp_ref,
                 state_ref, *, inner, nstate, per):
    tokens = act_ref.shape[0]
    width = 2 * inner + 2 * nstate + LANES
    tile = 384

    def matmul(i, _):
        columns = pl.ds(pl.multiple_of(i * tile, LANES), tile)
        value_ref[:, columns] = dot_rows(mixed_ref[...], w_ref[:, columns])
        return 0

    lax.fori_loop(0, width // tile, matmul, 0)

    def conv(i, _):
        at = pl.multiple_of(i * LANES, LANES)
        _, total = conv_pre(value_ref, inner + at, taps_ref, at, same_ref, tokens)
        act_ref[:, pl.ds(at, LANES)] = (total * sigmoid(total)).astype(bf16)
        return 0

    lax.fori_loop(0, (inner + 2 * nstate) // LANES, conv, 0)
    raw = value_ref[HALO:, 2 * inner + 2 * nstate :] + bias_ref[...]
    step = jnp.maximum(raw, 0.0) + jnp.log1p(jnp.exp(-jnp.abs(raw)))
    log_decay = step * -jnp.exp(decay_ref[...])
    tri = (row_iota((tokens, tokens)) >= col_iota((tokens, tokens))).astype(bf16)
    running = left_sums(tri, log_decay)
    step_ref[...] = step
    run_ref[...] = running
    grow = expander(LANES, inner, per)
    run_exp_ref[...] = spread_lanes(running, grow)
    signal = act_ref[:, :inner].astype(f32)
    scaled_ref[...] = (signal * spread_lanes(step, grow)).astype(bf16)
    toward = step * jnp.exp(running[tokens - 1 :] - running) * end_ref[...]
    pushed = (signal * spread_lanes(toward, grow)).astype(bf16)
    through = jnp.exp(running[tokens - 1 :]) * link_ref[tokens - 1 :]
    state_ref[...] = pack_state(dot_inner(pushed, act_ref[:, inner : inner + nstate]), through)


def whole(a):
    return pl.BlockSpec(a.shape, lambda i: (0,) * len(a.shape))


def columns(a, width, at=0):
    assert at % width == 0
    return pl.BlockSpec((a.shape[0], width), lambda i: (0, at // width))


def enter(mixed_ext, weights, taps, same, bias, decay, at_end, link, inner, nstate, per):
    ext = mixed_ext.shape[0]
    tokens = ext - HALO
    wide = 2 * inner + 2 * nstate + LANES
    shape = jax.ShapeDtypeStruct
    outs = [
        shape((ext, wide), f32), shape((tokens, inner + 2 * nstate), bf16),
        shape((tokens, inner), bf16), shape((tokens, LANES), f32), shape((tokens, LANES), f32),
        shape((tokens, inner), f32), shape((inner + 16, nstate), bf16),
    ]
    return pl.pallas_call(
        partial(enter_kernel, inner=inner, nstate=nstate, per=per),
        grid=(1,),
        in_specs=[whole(mixed_ext), columns(weights, wide)]
        + [whole(a) for a in (taps, same, bias, decay, at_end, link)],
        out_specs=[whole(o) for o in outs],
        out_shape=outs,
        compiler_params=BIG,
        cost_estimate=cost(8),
        name="enter",
    )(mixed_ext, weights, taps, same, bias, decay, at_end, link)


def masked_scores(query, keys, seg_col_ref, seg_row_ref, start, stop):
    shape = (stop - start, stop)
    allowed = (row_iota(shape) + start >= col_iota(shape)) & (
        seg_col_ref[start:stop, :1] == seg_row_ref[:, :stop]
    )
    return jnp.where(allowed, dot_outer(query[start:stop], keys[:stop]), 0.0)


def intra_kernel(act_ref, scaled_ref, run_t_ref, run_exp_ref, seg_col_ref, seg_row_ref,
                 inner_ref, scores_ref, *, inner, nstate, per, block):
    tokens = act_ref.shape[0]
    keys = act_ref[:, inner : inner + nstate]
    query = act_ref[:, inner + nstate :]
    for start in range(0, tokens, block):
        stop = start + block
        scores_ref[start:stop, :stop] = masked_scores(
            query, keys, seg_col_ref, seg_row_ref, start, stop
        )

    def pair(i, _):
        columns = pl.ds(pl.multiple_of(i * LANES, LANES), LANES)
        scaled = scaled_ref[:, columns]
        lane = col_iota(scaled.shape)
        run = run_exp_ref[:, columns]
        for start in range(0, tokens, block):
            stop = start + block
            total = None
            for h in range(LANES // per):
                mine = (lane >= h * per) & (lane < (h + 1) * per)
                vals = jnp.where(mine, scaled, jnp.zeros_like(scaled))[:stop]
                row = run_t_ref[i * (LANES // per) + h, :, :stop]
                decay = jnp.exp(jnp.minimum(run[start:stop, h * per : h * per + 1] - row, 0.0))
                weight = (decay * scores_ref[start:stop, :stop]).astype(bf16)
                term = dot_rows(weight, vals)
                total = term if total is None else total + term
            inner_ref[start:stop, columns] = total
        return 0

    lax.fori_loop(0, inner // LANES, pair, 0)


def intra(act, scaled, run_t, run_exp, seg_col, seg_row, inner, nstate, per):
    tokens = act.shape[0]
    return pl.pallas_call(
        partial(intra_kernel, inner=inner, nstate=nstate, per=per, block=128),
        out_shape=jax.ShapeDtypeStruct((tokens, inner), f32),
        scratch_shapes=[pltpu.VMEM((tokens, tokens), f32)],
        compiler_params=BIG,
        cost_estimate=cost(10),
        name="intra",
    )(act, scaled, run_t, run_exp, seg_col, seg_row)


def leave_kernel(act_ref, inner_ref, z_ref, far_ref, run_exp_ref, link_ref, skip_ref, gain_ref,
                 wa_ref, wb_ref, mixer_ref, part_ref, square_ref, state_ref, *, inner, nstate, per):
    query = act_ref[:, inner + nstate :]
    state = join_states(far_ref, inner, per)
    state_ref[...] = state
    carried = dot_outer(query, state.astype(bf16)) * (
        jnp.exp(run_exp_ref[...]) * link_ref[...]
    )
    mixer = inner_ref[...] + carried + skip_ref[...] * act_ref[:, :inner].astype(f32)
    mixer_ref[...] = mixer
    z = z_ref[HALO:, :]
    gated = mixer * (z * sigmoid(z))
    square_ref[...] = row_sums(gated * gated)
    lifted = (gated * gain_ref[...]).astype(bf16)
    half = inner // 2
    part_ref[...] = (
        dot_outer(lifted[:, :half], wa_ref[...]) + dot_outer(lifted[:, half:], wb_ref[...])
    ).astype(bf16)


def row_sums(value):
    folded = value[:, :LANES]
    for at in range(LANES, value.shape[1], LANES):
        folded = folded + value[:, at : at + LANES]
    ones = jnp.ones((8, LANES), bf16)
    high, low = halves(folded)
    return dot_outer(ones, high) + dot_outer(ones, low)


def as_column(row):
    n = row.shape[1]
    eye = row_iota((n, n)) == col_iota((n, n))
    return jnp.sum(jnp.where(eye, row, 0.0), axis=1, keepdims=True)


def leave(act, within, value, far, run_exp, link, skip, gain, weights, inner, nstate, per):
    tokens = act.shape[0]
    depth = weights.shape[0]
    half = inner // 2
    first = 2 * inner + 2 * nstate + LANES
    outs = [jax.ShapeDtypeStruct((tokens, inner), f32), jax.ShapeDtypeStruct((tokens, depth), bf16),
            jax.ShapeDtypeStruct((8, tokens), f32), jax.ShapeDtypeStruct((inner, nstate), f32)]
    return pl.pallas_call(
        partial(leave_kernel, inner=inner, nstate=nstate, per=per),
        grid=(1,),
        in_specs=[whole(act), whole(within), columns(value, inner), whole(far), whole(run_exp),
                  whole(link), whole(skip), whole(gain), columns(weights, half, first),
                  columns(weights, half, first + half)],
        out_specs=[whole(o) for o in outs],
        out_shape=outs,
        compiler_params=BIG,
        cost_estimate=cost(8),
        name="leave",
    )(act, within, value, far, run_exp, link, skip, gain, weights, weights)


def tensor_barrier(me, n):
    barrier = pltpu.get_barrier_semaphore()
    for d in range(1, n):
        pl.semaphore_signal(
            barrier, inc=1, device_id={"tensor": lax.rem(me + d, n)}, device_id_type=MESH
        )
    pl.semaphore_wait(barrier, n - 1)


def push(source, target, sems, slot, peer):
    send, receive = sems
    return pltpu.make_async_remote_copy(
        src_ref=source, dst_ref=target, send_sem=send.at[slot], recv_sem=receive.at[slot],
        device_id={"tensor": peer}, device_id_type=MESH,
    )


def residual_kernel(part_ref, square_ref, x_ref, res_ref, stat_ref, own_ref,
                    inbox, square_box, res_box, stat_box, *sems, di_all, n):
    me = lax.axis_index("tensor")
    rows, depth = part_ref.shape
    own = rows // n
    groups = [(sems[2 * i], sems[2 * i + 1]) for i in range(4)]
    mine = pl.ds(pl.multiple_of(me * own, own), own)
    tensor_barrier(me, n)
    first, second = [], []
    for d in range(1, n):
        peer = lax.rem(me + d, n)
        theirs = pl.ds(pl.multiple_of(peer * own, own), own)
        first.append(push(part_ref.at[theirs], inbox.at[d - 1], groups[0], d - 1, peer))
        first.append(push(square_ref.at[:, theirs], square_box.at[d - 1], groups[1], d - 1, peer))
    for copy in first:
        copy.start()
    total = part_ref[mine, :].astype(f32)
    square = square_ref[:, mine]
    for copy in first:
        copy.wait_recv()
    for d in range(1, n):
        total = total + inbox[d - 1].astype(f32)
        square = square + square_box[d - 1]
    own_ref[...] = total
    scale = lax.rsqrt(square / di_all + epsilon)
    stat_box[:, mine] = scale
    res_box[mine, :] = (x_ref[mine, :].astype(f32) + total * as_column(scale[:1])).astype(bf16)
    for d in range(1, n):
        peer = lax.rem(me + d, n)
        second.append(push(res_box.at[mine], res_box.at[mine], groups[2], d - 1, peer))
        second.append(push(stat_box.at[:, mine], stat_box.at[:, mine], groups[3], d - 1, peer))
    for copy in second:
        copy.start()
    for copy in first:
        copy.wait_send()
    for copy in second:
        copy.wait()
    res_ref[...] = res_box[...]
    stat_ref[...] = stat_box[...]


def pairs(count, n):
    return [pltpu.SemaphoreType.DMA((n - 1,))] * (2 * count)


def residual_step(part, square, x, di_all):
    n = lax.axis_size("tensor")
    tokens, depth = part.shape
    own = tokens // n
    shape = jax.ShapeDtypeStruct
    return pl.pallas_call(
        partial(residual_kernel, di_all=di_all, n=n),
        in_specs=[pl.BlockSpec(memory_space=pltpu.VMEM)] * 3,
        out_specs=[pl.BlockSpec(memory_space=pltpu.VMEM)] * 3,
        out_shape=[shape((tokens, depth), bf16), shape((8, tokens), f32), shape((own, depth), f32)],
        scratch_shapes=[
            pltpu.VMEM((n - 1, own, depth), bf16), pltpu.VMEM((n - 1, 8, own), f32),
            pltpu.VMEM((tokens, depth), bf16), pltpu.VMEM((8, tokens), f32),
        ] + pairs(4, n),
        compiler_params=pltpu.CompilerParams(
            vmem_limit_bytes=40 << 20, collective_id=1, has_side_effects=True
        ),
        cost_estimate=cost(60),
        name="residual_step",
    )(part, square, x)


def turn_kernel(dmix_ref, dgate_ref, res_ref, cot_ref, own_ref, gain_ref,
                dres_ref, notes_ref, gains_ref,
                inbox, gate_box, dres_box, notes_box, *sems, n):
    me = lax.axis_index("tensor")
    rows, depth = dmix_ref.shape
    own = rows // n
    groups = [(sems[2 * i], sems[2 * i + 1]) for i in range(4)]
    mine = pl.ds(pl.multiple_of(me * own, own), own)
    tensor_barrier(me, n)
    first, second = [], []
    for d in range(1, n):
        peer = lax.rem(me + d, n)
        theirs = pl.ds(pl.multiple_of(peer * own, own), own)
        first.append(push(dmix_ref.at[theirs], inbox.at[d - 1], groups[0], d - 1, peer))
        first.append(push(dgate_ref.at[theirs], gate_box.at[d - 1], groups[1], d - 1, peer))
    for copy in first:
        copy.start()
    res = res_ref[mine, :].astype(f32)
    scale = lax.rsqrt(jnp.mean(res * res, axis=1, keepdims=True) + epsilon)
    normed = res * scale
    dmix = dmix_ref[mine, :].astype(f32)
    dgate = dgate_ref[mine, :]
    for copy in first:
        copy.wait_recv()
    for d in range(1, n):
        dmix = dmix + inbox[d - 1].astype(f32)
        dgate = dgate + gate_box[d - 1]
    gains_ref[...] = jnp.broadcast_to(jnp.sum(dmix * normed, axis=0, keepdims=True), gains_ref.shape)
    lifted = dmix * gain_ref[...]
    inside = jnp.mean(lifted * normed, axis=1, keepdims=True)
    dres = (cot_ref[mine, :].astype(f32) + scale * (lifted - normed * inside)).astype(bf16)
    cross = jnp.sum(dres.astype(f32) * own_ref[...], axis=1, keepdims=True)
    dres_box[mine, :] = dres
    notes_box[mine, :] = jnp.where(col_iota(dgate.shape) == LANES - 1, cross, dgate)
    for d in range(1, n):
        peer = lax.rem(me + d, n)
        second.append(push(dres_box.at[mine], dres_box.at[mine], groups[2], d - 1, peer))
        second.append(push(notes_box.at[mine], notes_box.at[mine], groups[3], d - 1, peer))
    for copy in second:
        copy.start()
    for copy in first:
        copy.wait_send()
    for copy in second:
        copy.wait()
    dres_ref[...] = dres_box[...]
    notes_ref[...] = notes_box[...]


def turn_step(dmix, dgate, residual, cot, own_part, gain):
    n = lax.axis_size("tensor")
    tokens, depth = dmix.shape
    own = tokens // n
    shape = jax.ShapeDtypeStruct
    return pl.pallas_call(
        partial(turn_kernel, n=n),
        in_specs=[pl.BlockSpec(memory_space=pltpu.VMEM)] * 6,
        out_specs=[pl.BlockSpec(memory_space=pltpu.VMEM)] * 3,
        out_shape=[shape((tokens, depth), bf16), shape((tokens, LANES), f32),
                   shape((8, depth), f32)],
        scratch_shapes=[
            pltpu.VMEM((n - 1, own, depth), bf16), pltpu.VMEM((n - 1, own, LANES), f32),
            pltpu.VMEM((tokens, depth), bf16), pltpu.VMEM((tokens, LANES), f32),
        ] + pairs(4, n),
        compiler_params=pltpu.CompilerParams(
            vmem_limit_bytes=40 << 20, collective_id=2, has_side_effects=True
        ),
        cost_estimate=cost(60),
        name="turn_step",
    )(dmix, dgate, residual, cot, own_part, gain)


def finish_kernel(grad_ref, halo_ref, w_ref, x_ref, dres_ref, gain_ref, mid_ref, state_ref,
                  out_ref, gains_ref, state_out_ref,
                  outbox, inbox, cross_box, cross_in, gains_box, gains_in, state_in, *sems, n):
    me = lax.axis_index("tensor")
    rows, depth = x_ref.shape
    quarter = depth // n
    groups = [(sems[2 * i], sems[2 * i + 1]) for i in range(4)]
    tensor_barrier(me, n)
    x = x_ref[...].astype(f32)
    scale = lax.rsqrt(jnp.mean(x * x, axis=1, keepdims=True) + epsilon)
    copies = []
    for d in range(1, n):
        peer = lax.rem(me + d, n)
        copies.append(push(state_ref, state_in.at[d - 1], groups[3], d - 1, peer))
        copies[-1].start()
    cross = jnp.zeros((8, rows), f32)
    kept = None
    for d in tuple(range(1, n)) + (0,):
        peer = lax.rem(me + d, n)
        theirs = pl.ds(pl.multiple_of(peer * quarter, LANES), quarter)
        w = w_ref[theirs, :]
        block = dot_outer(grad_ref[HALO:, :], w)
        tail = dot_outer(halo_ref[...], w)
        block = jnp.concatenate([block[: rows - HALO], block[rows - HALO :] + tail], axis=0)
        normed = x_ref[:, theirs].astype(f32) * scale
        cross = cross + row_sums(block * normed * gain_ref[:, theirs])
        gains = jnp.where(
            row_iota((8, quarter)) == 0, jnp.sum(block * normed, axis=0, keepdims=True),
            mid_ref[:, theirs],
        )
        if d == 0:
            kept, kept_gains, kept_normed = block, gains, normed
            continue
        gains_box[d - 1] = gains
        outbox[d - 1] = block.astype(bf16)
        copies.append(push(outbox.at[d - 1], inbox.at[d - 1], groups[0], d - 1, peer))
        copies[-1].start()
        copies.append(push(gains_box.at[d - 1], gains_in.at[d - 1], groups[1], d - 1, peer))
        copies[-1].start()
    cross_box[...] = cross
    for d in range(1, n):
        copies.append(
            push(cross_box, cross_in.at[d - 1], groups[2], d - 1, lax.rem(me + d, n))
        )
        copies[-1].start()
    for copy in copies:
        copy.wait()
    state = state_ref[...]
    for d in range(1, n):
        kept = kept + inbox[d - 1].astype(f32)
        kept_gains = kept_gains + gains_in[d - 1]
        cross = cross + cross_in[d - 1]
        state = state + state_in[d - 1]
    gains_ref[...] = kept_gains
    state_out_ref[...] = state
    here = pl.ds(pl.multiple_of(me * quarter, LANES), quarter)
    inside = jnp.concatenate(
        [as_column(cross[:1, at : at + LANES]) for at in range(0, rows, LANES)], axis=0
    ) / depth
    out_ref[...] = dres_ref[:, here].astype(f32) + scale * (
        kept * gain_ref[:, here] - kept_normed * inside
    )


def finish_step(value_grad, halo, weights, x, dres, gain, gains_mid, state):
    n = lax.axis_size("tensor")
    tokens, depth = x.shape
    quarter = depth // n
    shape = jax.ShapeDtypeStruct
    outs = [shape((tokens, quarter), f32), shape((8, quarter), f32), shape(state.shape, f32)]
    args = (value_grad, halo, weights, x, dres, gain, gains_mid, state)
    return pl.pallas_call(
        partial(finish_kernel, n=n),
        grid=(1,),
        in_specs=[whole(a) if a is not weights else columns(a, value_grad.shape[1]) for a in args],
        out_specs=[whole(o) for o in outs],
        out_shape=outs,
        scratch_shapes=[
            pltpu.VMEM((n - 1, tokens, quarter), bf16), pltpu.VMEM((n - 1, tokens, quarter), bf16),
            pltpu.VMEM((8, tokens), f32), pltpu.VMEM((n - 1, 8, tokens), f32),
            pltpu.VMEM((n - 1, 8, quarter), f32), pltpu.VMEM((n - 1, 8, quarter), f32),
            pltpu.VMEM((n - 1,) + state.shape, f32),
        ] + pairs(4, n),
        compiler_params=pltpu.CompilerParams(
            vmem_limit_bytes=56 << 20, collective_id=3, has_side_effects=True
        ),
        cost_estimate=cost(45),
        name="finish_step",
    )(*args)


def back_kernel(dout_ref, wa_ref, wb_ref, mixer_ref, z_ref, act_ref, run_exp_ref, link_ref, gain_ref,
                stat_ref, through_ref, heads_ref, zgrad_ref, gated_ref, direct_ref, sums_ref,
                *, inner, nstate, di_all):
    scale = stat_ref[:, 0:1]
    cross = stat_ref[:, 1:2]
    mixer = mixer_ref[...]
    z = z_ref[HALO:, :]
    sig = sigmoid(z)
    act = z * sig
    gated = mixer * act
    dout = dout_ref[...]
    grad = jnp.concatenate([dot_rows(dout, wa_ref[...]), dot_rows(dout, wb_ref[...])], axis=1)
    gated_ref[...] = (gated * scale * gain_ref[...]).astype(bf16)
    sums_ref[0:1, :] = jnp.sum(grad * gated * scale, axis=0, keepdims=True)
    gated_grad = scale * (grad * gain_ref[...]) - gated * (scale * scale * scale * cross / di_all)
    zgrad_ref[...] = (gated_grad * mixer * (sig * (1.0 + z * (1.0 - sig)))).astype(bf16)
    heads = gated_grad * act
    heads_ref[...] = heads
    sums_ref[1:2, :] = jnp.sum(heads * act_ref[:, :inner].astype(f32), axis=0, keepdims=True)
    sums_ref[2:, :] = jnp.zeros((6, inner), f32)
    carried = (heads * (jnp.exp(run_exp_ref[...]) * link_ref[...])).astype(bf16)
    direct_ref[:inner, :] = dot_inner(carried, act_ref[:, inner + nstate :]).astype(bf16)
    direct_ref[inner:, :] = through_ref[...]


def back(dout, weights, mixer, value, act, run_exp, link, gain, stats, through, inner, nstate, di_all):
    tokens = act.shape[0]
    half = inner // 2
    first = 2 * inner + 2 * nstate + LANES
    shape = jax.ShapeDtypeStruct
    outs = [shape((tokens, inner), f32), shape((tokens, inner), bf16), shape((tokens, inner), bf16),
            shape((inner + 16, nstate), bf16), shape((8, inner), f32)]
    return pl.pallas_call(
        partial(back_kernel, inner=inner, nstate=nstate, di_all=di_all),
        grid=(1,),
        in_specs=[whole(dout), columns(weights, half, first), columns(weights, half, first + half),
                  whole(mixer), columns(value, inner), whole(act), whole(run_exp), whole(link),
                  whole(gain), whole(stats), whole(through)],
        out_specs=[whole(o) for o in outs],
        out_shape=outs,
        compiler_params=BIG,
        cost_estimate=cost(8),
        name="back",
    )(dout, weights, weights, mixer, value, act, run_exp, link, gain, stats, through)


def intra_back_kernel(heads_ref, act_ref, scaled_ref, run_t_ref, run_exp_ref, seg_col_ref,
                      seg_row_ref, dscaled_ref, dstate_ref, drun_ref, scores_ref, dscores_ref,
                      rows_ref, *, inner, nstate, per, block):
    tokens = act_ref.shape[0]
    keys = act_ref[:, inner : inner + nstate]
    query = act_ref[:, inner + nstate :]
    for start in range(0, tokens, block):
        stop = start + block
        scores_ref[start:stop, :stop] = masked_scores(
            query, keys, seg_col_ref, seg_row_ref, start, stop
        )
    dscores_ref[...] = jnp.zeros_like(dscores_ref)
    drun_ref[...] = jnp.zeros_like(drun_ref)

    def pair(i, _):
        columns = pl.ds(pl.multiple_of(i * LANES, LANES), LANES)
        scaled = scaled_ref[:, columns]
        heads = heads_ref[:, columns].astype(bf16)
        lane = col_iota(scaled.shape)
        run = run_exp_ref[:, columns]
        dscaled_ref[:, columns] = jnp.zeros((tokens, LANES), f32)
        for h in range(LANES // per):
            head = i * (LANES // per) + h
            mine = (lane >= h * per) & (lane < (h + 1) * per)
            vals = jnp.where(mine, scaled, jnp.zeros_like(scaled))
            grads = jnp.where(mine, heads, jnp.zeros_like(heads))
            pick = (col_iota((block, LANES)) == head).astype(bf16)
            for start in range(0, tokens, block):
                stop = start + block
                row = run_t_ref[head, :, :stop]
                decay = jnp.exp(jnp.minimum(run[start:stop, h * per : h * per + 1] - row, 0.0))
                weight = decay * scores_ref[start:stop, :stop]
                dweight = dot_outer(grads[start:stop], vals[:stop])
                dscores_ref[start:stop, :stop] += dweight * decay
                flow = (dweight * weight).astype(bf16)
                dscaled_ref[:stop, columns] += dot_inner(weight.astype(bf16), grads[start:stop])
                picks = jnp.broadcast_to(pick[:1], (stop, LANES))
                drun_ref[start:stop, :] += dot_rows(flow, picks)
                drun_ref[:stop, :] -= dot_inner(flow, pick)
        return 0

    lax.fori_loop(0, inner // LANES, pair, 0)
    dkeys = jnp.zeros((tokens, nstate), f32)
    dstate_ref[:, :nstate] = dkeys
    for start in range(0, tokens, block):
        stop = start + block
        shape = (block, stop)
        allowed = (row_iota(shape) + start >= col_iota(shape)) & (
            seg_col_ref[start:stop, :1] == seg_row_ref[:, :stop]
        )
        grad = jnp.where(allowed, dscores_ref[start:stop, :stop], 0.0).astype(bf16)
        dstate_ref[start:stop, nstate:] = dot_rows(grad, keys[:stop])
        dstate_ref[:stop, :nstate] += dot_inner(grad, query[start:stop])


def intra_back(heads, act, scaled, run_t, run_exp, seg_col, seg_row, inner, nstate, per):
    tokens = act.shape[0]
    shape = jax.ShapeDtypeStruct
    return pl.pallas_call(
        partial(intra_back_kernel, inner=inner, nstate=nstate, per=per, block=128),
        out_shape=[shape((tokens, inner), f32), shape((tokens, 2 * nstate), f32),
                   shape((tokens, LANES), f32)],
        scratch_shapes=[pltpu.VMEM((tokens, tokens), f32), pltpu.VMEM((tokens, tokens), f32),
                        pltpu.VMEM((8, LANES), f32)],
        compiler_params=BIG,
        cost_estimate=cost(20),
        name="intra_back",
    )(heads, act, scaled, run_t, run_exp, seg_col, seg_row)


def conv_back(value_ref, column, taps_ref, same_ref, dact, at, dtaps_ref, tokens):
    ext = tokens + HALO
    rows, total = conv_pre(value_ref, column, taps_ref, at, same_ref, tokens)
    sig = sigmoid(total)
    dpre = dact * (sig * (1.0 + total * (1.0 - sig)))
    drows = None
    for offset in range(CONV):
        first = HALO - CONV + 1 + offset
        kept = dpre * same_ref[offset]
        dtaps_ref[offset : offset + 1, pl.ds(at, LANES)] = jnp.sum(
            kept * rows[first : first + tokens], axis=0, keepdims=True
        )
        term = kept * taps_ref[offset : offset + 1, pl.ds(at, LANES)]
        after = ext - first - tokens
        pieces = [jnp.zeros((first, LANES), f32), term]
        if after:
            pieces.append(jnp.zeros((after, LANES), f32))
        term = jnp.concatenate(pieces, axis=0)
        drows = term if drows is None else drows + term
    return drows


def state_back_kernel(heads_ref, act_ref, step_ref, run_ref, run_exp_ref, link_ref, end_ref,
                      value_ref, taps_ref, same_ref, dstate_ref, in_ref, far_ref,
                      rows_ref, dtaps_ref, leaving_ref, kept_ref, dact_ref, *, inner, nstate, per):
    tokens = act_ref.shape[0]
    keys = act_ref[:, inner : inner + nstate]
    signal = act_ref[:, :inner].astype(f32)
    grow = expander(LANES, inner, per)
    running = run_ref[...]
    state_grad = join_states(far_ref, inner, per)
    lifted = (heads_ref[...] * (jnp.exp(run_exp_ref[...]) * link_ref[...])).astype(bf16)
    dact_ref[:, nstate:] = dot_rows(lifted, in_ref[...].astype(bf16)) + dstate_ref[:, nstate:]
    toward = jnp.exp(running[tokens - 1 :] - running) * end_ref[...]
    toward_exp = spread_lanes(toward, grow)
    pushed = (signal * spread_lanes(step_ref[...] * toward, grow)).astype(bf16)
    leaving_ref[...] = dot_outer(keys, state_grad.astype(bf16)) * toward_exp
    dact_ref[:, :nstate] = dot_rows(pushed, state_grad.astype(bf16)) + dstate_ref[:, :nstate]
    kept = jnp.sum(in_ref[...] * state_grad, axis=1, keepdims=True)
    kept = jnp.sum(head_fold(inner, LANES, per) * kept, axis=0, keepdims=True)
    kept = kept * jnp.exp(running[tokens - 1 :]) * link_ref[tokens - 1 :]
    kept_ref[...] = jnp.broadcast_to(kept, kept_ref.shape)

    def conv(i, _):
        at = pl.multiple_of(i * LANES, LANES)
        drows = conv_back(value_ref, at, taps_ref, same_ref, dact_ref[:, pl.ds(at, LANES)], at,
                          dtaps_ref, tokens)
        rows_ref[:, pl.ds(at, LANES)] = drows.astype(bf16)
        return 0

    lax.fori_loop(0, 2 * nstate // LANES, conv, 0)


def state_back(heads, act, step, running, run_exp, link, at_end, value, taps, same, dstate, state_in,
               far, inner, nstate, per):
    tokens = act.shape[0]
    shape = jax.ShapeDtypeStruct
    outs = [shape((tokens + HALO, 2 * nstate), bf16), shape((CONV, 2 * nstate), f32),
            shape((tokens, inner), f32), shape((8, LANES), f32)]
    args = (heads, act, step, running, run_exp, link, at_end, value, taps, same, dstate, state_in, far)
    specs = [whole(a) for a in args]
    specs[7] = columns(value, 2 * nstate, 2 * inner)
    specs[8] = columns(taps, 2 * nstate, inner)
    return pl.pallas_call(
        partial(state_back_kernel, inner=inner, nstate=nstate, per=per),
        grid=(1,),
        in_specs=specs,
        out_specs=[whole(o) for o in outs],
        out_shape=outs,
        scratch_shapes=[pltpu.VMEM((tokens, 2 * nstate), f32)],
        compiler_params=BIG,
        cost_estimate=cost(6),
        name="state_back",
    )(*args)


def signal_back_kernel(heads_ref, act_ref, step_ref, value_ref, raw_ref, taps_ref, same_ref, bias_ref,
                       decay_ref, skip_ref, mixer_ref, inner_ref, dscaled_ref, drun_ref, leaving_ref,
                       kept_ref, zgrad_ref, state_ref,
                       grad_ref, dtaps_ref, small_ref, dact_ref, *, inner, nstate, per):
    tokens = act_ref.shape[0]
    signal = act_ref[:, :inner].astype(f32)
    grow = expander(LANES, inner, per)
    folds = head_fold(inner, LANES, per).astype(bf16)
    step = step_ref[...]
    heads = heads_ref[...]
    leaving = leaving_ref[...]
    step_exp = spread_lanes(step, grow)
    dscaled = dscaled_ref[...] + leaving
    dact_ref[...] = dscaled * step_exp + skip_ref[...] * heads

    def conv(i, _):
        at = pl.multiple_of(i * LANES, LANES)
        drows = conv_back(value_ref, at, taps_ref, same_ref, dact_ref[:, pl.ds(at, LANES)], at,
                          dtaps_ref, tokens)
        grad_ref[:, pl.ds(inner + at, LANES)] = drows.astype(bf16)
        return 0

    lax.fori_loop(0, inner // LANES, conv, 0)
    carried = mixer_ref[...] - inner_ref[...] - skip_ref[...] * signal
    tri = (row_iota((tokens, tokens)) <= col_iota((tokens, tokens))).astype(bf16)
    strict = (row_iota((tokens, tokens)) > col_iota((tokens, tokens))).astype(bf16)
    back_sum = drun_ref[...] + fold_heads(heads * carried, folds)
    front_sum = fold_heads(signal * step_exp * leaving, folds)
    dlog = left_sums(tri, back_sum) + left_sums(strict, front_sum) + kept_ref[0:1, :]
    rate = -jnp.exp(decay_ref[...])
    dstep = dlog * rate + fold_heads(dscaled * signal, folds)
    draw = dstep * sigmoid(raw_ref[HALO:, :] + bias_ref[...])
    small_ref[0:1, :] = jnp.sum(draw, axis=0, keepdims=True)
    small_ref[1:2, :] = jnp.sum(dlog * step, axis=0, keepdims=True) * rate
    small_ref[2:, :] = jnp.zeros((6, LANES), f32)
    state_at = 2 * inner
    step_at = state_at + 2 * nstate
    grad_ref[:HALO, :inner] = jnp.zeros((HALO, inner), bf16)
    grad_ref[HALO:, :inner] = zgrad_ref[...]
    grad_ref[:, state_at:step_at] = state_ref[...]
    grad_ref[:HALO, step_at:] = jnp.zeros((HALO, LANES), bf16)
    used = col_iota((tokens, LANES)) < inner // per
    grad_ref[HALO:, step_at:] = jnp.where(used, draw, 0.0).astype(bf16)


def signal_back(heads, act, step, value, taps, same, bias, decay, skip, mixer, within, dscaled, drun,
                leaving, kept, z_grad, state_rows, inner, nstate, per):
    tokens = act.shape[0]
    wide = value.shape[1]
    shape = jax.ShapeDtypeStruct
    outs = [shape((tokens + HALO, wide), bf16), shape((CONV, inner), f32), shape((8, LANES), f32)]
    args = (heads, act, step, value, value, taps, same, bias, decay, skip, mixer, within, dscaled, drun,
            leaving, kept, z_grad, state_rows)
    specs = [whole(a) for a in args]
    specs[3] = columns(value, inner, inner)
    specs[4] = columns(value, LANES, wide - LANES)
    specs[5] = columns(taps, inner)
    return pl.pallas_call(
        partial(signal_back_kernel, inner=inner, nstate=nstate, per=per),
        grid=(1,),
        in_specs=specs,
        out_specs=[whole(o) for o in outs],
        out_shape=outs,
        scratch_shapes=[pltpu.VMEM((tokens, inner), f32)],
        compiler_params=BIG,
        cost_estimate=cost(12),
        name="signal_back",
    )(*args)


def swiglu(first, second):
    sig = sigmoid(first)
    act = first * sig
    return act, sig * (1.0 + first * (1.0 - sig)), (act * second).astype(bf16)


def shared_kernel(res_ref, cot_ref, gain_ref, router_ref, chosen_ref, w_ref,
                  out_ref, dmix_ref, mix_ref, gates_ref, dw_ref, first_ref, down_ref, hidden_ref,
                  dval_ref, *, tile):
    rows, depth = res_ref.shape
    wrows = w_ref.shape[1] // 3
    wide = w_ref.shape[2]
    hid = wide // 2
    for p in range(2):
        first_ref[p] = w_ref[:, p * wrows : (p + 1) * wrows, :].reshape(depth, wide)
    down_ref[...] = w_ref[:, 2 * wrows :, :].reshape(depth, wide)

    def part(i, _):
        at = pl.ds(pl.multiple_of(i * tile, tile), tile)
        res = res_ref[at, :].astype(f32)
        scale = lax.rsqrt(jnp.mean(res * res, axis=1, keepdims=True) + epsilon)
        mix_ref[at, :] = (res * scale * gain_ref[...]).astype(bf16)
        mix = mix_ref[at, :]
        chosen = chosen_ref[at, :] > 0.0
        logits = dot_rows(mix, router_ref[...])
        top = jnp.max(jnp.where(chosen, logits, -1e30), axis=1, keepdims=True)
        weight = jnp.where(chosen, jnp.exp(jnp.where(chosen, logits - top, 0.0)), 0.0)
        gates_ref[at, :] = weight / jnp.sum(weight, axis=1, keepdims=True)
        raw = dot_rows(cot_ref[at, :], down_ref[...])
        dmix = None
        for p in range(2):
            value = dot_rows(mix, first_ref[p])
            act, slope, hidden = swiglu(value[:, :hid], value[:, hid:])
            here = pl.ds(p * hid, hid)
            dh = raw[:, p * hid : (p + 1) * hid]
            dval_ref[p, at, :hid] = (dh * value[:, hid:] * slope).astype(bf16)
            dval_ref[p, at, hid:] = (dh * act).astype(bf16)
            hidden_ref[at, here] = hidden
            term = dot_outer(dval_ref[p, at, :], first_ref[p])
            dmix = term if dmix is None else dmix + term
        out_ref[at, :] = dot_outer(hidden_ref[at, :], down_ref[...])
        dmix_ref[at, :] = dmix
        return 0

    lax.fori_loop(0, rows // tile, part, 0)
    for p in range(2):
        dw_ref[:, p * wrows : (p + 1) * wrows, :] = (
            dot_inner(mix_ref[...], dval_ref[p]).astype(bf16).reshape(-1, wrows, wide)
        )
    dw_ref[:, 2 * wrows :, :] = (
        dot_inner(cot_ref[...], hidden_ref[...]).astype(bf16).reshape(-1, wrows, wide)
    )


def shared_expert(residual, cot, gain, weights, router_at, chosen, experts_w):
    rows, depth = residual.shape
    senders, deep, wide = experts_w.shape
    part = 3 * (depth // senders)
    own = deep - part
    assert own % part == 0
    shape = jax.ShapeDtypeStruct
    block = pl.BlockSpec((senders, part, wide), lambda i: (0, own // part, 0))
    grads = shape((senders, part, wide), bf16)
    outs = [shape((rows, depth), f32), shape((rows, depth), f32), shape((rows, depth), bf16),
            shape((rows, LANES), f32)]
    return pl.pallas_call(
        partial(shared_kernel, tile=min(256, rows)),
        grid=(1,),
        in_specs=[whole(residual), whole(cot), whole(gain), columns(weights, LANES, router_at),
                  whole(chosen), block],
        out_specs=[whole(o) for o in outs + [grads]],
        out_shape=outs + [grads],
        scratch_shapes=[
            pltpu.VMEM((2, depth, wide), bf16), pltpu.VMEM((depth, wide), bf16),
            pltpu.VMEM((rows, wide), bf16), pltpu.VMEM((2, rows, wide), bf16),
        ],
        compiler_params=BIG,
        cost_estimate=cost(10),
        name="shared_expert",
    )(residual, cot, gain, weights, chosen, experts_w)


def experts_kernel(mix_ref, cot_ref, gates_ref, router_ref, w_ref, out_in, dmix_in, ds_ref,
                   out_ref, dmix_ref, dgate_ref, dw_ref,
                   total_ref, grads_ref, down_ref, hidden_ref, dval_ref, grad_ref, load_sem,
                   *remote, tile, senders, core):
    step = pl.program_id(0)
    last = step == pl.num_programs(0) - 1
    rows, depth = mix_ref.shape
    wide = w_ref.shape[2]
    hid = wide // 2
    chunks = depth // wide
    deep = depth + depth // 2
    if core == 2:
        inbox, shared_box, send, receive, shared_send, shared_receive = remote
        me = lax.axis_index("core")
        other = 1 - me
        slot = lax.rem(step + me, 2)

        def to_sibling(source, target, send_sem, recv_sem):
            return pltpu.make_async_remote_copy(
                src_ref=source, dst_ref=target, send_sem=send_sem, recv_sem=recv_sem,
                device_id={"core": other}, device_id_type=MESH,
            )

        shared_copy = to_sibling(ds_ref.at[other], shared_box, shared_send, shared_receive)
        pair_copy = lambda k: to_sibling(grad_ref.at[1], inbox.at[k], send.at[k], receive.at[k])
    else:
        slot = 0

    @pl.when(step == 0)
    def _():
        loads = [pltpu.make_async_copy(out_in, total_ref, load_sem.at[0]),
                 pltpu.make_async_copy(dmix_in, grads_ref, load_sem.at[1])]
        for copy in loads:
            copy.start()
        dgate_ref[...] = jnp.zeros_like(dgate_ref)
        if core == 2:
            barrier = pltpu.get_barrier_semaphore()
            pl.semaphore_signal(barrier, inc=1, device_id={"core": other}, device_id_type=MESH)
            pl.semaphore_wait(barrier, 1)
            shared_copy.start()
        for copy in loads:
            copy.wait()

    if core == 2:
        @pl.when((step >= 2) & (step < senders) & (slot == 1))
        def _():
            pair_copy((step - 2) // 2).wait_send()

    @pl.when(step < senders)
    def _():
        pair_grads(
            step, slot, mix_ref, cot_ref, gates_ref, w_ref, dgate_ref, total_ref, grads_ref, down_ref,
            hidden_ref, dval_ref, grad_ref, tile
        )

    if core == 2:
        @pl.when((step < senders) & (slot == 1))
        def _():
            pair_copy(step // 2).start()

        @pl.when((step >= 1) & (slot == 1))
        def _():
            at = (step - 1) // 2

            @pl.when(step <= 2)
            def _():
                shared_copy.wait()

            pair_copy(at).wait_recv()
            dw_ref[0, : 3 * depth, :] = grad_ref[0] + inbox[at]
            dw_ref[0, 3 * depth :, :] = ds_ref[me, at] + shared_box[at]

        @pl.when(last)
        def _():
            pair_copy(senders // 2 - 1).wait_send()
    else:
        dw_ref[0, : 3 * depth, :] = grad_ref[0]
        dw_ref[0, 3 * depth :, :] = ds_ref[0, step]

    @pl.when(last)
    def _():
        gates = gates_ref[...]
        dgate = dgate_ref[...]
        inside = jnp.sum(gates * dgate, axis=1, keepdims=True)
        dlogits = (gates * (dgate - inside)).astype(bf16)
        dmix_ref[...] = (grads_ref[...] + dot_outer(dlogits, router_ref[...])).astype(bf16)
        out_ref[...] = total_ref[...].astype(bf16)


def pair_grads(step, slot, mix_ref, cot_ref, gates_ref, w_ref, dgate_ref, total_ref, grads_ref,
               down_ref, hidden_ref, dval_ref, grad_ref, tile):
    rows, depth = mix_ref.shape
    wide = w_ref.shape[2]
    hid = wide // 2
    chunks = depth // wide
    deep = depth + depth // 2
    for p in range(2):
        for c in range(chunks):
            down_ref[p * hid : (p + 1) * hid, c * wide : (c + 1) * wide] = (
                w_ref[0, p * deep + depth + c * hid : p * deep + depth + (c + 1) * hid, :]
            )
    down = down_ref[...]

    def part(i, _):
        at = pl.ds(pl.multiple_of(i * tile, tile), tile)
        mix = mix_ref[at, :]
        raw = dot_outer(cot_ref[at, :], down)
        gates = gates_ref[at, :]
        lane = col_iota(gates.shape)
        dmix, noted = None, jnp.zeros_like(gates)
        for p in range(2):
            here = lane == 2 * step + p
            gate = jnp.sum(jnp.where(here, gates, 0.0), axis=1, keepdims=True)
            weights = w_ref[0, p * deep : p * deep + depth, :]
            value = dot_rows(mix, weights)
            act, slope, hidden = swiglu(value[:, :hid], value[:, hid:])
            hidden = hidden.astype(f32)
            dh = raw[:, p * hid : (p + 1) * hid]
            noted = noted + jnp.where(here, jnp.sum(hidden * dh, axis=1, keepdims=True), 0.0)
            dh = gate * dh
            dval_ref[p, at, :hid] = (dh * value[:, hid:] * slope).astype(bf16)
            dval_ref[p, at, hid:] = (dh * act).astype(bf16)
            hidden_ref[at, p * hid : (p + 1) * hid] = (gate * hidden).astype(bf16)
            term = dot_outer(dval_ref[p, at, :], weights)
            dmix = term if dmix is None else dmix + term
        dgate_ref[at, :] += noted
        total_ref[at, :] += dot_rows(hidden_ref[at, :], down)
        grads_ref[at, :] += dmix
        return 0

    lax.fori_loop(0, rows // tile, part, 0)
    for c in range(chunks):
        grad = dot_inner(hidden_ref[...], cot_ref[:, c * wide : (c + 1) * wide]).astype(bf16)
        for p in range(2):
            first = p * deep + depth + c * hid
            grad_ref[slot, first : first + hid, :] = grad[p * hid : (p + 1) * hid]
    for p in range(2):
        grad_ref[slot, p * deep : p * deep + depth, :] = (
            dot_inner(mix_ref[...], dval_ref[p]).astype(bf16)
        )


def experts(mix, cot, gates, weights, router_at, experts_w, out, dmix, ds):
    senders, deep, wide = experts_w.shape
    rows, depth = mix.shape
    core = lax.axis_size("core")
    kept = senders // core
    part = deep - 3 * depth
    ds = ds.reshape(kept, core, part, wide).transpose(1, 0, 2, 3)
    shape = jax.ShapeDtypeStruct
    once = lambda a: pl.BlockSpec(
        a.shape, lambda i: (0,) * a.ndim, pipeline_mode=pl.Buffered(1)
    )
    outs = [shape((rows, depth), bf16), shape((rows, depth), bf16), shape((rows, LANES), f32)]
    if core == 2:
        steps = senders + 1
        kept_map = lambda i: (jnp.maximum(i - 1, 0) // 2, 0, 0)
        remote = [
            pltpu.VMEM((kept, 3 * depth, wide), bf16), pltpu.VMEM((kept, part, wide), bf16),
            pltpu.SemaphoreType.DMA((kept,)), pltpu.SemaphoreType.DMA((kept,)),
            pltpu.SemaphoreType.DMA, pltpu.SemaphoreType.DMA,
        ]
        params = pltpu.CompilerParams(
            vmem_limit_bytes=60 << 20, collective_id=4, has_side_effects=True
        )
    else:
        steps, remote, params = senders, [], pltpu.CompilerParams(vmem_limit_bytes=60 << 20)
        kept_map = lambda i: (i, 0, 0)
    return pl.pallas_call(
        partial(experts_kernel, tile=min(256, rows), senders=senders, core=core),
        grid=(steps,),
        in_specs=[once(mix), once(cot), once(gates),
                  pl.BlockSpec((depth, LANES), lambda i: (0, router_at // LANES)),
                  pl.BlockSpec((1, 3 * depth, wide), lambda i: (jnp.minimum(i, senders - 1), 0, 0)),
                  pl.BlockSpec(memory_space=pl.ANY), pl.BlockSpec(memory_space=pl.ANY), once(ds)],
        out_specs=[whole(o) for o in outs] + [pl.BlockSpec((1, deep, wide), kept_map)],
        out_shape=outs + [shape((kept, deep, wide), bf16)],
        scratch_shapes=[
            pltpu.VMEM((rows, depth), f32), pltpu.VMEM((rows, depth), f32),
            pltpu.VMEM((wide, depth), bf16), pltpu.VMEM((rows, wide), bf16),
            pltpu.VMEM((2, rows, wide), bf16), pltpu.VMEM((core, 3 * depth, wide), bf16),
            pltpu.SemaphoreType.DMA((2,)),
        ] + remote,
        compiler_params=params,
        cost_estimate=cost(6 * senders),
        name="experts",
    )(mix, cot, gates, weights, experts_w, out, dmix, ds)


def local(
    block_input, gain_input, proj_main, proj_state, proj_step, conv_main, conv_state, step_bias,
    decay_log, skip_gain, gain_gate, proj_out, gain_mix, router_weight, shared_gates, shared_down,
    expert_gates, expert_down, segments, routes, cotangent,
):
    tokens, quarter = block_input.shape
    heads = step_bias.shape[0]
    inner = conv_main.shape[1]
    nstate = conv_state.shape[1] // 2
    per = inner // heads
    tensors = lax.axis_size("tensor")
    zi = lax.axis_index("tensor")
    senders = lax.axis_size(ROWS)
    depth = quarter * tensors
    di_all = inner * tensors
    own = tokens // tensors
    column = zi * quarter
    row0 = zi * own
    wrows = proj_main.shape[0]
    hid = expert_gates.shape[3]
    local_experts = expert_gates.shape[0]
    experts_all = local_experts * senders
    shared_here = shared_down.shape[1]
    router_pad = -experts_all % LANES

    main_wide = 2 * inner + 2 * nstate + LANES
    router_at = main_wide + inner
    weights = gather_rows(
        jnp.concatenate(
            [proj_main[:, 0], proj_main[:, 1], proj_state,
             jnp.pad(proj_step, ((0, 0), (0, LANES - heads))), proj_out,
             jnp.pad(router_weight, ((0, 0), (0, router_pad)))], axis=1
        )
    )
    pair_down = expert_down.reshape(local_experts, hid, depth // (2 * hid), 2 * hid)
    pair = jnp.concatenate(
        [expert_gates.reshape(local_experts, depth, 2 * hid),
         pair_down.transpose(0, 2, 1, 3).reshape(local_experts, -1, 2 * hid)], axis=1
    )
    shared_pair = shared_gates.reshape(wrows, 2, 2, shared_here // 2).transpose(2, 0, 1, 3)
    packed = jnp.concatenate(
        [pair.reshape(-1, 2 * hid), shared_pair.reshape(-1, shared_here), shared_down], axis=0
    )
    experts_w = gather_rows(packed[None])

    seg_row = segments[0]
    last = jnp.concatenate(
        [block_input[tokens - CONV + 1 :],
         jnp.pad(seg_row[None, tokens - CONV + 1 :].astype(bf16), ((0, 0), (0, quarter - CONV + 1)))], axis=0
    )
    halo = shifted(last, CTX, 1)
    halo_seg = halo[CONV - 1, : CONV - 1].astype(jnp.int32)
    extra = jnp.concatenate(
        [jnp.zeros((HALO - CONV + 1, quarter), bf16), halo[: CONV - 1], gain_input[None],
         gain_mix[None], jnp.zeros((14, quarter), bf16)], axis=0
    )
    wide = lambda got: got.transpose(1, 0, 2).reshape(got.shape[1], depth)
    got = spread(block_input)
    cotangent, got = lax.optimization_barrier((cotangent, got))
    got = wide(got)
    got_extra = spread_small(extra)
    cot_raw = spread(cotangent)
    gain_row = got_extra[HALO].astype(f32)
    gain_mid = got_extra[HALO + 1].astype(f32)
    x_ext = jnp.concatenate([got_extra[:HALO], got], axis=0).astype(f32)
    scale_ext = lax.rsqrt(jnp.mean(x_ext * x_ext, axis=-1, keepdims=True) + epsilon)
    normed_ext = x_ext * scale_ext
    mixed_ext = (normed_ext * gain_row).astype(bf16)

    segments_ext = jnp.concatenate([halo_seg, seg_row], axis=0)
    same = jnp.stack(
        [segments_ext[offset : offset + tokens] == seg_row for offset in range(CONV)]
    ).astype(f32)
    same = jnp.broadcast_to(same[:, :, None], (CONV, tokens, LANES))
    taps = jnp.concatenate([conv_main, conv_state], axis=1).astype(f32)
    lanes = lambda v: jnp.pad(v, (0, LANES - heads))[None]
    bias = lanes(step_bias)
    decay = lanes(decay_log)
    skip = jnp.repeat(skip_gain, per)[None]
    link = (seg_row == halo_seg[-1]).astype(f32)[:, None]
    at_end = (seg_row == seg_row[-1]).astype(f32)[:, None]
    seg_col = seg_row[:, None]
    seg_line = seg_row[None]
    value, act, scaled, step, running, run_exp, state_local = enter(
        mixed_ext, weights, taps, same, bias, decay, at_end, link, inner, nstate, per
    )
    run_t = running[:, :heads].T[:, None, :]
    far_in = far_states(state_local, False)
    within = intra(act, scaled, run_t, run_exp, seg_col, seg_line, inner, nstate, per)
    gain_gate_f = gain_gate.astype(f32)[None, :]
    mixer, part, square, state_in = leave(
        act, within, value, far_in, run_exp, link, skip, gain_gate_f, weights, inner, nstate, per
    )
    part, cot_raw = lax.optimization_barrier((part, cot_raw))
    cot_full = wide(cot_raw)
    residual, scale_rows, own_part = residual_step(part, square, got, di_all)

    gain_mid = gain_mid[None]
    chosen = jnp.any(
        routes[:, :, None] == jnp.arange(LANES, dtype=jnp.int32)[None, None, :], axis=1
    ).astype(f32)
    out_part, dmix_part, mixed_two, gates, shared_grad = shared_expert(
        residual, cot_full, gain_mid, weights, router_at, chosen, experts_w
    )
    out_part, dmix_part, dgate, dw = experts(
        mixed_two, cot_full, gates, weights, router_at, experts_w, out_part, dmix_part, shared_grad
    )
    expert_rows = scatter_chips(dw.reshape(-1, 2 * hid))
    dmixer, notes, gains_mid = turn_step(
        dmix_part, dgate, residual, cot_full, own_part, gain_mid
    )

    stats = jnp.stack([scale_rows[0], notes[:, LANES - 1]], axis=1)
    heads_grad, z_grad, gated_out, direct, sums = back(
        dmixer, weights, mixer, value, act, run_exp, link, gain_gate_f, stats, state_local[inner:],
        inner, nstate, di_all
    )
    out_part, dmixer = lax.optimization_barrier((out_part, dmixer))
    out_blocks = out_part.reshape(tokens, tensors, quarter).transpose(1, 0, 2)
    out_raw = exchange(out_blocks)
    far_out = far_states(direct, True)
    dscaled, dstate, drun = intra_back(
        heads_grad, act, scaled, run_t, run_exp, seg_col, seg_line, inner, nstate, per
    )
    state_rows, state_taps, leaving, kept = state_back(
        heads_grad, act, step, running, run_exp, link, at_end, value, taps, same, dstate, state_in,
        far_out, inner, nstate, per
    )
    state_rows, out_raw = lax.optimization_barrier((state_rows, out_raw))
    state_raw = spread(state_rows)
    value_grad, dtaps, small_sums = signal_back(
        heads_grad, act, step, value, taps, same, bias, decay, skip, mixer, within, dscaled, drun,
        leaving, kept, z_grad, state_rows, inner, nstate, per
    )
    first = 2 * inner
    last = first + 2 * nstate
    halo_back = shifted(value_grad[:HALO], CTX, -1)
    state_taps = jnp.pad(state_taps, ((0, 8 - CONV), (0, 0)))
    grad_input, gains, state_taps = finish_step(
        value_grad, halo_back, weights, got, dmixer, gain_row[None], gains_mid, state_taps
    )
    block_sum = jnp.sum(out_raw.astype(f32), axis=0)
    output = (
        lax.dynamic_slice_in_dim(residual, column, quarter, 1).astype(f32) + block_sum
    ).astype(bf16)

    grad_main = dot_inner(mixed_ext, value_grad)
    grad_state = dot_inner(mixed_ext, jnp.sum(state_raw.astype(f32), axis=0).astype(bf16))
    grad_proj_out = dot_inner(dmixer, gated_out)
    moved = jnp.where(col_iota(notes.shape) < experts_all, notes, 0.0)
    dlogits = (gates * (moved - jnp.sum(gates * moved, axis=1, keepdims=True))).astype(bf16)
    grad_router = dot_inner(mixed_two, dlogits)
    main_local = jnp.concatenate(
        [grad_main[:, :first].astype(bf16), grad_state.astype(bf16),
         grad_main[:, last:].astype(bf16), grad_proj_out.astype(bf16), grad_router.astype(bf16)], axis=1
    )
    main_local, expert_rows = lax.optimization_barrier((main_local, expert_rows))
    main_grad = scatter_rows(main_local).astype(f32)
    pair_rows = expert_rows[: local_experts * 3 * depth // 2].reshape(local_experts, -1, 2 * hid)
    down_rows = pair_rows[:, depth:].reshape(local_experts, depth // (2 * hid), hid, 2 * hid)
    shared_rows = expert_rows[local_experts * 3 * depth // 2 :]
    shared_up = shared_rows[: 2 * wrows].reshape(2, wrows, 2, shared_here // 2)
    small = lax.psum((dtaps, small_sums[:2], sums[:2], gains[:2], state_taps[:CONV]), ROWS)
    return (
        output,
        grad_input,
        small[3][0],
        jnp.stack([main_grad[:, :inner], main_grad[:, inner:first]], axis=1),
        main_grad[:, first:last],
        main_grad[:, last : last + heads],
        small[0],
        small[4],
        small[1][0, :heads],
        small[1][1, :heads],
        jnp.sum(small[2][1].reshape(heads, per), axis=1),
        small[2][0],
        main_grad[:, main_wide:router_at],
        small[3][1],
        main_grad[:, router_at : router_at + experts_all],
        shared_up.transpose(1, 2, 0, 3).reshape(wrows, 2, shared_here).astype(f32),
        shared_rows[2 * wrows :].astype(f32),
        pair_rows[:, :depth].reshape(expert_gates.shape).astype(f32),
        down_rows.transpose(0, 2, 1, 3).reshape(expert_down.shape).astype(f32),
    )


def solution(mesh):
    shard, ctx, tensor = (mesh.shape[name] for name in ("shard", "ctx", "tensor"))
    core = 2 if shard * ctx == 8 else 1
    split = jax.sharding.Mesh(
        mesh.devices.reshape(shard, ctx // core, core, tensor), ("shard", "cy", "core", "tensor")
    )
    return jax.shard_map(
        local,
        mesh=split,
        in_specs=(
            P(ROWS, "tensor"),
            P("tensor"),
            P(ROWS, None, "tensor"),
            P(ROWS, None),
            P(ROWS, "tensor"),
            P(None, "tensor"),
            P(),
            P("tensor"),
            P("tensor"),
            P("tensor"),
            P("tensor"),
            P(ROWS, "tensor"),
            P("tensor"),
            P(ROWS, None),
            P(ROWS, None, "tensor"),
            P(ROWS, "tensor"),
            P(ROWS, None, None, "tensor"),
            P(ROWS, "tensor", None),
            P("shard", CTX),
            P(ROWS, None),
            P(ROWS, "tensor"),
        ),
        out_specs=(
            P(ROWS, "tensor"),
            P(ROWS, "tensor"),
            P("tensor"),
            P(ROWS, None, "tensor"),
            P(ROWS, None),
            P(ROWS, "tensor"),
            P(None, "tensor"),
            P(),
            P("tensor"),
            P("tensor"),
            P("tensor"),
            P("tensor"),
            P(ROWS, "tensor"),
            P("tensor"),
            P(ROWS, None),
            P(ROWS, None, "tensor"),
            P(ROWS, "tensor"),
            P(ROWS, None, None, "tensor"),
            P(ROWS, "tensor", None),
        ),
        check_vma=False,
    )
```

```python
from functools import partial

import jax
import jax.numpy as jnp
from jax import lax
from jax.experimental import pallas as pl
from jax.experimental.pallas import tpu as pltpu
from jax.sharding import PartitionSpec as P

CONV = 4
HALO = 16
LANES = 128
LANES = 128
LANES = 128


epsilon = 1e-05
highest = lax.Precision.HIGHEST
CTX = ("cy", "core")
CHIPS = ("shard", "cy")
ROWS = ("shard", "cy", "core")
f32 = jnp.float32
MESH = pl.DeviceIdType.MESH
bf16 = jnp.bfloat16
BIG = pltpu.CompilerParams(vmem_limit_bytes=60 << 20)


def cost(micros):
    return pl.CostEstimate(flops=micros * 900_000_000, transcendentals=0, bytes_accessed=1 << 20)
BIG = pltpu.CompilerParams(vmem_limit_bytes=60 << 20)


def cost(micros):
    return pl.CostEstimate(flops=micros * 900_000_000, transcendentals=0, bytes_accessed=1 << 20)
BIG = pltpu.CompilerParams(vmem_limit_bytes=60 << 20)


def cost(micros):
    return pl.CostEstimate(flops=micros * 900_000_000, transcendentals=0, bytes_accessed=1 << 20)


def shifted(value, axis, steps):
    count = lax.axis_size(axis)
    leading, last = (max(0, -steps), min(count, count - steps))
    return lax.ppermute(value, axis, [(source, source + steps) for source in range(leading, last)])


def dot_rows(left, right, precision=None):
    return jnp.dot(left, right, preferred_element_type=f32, precision=precision)


def dot_inner(left, right):
    return lax.dot_general(left, right, (((0,), (0,)), ((), ())), preferred_element_type=f32)


def dot_outer(left, right):
    return lax.dot_general(left, right, (((1,), (1,)), ((), ())), preferred_element_type=f32)


def sigmoid(value):
    return 1.0 / (1.0 + jnp.exp(-value))


def gather_rows(value):
    return lax.all_gather(value, ROWS, axis=0, tiled=True)


def scatter_rows(value):
    return lax.psum_scatter(value, ROWS, scatter_dimension=0, tiled=True)


def scatter_chips(value):
    axes = CHIPS if lax.axis_size("core") == 2 else ROWS
    return lax.psum_scatter(value, axes, scatter_dimension=0, tiled=True)


def exchange(blocks):
    return lax.all_to_all(blocks, "tensor", split_axis=0, concat_axis=0, tiled=True)


def spread(block):
    count = lax.axis_size("tensor")
    return exchange(jnp.broadcast_to(block[None], (count,) + block.shape))


def spread_small(block):
    count, index = lax.axis_size("tensor"), lax.axis_index("tensor")
    width = block.shape[1]
    full = jnp.zeros((block.shape[0], count * width), block.dtype)
    for away in range(count):
        moved = block if away == 0 else lax.ppermute(
            block, "tensor", [(i, (i + away) % count) for i in range(count)]
        )
        origin = lax.rem(index - away + count, count)
        full = lax.dynamic_update_slice_in_dim(full, moved, origin * width, 1)
    return full


def halves(value):
    high = value.astype(bf16)
    return high, (value - high.astype(f32)).astype(bf16)


def far_states(packed, reverse):
    count = lax.axis_size(CTX)
    return jnp.stack([
        shifted(packed, CTX, -away if reverse else away) for away in range(1, count)
    ])


def row_iota(shape):
    return lax.broadcasted_iota(jnp.int32, shape, 0)


def col_iota(shape):
    return lax.broadcasted_iota(jnp.int32, shape, 1)


def expander(lanes, width, per):
    low = row_iota((lanes, width)) * per
    at = col_iota((lanes, width))
    return ((at >= low) & (at < low + per)).astype(f32)


def head_fold(width, lanes, per):
    low = col_iota((width, lanes)) * per
    at = row_iota((width, lanes))
    return ((at >= low) & (at < low + per)).astype(f32)


def pack_state(state, through):
    high, low = halves(through)
    row = row_iota((16, LANES))
    tail = jnp.where(row == 0, high.astype(f32), jnp.where(row == 1, low.astype(f32), 0.0))
    return jnp.concatenate([state, tail], axis=0).astype(bf16)


def join_states(far_ref, inner, per):
    spread_heads = head_fold(inner, LANES, per)
    total = None
    for k in reversed(range(far_ref.shape[0])):
        state = far_ref[k, :inner, :].astype(f32)
        if total is not None:
            through = far_ref[k, inner : inner + 16, :].astype(f32)
            through = through[0:1] + through[1:2]
            state = state + jnp.sum(spread_heads * through, axis=1, keepdims=True) * total
        total = state
    return total


def thirds(value):
    high = value.astype(bf16)
    rest = value - high.astype(f32)
    middle = rest.astype(bf16)
    return high, middle, (rest - middle.astype(f32)).astype(bf16)


def spread_lanes(value, grow):
    ones = grow.astype(bf16)
    return sum(dot_rows(part, ones) for part in thirds(value))


def left_sums(zero_one, value):
    return sum(dot_rows(zero_one, part) for part in thirds(value))


def fold_heads(value, folds):
    high, low = halves(value)
    return dot_rows(high, folds) + dot_rows(low, folds)


def conv_pre(value_ref, column, taps_ref, taps_column, same_ref, tokens):
    rows = value_ref[:, pl.ds(column, LANES)]
    total = None
    for offset in range(CONV):
        first = HALO - CONV + 1 + offset
        term = rows[first : first + tokens] * (
            same_ref[offset] * taps_ref[offset : offset + 1, pl.ds(taps_column, LANES)]
        )
        total = term if total is None else total + term
    return rows, total


def enter_part(mixed_ref, w_ref, taps_ref, same_ref, bias_ref, decay_ref, end_ref, link_ref,
                 value_ref, act_ref, scaled_ref, step_ref, run_ref, run_exp_ref,
                 state_ref, *, inner, nstate, per):
    tokens = act_ref.shape[0]
    width = 2 * inner + 2 * nstate + LANES
    tile = 384

    def matmul(i, _):
        columns = pl.ds(pl.multiple_of(i * tile, LANES), tile)
        value_ref[:, columns] = dot_rows(mixed_ref[...], w_ref[:, columns])
        return 0

    lax.fori_loop(0, width // tile, matmul, 0)

    def conv(i, _):
        at = pl.multiple_of(i * LANES, LANES)
        _, total = conv_pre(value_ref, inner + at, taps_ref, at, same_ref, tokens)
        act_ref[:, pl.ds(at, LANES)] = (total * sigmoid(total)).astype(bf16)
        return 0

    lax.fori_loop(0, (inner + 2 * nstate) // LANES, conv, 0)
    raw = value_ref[HALO:, 2 * inner + 2 * nstate :] + bias_ref[...]
    step = jnp.maximum(raw, 0.0) + jnp.log1p(jnp.exp(-jnp.abs(raw)))
    log_decay = step * -jnp.exp(decay_ref[...])
    tri = (row_iota((tokens, tokens)) >= col_iota((tokens, tokens))).astype(bf16)
    running = left_sums(tri, log_decay)
    step_ref[...] = step
    run_ref[...] = running
    grow = expander(LANES, inner, per)
    run_exp_ref[...] = spread_lanes(running, grow)
    signal = act_ref[:, :inner].astype(f32)
    scaled_ref[...] = (signal * spread_lanes(step, grow)).astype(bf16)
    toward = step * jnp.exp(running[tokens - 1 :] - running) * end_ref[...]
    pushed = (signal * spread_lanes(toward, grow)).astype(bf16)
    through = jnp.exp(running[tokens - 1 :]) * link_ref[tokens - 1 :]
    state_ref[...] = pack_state(dot_inner(pushed, act_ref[:, inner : inner + nstate]), through)


def whole(a):
    return pl.BlockSpec(a.shape, lambda i: (0,) * len(a.shape))


def columns(a, width, at=0):
    assert at % width == 0
    return pl.BlockSpec((a.shape[0], width), lambda i: (0, at // width))


def masked_scores(query, keys, seg_col_ref, seg_row_ref, start, stop):
    shape = (stop - start, stop)
    allowed = (row_iota(shape) + start >= col_iota(shape)) & (
        seg_col_ref[start:stop, :1] == seg_row_ref[:, :stop]
    )
    return jnp.where(allowed, dot_outer(query[start:stop], keys[:stop]), 0.0)


def intra_part(act_ref, scaled_ref, run_t_ref, run_exp_ref, seg_col_ref, seg_row_ref,
                 inner_ref, scores_ref, *, inner, nstate, per, block):
    tokens = act_ref.shape[0]
    keys = act_ref[:, inner : inner + nstate]
    query = act_ref[:, inner + nstate :]
    for start in range(0, tokens, block):
        stop = start + block
        scores_ref[start:stop, :stop] = masked_scores(
            query, keys, seg_col_ref, seg_row_ref, start, stop
        )

    def pair(i, _):
        columns = pl.ds(pl.multiple_of(i * LANES, LANES), LANES)
        scaled = scaled_ref[:, columns]
        lane = col_iota(scaled.shape)
        run = run_exp_ref[:, columns]
        for start in range(0, tokens, block):
            stop = start + block
            total = None
            for h in range(LANES // per):
                mine = (lane >= h * per) & (lane < (h + 1) * per)
                vals = jnp.where(mine, scaled, jnp.zeros_like(scaled))[:stop]
                row = run_t_ref[i * (LANES // per) + h, :, :stop]
                decay = jnp.exp(jnp.minimum(run[start:stop, h * per : h * per + 1] - row, 0.0))
                weight = (decay * scores_ref[start:stop, :stop]).astype(bf16)
                term = dot_rows(weight, vals)
                total = term if total is None else total + term
            inner_ref[start:stop, columns] = total
        return 0

    lax.fori_loop(0, inner // LANES, pair, 0)


def row_sums(value):
    folded = value[:, :LANES]
    for at in range(LANES, value.shape[1], LANES):
        folded = folded + value[:, at : at + LANES]
    ones = jnp.ones((8, LANES), bf16)
    high, low = halves(folded)
    return dot_outer(ones, high) + dot_outer(ones, low)


def as_column(row):
    n = row.shape[1]
    eye = row_iota((n, n)) == col_iota((n, n))
    return jnp.sum(jnp.where(eye, row, 0.0), axis=1, keepdims=True)


def tensor_barrier(me, n):
    barrier = pltpu.get_barrier_semaphore()
    for d in range(1, n):
        pl.semaphore_signal(
            barrier, inc=1, device_id={"tensor": lax.rem(me + d, n)}, device_id_type=MESH
        )
    pl.semaphore_wait(barrier, n - 1)


def push(source, target, sems, slot, peer):
    send, receive = sems
    return pltpu.make_async_remote_copy(
        src_ref=source, dst_ref=target, send_sem=send.at[slot], recv_sem=receive.at[slot],
        device_id=peer if isinstance(peer, dict) else {"tensor": peer}, device_id_type=MESH,
    )


def ctx_place():
    core = lax.axis_size("core")
    return lax.axis_index("cy") * core + lax.axis_index("core"), lax.axis_size("cy") * core


def ctx_peer(place):
    core = lax.axis_size("core")
    return {"cy": place // core, "core": lax.rem(place, core)}


def front_barrier(me, n):
    barrier = pltpu.get_barrier_semaphore()
    place, count = ctx_place()
    for d in range(1, n):
        pl.semaphore_signal(
            barrier, inc=1, device_id={"tensor": lax.rem(me + d, n)}, device_id_type=MESH
        )
    for d in range(1, count):
        pl.semaphore_signal(
            barrier, inc=1, device_id=ctx_peer(lax.rem(place + d, count)), device_id_type=MESH
        )
    pl.semaphore_wait(barrier, n - 1 + count - 1)


class StatePush:
    def __init__(self, source, far_ref, sems, reverse):
        place, count = ctx_place()
        sign = -1 if reverse else 1
        self.copies = []
        for d in range(1, count):
            to, origin = place + sign * d, place - sign * d
            copy = push(source, far_ref.at[d - 1], sems, d - 1,
                        ctx_peer(lax.rem(to + count, count)))
            self.copies.append((copy, (to >= 0) & (to < count), (origin >= 0) & (origin < count)))

    def start(self):
        for copy, sends, _ in self.copies:
            pl.when(sends)(copy.start)

    def wait_recv(self):
        for copy, _, gets in self.copies:
            pl.when(gets)(copy.wait_recv)

    def wait_send(self):
        for copy, sends, _ in self.copies:
            pl.when(sends)(copy.wait_send)


class LineReduce:
    def __init__(self, me, n, blocks, right, left, sems):
        self.me, self.n, self.blocks, self.right, self.left = me, n, blocks, right, left
        self.right_sems, self.left_sems = sems
        self.keep = lambda d: jnp.minimum(jnp.maximum(d, 0), n - 1)

    def rightward(self, d):
        return push(self.blocks(d), self.right.at[d], self.right_sems, d,
                    jnp.minimum(self.me + 1, self.n - 1))

    def leftward(self, d):
        return push(self.blocks(d), self.left.at[d], self.left_sems, d, jnp.maximum(self.me - 1, 0))

    def step(self, t):
        me, n = self.me, self.n
        ways = []
        if t < n:
            ways.append((n - 1 - t + me, me >= 1, lambda d: d > me, t >= me, self.rightward, self.right))
            ways.append((t - (n - 1 - me), me <= n - 2, lambda d: d < me, t >= n - 1 - me,
                         self.leftward, self.left))
        for d, gets, passes, ready, copy_of, box in ways:
            at = self.keep(d)
            copy = copy_of(at)

            @pl.when(gets & ready)
            def _():
                copy.wait_recv()

            @pl.when(gets & ready & passes(d))
            def _():
                view = self.blocks(at)
                view[...] = view[...] + box[at]

            @pl.when(ready & passes(d))
            def _():
                copy.start()

    def total(self):
        me, n = self.me, self.n
        value = self.blocks(me)[...].astype(f32)
        value = value + jnp.where(me >= 1, self.right[me].astype(f32), 0.0)
        return value + jnp.where(me <= n - 2, self.left[me].astype(f32), 0.0)

    def wait_send(self):
        for d in range(self.n):
            pl.when(self.me < d)(self.rightward(d).wait_send)
            pl.when(self.me > d)(self.leftward(d).wait_send)


class LineGather:
    def __init__(self, me, n, blocks, sems):
        self.me, self.n, self.blocks = me, n, blocks
        self.right_sems, self.left_sems = sems

    def rightward(self, d):
        return push(self.blocks(d), self.blocks(d), self.right_sems, d,
                    jnp.minimum(self.me + 1, self.n - 1))

    def leftward(self, d):
        return push(self.blocks(d), self.blocks(d), self.left_sems, d, jnp.maximum(self.me - 1, 0))

    def step(self, t):
        me, n = self.me, self.n
        from_left, from_right = me - t, me + t
        right = self.rightward(jnp.maximum(from_left, 0))
        left = self.leftward(jnp.minimum(from_right, n - 1))
        if t > 0:
            pl.when(from_left >= 0)(right.wait_recv)
        pl.when((from_left >= 0) & (me <= n - 2))(right.start)
        if t > 0:
            pl.when(from_right <= n - 1)(left.wait_recv)
        pl.when((from_right <= n - 1) & (me >= 1))(left.start)

    def wait_send(self):
        for d in range(self.n):
            pl.when((self.me >= d) & (self.me <= self.n - 2))(self.rightward(d).wait_send)
            pl.when((self.me <= d) & (self.me >= 1))(self.leftward(d).wait_send)


def line_sems(n):
    return [pltpu.SemaphoreType.DMA((n,))] * 4


def line_groups(sems):
    return (sems[0], sems[1]), (sems[2], sems[3])


def line_barrier(me, n):
    barrier = pltpu.get_barrier_semaphore()
    for d in range(1, n):
        pl.semaphore_signal(
            barrier, inc=1, device_id={"tensor": lax.rem(me + d, n)}, device_id_type=MESH
        )
    return barrier


def intake_kernel(x_ref, gains_ref, mixed_ref, mixed_t_ref, full_ref, gain_out,
                  x_box, gains_box, halo_box, *sems, n):
    me = lax.axis_index("tensor")
    place, count = ctx_place()
    rows, quarter = x_ref.shape
    column = lambda d: pl.ds(pl.multiple_of(d * quarter, LANES), quarter)
    gain_sems, halo_sems = (sems[0], sems[1]), (sems[2], sems[3])
    halo_box[...] = jnp.zeros_like(halo_box)
    x_box[:, column(me)] = x_ref[...]
    gains_box[:, column(me)] = gains_ref[...]
    barrier = line_barrier(me, n)
    for away in (1, count - 1):
        for z in range(n):
            pl.semaphore_signal(
                barrier, inc=1, device_id={**ctx_peer(lax.rem(place + away, count)), "tensor": z},
                device_id_type=MESH,
            )
    pl.semaphore_wait(barrier, n - 1 + 2 * n)
    x_line = LineGather(me, n, lambda d: x_box.at[:, column(d)], line_groups(sems[4:8]))
    x_line.step(0)
    gains = [push(gains_box.at[:, column(me)], gains_box.at[:, column(me)], gain_sems, d - 1,
                  lax.rem(me + d, n)) for d in range(1, n)]
    for copy in gains:
        copy.start()
    sends, gets = place < count - 1, place > 0
    halos = []
    for d in range(n):
        peer = {**ctx_peer(jnp.minimum(place + 1, count - 1)), "tensor": lax.rem(me + d, n)}
        halos.append(push(x_ref.at[rows - HALO :], halo_box.at[:, column(me)], halo_sems, d, peer))
        pl.when(sends)(halos[-1].start)
    for t in range(1, n):
        x_line.step(t)
    for copy in gains:
        copy.wait_recv()
    for copy in halos:
        pl.when(gets)(copy.wait_recv)
    gain = gains_box[0:1, :].astype(f32)
    gain_out[...] = gains_box[...].astype(f32)

    def normed(x):
        x = x.astype(f32)
        scale = lax.rsqrt(jnp.mean(x * x, axis=1, keepdims=True) + epsilon)
        return (x * scale * gain).astype(bf16)

    mixed_ref[:HALO, :] = normed(halo_box[...])
    full_ref[...] = x_box[...]
    mixed_ref[HALO:, :] = normed(x_box[...])
    mixed_t_ref[...] = mixed_ref[HALO:, :].T
    for copy in gains:
        copy.wait_send()
    for copy in halos:
        pl.when(sends)(copy.wait_send)
    x_line.wait_send()


def intake(x, gains):
    n = lax.axis_size("tensor")
    rows, quarter = x.shape
    depth = n * quarter
    shape = jax.ShapeDtypeStruct
    dma = pltpu.SemaphoreType.DMA
    return pl.pallas_call(
        partial(intake_kernel, n=n),
        in_specs=[VMEM] * 2,
        out_specs=[VMEM] * 4,
        out_shape=[shape((rows + HALO, depth), bf16), shape((depth, rows), bf16),
                   shape((rows, depth), bf16), shape((16, depth), f32)],
        scratch_shapes=[
            pltpu.VMEM((rows, depth), bf16),
            pltpu.VMEM((16, depth), bf16), pltpu.VMEM((HALO, depth), bf16),
            dma((n - 1,)), dma((n - 1,)), dma((n,)), dma((n,)),
        ] + line_sems(n),
        compiler_params=pltpu.CompilerParams(
            vmem_limit_bytes=60 << 20, collective_id=7, has_side_effects=True
        ),
        cost_estimate=cost(50),
        name="intake",
    )(x, gains)


def row_columns(row):
    return jnp.concatenate(
        [as_column(row[:, at : at + LANES]) for at in range(0, row.shape[1], LANES)], axis=0
    )


def front_kernel(mixed_ref, taps_ref, same_ref, bias_ref, decay_ref, end_ref, link_ref, seg_col_ref,
                 seg_row_ref, skip_ref, gain_ref, x_ref, cot_ref, w_ref,
                 value_ref, act_ref, scaled_ref, step_ref, run_ref, run_exp_ref, inner_ref, mixer_ref,
                 state_ref, packed_ref, res_ref, stat_ref, own_ref, cot_full_ref,
                 wm_ref, wo_ref, run_t_ref, scores_ref, part_ref, square_ref, lifted_ref, far_ref,
                 right_box, left_box, square_box, res_box, stat_box, cot_box, local_sem, *sems,
                 inner, nstate, per, heads, di_all, n):
    me = lax.axis_index("tensor")
    rows, depth = x_ref.shape
    own = rows // n
    groups = [(sems[2 * i], sems[2 * i + 1]) for i in range(3)]
    block_at = lambda d: pl.ds(pl.multiple_of(d * own, own), own)
    mine = pl.ds(pl.multiple_of(me * own, own), own)
    wide = wm_ref.shape[1]
    loads = [
        pltpu.make_async_copy(w_ref.at[:, pl.ds(0, wide)], wm_ref, local_sem.at[0]),
        pltpu.make_async_copy(w_ref.at[:, pl.ds(wide, inner)], wo_ref, local_sem.at[1]),
    ]
    for copy in loads:
        copy.start()
    far_ref[...] = jnp.zeros_like(far_ref)
    quarter = cot_ref.shape[1]
    column = pl.ds(pl.multiple_of(me * quarter, LANES), quarter)
    cot_box[:, column] = cot_ref[...]
    front_barrier(me, n)
    cots = LineGather(
        me, n, lambda d: cot_box.at[:, pl.ds(pl.multiple_of(d * quarter, LANES), quarter)],
        line_groups(sems[14:18]),
    )
    cots.step(0)
    loads[0].wait()
    enter_part(mixed_ref, wm_ref, taps_ref, same_ref, bias_ref, decay_ref, end_ref, link_ref,
               value_ref, act_ref, scaled_ref, step_ref, run_ref, run_exp_ref, packed_ref,
               inner=inner, nstate=nstate, per=per)
    states = StatePush(packed_ref, far_ref, groups[0], False)
    states.start()
    cots.step(1)
    run_t = run_ref[...].T
    for h in range(heads):
        run_t_ref[h] = run_t[h : h + 1, :]
    intra_part(act_ref, scaled_ref, run_t_ref, run_exp_ref, seg_col_ref, seg_row_ref, inner_ref,
               scores_ref, inner=inner, nstate=nstate, per=per, block=128)
    cots.step(2)
    states.wait_recv()
    state = join_states(far_ref, inner, per)
    state_ref[...] = state
    carried = dot_outer(act_ref[:, inner + nstate :], state.astype(bf16)) * (
        jnp.exp(run_exp_ref[...]) * link_ref[...]
    )
    mixer = inner_ref[...] + carried + skip_ref[...] * act_ref[:, :inner].astype(f32)
    mixer_ref[...] = mixer
    z = value_ref[HALO:, :inner]
    gated = mixer * (z * sigmoid(z))
    square_ref[...] = row_sums(gated * gated)
    lifted_ref[...] = (gated * gain_ref[...]).astype(bf16)
    loads[1].wait()
    for t in range(3, n):
        cots.step(t)
    squares, stats = [], []
    for d in range(1, n):
        peer = lax.rem(me + d, n)
        squares.append(push(square_ref.at[:, block_at(peer)], square_box.at[d - 1], groups[1], d - 1, peer))
        squares[-1].start()
    line = LineReduce(me, n, lambda d: part_ref.at[d], right_box, left_box, line_groups(sems[6:10]))
    for k in range(n):
        d = jnp.where(2 * me < n, n - 1 - k, k)
        part_ref[d] = dot_outer(lifted_ref[block_at(d), :], wo_ref[...]).astype(bf16)
        if k == 0:
            line.step(0)
    for t in range(1, n):
        line.step(t)
    total = line.total()
    square = square_ref[:, mine]
    for copy in squares:
        copy.wait_recv()
    for d in range(1, n):
        square = square + square_box[d - 1]
    own_ref[...] = total
    scale = lax.rsqrt(square / di_all + epsilon)
    stat_box[:, mine] = scale
    res_box[mine, :] = (x_ref[mine, :].astype(f32) + total * as_column(scale[:1])).astype(bf16)
    gather = LineGather(me, n, lambda d: res_box.at[block_at(d)], line_groups(sems[10:14]))
    gather.step(0)
    for d in range(1, n):
        stats.append(push(stat_box.at[:, mine], stat_box.at[:, mine], groups[2], d - 1,
                          lax.rem(me + d, n)))
        stats[-1].start()
    for t in range(1, n):
        gather.step(t)
    cot_full_ref[...] = cot_box[...]
    states.wait_send()
    cots.wait_send()
    line.wait_send()
    gather.wait_send()
    for copy in squares:
        copy.wait_send()
    for copy in stats:
        copy.wait()
    res_ref[...] = res_box[...]
    stat_ref[...] = stat_box[...]


def pairs(count, n):
    return [pltpu.SemaphoreType.DMA((n - 1,))] * (2 * count)


VMEM = pl.BlockSpec(memory_space=pltpu.VMEM)
HBM = pl.BlockSpec(memory_space=pl.ANY)


def front(mixed_ext, taps, same, bias, decay, at_end, link, seg_col, seg_row, skip, gain, x, cot, weights,
          inner, nstate, per, heads, di_all):
    n = lax.axis_size("tensor")
    others = lax.axis_size(CTX) - 1
    tokens, depth = x.shape
    ext = tokens + HALO
    own = tokens // n
    wide = 2 * inner + 2 * nstate + LANES
    shape = jax.ShapeDtypeStruct
    outs = [
        shape((ext, wide), f32), shape((tokens, inner + 2 * nstate), bf16),
        shape((tokens, inner), bf16), shape((tokens, LANES), f32), shape((tokens, LANES), f32),
        shape((tokens, inner), f32), shape((tokens, inner), f32), shape((tokens, inner), f32),
        shape((inner, nstate), f32), shape((inner + 16, nstate), bf16),
        shape((tokens, depth), bf16), shape((8, tokens), f32), shape((own, depth), f32),
        shape((tokens, depth), bf16),
    ]
    dma = pltpu.SemaphoreType.DMA
    return pl.pallas_call(
        partial(front_kernel, inner=inner, nstate=nstate, per=per, heads=heads, di_all=di_all, n=n),
        in_specs=[VMEM] * 13 + [HBM],
        out_specs=[VMEM] * 14,
        out_shape=outs,
        scratch_shapes=[
            pltpu.VMEM((depth, wide), bf16), pltpu.VMEM((depth, inner), bf16),
            pltpu.VMEM((heads, 1, tokens), f32), pltpu.VMEM((tokens, tokens), f32),
            pltpu.VMEM((n, own, depth), bf16), pltpu.VMEM((8, tokens), f32),
            pltpu.VMEM((tokens, inner), bf16), pltpu.VMEM((others, inner + 16, nstate), bf16),
            pltpu.VMEM((n, own, depth), bf16), pltpu.VMEM((n, own, depth), bf16),
            pltpu.VMEM((n - 1, 8, own), f32),
            pltpu.VMEM((tokens, depth), bf16), pltpu.VMEM((8, tokens), f32),
            pltpu.VMEM((tokens, depth), bf16), dma((2,)), dma((others,)), dma((others,)),
        ] + pairs(2, n) + line_sems(n) * 3,
        compiler_params=pltpu.CompilerParams(
            vmem_limit_bytes=60 << 20, collective_id=1, has_side_effects=True
        ),
        cost_estimate=cost(100),
        name="front",
    )(mixed_ext, taps, same, bias, decay, at_end, link, seg_col, seg_row, skip, gain, x, cot, weights)


def turn_kernel(dmix_hbm, dgate_ref, res_ref, cot_ref, own_ref, gain_ref,
                dres_ref, notes_ref, gains_ref,
                dmix_ref, right_box, left_box, gate_box, dres_box, notes_box, load_sem, *sems, n):
    me = lax.axis_index("tensor")
    rows, depth = res_ref.shape
    own = rows // n
    groups = [(sems[2 * i], sems[2 * i + 1]) for i in range(2)]
    block_at = lambda d: pl.ds(pl.multiple_of(d * own, own), own)
    mine = block_at(me)
    load = pltpu.make_async_copy(dmix_hbm, dmix_ref, load_sem)
    load.start()
    tensor_barrier(me, n)
    load.wait()
    line = LineReduce(me, n, lambda d: dmix_ref.at[block_at(d)], right_box, left_box,
                      line_groups(sems[4:8]))
    gather = LineGather(me, n, lambda d: dres_box.at[block_at(d)], line_groups(sems[8:12]))
    line.step(0)
    first, second = [], []
    for d in range(1, n):
        peer = lax.rem(me + d, n)
        first.append(push(dgate_ref.at[:, block_at(peer)], gate_box.at[d - 1], groups[0], d - 1, peer))
        first[-1].start()
    res = res_ref[mine, :].astype(f32)
    scale = lax.rsqrt(jnp.mean(res * res, axis=1, keepdims=True) + epsilon)
    normed = res * scale
    for t in range(1, n):
        line.step(t)
    dmix = line.total()
    lifted = dmix * gain_ref[...]
    inside = jnp.mean(lifted * normed, axis=1, keepdims=True)
    dres = (cot_ref[mine, :].astype(f32) + scale * (lifted - normed * inside)).astype(bf16)
    dres_box[mine, :] = dres
    gather.step(0)
    gains_ref[...] = jnp.broadcast_to(jnp.sum(dmix * normed, axis=0, keepdims=True), gains_ref.shape)
    dgate = dgate_ref[:, mine]
    for copy in first:
        copy.wait_recv()
    for d in range(1, n):
        dgate = dgate + gate_box[d - 1]
    gates = dgate.shape[0]
    notes_box[:gates, mine] = dgate
    notes_box[gates:, mine] = row_sums(dres.astype(f32) * own_ref[...])
    for d in range(1, n):
        peer = lax.rem(me + d, n)
        second.append(push(notes_box.at[:, mine], notes_box.at[:, mine], groups[1], d - 1, peer))
        second[-1].start()
    for t in range(1, n):
        gather.step(t)
    line.wait_send()
    gather.wait_send()
    for copy in first:
        copy.wait_send()
    for copy in second:
        copy.wait()
    dres_ref[...] = dres_box[...]
    notes_ref[...] = notes_box[...]


def turn_step(dmix, dgate, residual, cot, own_part, gain):
    n = lax.axis_size("tensor")
    tokens, depth = dmix.shape
    own = tokens // n
    shape = jax.ShapeDtypeStruct
    return pl.pallas_call(
        partial(turn_kernel, n=n),
        in_specs=[HBM] + [VMEM] * 5,
        out_specs=[VMEM] * 3,
        out_shape=[shape((tokens, depth), bf16), shape((dgate.shape[0] + 8, tokens), f32),
                   shape((8, depth), f32)],
        scratch_shapes=[
            pltpu.VMEM((tokens, depth), bf16),
            pltpu.VMEM((n, own, depth), bf16), pltpu.VMEM((n, own, depth), bf16),
            pltpu.VMEM((n - 1, dgate.shape[0], own), f32),
            pltpu.VMEM((tokens, depth), bf16), pltpu.VMEM((dgate.shape[0] + 8, tokens), f32),
            pltpu.SemaphoreType.DMA,
        ] + pairs(2, n) + line_sems(n) * 2,
        compiler_params=pltpu.CompilerParams(
            vmem_limit_bytes=60 << 20, collective_id=2, has_side_effects=True
        ),
        cost_estimate=cost(60),
        name="turn_step",
    )(dmix, dgate, residual, cot, own_part, gain)


def in_order(box, me, count):
    total = None
    for source in range(count):
        term = box[lax.rem(me - source + 2 * count - 1, count)].astype(f32)
        total = term if total is None else total + term
    return total


def row_place():
    cy, core = lax.axis_size("cy"), lax.axis_size("core")
    return (lax.axis_index("shard") * cy + lax.axis_index("cy")) * core + lax.axis_index("core")


def row_peer(place):
    cy, core = lax.axis_size("cy"), lax.axis_size("core")
    return {"shard": place // (cy * core), "cy": lax.rem(place // core, cy), "core": lax.rem(place, core)}


def finish_kernel(grad_ref, x_ref, dres_ref, gain_ref, mid_ref, state_ref, early_ref,
                  w_hbm, pair_hbm,
                  out_ref, early_out, late_out, gates_out, down_out,
                  w_ref, pair_ref, blocks_ref, right_box, left_box, cross_box, cross_in, gains_box, gains_in,
                  state_in, early_in, late_ref, late_in, load_sem, *sems, n, count):
    me = lax.axis_index("tensor")
    place = row_place()
    rows, depth = x_ref.shape
    quarter = depth // n
    wide = w_ref.shape[1]
    groups = [(sems[2 * i], sems[2 * i + 1]) for i in range(3)]
    row_groups = [(sems[6 + 2 * i], sems[7 + 2 * i]) for i in range(2)]
    loads = [pltpu.make_async_copy(w_hbm.at[:, pl.ds(0, wide)], w_ref, load_sem.at[0]),
             pltpu.make_async_copy(pair_hbm, pair_ref, load_sem.at[1])]
    for copy in loads:
        copy.start()
    barrier = line_barrier(me, n)
    for d in range(1, count):
        pl.semaphore_signal(barrier, inc=1, device_id=row_peer(lax.rem(place + d, count)),
                            device_id_type=MESH)
    pl.semaphore_wait(barrier, n - 1 + count - 1)
    copies, states, lates = [], [], []
    for d in range(1, n):
        states.append(push(state_ref, state_in.at[d - 1], groups[2], d - 1, lax.rem(me + d, n)))
        states[-1].start()
    x = x_ref[...].astype(f32)
    scale = lax.rsqrt(jnp.mean(x * x, axis=1, keepdims=True) + epsilon)
    loads[0].wait()
    line = LineReduce(me, n, lambda d: blocks_ref.at[d], right_box, left_box, line_groups(sems[10:14]))
    cross = jnp.zeros((8, rows), f32)
    for k in range(n):
        d = jnp.where(2 * me < n, n - 1 - k, k)
        theirs = pl.ds(pl.multiple_of(d * quarter, LANES), quarter)
        w = w_ref[theirs, :]
        block = dot_outer(grad_ref[...], w)
        blocks_ref[d] = block.astype(bf16)
        if k == 0:
            line.step(0)
        normed = x_ref[:, theirs].astype(f32) * scale
        cross = cross + row_sums(block * normed * gain_ref[:, theirs])
        gains_box[d] = jnp.where(
            row_iota((8, quarter)) == 0, jnp.sum(block * normed, axis=0, keepdims=True),
            mid_ref[:, theirs],
        )
    cross_box[...] = cross
    for d in range(1, n):
        peer = lax.rem(me + d, n)
        copies.append(push(gains_box.at[peer], gains_in.at[d - 1], groups[0], d - 1, peer))
        copies.append(push(cross_box, cross_in.at[d - 1], groups[1], d - 1, peer))
    for d in range(1, count):
        copies.append(push(early_ref, early_in.at[d - 1], row_groups[0], d - 1,
                           row_peer(lax.rem(place + d, count))))
    for copy in copies:
        copy.start()
    if n > 1:
        line.step(1)
    loads[1].wait()
    hid = down_out.shape[1]
    wides = 2 * hid
    deep = pair_ref.shape[0] // 2
    for p in range(2):
        top = pair_ref[p * deep : p * deep + depth, :].astype(f32)
        gates_out[p * depth : (p + 1) * depth, 0, :] = top[:, :hid]
        gates_out[p * depth : (p + 1) * depth, 1, :] = top[:, hid:]
        for c in range(depth // wides):
            at = p * deep + depth + c * hid
            down_out[p, :, c * wides : (c + 1) * wides] = pair_ref[at : at + hid, :].astype(f32)
    for copy in copies[: 2 * (n - 1)] + states:
        copy.wait_recv()
    gains = gains_box[me]
    state = state_ref[...]
    for d in range(1, n):
        gains = gains + gains_in[d - 1]
        cross = cross + cross_in[d - 1]
    state_in[n - 1] = state
    state = in_order(state_in, me, n)
    late_ref[:, :quarter] = gains
    late_ref[:, quarter:] = state
    for d in range(1, count):
        lates.append(push(late_ref, late_in.at[d - 1], row_groups[1], d - 1,
                          row_peer(lax.rem(place + d, count))))
        lates[-1].start()
    for t in range(2, n):
        line.step(t)
    total = line.total()
    here = pl.ds(pl.multiple_of(me * quarter, LANES), quarter)
    inside = row_columns(cross[:1]) / depth
    out_ref[...] = dres_ref[:, here].astype(f32) + scale * (
        total * gain_ref[:, here] - x_ref[:, here].astype(f32) * scale * inside
    )
    for copy in copies[2 * (n - 1) :] + lates:
        copy.wait_recv()
    early_in[count - 1] = early_ref[...]
    late_in[count - 1] = late_ref[...]
    early_out[...] = in_order(early_in, place, count)
    late_out[...] = in_order(late_in, place, count)
    for copy in copies + states + lates:
        copy.wait_send()
    line.wait_send()


def finish_step(value_grad, weights, x, dres, gain, gains_mid, state, early, pair_rows, hid):
    n, count = lax.axis_size("tensor"), lax.axis_size(ROWS)
    tokens, depth = x.shape
    quarter = depth // n
    wide = value_grad.shape[1]
    late = quarter + state.shape[1]
    shape = jax.ShapeDtypeStruct
    dma = pltpu.SemaphoreType.DMA
    return pl.pallas_call(
        partial(finish_kernel, n=n, count=count),
        in_specs=[VMEM] * 7 + [HBM] * 2,
        out_specs=[VMEM] * 5,
        out_shape=[shape((tokens, quarter), f32), shape(early.shape, f32), shape((8, late), f32),
                   shape((2 * depth, 2, hid), f32), shape((2, hid, depth), f32)],
        scratch_shapes=[
            pltpu.VMEM((depth, wide), bf16), pltpu.VMEM((3 * depth, 2 * hid), bf16),
            pltpu.VMEM((n, tokens, quarter), bf16),
            pltpu.VMEM((n, tokens, quarter), bf16), pltpu.VMEM((n, tokens, quarter), bf16),
            pltpu.VMEM((8, tokens), f32), pltpu.VMEM((n - 1, 8, tokens), f32),
            pltpu.VMEM((n, 8, quarter), f32), pltpu.VMEM((n - 1, 8, quarter), f32),
            pltpu.VMEM((n,) + state.shape, f32), pltpu.VMEM((count,) + early.shape, f32),
            pltpu.VMEM((8, late), f32), pltpu.VMEM((count, 8, late), f32), dma((2,)),
        ] + pairs(3, n) + [dma((count - 1,))] * 4 + line_sems(n),
        compiler_params=pltpu.CompilerParams(
            vmem_limit_bytes=60 << 20, collective_id=3, has_side_effects=True
        ),
        cost_estimate=cost(45),
        name="finish_step",
    )(value_grad, x, dres, gain, gains_mid, state, early, weights, pair_rows)


def back_part(dout_ref, w_ref, mixer_ref, value_ref, act_ref, run_exp_ref, link_ref, gain_ref,
                scale, cross, through_ref, heads_ref, zgrad_ref, gated_ref, direct_ref, sums_ref,
                *, inner, nstate, di_all):
    mixer = mixer_ref[...]
    z = value_ref[HALO:, :inner]
    sig = sigmoid(z)
    act = z * sig
    gated = mixer * act
    grad = dot_rows(dout_ref[...], w_ref[...])
    gated_ref[...] = (gated * scale * gain_ref[...]).astype(bf16)
    sums_ref[0:1, :] = jnp.sum(grad * gated * scale, axis=0, keepdims=True)
    gated_grad = scale * (grad * gain_ref[...]) - gated * (scale * scale * scale * cross / di_all)
    zgrad_ref[...] = (gated_grad * mixer * (sig * (1.0 + z * (1.0 - sig)))).astype(bf16)
    heads = gated_grad * act
    heads_ref[...] = heads
    sums_ref[1:2, :] = jnp.sum(heads * act_ref[:, :inner].astype(f32), axis=0, keepdims=True)
    sums_ref[2:, :] = jnp.zeros((6, inner), f32)
    carried = (heads * (jnp.exp(run_exp_ref[...]) * link_ref[...])).astype(bf16)
    direct_ref[:inner, :] = dot_inner(carried, act_ref[:, inner + nstate :]).astype(bf16)
    direct_ref[inner:, :] = through_ref[...]


def intra_back_part(heads_ref, act_ref, scaled_ref, run_t_ref, run_exp_ref, seg_col_ref,
                      seg_row_ref, dscaled_ref, dstate_ref, drun_ref, scores_ref, dscores_ref, *, inner, nstate, per, block):
    tokens = act_ref.shape[0]
    keys = act_ref[:, inner : inner + nstate]
    query = act_ref[:, inner + nstate :]
    for start in range(0, tokens, block):
        stop = start + block
        scores_ref[start:stop, :stop] = masked_scores(
            query, keys, seg_col_ref, seg_row_ref, start, stop
        )
    dscores_ref[...] = jnp.zeros_like(dscores_ref)
    drun_ref[...] = jnp.zeros_like(drun_ref)

    def pair(i, _):
        columns = pl.ds(pl.multiple_of(i * LANES, LANES), LANES)
        scaled = scaled_ref[:, columns]
        heads = heads_ref[:, columns].astype(bf16)
        lane = col_iota(scaled.shape)
        run = run_exp_ref[:, columns]
        dscaled_ref[:, columns] = jnp.zeros((tokens, LANES), f32)
        for h in range(LANES // per):
            head = i * (LANES // per) + h
            mine = (lane >= h * per) & (lane < (h + 1) * per)
            vals = jnp.where(mine, scaled, jnp.zeros_like(scaled))
            grads = jnp.where(mine, heads, jnp.zeros_like(heads))
            pick = (col_iota((block, LANES)) == head).astype(bf16)
            for start in range(0, tokens, block):
                stop = start + block
                row = run_t_ref[head, :, :stop]
                decay = jnp.exp(jnp.minimum(run[start:stop, h * per : h * per + 1] - row, 0.0))
                weight = decay * scores_ref[start:stop, :stop]
                dweight = dot_outer(grads[start:stop], vals[:stop])
                dscores_ref[start:stop, :stop] += dweight * decay
                flow = (dweight * weight).astype(bf16)
                dscaled_ref[:stop, columns] += dot_inner(weight.astype(bf16), grads[start:stop])
                picks = jnp.broadcast_to(pick[:1], (stop, LANES))
                drun_ref[start:stop, :] += dot_rows(flow, picks)
                drun_ref[:stop, :] -= dot_inner(flow, pick)
        return 0

    lax.fori_loop(0, inner // LANES, pair, 0)
    dkeys = jnp.zeros((tokens, nstate), f32)
    dstate_ref[:, :nstate] = dkeys
    for start in range(0, tokens, block):
        stop = start + block
        shape = (block, stop)
        allowed = (row_iota(shape) + start >= col_iota(shape)) & (
            seg_col_ref[start:stop, :1] == seg_row_ref[:, :stop]
        )
        grad = jnp.where(allowed, dscores_ref[start:stop, :stop], 0.0).astype(bf16)
        dstate_ref[start:stop, nstate:] = dot_rows(grad, keys[:stop])
        dstate_ref[:stop, :nstate] += dot_inner(grad, query[start:stop])


def conv_back(value_ref, column, taps_ref, same_ref, dact, at, dtaps_ref, tokens):
    ext = tokens + HALO
    rows, total = conv_pre(value_ref, column, taps_ref, at, same_ref, tokens)
    sig = sigmoid(total)
    dpre = dact * (sig * (1.0 + total * (1.0 - sig)))
    drows = None
    for offset in range(CONV):
        first = HALO - CONV + 1 + offset
        kept = dpre * same_ref[offset]
        dtaps_ref[offset : offset + 1, pl.ds(at, LANES)] = jnp.sum(
            kept * rows[first : first + tokens], axis=0, keepdims=True
        )
        term = kept * taps_ref[offset : offset + 1, pl.ds(at, LANES)]
        after = ext - first - tokens
        pieces = [jnp.zeros((first, LANES), f32), term]
        if after:
            pieces.append(jnp.zeros((after, LANES), f32))
        term = jnp.concatenate(pieces, axis=0)
        drows = term if drows is None else drows + term
    return drows


def state_back_part(heads_ref, act_ref, step_ref, run_ref, run_exp_ref, link_ref, end_ref,
                      value_ref, taps_ref, same_ref, dstate_ref, in_ref, far_ref,
                      rows_ref, dtaps_ref, leaving_ref, kept_ref, dact_ref, *, inner, nstate, per):
    tokens = act_ref.shape[0]
    keys = act_ref[:, inner : inner + nstate]
    signal = act_ref[:, :inner].astype(f32)
    grow = expander(LANES, inner, per)
    running = run_ref[...]
    state_grad = join_states(far_ref, inner, per)
    lifted = (heads_ref[...] * (jnp.exp(run_exp_ref[...]) * link_ref[...])).astype(bf16)
    dact_ref[:, nstate:] = dot_rows(lifted, in_ref[...].astype(bf16)) + dstate_ref[:, nstate:]
    toward = jnp.exp(running[tokens - 1 :] - running) * end_ref[...]
    toward_exp = spread_lanes(toward, grow)
    pushed = (signal * spread_lanes(step_ref[...] * toward, grow)).astype(bf16)
    leaving_ref[...] = dot_outer(keys, state_grad.astype(bf16)) * toward_exp
    dact_ref[:, :nstate] = dot_rows(pushed, state_grad.astype(bf16)) + dstate_ref[:, :nstate]
    kept = jnp.sum(in_ref[...] * state_grad, axis=1, keepdims=True)
    kept = jnp.sum(head_fold(inner, LANES, per) * kept, axis=0, keepdims=True)
    kept = kept * jnp.exp(running[tokens - 1 :]) * link_ref[tokens - 1 :]
    kept_ref[...] = jnp.broadcast_to(kept, kept_ref.shape)

    def conv(i, _):
        at = pl.multiple_of(i * LANES, LANES)
        drows = conv_back(value_ref, 2 * inner + at, taps_ref, same_ref, dact_ref[:, pl.ds(at, LANES)],
                          inner + at, dtaps_ref, tokens)
        rows_ref[:, pl.ds(at, LANES)] = drows.astype(bf16)
        return 0

    lax.fori_loop(0, 2 * nstate // LANES, conv, 0)


def signal_back_part(heads_ref, act_ref, step_ref, value_ref, taps_ref, same_ref, bias_ref,
                       decay_ref, skip_ref, mixer_ref, inner_ref, dscaled_ref, drun_ref, leaving_ref,
                       kept_ref, zgrad_ref, state_ref,
                       grad_ref, dtaps_ref, small_ref, dact_ref, middle, between, *, inner, nstate, per):
    tokens = act_ref.shape[0]
    signal = act_ref[:, :inner].astype(f32)
    grow = expander(LANES, inner, per)
    folds = head_fold(inner, LANES, per).astype(bf16)
    step = step_ref[...]
    heads = heads_ref[...]
    leaving = leaving_ref[...]
    step_exp = spread_lanes(step, grow)
    dscaled = dscaled_ref[...] + leaving
    dact_ref[...] = dscaled * step_exp + skip_ref[...] * heads

    def conv(i, _):
        at = pl.multiple_of(i * LANES, LANES)
        drows = conv_back(value_ref, inner + at, taps_ref, same_ref, dact_ref[:, pl.ds(at, LANES)], at,
                          dtaps_ref, tokens)
        grad_ref[:, pl.ds(inner + at, LANES)] = drows.astype(bf16)
        return 0

    half = inner // LANES // 2
    lax.fori_loop(0, half, conv, 0)
    middle()
    lax.fori_loop(half, inner // LANES, conv, 0)
    between()
    carried = mixer_ref[...] - inner_ref[...] - skip_ref[...] * signal
    tri = (row_iota((tokens, tokens)) <= col_iota((tokens, tokens))).astype(bf16)
    strict = (row_iota((tokens, tokens)) > col_iota((tokens, tokens))).astype(bf16)
    back_sum = drun_ref[...] + fold_heads(heads * carried, folds)
    front_sum = fold_heads(signal * step_exp * leaving, folds)
    dlog = left_sums(tri, back_sum) + left_sums(strict, front_sum) + kept_ref[0:1, :]
    rate = -jnp.exp(decay_ref[...])
    dstep = dlog * rate + fold_heads(dscaled * signal, folds)
    draw = dstep * sigmoid(value_ref[HALO:, 2 * inner + 2 * nstate :] + bias_ref[...])
    small_ref[0:1, :] = jnp.sum(draw, axis=0, keepdims=True)
    small_ref[1:2, :] = jnp.sum(dlog * step, axis=0, keepdims=True) * rate
    small_ref[2:, :] = jnp.zeros((6, LANES), f32)
    state_at = 2 * inner
    step_at = state_at + 2 * nstate
    grad_ref[:HALO, :inner] = jnp.zeros((HALO, inner), bf16)
    grad_ref[HALO:, :inner] = zgrad_ref[...]
    grad_ref[:, state_at:step_at] = state_ref[...]
    grad_ref[:HALO, step_at:] = jnp.zeros((HALO, LANES), bf16)
    used = col_iota((tokens, LANES)) < inner // per
    grad_ref[HALO:, step_at:] = jnp.where(used, draw, 0.0).astype(bf16)


def rear_kernel(dout_ref, stat_ref, notes_ref, mixer_ref, inner_ref, act_ref, scaled_ref, step_ref,
                run_ref, run_exp_ref, state_ref, taps_ref, same_ref, bias_ref, decay_ref, skip_ref,
                gain_ref, end_ref, link_ref, seg_col_ref, seg_row_ref, packed_ref,
                part_hbm, value_hbm, w_hbm, res_hbm,
                grad_ref, gated_ref, dtaps_ref, sums_ref, small_ref, state_all_ref, out_ref,
                value_ref, w_ref, res_ref, run_t_ref, heads_ref, zgrad_ref, direct_ref, dscaled_ref,
                dstate_ref, drun_ref, scores_ref, dscores_ref, leaving_ref, kept_ref, rows_ref, dact_ref,
                far_ref, part_ref, right_box, left_box, rows_box, sum_box, ext_ref, state_halo, signal_halo,
                local_sem, *sems,
                inner, nstate, per, heads, di_all, n):
    me = lax.axis_index("tensor")
    tokens = act_ref.shape[0]
    quarter = part_ref.shape[1] // n
    own = tokens // n
    wide = value_ref.shape[1]
    groups = [(sems[2 * i], sems[2 * i + 1]) for i in range(4)]
    column = lambda k: pl.ds(pl.multiple_of(k * quarter, LANES), quarter)
    loads = [
        pltpu.make_async_copy(part_hbm, part_ref, local_sem.at[3]),
        pltpu.make_async_copy(w_hbm.at[:, pl.ds(wide, inner)], w_ref, local_sem.at[0]),
        pltpu.make_async_copy(value_hbm, value_ref, local_sem.at[1]),
        pltpu.make_async_copy(res_hbm.at[:, column(me)], res_ref, local_sem.at[2]),
    ]
    for copy in loads:
        copy.start()
    far_ref[...] = jnp.zeros_like(far_ref)
    state_halo[...] = jnp.zeros_like(state_halo)
    signal_halo[...] = jnp.zeros_like(signal_halo)
    front_barrier(me, n)
    line = LineReduce(me, n, lambda d: part_ref.at[:, column(d)], right_box, left_box,
                      line_groups(sems[8:12]))
    loads[0].wait()
    line.step(0)
    for copy in loads[1:]:
        copy.wait()
    scale = row_columns(stat_ref[0:1, :])
    gates = notes_ref.shape[0] - 8
    cross = row_columns(notes_ref[gates : gates + 1, :])
    back_part(dout_ref, w_ref, mixer_ref, value_ref, act_ref, run_exp_ref, link_ref, gain_ref,
              scale, cross, packed_ref, heads_ref, zgrad_ref, gated_ref, direct_ref, sums_ref,
              inner=inner, nstate=nstate, di_all=di_all)
    states = StatePush(direct_ref, far_ref, groups[0], True)
    states.start()
    line.step(1)
    run_t = run_ref[...].T
    for h in range(heads):
        run_t_ref[h] = run_t[h : h + 1, :]
    intra_back_part(heads_ref, act_ref, scaled_ref, run_t_ref, run_exp_ref, seg_col_ref, seg_row_ref,
                    dscaled_ref, dstate_ref, drun_ref, scores_ref, dscores_ref,
                    inner=inner, nstate=nstate, per=per, block=128)
    line.step(2)
    states.wait_recv()
    state_back_part(heads_ref, act_ref, step_ref, run_ref, run_exp_ref, link_ref, end_ref, value_ref,
                    taps_ref, same_ref, dstate_ref, state_ref, far_ref, rows_ref, dtaps_ref,
                    leaving_ref, kept_ref, dact_ref.at[:, pl.ds(0, 2 * nstate)],
                    inner=inner, nstate=nstate, per=per)
    body = lambda d: pl.ds(pl.multiple_of(HALO + d * own, 16), own)
    reduces, gathers = [], []
    place, count = ctx_place()
    sends, gets = place > 0, place < count - 1
    before = ctx_peer(jnp.maximum(place - 1, 0))
    state_copy = push(rows_ref.at[pl.ds(0, HALO)], state_halo, groups[2], 0, before)
    signal_copy = push(ext_ref.at[pl.ds(0, HALO), pl.ds(inner, inner)], signal_halo, groups[2], 1, before)
    pl.when(sends)(state_copy.start)

    def middle():
        pl.when(gets)(state_copy.wait_recv)
        rows_ref[tokens:, :] = rows_ref[tokens:, :] + state_halo[...]
        for d in range(1, n):
            peer = lax.rem(me + d, n)
            reduces.append(push(rows_ref.at[body(peer)], rows_box.at[d - 1], groups[1], d - 1, peer))
            reduces[-1].start()

    def between():
        pl.when(sends)(signal_copy.start)
        total = rows_ref[body(me), :].astype(f32)
        for copy in reduces:
            copy.wait_recv()
        for d in range(1, n):
            total = total + rows_box[d - 1].astype(f32)
        sum_box[body(me), :] = total.astype(bf16)
        for d in range(1, n):
            peer = lax.rem(me + d, n)
            gathers.append(push(sum_box.at[body(me)], sum_box.at[body(me)], groups[3], d - 1, peer))
            gathers[-1].start()

    signal_back_part(heads_ref, act_ref, step_ref, value_ref, taps_ref, same_ref, bias_ref, decay_ref,
                     skip_ref, mixer_ref, inner_ref, dscaled_ref, drun_ref, leaving_ref, kept_ref,
                     zgrad_ref, rows_ref, ext_ref, dtaps_ref, small_ref, dact_ref, middle, between,
                     inner=inner, nstate=nstate, per=per)
    grad_ref[...] = ext_ref[HALO:, :]
    pl.when(gets)(signal_copy.wait_recv)
    grad_ref[tokens - HALO :, inner : 2 * inner] = (
        ext_ref[tokens:, inner : 2 * inner] + signal_halo[...]
    )
    for t in range(3, n):
        line.step(t)
    out_ref[...] = (line.total() + res_ref[...].astype(f32)).astype(bf16)
    for copy in gathers:
        copy.wait_recv()
    state_all_ref[...] = sum_box[HALO:, :]
    states.wait_send()
    line.wait_send()
    pl.when(sends)(state_copy.wait_send)
    pl.when(sends)(signal_copy.wait_send)
    for copy in reduces + gathers:
        copy.wait_send()


def rear(vmem_args, part, value, weights, residual, inner, nstate, per, heads, di_all):
    n = lax.axis_size("tensor")
    others = lax.axis_size(CTX) - 1
    ext, wide = value.shape
    tokens = ext - HALO
    depth = residual.shape[1]
    quarter = depth // n
    shape = jax.ShapeDtypeStruct
    outs = [
        shape((tokens, wide), bf16), shape((tokens, inner), bf16), shape((CONV, inner + 2 * nstate), f32),
        shape((8, inner), f32), shape((8, LANES), f32), shape((tokens, 2 * nstate), bf16),
        shape((tokens, quarter), bf16),
    ]
    dma = pltpu.SemaphoreType.DMA
    return pl.pallas_call(
        partial(rear_kernel, inner=inner, nstate=nstate, per=per, heads=heads, di_all=di_all, n=n),
        in_specs=[VMEM] * len(vmem_args) + [HBM] * 4,
        out_specs=[VMEM] * len(outs),
        out_shape=outs,
        scratch_shapes=[
            pltpu.VMEM((ext, wide), f32), pltpu.VMEM((depth, inner), bf16),
            pltpu.VMEM((tokens, quarter), bf16), pltpu.VMEM((heads, 1, tokens), f32),
            pltpu.VMEM((tokens, inner), f32), pltpu.VMEM((tokens, inner), bf16),
            pltpu.VMEM((inner + 16, nstate), bf16), pltpu.VMEM((tokens, inner), f32),
            pltpu.VMEM((tokens, 2 * nstate), f32), pltpu.VMEM((tokens, LANES), f32),
            pltpu.VMEM((tokens, tokens), f32), pltpu.VMEM((tokens, tokens), f32),
            pltpu.VMEM((tokens, inner), f32), pltpu.VMEM((8, LANES), f32),
            pltpu.VMEM((ext, 2 * nstate), bf16), pltpu.VMEM((tokens, inner), f32),
            pltpu.VMEM((others, inner + 16, nstate), bf16),
            pltpu.VMEM((tokens, depth), bf16),
            pltpu.VMEM((n, tokens, quarter), bf16), pltpu.VMEM((n, tokens, quarter), bf16),
            pltpu.VMEM((n - 1, tokens // n, 2 * nstate), bf16),
            pltpu.VMEM((ext, 2 * nstate), bf16), pltpu.VMEM((ext, wide), bf16),
            pltpu.VMEM((HALO, 2 * nstate), bf16), pltpu.VMEM((HALO, inner), bf16),
            dma((4,)), dma((others,)), dma((others,)), dma((n - 1,)), dma((n - 1,)), dma((2,)), dma((2,)),
            dma((n - 1,)), dma((n - 1,)),
        ] + line_sems(n),
        compiler_params=pltpu.CompilerParams(
            vmem_limit_bytes=60 << 20, collective_id=5, has_side_effects=True
        ),
        cost_estimate=cost(50),
        name="rear",
    )(*vmem_args, part, value, weights, residual)


def weight_kernel(mixed_ref, value_ref, state_ref, dout_ref, gated_ref, mix_ref, gates_ref, notes_ref,
                  out_ref, stage_ref, *remote, first, last, inner, core):
    depth, width = stage_ref.shape
    wide = value_ref.shape[1]
    block = depth // 2
    blocks = depth // block
    me = lax.axis_index("core") if core == 2 else 0
    count = remote[0].shape[0] if core == 2 else 0
    owner = depth // (2 * count) if core == 2 else 0
    copies = []
    if core == 2:
        inbox, send, receive = remote
        other = 1 - me
        barrier = pltpu.get_barrier_semaphore()
        pl.semaphore_signal(barrier, inc=1, device_id={"core": other}, device_id_type=MESH)
        pl.semaphore_wait(barrier, 1)

    def segment(number, lhs_ref, rhs, at, transposed=True):
        span = rhs.shape[1]

        def rows(m, _):
            here = pl.ds(pl.multiple_of(m * block, block), block)
            if transposed:
                product = dot_rows(lhs_ref[here, :], rhs[...])
            else:
                product = dot_inner(lhs_ref[:, here], rhs[...])
            stage_ref[here, at : at + span] = product.astype(bf16)
            return 0

        lax.fori_loop(0, blocks, rows, 0)
        if core == 2:
            for j in range(count):
                theirs = pl.ds(pl.multiple_of((2 * j + other) * owner, 64), owner)
                copy = pltpu.make_async_remote_copy(
                    src_ref=stage_ref.at[theirs, pl.ds(at, span)],
                    dst_ref=inbox.at[j, :, pl.ds(at, span)],
                    send_sem=send.at[number * count + j], recv_sem=receive.at[number * count + j],
                    device_id={"core": other}, device_id_type=MESH,
                )
                copy.start()
                copies.append(copy)

    gates = gates_ref[...]
    kinds = notes_ref.shape[0] - 8
    moved = jnp.concatenate(
        [notes_ref[:kinds, :], jnp.zeros((LANES - kinds, gates.shape[0]), f32)], axis=0
    ).T
    inside = jnp.sum(gates * moved, axis=1, keepdims=True)
    segment(0, mix_ref, (gates * (moved - inside)).astype(bf16), wide + inner)
    segment(1, dout_ref, gated_ref, wide, False)
    segment(2, mixed_ref, value_ref.at[:, pl.ds(0, inner)], 0)
    segment(3, mixed_ref, value_ref.at[:, pl.ds(inner, inner)], inner)
    segment(4, mixed_ref, state_ref, first)
    segment(5, mixed_ref, value_ref.at[:, pl.ds(last, LANES)], last)
    if core == 2:
        for copy in copies:
            copy.wait_recv()
        for j in range(count):
            kept = pl.ds(pl.multiple_of((2 * j + me) * owner, 64), owner)
            out_ref[j * owner : (j + 1) * owner, :] = stage_ref[kept, :] + inbox[j]
        for copy in copies:
            copy.wait_send()
    else:
        out_ref[...] = stage_ref[...]


def weight_grads(mixed_ext, value_grad, state_all, dout, gated_out, mix, gates, notes, inner, nstate):
    core = lax.axis_size("core")
    count = lax.axis_size(CHIPS)
    depth = mix.shape[0]
    wide = value_grad.shape[1]
    width = wide + inner + LANES
    first = 2 * inner
    remote, params = [], pltpu.CompilerParams(vmem_limit_bytes=60 << 20)
    if core == 2:
        owner = depth // (2 * count)
        remote = [pltpu.VMEM((count, owner, width), bf16), pltpu.SemaphoreType.DMA((6 * count,)),
                  pltpu.SemaphoreType.DMA((6 * count,))]
        params = pltpu.CompilerParams(
            vmem_limit_bytes=60 << 20, collective_id=6, has_side_effects=True
        )
    return pl.pallas_call(
        partial(weight_kernel, first=first, last=first + 2 * nstate, inner=inner, core=core),
        in_specs=[VMEM] * 8,
        out_specs=VMEM,
        out_shape=jax.ShapeDtypeStruct((depth // core, width), bf16),
        scratch_shapes=[pltpu.VMEM((depth, width), bf16)] + remote,
        compiler_params=params,
        cost_estimate=cost(12),
        name="weight_grads",
    )(mixed_ext, value_grad, state_all, dout, gated_out, mix, gates, notes)


def swiglu(first, second):
    sig = sigmoid(first)
    act = first * sig
    return act, sig * (1.0 + first * (1.0 - sig)), (act * second).astype(bf16)


def shared_kernel(res_ref, cot_ref, gain_ref, router_ref, chosen_ref, w_ref,
                  out_ref, dmix_ref, mix_ref, mix_t_ref, gates_ref, dw_ref, first_ref, down_ref, hidden_ref,
                  dval_ref, *, tile):
    rows, depth = res_ref.shape
    wrows = w_ref.shape[1] // 3
    wide = w_ref.shape[2]
    hid = wide // 2
    for p in range(2):
        first_ref[p] = w_ref[:, p * wrows : (p + 1) * wrows, :].reshape(depth, wide)
    down_ref[...] = w_ref[:, 2 * wrows :, :].reshape(depth, wide)

    def part(i, _):
        at = pl.ds(pl.multiple_of(i * tile, tile), tile)
        res = res_ref[at, :].astype(f32)
        scale = lax.rsqrt(jnp.mean(res * res, axis=1, keepdims=True) + epsilon)
        mix_ref[at, :] = (res * scale * gain_ref[...]).astype(bf16)
        mix = mix_ref[at, :]
        chosen = chosen_ref[at, :] > 0.0
        logits = dot_rows(mix, router_ref[...])
        top = jnp.max(jnp.where(chosen, logits, -1e30), axis=1, keepdims=True)
        weight = jnp.where(chosen, jnp.exp(jnp.where(chosen, logits - top, 0.0)), 0.0)
        gates_ref[at, :] = weight / jnp.sum(weight, axis=1, keepdims=True)
        raw = dot_rows(cot_ref[at, :], down_ref[...])
        dmix = None
        for p in range(2):
            value = dot_rows(mix, first_ref[p])
            act, slope, hidden = swiglu(value[:, :hid], value[:, hid:])
            here = pl.ds(p * hid, hid)
            dh = raw[:, p * hid : (p + 1) * hid]
            dval_ref[p, at, :hid] = (dh * value[:, hid:] * slope).astype(bf16)
            dval_ref[p, at, hid:] = (dh * act).astype(bf16)
            hidden_ref[at, here] = hidden
            term = dot_outer(dval_ref[p, at, :], first_ref[p])
            dmix = term if dmix is None else dmix + term
        out_ref[at, :] = dot_outer(hidden_ref[at, :], down_ref[...])
        dmix_ref[at, :] = dmix
        return 0

    lax.fori_loop(0, rows // tile, part, 0)
    mix_t_ref[...] = mix_ref[...].T
    for p in range(2):
        dw_ref[:, p * wrows : (p + 1) * wrows, :] = (
            dot_rows(mix_t_ref[...], dval_ref[p]).astype(bf16).reshape(-1, wrows, wide)
        )
    dw_ref[:, 2 * wrows :, :] = (
        dot_inner(cot_ref[...], hidden_ref[...]).astype(bf16).reshape(-1, wrows, wide)
    )


def shared_expert(residual, cot, gain, weights, router_at, chosen, experts_w):
    rows, depth = residual.shape
    senders, deep, wide = experts_w.shape
    part = 3 * (depth // senders)
    own = deep - part
    assert own % part == 0
    shape = jax.ShapeDtypeStruct
    block = pl.BlockSpec((senders, part, wide), lambda i: (0, own // part, 0))
    grads = shape((senders, part, wide), bf16)
    outs = [shape((rows, depth), f32), shape((rows, depth), f32), shape((rows, depth), bf16),
            shape((depth, rows), bf16), shape((rows, LANES), f32)]
    return pl.pallas_call(
        partial(shared_kernel, tile=min(512, rows)),
        grid=(1,),
        in_specs=[whole(residual), whole(cot), whole(gain), columns(weights, LANES, router_at),
                  whole(chosen), block],
        out_specs=[whole(o) for o in outs + [grads]],
        out_shape=outs + [grads],
        scratch_shapes=[
            pltpu.VMEM((2, depth, wide), bf16), pltpu.VMEM((depth, wide), bf16),
            pltpu.VMEM((rows, wide), bf16), pltpu.VMEM((2, rows, wide), bf16),
        ],
        compiler_params=BIG,
        cost_estimate=cost(10),
        name="shared_expert",
    )(residual, cot, gain, weights, chosen, experts_w)


def experts_kernel(mix_ref, mix_t_ref, cot_ref, gates_ref, router_ref, w_ref, out_in, dmix_in, ds_ref,
                   out_ref, dmix_ref, dgate_t_ref, dw_ref,
                   dgate_ref, total_ref, grads_ref, down_ref, hidden_ref, dval_ref, grad_ref, load_sem,
                   *remote, tile, senders, core):
    step = pl.program_id(0)
    last = step == pl.num_programs(0) - 1
    rows, depth = mix_ref.shape
    wide = w_ref.shape[2]
    hid = wide // 2
    chunks = depth // wide
    deep = depth + depth // 2
    if core == 2:
        inbox, shared_box, send, receive, shared_send, shared_receive = remote
        me = lax.axis_index("core")
        other = 1 - me
        slot = lax.rem(step + me, 2)

        def to_sibling(source, target, send_sem, recv_sem):
            return pltpu.make_async_remote_copy(
                src_ref=source, dst_ref=target, send_sem=send_sem, recv_sem=recv_sem,
                device_id={"core": other}, device_id_type=MESH,
            )

        shared_copy = to_sibling(ds_ref.at[other], shared_box, shared_send, shared_receive)
        pair_copy = lambda k: to_sibling(grad_ref.at[1], inbox.at[k], send.at[k], receive.at[k])
    else:
        slot = 0

    @pl.when(step == 0)
    def _():
        loads = [pltpu.make_async_copy(out_in, total_ref, load_sem.at[0]),
                 pltpu.make_async_copy(dmix_in, grads_ref, load_sem.at[1])]
        for copy in loads:
            copy.start()
        dgate_ref[...] = jnp.zeros_like(dgate_ref)
        if core == 2:
            barrier = pltpu.get_barrier_semaphore()
            pl.semaphore_signal(barrier, inc=1, device_id={"core": other}, device_id_type=MESH)
            pl.semaphore_wait(barrier, 1)
            shared_copy.start()
        for copy in loads:
            copy.wait()

    if core == 2:
        @pl.when((step >= 2) & (step < senders) & (slot == 1))
        def _():
            pair_copy((step - 2) // 2).wait_send()

    @pl.when(step < senders)
    def _():
        pair_grads(
            step, slot, mix_ref, mix_t_ref, cot_ref, gates_ref, w_ref, dgate_ref, total_ref, grads_ref, down_ref,
            hidden_ref, dval_ref, grad_ref, tile
        )

    if core == 2:
        @pl.when((step < senders) & (slot == 1))
        def _():
            pair_copy(step // 2).start()

        @pl.when((step >= 1) & (slot == 1))
        def _():
            at = (step - 1) // 2

            @pl.when(step <= 2)
            def _():
                shared_copy.wait()

            pair_copy(at).wait_recv()
            dw_ref[0, : 3 * depth, :] = grad_ref[0] + inbox[at]
            dw_ref[0, 3 * depth :, :] = ds_ref[me, at] + shared_box[at]

        @pl.when(last)
        def _():
            pair_copy(senders // 2 - 1).wait_send()
    else:
        dw_ref[0, : 3 * depth, :] = grad_ref[0]
        dw_ref[0, 3 * depth :, :] = ds_ref[0, step]

    @pl.when(last)
    def _():
        gates = gates_ref[...]
        dgate = dgate_ref[...]
        inside = jnp.sum(gates * dgate, axis=1, keepdims=True)
        dlogits = (gates * (dgate - inside)).astype(bf16)
        dmix_ref[...] = (grads_ref[...] + dot_outer(dlogits, router_ref[...])).astype(bf16)
        out_ref[...] = total_ref[...].astype(bf16)
        dgate_t_ref[...] = dgate.T[: dgate_t_ref.shape[0], :]


def pair_grads(step, slot, mix_ref, mix_t_ref, cot_ref, gates_ref, w_ref, dgate_ref, total_ref, grads_ref,
               down_ref, hidden_ref, dval_ref, grad_ref, tile):
    rows, depth = mix_ref.shape
    wide = w_ref.shape[2]
    hid = wide // 2
    chunks = depth // wide
    deep = depth + depth // 2
    for p in range(2):
        for c in range(chunks):
            down_ref[p * hid : (p + 1) * hid, c * wide : (c + 1) * wide] = (
                w_ref[0, p * deep + depth + c * hid : p * deep + depth + (c + 1) * hid, :]
            )
    down = down_ref[...]

    def part(i, _):
        at = pl.ds(pl.multiple_of(i * tile, tile), tile)
        mix = mix_ref[at, :]
        raw = dot_outer(cot_ref[at, :], down)
        gates = gates_ref[at, :]
        lane = col_iota(gates.shape)
        dmix, noted = None, jnp.zeros_like(gates)
        for p in range(2):
            here = lane == 2 * step + p
            gate = jnp.sum(jnp.where(here, gates, 0.0), axis=1, keepdims=True)
            weights = w_ref[0, p * deep : p * deep + depth, :]
            value = dot_rows(mix, weights)
            act, slope, hidden = swiglu(value[:, :hid], value[:, hid:])
            hidden = hidden.astype(f32)
            dh = raw[:, p * hid : (p + 1) * hid]
            noted = noted + jnp.where(here, jnp.sum(hidden * dh, axis=1, keepdims=True), 0.0)
            dh = gate * dh
            dval_ref[p, at, :hid] = (dh * value[:, hid:] * slope).astype(bf16)
            dval_ref[p, at, hid:] = (dh * act).astype(bf16)
            hidden_ref[at, p * hid : (p + 1) * hid] = (gate * hidden).astype(bf16)
            term = dot_outer(dval_ref[p, at, :], weights)
            dmix = term if dmix is None else dmix + term
        dgate_ref[at, :] += noted
        total_ref[at, :] += dot_rows(hidden_ref[at, :], down)
        grads_ref[at, :] += dmix
        return 0

    lax.fori_loop(0, rows // tile, part, 0)
    for c in range(chunks):
        grad = dot_inner(hidden_ref[...], cot_ref[:, c * wide : (c + 1) * wide]).astype(bf16)
        for p in range(2):
            first = p * deep + depth + c * hid
            grad_ref[slot, first : first + hid, :] = grad[p * hid : (p + 1) * hid]
    for p in range(2):
        grad_ref[slot, p * deep : p * deep + depth, :] = (
            dot_rows(mix_t_ref[...], dval_ref[p]).astype(bf16)
        )


def experts(mix, mix_t, cot, gates, weights, router_at, experts_w, out, dmix, ds):
    senders, deep, wide = experts_w.shape
    rows, depth = mix.shape
    core = lax.axis_size("core")
    kept = senders // core
    part = deep - 3 * depth
    ds = ds.reshape(kept, core, part, wide).transpose(1, 0, 2, 3)
    shape = jax.ShapeDtypeStruct
    once = lambda a: pl.BlockSpec(
        a.shape, lambda i: (0,) * a.ndim, pipeline_mode=pl.Buffered(1)
    )
    kinds = 2 * senders + -2 * senders % 8
    outs = [shape((rows, depth), bf16), shape((rows, depth), bf16), shape((kinds, rows), f32)]
    if core == 2:
        steps = senders + 1
        kept_map = lambda i: (jnp.maximum(i - 1, 0) // 2, 0, 0)
        remote = [
            pltpu.VMEM((kept, 3 * depth, wide), bf16), pltpu.VMEM((kept, part, wide), bf16),
            pltpu.SemaphoreType.DMA((kept,)), pltpu.SemaphoreType.DMA((kept,)),
            pltpu.SemaphoreType.DMA, pltpu.SemaphoreType.DMA,
        ]
        params = pltpu.CompilerParams(
            vmem_limit_bytes=60 << 20, collective_id=4, has_side_effects=True
        )
    else:
        steps, remote, params = senders, [], pltpu.CompilerParams(vmem_limit_bytes=60 << 20)
        kept_map = lambda i: (i, 0, 0)
    return pl.pallas_call(
        partial(experts_kernel, tile=min(512, rows), senders=senders, core=core),
        grid=(steps,),
        in_specs=[once(mix), once(mix_t), once(cot), once(gates),
                  pl.BlockSpec((depth, LANES), lambda i: (0, router_at // LANES)),
                  pl.BlockSpec((1, 3 * depth, wide), lambda i: (jnp.minimum(i, senders - 1), 0, 0)),
                  pl.BlockSpec(memory_space=pl.ANY), pl.BlockSpec(memory_space=pl.ANY), once(ds)],
        out_specs=[whole(o) for o in outs] + [pl.BlockSpec((1, deep, wide), kept_map)],
        out_shape=outs + [shape((kept, deep, wide), bf16)],
        scratch_shapes=[
            pltpu.VMEM((rows, LANES), f32), pltpu.VMEM((rows, depth), f32),
            pltpu.VMEM((rows, depth), f32),
            pltpu.VMEM((wide, depth), bf16), pltpu.VMEM((rows, wide), bf16),
            pltpu.VMEM((2, rows, wide), bf16), pltpu.VMEM((core, 3 * depth, wide), bf16),
            pltpu.SemaphoreType.DMA((2,)),
        ] + remote,
        compiler_params=params,
        cost_estimate=cost(6 * senders),
        name="experts",
    )(mix, mix_t, cot, gates, weights, experts_w, out, dmix, ds)


def local(
    block_input, gain_input, proj_main, proj_state, proj_step, conv_main, conv_state, step_bias,
    decay_log, skip_gain, gain_gate, proj_out, gain_mix, router_weight, shared_gates, shared_down,
    expert_gates, expert_down, segments, routes, cotangent,
):
    tokens, quarter = block_input.shape
    heads = step_bias.shape[0]
    inner = conv_main.shape[1]
    nstate = conv_state.shape[1] // 2
    per = inner // heads
    tensors = lax.axis_size("tensor")
    zi = lax.axis_index("tensor")
    senders = lax.axis_size(ROWS)
    depth = quarter * tensors
    di_all = inner * tensors
    own = tokens // tensors
    column = zi * quarter
    row0 = zi * own
    wrows = proj_main.shape[0]
    hid = expert_gates.shape[3]
    local_experts = expert_gates.shape[0]
    experts_all = local_experts * senders
    shared_here = shared_down.shape[1]
    router_pad = -experts_all % LANES

    main_wide = 2 * inner + 2 * nstate + LANES
    router_at = main_wide + inner
    weights = gather_rows(
        jnp.concatenate(
            [proj_main[:, 0], proj_main[:, 1], proj_state,
             jnp.pad(proj_step, ((0, 0), (0, LANES - heads))), proj_out,
             jnp.pad(router_weight, ((0, 0), (0, router_pad)))], axis=1
        )
    )
    pair_down = expert_down.reshape(local_experts, hid, depth // (2 * hid), 2 * hid)
    pair = jnp.concatenate(
        [expert_gates.reshape(local_experts, depth, 2 * hid),
         pair_down.transpose(0, 2, 1, 3).reshape(local_experts, -1, 2 * hid)], axis=1
    )
    shared_pair = shared_gates.reshape(wrows, 2, 2, shared_here // 2).transpose(2, 0, 1, 3)
    packed = jnp.concatenate(
        [pair.reshape(-1, 2 * hid), shared_pair.reshape(-1, shared_here), shared_down], axis=0
    )
    experts_w = gather_rows(packed[None])

    seg_row = segments[0]
    halo_seg = shifted(seg_row[tokens - CONV + 1 :], CTX, 1)
    gains = jnp.concatenate(
        [gain_input[None], gain_mix[None], jnp.zeros((14, quarter), bf16)], axis=0
    )
    mixed_ext, mixed_t, got, gain_rows = intake(block_input, gains)
    gain_row, gain_mid = gain_rows[0:1], gain_rows[1:2]

    segments_ext = jnp.concatenate([halo_seg, seg_row], axis=0)
    same = jnp.stack(
        [segments_ext[offset : offset + tokens] == seg_row for offset in range(CONV)]
    ).astype(f32)
    same = jnp.broadcast_to(same[:, :, None], (CONV, tokens, LANES))
    taps = jnp.concatenate([conv_main, conv_state], axis=1).astype(f32)
    lanes = lambda v: jnp.pad(v, (0, LANES - heads))[None]
    bias = lanes(step_bias)
    decay = lanes(decay_log)
    skip = jnp.repeat(skip_gain, per)[None]
    link = (seg_row == halo_seg[-1]).astype(f32)[:, None]
    at_end = (seg_row == seg_row[-1]).astype(f32)[:, None]
    seg_col = seg_row[:, None]
    seg_line = seg_row[None]
    gain_gate_f = gain_gate.astype(f32)[None, :]
    (value, act, scaled, step, running, run_exp, within, mixer, state_in, packed, residual, scale_rows,
     own_part, cot_full) = front(
        mixed_ext, taps, same, bias, decay, at_end, link, seg_col, seg_line, skip, gain_gate_f, got,
        cotangent, weights, inner, nstate, per, heads, di_all
    )

    chosen = jnp.any(
        routes[:, :, None] == jnp.arange(LANES, dtype=jnp.int32)[None, None, :], axis=1
    ).astype(f32)
    out_part, dmix_part, mixed_two, mix_t, gates, shared_grad = shared_expert(
        residual, cot_full, gain_mid, weights, router_at, chosen, experts_w
    )
    out_part, dmix_part, dgate, dw = experts(
        mixed_two, mix_t, cot_full, gates, weights, router_at, experts_w, out_part, dmix_part, shared_grad
    )
    expert_rows = scatter_chips(dw.reshape(-1, 2 * hid))
    dmixer, notes, gains_mid = turn_step(
        dmix_part, dgate, residual, cot_full, own_part, gain_mid
    )

    value_grad, gated_out, dtaps, sums, small_sums, state_all, output = rear(
        (dmixer, scale_rows, notes, mixer, within, act, scaled, step, running, run_exp, state_in, taps,
         same, bias, decay, skip, gain_gate_f, at_end, link, seg_col, seg_line, packed[inner:]),
        out_part, value, weights, residual, inner, nstate, per, heads, di_all
    )
    first = 2 * inner
    last = first + 2 * nstate
    main_local = weight_grads(
        mixed_t, value_grad, state_all, dmixer, gated_out, mix_t, gates, notes, inner, nstate
    )
    shared_rows = expert_rows[3 * depth :]
    shared_up = shared_rows[: 2 * wrows].reshape(2, wrows, 2, shared_here // 2)
    early = jnp.concatenate(
        [dtaps[:, :inner], sums[:2], jnp.pad(small_sums[:2], ((0, 0), (0, inner - LANES)))], axis=0
    )
    main_local, early, expert_rows = lax.optimization_barrier((main_local, early, expert_rows))
    main_grad = scatter_chips(main_local).astype(f32)
    grad_input, early, late, gates_rows, down_rows = finish_step(
        value_grad, weights, got, dmixer, gain_row, gains_mid,
        jnp.pad(dtaps[:, inner:], ((0, 8 - CONV), (0, 0))), early, expert_rows[: 3 * depth], hid
    )
    return (
        output,
        grad_input,
        late[0, :quarter],
        jnp.stack([main_grad[:, :inner], main_grad[:, inner:first]], axis=1),
        main_grad[:, first:last],
        main_grad[:, last : last + heads],
        early[:CONV],
        late[:CONV, quarter:],
        early[CONV + 2, :heads],
        early[CONV + 3, :heads],
        jnp.sum(early[CONV + 1].reshape(heads, per), axis=1),
        early[CONV],
        main_grad[:, main_wide:router_at],
        late[1, :quarter],
        main_grad[:, router_at : router_at + experts_all],
        shared_up.transpose(1, 2, 0, 3).reshape(wrows, 2, shared_here).astype(f32),
        shared_rows[2 * wrows :].astype(f32),
        gates_rows.reshape(expert_gates.shape),
        down_rows,
    )


def solution(mesh):
    shard, ctx, tensor = (mesh.shape[name] for name in ("shard", "ctx", "tensor"))
    core = 2 if shard * ctx == 8 else 1
    split = jax.sharding.Mesh(
        mesh.devices.reshape(shard, ctx // core, core, tensor), ("shard", "cy", "core", "tensor")
    )
    return jax.shard_map(
        local,
        mesh=split,
        in_specs=(
            P(ROWS, "tensor"),
            P("tensor"),
            P(ROWS, None, "tensor"),
            P(ROWS, None),
            P(ROWS, "tensor"),
            P(None, "tensor"),
            P(),
            P("tensor"),
            P("tensor"),
            P("tensor"),
            P("tensor"),
            P(ROWS, "tensor"),
            P("tensor"),
            P(ROWS, None),
            P(ROWS, None, "tensor"),
            P(ROWS, "tensor"),
            P(ROWS, None, None, "tensor"),
            P(ROWS, "tensor", None),
            P("shard", CTX),
            P(ROWS, None),
            P(ROWS, "tensor"),
        ),
        out_specs=(
            P(ROWS, "tensor"),
            P(ROWS, "tensor"),
            P("tensor"),
            P(ROWS, None, "tensor"),
            P(ROWS, None),
            P(ROWS, "tensor"),
            P(None, "tensor"),
            P(),
            P("tensor"),
            P("tensor"),
            P("tensor"),
            P("tensor"),
            P(ROWS, "tensor"),
            P("tensor"),
            P(ROWS, None),
            P(ROWS, None, "tensor"),
            P(ROWS, "tensor"),
            P(ROWS, None, None, "tensor"),
            P(ROWS, "tensor", None),
        ),
        check_vma=False,
    )
```

```python
from functools import partial

import jax
import jax.numpy as jnp
from jax import lax
from jax.experimental import pallas as pl
from jax.experimental.pallas import tpu as pltpu
from jax.sharding import PartitionSpec as P

CONV = 4
HALO = 16
LANES = 128
LANES = 128
LANES = 128


epsilon = 1e-05
highest = lax.Precision.HIGHEST
CTX = ("cy", "core")
CHIPS = ("shard", "cy")
ROWS = ("shard", "cy", "core")
f32 = jnp.float32
MESH = pl.DeviceIdType.MESH
bf16 = jnp.bfloat16
BIG = pltpu.CompilerParams(vmem_limit_bytes=60 << 20)


def cost(micros):
    return pl.CostEstimate(flops=micros * 900_000_000, transcendentals=0, bytes_accessed=1 << 20)
BIG = pltpu.CompilerParams(vmem_limit_bytes=60 << 20)


def cost(micros):
    return pl.CostEstimate(flops=micros * 900_000_000, transcendentals=0, bytes_accessed=1 << 20)
BIG = pltpu.CompilerParams(vmem_limit_bytes=60 << 20)


def cost(micros):
    return pl.CostEstimate(flops=micros * 900_000_000, transcendentals=0, bytes_accessed=1 << 20)


def shifted(value, axis, steps):
    count = lax.axis_size(axis)
    leading, last = (max(0, -steps), min(count, count - steps))
    return lax.ppermute(value, axis, [(source, source + steps) for source in range(leading, last)])


def dot_rows(left, right, precision=None):
    return jnp.dot(left, right, preferred_element_type=f32, precision=precision)


def dot_inner(left, right):
    return lax.dot_general(left, right, (((0,), (0,)), ((), ())), preferred_element_type=f32)


def dot_outer(left, right):
    return lax.dot_general(left, right, (((1,), (1,)), ((), ())), preferred_element_type=f32)


def sigmoid(value):
    return 1.0 / (1.0 + jnp.exp(-value))


def gather_rows(value):
    return lax.all_gather(value, ROWS, axis=0, tiled=True)


def scatter_rows(value):
    return lax.psum_scatter(value, ROWS, scatter_dimension=0, tiled=True)


def scatter_chips(value):
    axes = CHIPS if lax.axis_size("core") == 2 else ROWS
    return lax.psum_scatter(value, axes, scatter_dimension=0, tiled=True)


def exchange(blocks):
    return lax.all_to_all(blocks, "tensor", split_axis=0, concat_axis=0, tiled=True)


def spread(block):
    count = lax.axis_size("tensor")
    return exchange(jnp.broadcast_to(block[None], (count,) + block.shape))


def spread_small(block):
    count, index = lax.axis_size("tensor"), lax.axis_index("tensor")
    width = block.shape[1]
    full = jnp.zeros((block.shape[0], count * width), block.dtype)
    for away in range(count):
        moved = block if away == 0 else lax.ppermute(
            block, "tensor", [(i, (i + away) % count) for i in range(count)]
        )
        origin = lax.rem(index - away + count, count)
        full = lax.dynamic_update_slice_in_dim(full, moved, origin * width, 1)
    return full


def halves(value):
    high = value.astype(bf16)
    return high, (value - high.astype(f32)).astype(bf16)


def far_states(packed, reverse):
    count = lax.axis_size(CTX)
    return jnp.stack([
        shifted(packed, CTX, -away if reverse else away) for away in range(1, count)
    ])


def row_iota(shape):
    return lax.broadcasted_iota(jnp.int32, shape, 0)


def col_iota(shape):
    return lax.broadcasted_iota(jnp.int32, shape, 1)


def expander(lanes, width, per):
    low = row_iota((lanes, width)) * per
    at = col_iota((lanes, width))
    return ((at >= low) & (at < low + per)).astype(f32)


def head_fold(width, lanes, per):
    low = col_iota((width, lanes)) * per
    at = row_iota((width, lanes))
    return ((at >= low) & (at < low + per)).astype(f32)


def pack_state(state, through):
    high, low = halves(through)
    row = row_iota((16, LANES))
    tail = jnp.where(row == 0, high.astype(f32), jnp.where(row == 1, low.astype(f32), 0.0))
    return jnp.concatenate([state, tail], axis=0).astype(bf16)


def join_states(far_ref, inner, per):
    spread_heads = head_fold(inner, LANES, per)
    total = None
    for k in reversed(range(far_ref.shape[0])):
        state = far_ref[k, :inner, :].astype(f32)
        if total is not None:
            through = far_ref[k, inner : inner + 16, :].astype(f32)
            through = through[0:1] + through[1:2]
            state = state + jnp.sum(spread_heads * through, axis=1, keepdims=True) * total
        total = state
    return total


def thirds(value):
    high = value.astype(bf16)
    rest = value - high.astype(f32)
    middle = rest.astype(bf16)
    return high, middle, (rest - middle.astype(f32)).astype(bf16)


def spread_lanes(value, grow):
    ones = grow.astype(bf16)
    return sum(dot_rows(part, ones) for part in thirds(value))


def left_sums(zero_one, value):
    return sum(dot_rows(zero_one, part) for part in thirds(value))


def fold_heads(value, folds):
    high, low = halves(value)
    return dot_rows(high, folds) + dot_rows(low, folds)


def conv_pre(value_ref, column, taps_ref, taps_column, same_ref, tokens):
    rows = value_ref[:, pl.ds(column, LANES)]
    total = None
    for offset in range(CONV):
        first = HALO - CONV + 1 + offset
        term = rows[first : first + tokens] * (
            same_ref[offset] * taps_ref[offset : offset + 1, pl.ds(taps_column, LANES)]
        )
        total = term if total is None else total + term
    return rows, total


def enter_part(mixed_ref, w_ref, taps_ref, same_ref, bias_ref, decay_ref, end_ref, link_ref,
                 value_ref, act_ref, scaled_ref, step_ref, run_ref, run_exp_ref,
                 state_ref, *, inner, nstate, per):
    tokens = act_ref.shape[0]
    width = 2 * inner + 2 * nstate + LANES
    tile = 384

    def matmul(i, _):
        columns = pl.ds(pl.multiple_of(i * tile, LANES), tile)
        value_ref[:, columns] = dot_rows(mixed_ref[...], w_ref[:, columns])
        return 0

    lax.fori_loop(0, width // tile, matmul, 0)

    def conv(i, _):
        at = pl.multiple_of(i * LANES, LANES)
        _, total = conv_pre(value_ref, inner + at, taps_ref, at, same_ref, tokens)
        act_ref[:, pl.ds(at, LANES)] = (total * sigmoid(total)).astype(bf16)
        return 0

    lax.fori_loop(0, (inner + 2 * nstate) // LANES, conv, 0)
    raw = value_ref[HALO:, 2 * inner + 2 * nstate :] + bias_ref[...]
    step = jnp.maximum(raw, 0.0) + jnp.log1p(jnp.exp(-jnp.abs(raw)))
    log_decay = step * -jnp.exp(decay_ref[...])
    tri = (row_iota((tokens, tokens)) >= col_iota((tokens, tokens))).astype(bf16)
    running = left_sums(tri, log_decay)
    step_ref[...] = step
    run_ref[...] = running
    grow = expander(LANES, inner, per)
    run_exp_ref[...] = spread_lanes(running, grow)
    signal = act_ref[:, :inner].astype(f32)
    scaled_ref[...] = (signal * spread_lanes(step, grow)).astype(bf16)
    toward = step * jnp.exp(running[tokens - 1 :] - running) * end_ref[...]
    pushed = (signal * spread_lanes(toward, grow)).astype(bf16)
    through = jnp.exp(running[tokens - 1 :]) * link_ref[tokens - 1 :]
    state_ref[...] = pack_state(dot_inner(pushed, act_ref[:, inner : inner + nstate]), through)


def whole(a):
    return pl.BlockSpec(a.shape, lambda i: (0,) * len(a.shape))


def columns(a, width, at=0):
    assert at % width == 0
    return pl.BlockSpec((a.shape[0], width), lambda i: (0, at // width))


def masked_scores(query, keys, seg_col_ref, seg_row_ref, start, stop):
    shape = (stop - start, stop)
    allowed = (row_iota(shape) + start >= col_iota(shape)) & (
        seg_col_ref[start:stop, :1] == seg_row_ref[:, :stop]
    )
    return jnp.where(allowed, dot_outer(query[start:stop], keys[:stop]), 0.0)


def intra_part(act_ref, scaled_ref, run_t_ref, run_exp_ref, seg_col_ref, seg_row_ref,
                 inner_ref, scores_ref, *, inner, nstate, per, block):
    tokens = act_ref.shape[0]
    keys = act_ref[:, inner : inner + nstate]
    query = act_ref[:, inner + nstate :]
    for start in range(0, tokens, block):
        stop = start + block
        scores_ref[start:stop, :stop] = masked_scores(
            query, keys, seg_col_ref, seg_row_ref, start, stop
        )

    def pair(i, _):
        columns = pl.ds(pl.multiple_of(i * LANES, LANES), LANES)
        scaled = scaled_ref[:, columns]
        lane = col_iota(scaled.shape)
        run = run_exp_ref[:, columns]
        for start in range(0, tokens, block):
            stop = start + block
            total = None
            for h in range(LANES // per):
                mine = (lane >= h * per) & (lane < (h + 1) * per)
                vals = jnp.where(mine, scaled, jnp.zeros_like(scaled))[:stop]
                row = run_t_ref[i * (LANES // per) + h, :, :stop]
                decay = jnp.exp(jnp.minimum(run[start:stop, h * per : h * per + 1] - row, 0.0))
                weight = (decay * scores_ref[start:stop, :stop]).astype(bf16)
                term = dot_rows(weight, vals)
                total = term if total is None else total + term
            inner_ref[start:stop, columns] = total
        return 0

    lax.fori_loop(0, inner // LANES, pair, 0)


def row_sums(value):
    folded = value[:, :LANES]
    for at in range(LANES, value.shape[1], LANES):
        folded = folded + value[:, at : at + LANES]
    ones = jnp.ones((8, LANES), bf16)
    high, low = halves(folded)
    return dot_outer(ones, high) + dot_outer(ones, low)


def as_column(row):
    n = row.shape[1]
    eye = row_iota((n, n)) == col_iota((n, n))
    return jnp.sum(jnp.where(eye, row, 0.0), axis=1, keepdims=True)


def tensor_barrier(me, n):
    barrier = pltpu.get_barrier_semaphore()
    for d in range(1, n):
        pl.semaphore_signal(
            barrier, inc=1, device_id={"tensor": lax.rem(me + d, n)}, device_id_type=MESH
        )
    pl.semaphore_wait(barrier, n - 1)


def push(source, target, sems, slot, peer):
    send, receive = sems
    return pltpu.make_async_remote_copy(
        src_ref=source, dst_ref=target, send_sem=send.at[slot], recv_sem=receive.at[slot],
        device_id=peer if isinstance(peer, dict) else {"tensor": peer}, device_id_type=MESH,
    )


def ctx_place():
    core = lax.axis_size("core")
    return lax.axis_index("cy") * core + lax.axis_index("core"), lax.axis_size("cy") * core


def ctx_peer(place):
    core = lax.axis_size("core")
    return {"cy": place // core, "core": lax.rem(place, core)}


def front_barrier(me, n):
    barrier = pltpu.get_barrier_semaphore()
    place, count = ctx_place()
    for d in range(1, n):
        pl.semaphore_signal(
            barrier, inc=1, device_id={"tensor": lax.rem(me + d, n)}, device_id_type=MESH
        )
    for d in range(1, count):
        pl.semaphore_signal(
            barrier, inc=1, device_id=ctx_peer(lax.rem(place + d, count)), device_id_type=MESH
        )
    pl.semaphore_wait(barrier, n - 1 + count - 1)


def rows_barrier(me, n):
    barrier = line_barrier(me, n)
    place, count = row_place(), lax.axis_size(ROWS)
    for d in range(1, count):
        pl.semaphore_signal(barrier, inc=1, device_id=row_peer(lax.rem(place + d, count)),
                            device_id_type=MESH)
    pl.semaphore_wait(barrier, n - 1 + count - 1)


class RowGather:
    def __init__(self, source, full, sems):
        self.cy, self.core = lax.axis_size("cy"), lax.axis_size("core")
        self.chips = lax.axis_size(CHIPS)
        me = lax.axis_index("core")
        chip = lax.axis_index("shard") * self.cy + lax.axis_index("cy")
        slot = lambda c: c * self.core + me
        self.far, self.near = [], []
        for d in range(1, self.chips):
            peer = lax.rem(chip + d, self.chips)
            self.far.append(push(source, full.at[slot(chip)], sems[0], d - 1,
                                 {"shard": peer // self.cy, "cy": lax.rem(peer, self.cy)}))
        if self.core == 2:
            for d in range(self.chips):
                origin = lax.rem(chip - d + self.chips, self.chips)
                self.near.append(push(source if d == 0 else full.at[slot(origin)], full.at[slot(origin)],
                                      sems[1], d, {"core": 1 - me}))

    def start(self):
        for copy in self.far + self.near[:1]:
            copy.start()

    def relay(self):
        for d, copy in enumerate(self.far):
            copy.wait_recv()
            if self.near:
                self.near[d + 1].start()

    def finish(self):
        for copy in self.near:
            copy.wait()
        for copy in self.far:
            copy.wait_send()


class WeightSum:
    def __init__(self, stage, boxes):
        self.stage, self.boxes = stage, boxes
        self.depth = stage.shape[0]
        self.core, self.cy = lax.axis_index("core"), lax.axis_size("cy")
        self.chip = lax.axis_index("shard") * self.cy + lax.axis_index("cy")
        self.chips = boxes[0].shape[0] if boxes else 0
        self.paired = boxes[1:3] if len(boxes) == 3 else boxes[3:5]
        self.owner = boxes[0].shape[1] if boxes else 0
        self.siblings, self.mains, self.units = [], [], []

    def rows(self, k):
        return pl.ds(pl.multiple_of(k * self.owner, 16), self.owner)

    def product(self, lhs_ref, rhs, at, transposed=True):
        span = rhs.shape[1]
        tall = self.depth // 2

        def part(m, _):
            here = pl.ds(pl.multiple_of(m * tall, tall), tall)
            if transposed:
                value = dot_rows(lhs_ref[here, :], rhs[...])
            else:
                value = dot_inner(lhs_ref[:, here], rhs[...])
            self.stage[here, at : at + span] = value.astype(bf16)
            return 0

        lax.fori_loop(0, 2, part, 0)

    def to_sibling(self, at, span):
        unit = len(self.units)
        self.units.append((at, span))
        copies = []
        for j in range(self.chips):
            copies.append(push(
                self.stage.at[self.rows(2 * j + 1 - self.core), pl.ds(at, span)],
                self.boxes[0].at[j, :, pl.ds(at, span)], self.paired, unit * self.chips + j,
                {"core": 1 - self.core},
            ))
            copies[-1].start()
        self.siblings.append(copies)

    def to_chips(self, unit):
        if not self.chips:
            return
        sib_in, sum_ref, main_in = self.boxes[:3]
        at, span = self.units[unit]
        for j, copy in enumerate(self.siblings[unit]):
            copy.wait_recv()
            sum_ref[j * self.owner : (j + 1) * self.owner, at : at + span] = (
                self.stage[self.rows(2 * j + self.core), at : at + span] + sib_in[j, :, at : at + span]
            )
        for d in range(1, self.chips):
            peer = lax.rem(self.chip + d, self.chips)
            self.mains.append(push(
                sum_ref.at[self.rows(peer), pl.ds(at, span)], main_in.at[d - 1, :, pl.ds(at, span)],
                self.boxes[5:7], unit * (self.chips - 1) + d - 1,
                {"shard": peer // self.cy, "cy": lax.rem(peer, self.cy)},
            ))
            self.mains[-1].start()

    def pair(self, unit, out_ref):
        at, span = self.units[unit]
        if not self.chips:
            out_ref[:, at : at + span] = self.stage[:, at : at + span]
            return
        for j, copy in enumerate(self.siblings[unit]):
            copy.wait_recv()
            out_ref[j * self.owner : (j + 1) * self.owner, at : at + span] = (
                self.stage[self.rows(2 * j + self.core), at : at + span]
                + self.boxes[0][j, :, at : at + span]
            )

    def wait_send(self):
        for copies in self.siblings:
            for copy in copies:
                copy.wait_send()

    def finish(self, out_ref):
        if not self.chips:
            out_ref[...] = self.stage[...]
            return
        _, sum_ref, main_in = self.boxes[:3]
        main_in[self.chips - 1] = sum_ref[self.rows(self.chip), :]
        for copy in self.mains:
            copy.wait_recv()
        out_ref[...] = in_order(main_in, self.chip, self.chips)
        self.wait_send()
        for copy in self.mains:
            copy.wait_send()


def weight_boxes(depth, width, units, between_chips=True):
    dma = pltpu.SemaphoreType.DMA
    if lax.axis_size("core") != 2:
        return [pltpu.VMEM((depth, width), bf16)], jax.ShapeDtypeStruct((depth, width), bf16)
    chips = lax.axis_size(CHIPS)
    owner = depth // (2 * chips)
    if not between_chips:
        return [
            pltpu.VMEM((depth, width), bf16), pltpu.VMEM((chips, owner, width), bf16),
            dma((units * chips,)), dma((units * chips,)),
        ], jax.ShapeDtypeStruct((chips * owner, width), bf16)
    return [
        pltpu.VMEM((depth, width), bf16), pltpu.VMEM((chips, owner, width), bf16),
        pltpu.VMEM((chips * owner, width), bf16), pltpu.VMEM((chips, owner, width), bf16),
        dma((units * chips,)), dma((units * chips,)), dma((units * (chips - 1),)),
        dma((units * (chips - 1),)),
    ], jax.ShapeDtypeStruct((owner, width), f32)


class StatePush:
    def __init__(self, source, far_ref, sems, reverse):
        place, count = ctx_place()
        sign = -1 if reverse else 1
        self.copies = []
        for d in range(1, count):
            to, origin = place + sign * d, place - sign * d
            copy = push(source, far_ref.at[d - 1], sems, d - 1,
                        ctx_peer(lax.rem(to + count, count)))
            self.copies.append((copy, (to >= 0) & (to < count), (origin >= 0) & (origin < count)))

    def start(self):
        for copy, sends, _ in self.copies:
            pl.when(sends)(copy.start)

    def wait_recv(self):
        for copy, _, gets in self.copies:
            pl.when(gets)(copy.wait_recv)

    def wait_send(self):
        for copy, sends, _ in self.copies:
            pl.when(sends)(copy.wait_send)


class LineReduce:
    def __init__(self, me, n, blocks, right, left, sems):
        self.me, self.n, self.blocks, self.right, self.left = me, n, blocks, right, left
        self.right_sems, self.left_sems = sems
        self.keep = lambda d: jnp.minimum(jnp.maximum(d, 0), n - 1)

    def rightward(self, d):
        return push(self.blocks(d), self.right.at[d], self.right_sems, d,
                    jnp.minimum(self.me + 1, self.n - 1))

    def leftward(self, d):
        return push(self.blocks(d), self.left.at[d], self.left_sems, d, jnp.maximum(self.me - 1, 0))

    def step(self, t):
        me, n = self.me, self.n
        ways = []
        if t < n:
            ways.append((n - 1 - t + me, me >= 1, lambda d: d > me, t >= me, self.rightward, self.right))
            ways.append((t - (n - 1 - me), me <= n - 2, lambda d: d < me, t >= n - 1 - me,
                         self.leftward, self.left))
        for d, gets, passes, ready, copy_of, box in ways:
            at = self.keep(d)
            copy = copy_of(at)

            @pl.when(gets & ready)
            def _():
                copy.wait_recv()

            @pl.when(gets & ready & passes(d))
            def _():
                view = self.blocks(at)
                view[...] = view[...] + box[at]

            @pl.when(ready & passes(d))
            def _():
                copy.start()

    def total(self):
        me, n = self.me, self.n
        value = self.blocks(me)[...].astype(f32)
        value = value + jnp.where(me >= 1, self.right[me].astype(f32), 0.0)
        return value + jnp.where(me <= n - 2, self.left[me].astype(f32), 0.0)

    def wait_send(self):
        for d in range(self.n):
            pl.when(self.me < d)(self.rightward(d).wait_send)
            pl.when(self.me > d)(self.leftward(d).wait_send)


class LineGather:
    def __init__(self, me, n, blocks, sems):
        self.me, self.n, self.blocks = me, n, blocks
        self.right_sems, self.left_sems = sems

    def rightward(self, d):
        return push(self.blocks(d), self.blocks(d), self.right_sems, d,
                    jnp.minimum(self.me + 1, self.n - 1))

    def leftward(self, d):
        return push(self.blocks(d), self.blocks(d), self.left_sems, d, jnp.maximum(self.me - 1, 0))

    def step(self, t):
        me, n = self.me, self.n
        from_left, from_right = me - t, me + t
        right = self.rightward(jnp.maximum(from_left, 0))
        left = self.leftward(jnp.minimum(from_right, n - 1))
        if t > 0:
            pl.when(from_left >= 0)(right.wait_recv)
        pl.when((from_left >= 0) & (me <= n - 2))(right.start)
        if t > 0:
            pl.when(from_right <= n - 1)(left.wait_recv)
        pl.when((from_right <= n - 1) & (me >= 1))(left.start)

    def wait_send(self):
        for d in range(self.n):
            pl.when((self.me >= d) & (self.me <= self.n - 2))(self.rightward(d).wait_send)
            pl.when((self.me <= d) & (self.me >= 1))(self.leftward(d).wait_send)


def line_sems(n):
    return [pltpu.SemaphoreType.DMA((n,))] * 4


def line_groups(sems):
    return (sems[0], sems[1]), (sems[2], sems[3])


def line_barrier(me, n):
    barrier = pltpu.get_barrier_semaphore()
    for d in range(1, n):
        pl.semaphore_signal(
            barrier, inc=1, device_id={"tensor": lax.rem(me + d, n)}, device_id_type=MESH
        )
    return barrier


def intake_kernel(x_ref, gains_ref, mixed_ref, mixed_t_ref, full_ref, gain_out,
                  x_box, gains_box, halo_box, *sems, n):
    me = lax.axis_index("tensor")
    place, count = ctx_place()
    rows, quarter = x_ref.shape
    column = lambda d: pl.ds(pl.multiple_of(d * quarter, LANES), quarter)
    gain_sems, halo_sems = (sems[0], sems[1]), (sems[2], sems[3])
    halo_box[...] = jnp.zeros_like(halo_box)
    x_box[:, column(me)] = x_ref[...]
    gains_box[:, column(me)] = gains_ref[...]
    barrier = line_barrier(me, n)
    for away in (1, count - 1):
        for z in range(n):
            pl.semaphore_signal(
                barrier, inc=1, device_id={**ctx_peer(lax.rem(place + away, count)), "tensor": z},
                device_id_type=MESH,
            )
    pl.semaphore_wait(barrier, n - 1 + 2 * n)
    x_line = LineGather(me, n, lambda d: x_box.at[:, column(d)], line_groups(sems[4:8]))
    x_line.step(0)
    gains = [push(gains_box.at[:, column(me)], gains_box.at[:, column(me)], gain_sems, d - 1,
                  lax.rem(me + d, n)) for d in range(1, n)]
    for copy in gains:
        copy.start()
    sends, gets = place < count - 1, place > 0
    halos = []
    for d in range(n):
        peer = {**ctx_peer(jnp.minimum(place + 1, count - 1)), "tensor": lax.rem(me + d, n)}
        halos.append(push(x_ref.at[rows - HALO :], halo_box.at[:, column(me)], halo_sems, d, peer))
        pl.when(sends)(halos[-1].start)
    for t in range(1, n):
        x_line.step(t)
    for copy in gains:
        copy.wait_recv()
    for copy in halos:
        pl.when(gets)(copy.wait_recv)
    gain = gains_box[0:1, :].astype(f32)
    gain_out[...] = gains_box[...].astype(f32)

    def normed(x):
        x = x.astype(f32)
        scale = lax.rsqrt(jnp.mean(x * x, axis=1, keepdims=True) + epsilon)
        return (x * scale * gain).astype(bf16)

    mixed_ref[:HALO, :] = normed(halo_box[...])
    full_ref[...] = x_box[...]
    mixed_ref[HALO:, :] = normed(x_box[...])
    mixed_t_ref[...] = mixed_ref[HALO:, :].T
    for copy in gains:
        copy.wait_send()
    for copy in halos:
        pl.when(sends)(copy.wait_send)
    x_line.wait_send()


def intake(x, gains):
    n = lax.axis_size("tensor")
    rows, quarter = x.shape
    depth = n * quarter
    shape = jax.ShapeDtypeStruct
    dma = pltpu.SemaphoreType.DMA
    return pl.pallas_call(
        partial(intake_kernel, n=n),
        in_specs=[VMEM] * 2,
        out_specs=[VMEM] * 4,
        out_shape=[shape((rows + HALO, depth), bf16), shape((depth, rows), bf16),
                   shape((rows, depth), bf16), shape((16, depth), f32)],
        scratch_shapes=[
            pltpu.VMEM((rows, depth), bf16),
            pltpu.VMEM((16, depth), bf16), pltpu.VMEM((HALO, depth), bf16),
            dma((n - 1,)), dma((n - 1,)), dma((n,)), dma((n,)),
        ] + line_sems(n),
        compiler_params=pltpu.CompilerParams(
            vmem_limit_bytes=60 << 20, collective_id=7, has_side_effects=True
        ),
        cost_estimate=cost(50),
        name="intake",
    )(x, gains)


def row_columns(row):
    return jnp.concatenate(
        [as_column(row[:, at : at + LANES]) for at in range(0, row.shape[1], LANES)], axis=0
    )


def front_kernel(mixed_ref, taps_ref, same_ref, bias_ref, decay_ref, end_ref, link_ref, seg_col_ref,
                 seg_row_ref, skip_ref, gain_ref, x_ref, cot_ref, w_ref,
                 value_ref, act_ref, scaled_ref, step_ref, run_ref, run_exp_ref, inner_ref, mixer_ref,
                 state_ref, packed_ref, res_ref, stat_ref, own_ref, cot_full_ref,
                 wm_ref, wo_ref, run_t_ref, scores_ref, part_ref, square_ref, lifted_ref, far_ref,
                 right_box, left_box, square_box, res_box, stat_box, cot_box, local_sem, *sems,
                 inner, nstate, per, heads, di_all, n):
    me = lax.axis_index("tensor")
    rows, depth = x_ref.shape
    own = rows // n
    groups = [(sems[2 * i], sems[2 * i + 1]) for i in range(3)]
    block_at = lambda d: pl.ds(pl.multiple_of(d * own, own), own)
    half = own // 2
    half_at = lambda d, h: pl.ds(pl.multiple_of(d * own + h * half, half), half)
    lines_at = lambda k: line_groups(sems[6 + 4 * k : 10 + 4 * k])
    mine = pl.ds(pl.multiple_of(me * own, own), own)
    wide = wm_ref.shape[1]
    loads = [
        pltpu.make_async_copy(w_ref.at[:, pl.ds(0, wide)], wm_ref, local_sem.at[0]),
        pltpu.make_async_copy(w_ref.at[:, pl.ds(wide, inner)], wo_ref, local_sem.at[1]),
    ]
    for copy in loads:
        copy.start()
    far_ref[...] = jnp.zeros_like(far_ref)
    quarter = cot_ref.shape[1]
    column = pl.ds(pl.multiple_of(me * quarter, LANES), quarter)
    cot_box[:, column] = cot_ref[...]
    front_barrier(me, n)
    cots = LineGather(
        me, n, lambda d: cot_box.at[:, pl.ds(pl.multiple_of(d * quarter, LANES), quarter)],
        lines_at(0),
    )
    cots.step(0)
    loads[0].wait()
    enter_part(mixed_ref, wm_ref, taps_ref, same_ref, bias_ref, decay_ref, end_ref, link_ref,
               value_ref, act_ref, scaled_ref, step_ref, run_ref, run_exp_ref, packed_ref,
               inner=inner, nstate=nstate, per=per)
    states = StatePush(packed_ref, far_ref, groups[0], False)
    states.start()
    cots.step(1)
    run_t = run_ref[...].T
    for h in range(heads):
        run_t_ref[h] = run_t[h : h + 1, :]
    intra_part(act_ref, scaled_ref, run_t_ref, run_exp_ref, seg_col_ref, seg_row_ref, inner_ref,
               scores_ref, inner=inner, nstate=nstate, per=per, block=128)
    cots.step(2)
    states.wait_recv()
    state = join_states(far_ref, inner, per)
    state_ref[...] = state
    carried = dot_outer(act_ref[:, inner + nstate :], state.astype(bf16)) * (
        jnp.exp(run_exp_ref[...]) * link_ref[...]
    )
    mixer = inner_ref[...] + carried + skip_ref[...] * act_ref[:, :inner].astype(f32)
    mixer_ref[...] = mixer
    z = value_ref[HALO:, :inner]
    gated = mixer * (z * sigmoid(z))
    square_ref[...] = row_sums(gated * gated)
    lifted_ref[...] = (gated * gain_ref[...]).astype(bf16)
    loads[1].wait()
    for t in range(3, n):
        cots.step(t)
    squares, stats = [], []
    for d in range(1, n):
        peer = lax.rem(me + d, n)
        squares.append(push(square_ref.at[:, block_at(peer)], square_box.at[d - 1], groups[1], d - 1, peer))
        squares[-1].start()
    lines = [
        LineReduce(me, n, lambda d, h=h: part_ref.at[d, pl.ds(h * half, half)], right_box.at[h],
                   left_box.at[h], lines_at(1 + h)) for h in range(2)
    ]
    gathers = [LineGather(me, n, lambda d, h=h: res_box.at[half_at(d, h)], lines_at(3 + h))
               for h in range(2)]
    for k in range(n):
        d = jnp.where(2 * me < n, n - 1 - k, k)
        part_ref[d] = dot_outer(lifted_ref[block_at(d), :], wo_ref[...]).astype(bf16)
        if k == 0:
            for line in lines:
                line.step(0)
    square = square_ref[:, mine]
    for copy in squares:
        copy.wait_recv()
    for d in range(1, n):
        square = square + square_box[d - 1]
    scale = lax.rsqrt(square / di_all + epsilon)
    stat_box[:, mine] = scale
    for d in range(1, n):
        stats.append(push(stat_box.at[:, mine], stat_box.at[:, mine], groups[2], d - 1,
                          lax.rem(me + d, n)))
        stats[-1].start()
    scale = as_column(scale[:1])
    for t in range(1, n - 1):
        for line in lines:
            line.step(t)
    for h in range(2):
        lines[h].step(n - 1)
        total = lines[h].total()
        own_ref[h * half : (h + 1) * half, :] = total
        here = half_at(me, h)
        res_box[here, :] = (
            x_ref[here, :].astype(f32) + total * scale[h * half : (h + 1) * half]
        ).astype(bf16)
        gathers[h].step(0)
    for t in range(1, n):
        for gather in gathers:
            gather.step(t)
    cot_full_ref[...] = cot_box[...]
    states.wait_send()
    cots.wait_send()
    for line in lines + gathers:
        line.wait_send()
    for copy in squares:
        copy.wait_send()
    for copy in stats:
        copy.wait()
    res_ref[...] = res_box[...]
    stat_ref[...] = stat_box[...]


def pairs(count, n):
    return [pltpu.SemaphoreType.DMA((n - 1,))] * (2 * count)


VMEM = pl.BlockSpec(memory_space=pltpu.VMEM)
HBM = pl.BlockSpec(memory_space=pl.ANY)


def front(mixed_ext, taps, same, bias, decay, at_end, link, seg_col, seg_row, skip, gain, x, cot, weights,
          inner, nstate, per, heads, di_all):
    n = lax.axis_size("tensor")
    others = lax.axis_size(CTX) - 1
    tokens, depth = x.shape
    ext = tokens + HALO
    own = tokens // n
    wide = 2 * inner + 2 * nstate + LANES
    shape = jax.ShapeDtypeStruct
    outs = [
        shape((ext, wide), f32), shape((tokens, inner + 2 * nstate), bf16),
        shape((tokens, inner), bf16), shape((tokens, LANES), f32), shape((tokens, LANES), f32),
        shape((tokens, inner), f32), shape((tokens, inner), f32), shape((tokens, inner), f32),
        shape((inner, nstate), f32), shape((inner + 16, nstate), bf16),
        shape((tokens, depth), bf16), shape((8, tokens), f32), shape((own, depth), f32),
        shape((tokens, depth), bf16),
    ]
    dma = pltpu.SemaphoreType.DMA
    return pl.pallas_call(
        partial(front_kernel, inner=inner, nstate=nstate, per=per, heads=heads, di_all=di_all, n=n),
        in_specs=[VMEM] * 13 + [HBM],
        out_specs=[VMEM] * 14,
        out_shape=outs,
        scratch_shapes=[
            pltpu.VMEM((depth, wide), bf16), pltpu.VMEM((depth, inner), bf16),
            pltpu.VMEM((heads, 1, tokens), f32), pltpu.VMEM((tokens, tokens), f32),
            pltpu.VMEM((n, own, depth), bf16), pltpu.VMEM((8, tokens), f32),
            pltpu.VMEM((tokens, inner), bf16), pltpu.VMEM((others, inner + 16, nstate), bf16),
            pltpu.VMEM((2, n, own // 2, depth), bf16), pltpu.VMEM((2, n, own // 2, depth), bf16),
            pltpu.VMEM((n - 1, 8, own), f32),
            pltpu.VMEM((tokens, depth), bf16), pltpu.VMEM((8, tokens), f32),
            pltpu.VMEM((tokens, depth), bf16), dma((2,)), dma((others,)), dma((others,)),
        ] + pairs(2, n) + line_sems(n) * 5,
        compiler_params=pltpu.CompilerParams(
            vmem_limit_bytes=60 << 20, collective_id=1, has_side_effects=True
        ),
        cost_estimate=cost(100),
        name="front",
    )(mixed_ext, taps, same, bias, decay, at_end, link, seg_col, seg_row, skip, gain, x, cot, weights)


def turn_kernel(dmix_hbm, dgate_ref, res_ref, cot_ref, own_ref, gain_ref,
                dres_ref, notes_ref, gains_ref,
                dmix_ref, right_box, left_box, gate_box, dres_box, notes_box, load_sem, *sems, n):
    me = lax.axis_index("tensor")
    rows, depth = res_ref.shape
    own = rows // n
    groups = [(sems[2 * i], sems[2 * i + 1]) for i in range(2)]
    block_at = lambda d: pl.ds(pl.multiple_of(d * own, own), own)
    mine = block_at(me)
    load = pltpu.make_async_copy(dmix_hbm, dmix_ref, load_sem)
    load.start()
    tensor_barrier(me, n)
    load.wait()
    half = own // 2
    half_at = lambda d, h: pl.ds(pl.multiple_of(d * own + h * half, half), half)
    lines_at = lambda k: line_groups(sems[4 + 4 * k : 8 + 4 * k])
    lines = [LineReduce(me, n, lambda d, h=h: dmix_ref.at[half_at(d, h)], right_box.at[h],
                        left_box.at[h], lines_at(h)) for h in range(2)]
    gathers = [LineGather(me, n, lambda d, h=h: dres_box.at[half_at(d, h)], lines_at(2 + h))
               for h in range(2)]
    for line in lines:
        line.step(0)
    first, second = [], []
    for d in range(1, n):
        peer = lax.rem(me + d, n)
        first.append(push(dgate_ref.at[:, block_at(peer)], gate_box.at[d - 1], groups[0], d - 1, peer))
        first[-1].start()
    res = res_ref[mine, :].astype(f32)
    scale = lax.rsqrt(jnp.mean(res * res, axis=1, keepdims=True) + epsilon)
    normed = res * scale
    for t in range(1, n - 1):
        for line in lines:
            line.step(t)
    gain_sum = None
    for h in range(2):
        lines[h].step(n - 1)
        dmix = lines[h].total()
        part = slice(h * half, (h + 1) * half)
        here = half_at(me, h)
        lifted = dmix * gain_ref[...]
        inside = jnp.mean(lifted * normed[part], axis=1, keepdims=True)
        dres_box[here, :] = (
            cot_ref[here, :].astype(f32) + scale[part] * (lifted - normed[part] * inside)
        ).astype(bf16)
        gathers[h].step(0)
        term = jnp.sum(dmix * normed[part], axis=0, keepdims=True)
        gain_sum = term if gain_sum is None else gain_sum + term
    gains_ref[...] = jnp.broadcast_to(gain_sum, gains_ref.shape)
    dgate = dgate_ref[:, mine]
    for copy in first:
        copy.wait_recv()
    for d in range(1, n):
        dgate = dgate + gate_box[d - 1]
    gates = dgate.shape[0]
    notes_box[:gates, mine] = dgate
    notes_box[gates:, mine] = row_sums(dres_box[mine, :].astype(f32) * own_ref[...])
    for d in range(1, n):
        peer = lax.rem(me + d, n)
        second.append(push(notes_box.at[:, mine], notes_box.at[:, mine], groups[1], d - 1, peer))
        second[-1].start()
    for t in range(1, n):
        for gather in gathers:
            gather.step(t)
    for line in lines + gathers:
        line.wait_send()
    for copy in first:
        copy.wait_send()
    for copy in second:
        copy.wait()
    dres_ref[...] = dres_box[...]
    notes_ref[...] = notes_box[...]


def turn_step(dmix, dgate, residual, cot, own_part, gain):
    n = lax.axis_size("tensor")
    tokens, depth = dmix.shape
    own = tokens // n
    shape = jax.ShapeDtypeStruct
    return pl.pallas_call(
        partial(turn_kernel, n=n),
        in_specs=[HBM] + [VMEM] * 5,
        out_specs=[VMEM] * 3,
        out_shape=[shape((tokens, depth), bf16), shape((dgate.shape[0] + 8, tokens), f32),
                   shape((8, depth), f32)],
        scratch_shapes=[
            pltpu.VMEM((tokens, depth), bf16),
            pltpu.VMEM((2, n, own // 2, depth), bf16), pltpu.VMEM((2, n, own // 2, depth), bf16),
            pltpu.VMEM((n - 1, dgate.shape[0], own), f32),
            pltpu.VMEM((tokens, depth), bf16), pltpu.VMEM((dgate.shape[0] + 8, tokens), f32),
            pltpu.SemaphoreType.DMA,
        ] + pairs(2, n) + line_sems(n) * 4,
        compiler_params=pltpu.CompilerParams(
            vmem_limit_bytes=60 << 20, collective_id=2, has_side_effects=True
        ),
        cost_estimate=cost(60),
        name="turn_step",
    )(dmix, dgate, residual, cot, own_part, gain)


def in_order(box, me, count):
    total = None
    for source in range(count):
        term = box[lax.rem(me - source + 2 * count - 1, count)].astype(f32)
        total = term if total is None else total + term
    return total


def row_place():
    cy, core = lax.axis_size("cy"), lax.axis_size("core")
    return (lax.axis_index("shard") * cy + lax.axis_index("cy")) * core + lax.axis_index("core")


def row_peer(place):
    cy, core = lax.axis_size("cy"), lax.axis_size("core")
    return {"shard": place // (cy * core), "cy": lax.rem(place // core, cy), "core": lax.rem(place, core)}


def last_kernel(grad_ref, x_ref, dres_ref, gain_ref, mid_ref, state_ref, early_ref, mixed_t_ref, mix_t_ref,
                state_all_ref, gates_ref, notes_ref, w_hbm,
                out_ref, early_out, late_out, main_out,
                w_ref, blocks_ref, right_box, left_box, cross_box, cross_in, gains_box, gains_in, state_in,
                early_in, late_ref, late_in, load_sem, stage_ref, *sems, n, count, boxes, inner, last):
    weights = WeightSum(stage_ref, sems[:boxes])
    sems = sems[boxes:]
    me = lax.axis_index("tensor")
    place = row_place()
    rows, depth = x_ref.shape
    quarter = depth // n
    wide = w_ref.shape[1]
    groups = [(sems[2 * i], sems[2 * i + 1]) for i in range(3)]
    row_groups = [(sems[6 + 2 * i], sems[7 + 2 * i]) for i in range(2)]
    load = pltpu.make_async_copy(w_hbm.at[:, pl.ds(0, wide)], w_ref, load_sem)
    load.start()
    rows_barrier(me, n)
    copies, states, lates = [], [], []
    x = x_ref[...].astype(f32)
    scale = lax.rsqrt(jnp.mean(x * x, axis=1, keepdims=True) + epsilon)
    load.wait()
    half = rows // 2
    lines = [
        LineReduce(me, n, lambda d, h=h: blocks_ref.at[d, pl.ds(h * half, half)], right_box.at[h],
                   left_box.at[h], line_groups(sems[10 + 4 * h : 14 + 4 * h])) for h in range(2)
    ]
    cross = jnp.zeros((8, rows), f32)
    for k in range(n):
        d = jnp.where(2 * me < n, n - 1 - k, k)
        theirs = pl.ds(pl.multiple_of(d * quarter, LANES), quarter)
        w = w_ref[theirs, :]
        block = dot_outer(grad_ref[...], w)
        blocks_ref[d] = block.astype(bf16)
        if k == 0:
            for line in lines:
                line.step(0)
        normed = x_ref[:, theirs].astype(f32) * scale
        cross = cross + row_sums(block * normed * gain_ref[:, theirs])
        gains_box[d] = jnp.where(
            row_iota((8, quarter)) == 0, jnp.sum(block * normed, axis=0, keepdims=True),
            mid_ref[:, theirs],
        )
    cross_box[...] = cross
    sums = []
    for d in range(1, n):
        peer = lax.rem(me + d, n)
        sums.append(push(gains_box.at[peer], gains_in.at[d - 1], groups[0], d - 1, peer))
        sums.append(push(cross_box, cross_in.at[d - 1], groups[1], d - 1, peer))
        states.append(push(state_ref, state_in.at[d - 1], groups[2], d - 1, peer))
    for d in range(1, count):
        copies.append(push(early_ref, early_in.at[d - 1], row_groups[0], d - 1,
                           row_peer(lax.rem(place + d, count))))
    for copy in sums + states + copies:
        copy.start()

    gates = gates_ref[...]
    kinds = notes_ref.shape[0] - 8
    moved = jnp.concatenate(
        [notes_ref[:kinds, :], jnp.zeros((LANES - kinds, gates.shape[0]), f32)], axis=0
    ).T
    inside = jnp.sum(gates * moved, axis=1, keepdims=True)
    first = 2 * inner
    weights.product(mixed_t_ref, grad_ref.at[:, pl.ds(inner, inner)], 0)
    weights.to_sibling(0, inner)
    for line in lines:
        line.step(1)
    weights.product(mixed_t_ref, state_all_ref, inner)
    weights.product(mixed_t_ref, grad_ref.at[:, pl.ds(last, LANES)], inner + last - first)
    weights.product(mix_t_ref, (gates * (moved - inside)).astype(bf16), inner + wide - first)
    weights.to_sibling(inner, wide - first + LANES)
    weights.to_chips(0)
    for copy in sums + states:
        copy.wait_recv()
    gains = gains_box[me]
    for d in range(1, n):
        gains = gains + gains_in[d - 1]
        cross = cross + cross_in[d - 1]
    state_in[n - 1] = state_ref[...]
    late_ref[:, :quarter] = gains
    late_ref[:, quarter:] = in_order(state_in, me, n)
    for d in range(1, count):
        lates.append(push(late_ref, late_in.at[d - 1], row_groups[1], d - 1,
                          row_peer(lax.rem(place + d, count))))
        lates[-1].start()
    for t in range(2, n - 1):
        for line in lines:
            line.step(t)
    weights.to_chips(1)
    here = pl.ds(pl.multiple_of(me * quarter, LANES), quarter)
    inside = row_columns(cross[:1]) / depth
    for h in range(2):
        lines[h].step(n - 1)
        part = slice(h * half, (h + 1) * half)
        out_ref[part, :] = dres_ref[part, here].astype(f32) + scale[part] * (
            lines[h].total() * gain_ref[:, here]
            - x_ref[part, here].astype(f32) * scale[part] * inside[part]
        )
    for copy in copies + lates:
        copy.wait_recv()
    early_in[count - 1] = early_ref[...]
    late_in[count - 1] = late_ref[...]
    early_out[...] = in_order(early_in, place, count)
    late_out[...] = in_order(late_in, place, count)
    weights.finish(main_out)
    for copy in copies + states + lates + sums:
        copy.wait_send()
    for line in lines:
        line.wait_send()


def last_step(vmem_args, weights, inner, last):
    value_grad, x, early, state = (vmem_args[i] for i in (0, 1, 6, 5))
    n, count = lax.axis_size("tensor"), lax.axis_size(ROWS)
    tokens, depth = x.shape
    quarter = depth // n
    wide = value_grad.shape[1]
    late = quarter + state.shape[1]
    shape = jax.ShapeDtypeStruct
    dma = pltpu.SemaphoreType.DMA
    boxes, main = weight_boxes(depth, wide - inner + LANES, 2)
    return pl.pallas_call(
        partial(last_kernel, n=n, count=count, boxes=len(boxes) - 1, inner=inner, last=last),
        in_specs=[VMEM] * len(vmem_args) + [HBM],
        out_specs=[VMEM] * 4,
        out_shape=[shape((tokens, quarter), f32), shape(early.shape, f32), shape((8, late), f32), main],
        scratch_shapes=[
            pltpu.VMEM((depth, wide), bf16), pltpu.VMEM((n, tokens, quarter), bf16),
            pltpu.VMEM((2, n, tokens // 2, quarter), bf16), pltpu.VMEM((2, n, tokens // 2, quarter), bf16),
            pltpu.VMEM((8, tokens), f32), pltpu.VMEM((n - 1, 8, tokens), f32),
            pltpu.VMEM((n, 8, quarter), f32), pltpu.VMEM((n - 1, 8, quarter), f32),
            pltpu.VMEM((n,) + state.shape, f32), pltpu.VMEM((count,) + early.shape, f32),
            pltpu.VMEM((8, late), f32), pltpu.VMEM((count, 8, late), f32), dma,
        ] + boxes + pairs(3, n) + [dma((count - 1,))] * 4 + line_sems(n) * 2,
        compiler_params=pltpu.CompilerParams(
            vmem_limit_bytes=62 << 20, collective_id=3, has_side_effects=True
        ),
        cost_estimate=cost(60),
        name="last_step",
    )(*vmem_args, weights)


def emit_kernel(out_ref, grad_ref, early_ref, late_ref, rear_ref, main_ref, pair_ref, *outs, per):
    (out, grad, gain_in, pair_out, state_out, step_out, conv, conv_state, bias, decay, skip, gate, proj,
     gain_mid, router, shared_up, shared_down, gates, down) = outs
    out[...] = out_ref[...]
    grad[...] = grad_ref[...]
    taps, inner = conv.shape
    heads = bias.shape[1]
    quarter = grad.shape[1]
    conv[...] = early_ref[:taps]
    conv_state[...] = late_ref[:taps, quarter:]
    for i in range(inner // LANES):
        gate[i : i + 1, :] = early_ref[taps : taps + 1, i * LANES : (i + 1) * LANES]
    for i in range(quarter // LANES):
        columns = slice(i * LANES, (i + 1) * LANES)
        gain_in[i : i + 1, :] = late_ref[0:1, columns]
        gain_mid[i : i + 1, :] = late_ref[1:2, columns]
    skips = jnp.broadcast_to(early_ref[taps + 1 : taps + 2], (8, inner))
    skip[...] = fold_heads(skips, head_fold(inner, LANES, per).astype(bf16))[:1, :heads]
    bias[...] = early_ref[taps + 2 : taps + 3, :heads]
    decay[...] = early_ref[taps + 3 : taps + 4, :heads]
    last = inner + state_out.shape[1]
    wide = last + LANES
    proj[...] = rear_ref[:, :inner].astype(f32)
    pair_out[:, 0, :] = rear_ref[:, inner:].astype(f32)
    pair_out[:, 1, :] = main_ref[:, :inner].astype(f32)
    state_out[...] = main_ref[:, inner:last].astype(f32)
    step_out[...] = main_ref[:, last:wide].astype(f32).T[:heads, :]
    router[...] = main_ref[:, wide:].astype(f32).T[: router.shape[0], :]
    hid, depth = down.shape[1:]
    wides = 2 * hid
    deep = depth + depth // 2
    for p in range(2):
        top = pair_ref[p * deep : p * deep + depth, :].astype(f32)
        gates[p * depth : (p + 1) * depth, 0, :] = top[:, :hid]
        gates[p * depth : (p + 1) * depth, 1, :] = top[:, hid:]
        for c in range(depth // wides):
            at = p * deep + depth + c * hid
            down[p, :, c * wides : (c + 1) * wides] = pair_ref[at : at + hid, :].astype(f32)
    wrows = shared_down.shape[0]
    part = shared_down.shape[1] // 2
    for p in range(2):
        top = pair_ref[2 * deep + p * wrows : 2 * deep + (p + 1) * wrows, :].astype(f32)
        shared_up[:, 0, p * part : (p + 1) * part] = top[:, :part]
        shared_up[:, 1, p * part : (p + 1) * part] = top[:, part:]
    shared_down[...] = pair_ref[2 * deep + 2 * wrows :, :].astype(f32)


def emit(args, inner, nstate, per, heads, kinds, hid):
    out, grad, _, _, _, main, pair = args
    tokens, quarter = grad.shape
    wrows = main.shape[0]
    depth = pair.shape[0] // 3 - wrows
    wide = pair.shape[1]
    flat = lambda *size: jax.ShapeDtypeStruct(size, f32)
    outs = [
        jax.ShapeDtypeStruct(out.shape, bf16), flat(tokens, quarter), flat(quarter // LANES, LANES),
        flat(wrows, 2, inner), flat(wrows, 2 * nstate), flat(heads, wrows), flat(CONV, inner),
        flat(CONV, 2 * nstate), flat(1, heads), flat(1, heads), flat(1, heads),
        flat(inner // LANES, LANES), flat(wrows, inner), flat(quarter // LANES, LANES), flat(kinds, wrows),
        flat(wrows, 2, wide), flat(wrows, wide), flat(2 * depth, 2, hid), flat(2, hid, depth),
    ]
    return pl.pallas_call(
        partial(emit_kernel, per=per),
        in_specs=[VMEM] * 7,
        out_specs=[VMEM] * len(outs),
        out_shape=outs,
        compiler_params=BIG,
        cost_estimate=cost(8),
        name="emit",
    )(*args)


def back_part(dout_ref, w_ref, mixer_ref, value_ref, act_ref, run_exp_ref, link_ref, gain_ref,
                scale, cross, through_ref, heads_ref, zgrad_ref, gated_ref, direct_ref, sums_ref,
                *, inner, nstate, di_all):
    mixer = mixer_ref[...]
    z = value_ref[HALO:, :inner]
    sig = sigmoid(z)
    act = z * sig
    gated = mixer * act
    grad = dot_rows(dout_ref[...], w_ref[...])
    gated_ref[...] = (gated * scale * gain_ref[...]).astype(bf16)
    sums_ref[0:1, :] = jnp.sum(grad * gated * scale, axis=0, keepdims=True)
    gated_grad = scale * (grad * gain_ref[...]) - gated * (scale * scale * scale * cross / di_all)
    zgrad_ref[...] = (gated_grad * mixer * (sig * (1.0 + z * (1.0 - sig)))).astype(bf16)
    heads = gated_grad * act
    heads_ref[...] = heads
    sums_ref[1:2, :] = jnp.sum(heads * act_ref[:, :inner].astype(f32), axis=0, keepdims=True)
    sums_ref[2:, :] = jnp.zeros((6, inner), f32)
    carried = (heads * (jnp.exp(run_exp_ref[...]) * link_ref[...])).astype(bf16)
    direct_ref[:inner, :] = dot_inner(carried, act_ref[:, inner + nstate :]).astype(bf16)
    direct_ref[inner:, :] = through_ref[...]


def intra_back_part(heads_ref, act_ref, scaled_ref, run_t_ref, run_exp_ref, seg_col_ref,
                      seg_row_ref, dscaled_ref, dstate_ref, drun_ref, scores_ref, dscores_ref, *, inner, nstate, per, block):
    tokens = act_ref.shape[0]
    keys = act_ref[:, inner : inner + nstate]
    query = act_ref[:, inner + nstate :]
    for start in range(0, tokens, block):
        stop = start + block
        scores_ref[start:stop, :stop] = masked_scores(
            query, keys, seg_col_ref, seg_row_ref, start, stop
        )
    dscores_ref[...] = jnp.zeros_like(dscores_ref)
    drun_ref[...] = jnp.zeros_like(drun_ref)

    def pair(i, _):
        columns = pl.ds(pl.multiple_of(i * LANES, LANES), LANES)
        scaled = scaled_ref[:, columns]
        heads = heads_ref[:, columns].astype(bf16)
        lane = col_iota(scaled.shape)
        run = run_exp_ref[:, columns]
        dscaled_ref[:, columns] = jnp.zeros((tokens, LANES), f32)
        for h in range(LANES // per):
            head = i * (LANES // per) + h
            mine = (lane >= h * per) & (lane < (h + 1) * per)
            vals = jnp.where(mine, scaled, jnp.zeros_like(scaled))
            grads = jnp.where(mine, heads, jnp.zeros_like(heads))
            pick = (col_iota((block, LANES)) == head).astype(bf16)
            for start in range(0, tokens, block):
                stop = start + block
                row = run_t_ref[head, :, :stop]
                decay = jnp.exp(jnp.minimum(run[start:stop, h * per : h * per + 1] - row, 0.0))
                weight = decay * scores_ref[start:stop, :stop]
                dweight = dot_outer(grads[start:stop], vals[:stop])
                dscores_ref[start:stop, :stop] += dweight * decay
                flow = (dweight * weight).astype(bf16)
                dscaled_ref[:stop, columns] += dot_inner(weight.astype(bf16), grads[start:stop])
                picks = jnp.broadcast_to(pick[:1], (stop, LANES))
                drun_ref[start:stop, :] += dot_rows(flow, picks)
                drun_ref[:stop, :] -= dot_inner(flow, pick)
        return 0

    lax.fori_loop(0, inner // LANES, pair, 0)
    dkeys = jnp.zeros((tokens, nstate), f32)
    dstate_ref[:, :nstate] = dkeys
    for start in range(0, tokens, block):
        stop = start + block
        shape = (block, stop)
        allowed = (row_iota(shape) + start >= col_iota(shape)) & (
            seg_col_ref[start:stop, :1] == seg_row_ref[:, :stop]
        )
        grad = jnp.where(allowed, dscores_ref[start:stop, :stop], 0.0).astype(bf16)
        dstate_ref[start:stop, nstate:] = dot_rows(grad, keys[:stop])
        dstate_ref[:stop, :nstate] += dot_inner(grad, query[start:stop])


def conv_back(value_ref, column, taps_ref, same_ref, dact, at, dtaps_ref, tokens):
    ext = tokens + HALO
    rows, total = conv_pre(value_ref, column, taps_ref, at, same_ref, tokens)
    sig = sigmoid(total)
    dpre = dact * (sig * (1.0 + total * (1.0 - sig)))
    drows = None
    for offset in range(CONV):
        first = HALO - CONV + 1 + offset
        kept = dpre * same_ref[offset]
        dtaps_ref[offset : offset + 1, pl.ds(at, LANES)] = jnp.sum(
            kept * rows[first : first + tokens], axis=0, keepdims=True
        )
        term = kept * taps_ref[offset : offset + 1, pl.ds(at, LANES)]
        after = ext - first - tokens
        pieces = [jnp.zeros((first, LANES), f32), term]
        if after:
            pieces.append(jnp.zeros((after, LANES), f32))
        term = jnp.concatenate(pieces, axis=0)
        drows = term if drows is None else drows + term
    return drows


def state_back_part(heads_ref, act_ref, step_ref, run_ref, run_exp_ref, link_ref, end_ref,
                      value_ref, taps_ref, same_ref, dstate_ref, in_ref, far_ref,
                      rows_ref, dtaps_ref, leaving_ref, kept_ref, dact_ref, *, inner, nstate, per):
    tokens = act_ref.shape[0]
    keys = act_ref[:, inner : inner + nstate]
    signal = act_ref[:, :inner].astype(f32)
    grow = expander(LANES, inner, per)
    running = run_ref[...]
    state_grad = join_states(far_ref, inner, per)
    lifted = (heads_ref[...] * (jnp.exp(run_exp_ref[...]) * link_ref[...])).astype(bf16)
    dact_ref[:, nstate:] = dot_rows(lifted, in_ref[...].astype(bf16)) + dstate_ref[:, nstate:]
    toward = jnp.exp(running[tokens - 1 :] - running) * end_ref[...]
    toward_exp = spread_lanes(toward, grow)
    pushed = (signal * spread_lanes(step_ref[...] * toward, grow)).astype(bf16)
    leaving_ref[...] = dot_outer(keys, state_grad.astype(bf16)) * toward_exp
    dact_ref[:, :nstate] = dot_rows(pushed, state_grad.astype(bf16)) + dstate_ref[:, :nstate]
    kept = jnp.sum(in_ref[...] * state_grad, axis=1, keepdims=True)
    kept = jnp.sum(head_fold(inner, LANES, per) * kept, axis=0, keepdims=True)
    kept = kept * jnp.exp(running[tokens - 1 :]) * link_ref[tokens - 1 :]
    kept_ref[...] = jnp.broadcast_to(kept, kept_ref.shape)

    def conv(i, _):
        at = pl.multiple_of(i * LANES, LANES)
        drows = conv_back(value_ref, 2 * inner + at, taps_ref, same_ref, dact_ref[:, pl.ds(at, LANES)],
                          inner + at, dtaps_ref, tokens)
        rows_ref[:, pl.ds(at, LANES)] = drows.astype(bf16)
        return 0

    lax.fori_loop(0, 2 * nstate // LANES, conv, 0)


def signal_back_part(heads_ref, act_ref, step_ref, value_ref, taps_ref, same_ref, bias_ref,
                       decay_ref, skip_ref, mixer_ref, inner_ref, dscaled_ref, drun_ref, leaving_ref,
                       kept_ref, zgrad_ref, state_ref,
                       grad_ref, dtaps_ref, small_ref, dact_ref, middle, between, *, inner, nstate, per):
    tokens = act_ref.shape[0]
    signal = act_ref[:, :inner].astype(f32)
    grow = expander(LANES, inner, per)
    folds = head_fold(inner, LANES, per).astype(bf16)
    step = step_ref[...]
    heads = heads_ref[...]
    leaving = leaving_ref[...]
    step_exp = spread_lanes(step, grow)
    dscaled = dscaled_ref[...] + leaving
    dact_ref[...] = dscaled * step_exp + skip_ref[...] * heads

    def conv(i, _):
        at = pl.multiple_of(i * LANES, LANES)
        drows = conv_back(value_ref, inner + at, taps_ref, same_ref, dact_ref[:, pl.ds(at, LANES)], at,
                          dtaps_ref, tokens)
        grad_ref[:, pl.ds(inner + at, LANES)] = drows.astype(bf16)
        return 0

    half = inner // LANES // 2
    lax.fori_loop(0, half, conv, 0)
    middle()
    lax.fori_loop(half, inner // LANES, conv, 0)
    between()
    carried = mixer_ref[...] - inner_ref[...] - skip_ref[...] * signal
    tri = (row_iota((tokens, tokens)) <= col_iota((tokens, tokens))).astype(bf16)
    strict = (row_iota((tokens, tokens)) > col_iota((tokens, tokens))).astype(bf16)
    back_sum = drun_ref[...] + fold_heads(heads * carried, folds)
    front_sum = fold_heads(signal * step_exp * leaving, folds)
    dlog = left_sums(tri, back_sum) + left_sums(strict, front_sum) + kept_ref[0:1, :]
    rate = -jnp.exp(decay_ref[...])
    dstep = dlog * rate + fold_heads(dscaled * signal, folds)
    draw = dstep * sigmoid(value_ref[HALO:, 2 * inner + 2 * nstate :] + bias_ref[...])
    small_ref[0:1, :] = jnp.sum(draw, axis=0, keepdims=True)
    small_ref[1:2, :] = jnp.sum(dlog * step, axis=0, keepdims=True) * rate
    small_ref[2:, :] = jnp.zeros((6, LANES), f32)
    state_at = 2 * inner
    step_at = state_at + 2 * nstate
    grad_ref[:HALO, :inner] = jnp.zeros((HALO, inner), bf16)
    grad_ref[HALO:, :inner] = zgrad_ref[...]
    grad_ref[:, state_at:step_at] = state_ref[...]
    grad_ref[:HALO, step_at:] = jnp.zeros((HALO, LANES), bf16)
    used = col_iota((tokens, LANES)) < inner // per
    grad_ref[HALO:, step_at:] = jnp.where(used, draw, 0.0).astype(bf16)


def rear_kernel(dout_ref, stat_ref, notes_ref, mixer_ref, inner_ref, act_ref, scaled_ref, step_ref,
                run_ref, run_exp_ref, state_ref, taps_ref, same_ref, bias_ref, decay_ref, skip_ref,
                gain_ref, end_ref, link_ref, seg_col_ref, seg_row_ref, packed_ref, mixed_t_ref,
                part_hbm, value_hbm, w_hbm, res_hbm,
                grad_ref, main_ref, dtaps_ref, sums_ref, small_ref, state_all_ref, out_ref,
                gated_ref, value_ref, w_ref, res_ref, run_t_ref, heads_ref, zgrad_ref, direct_ref, dscaled_ref,
                dstate_ref, drun_ref, scores_ref, dscores_ref, leaving_ref, kept_ref, rows_ref, dact_ref,
                far_ref, part_ref, right_box, left_box, rows_box, sum_box, ext_ref, state_halo, signal_halo,
                local_sem, stage_ref, *sems,
                inner, nstate, per, heads, di_all, n, boxes):
    me = lax.axis_index("tensor")
    weights = WeightSum(stage_ref, sems[:boxes])
    sems = sems[boxes:]
    tokens = act_ref.shape[0]
    quarter = part_ref.shape[1] // n
    own = tokens // n
    wide = value_ref.shape[1]
    groups = [(sems[2 * i], sems[2 * i + 1]) for i in range(4)]
    column = lambda k: pl.ds(pl.multiple_of(k * quarter, LANES), quarter)
    loads = [
        pltpu.make_async_copy(part_hbm, part_ref, local_sem.at[3]),
        pltpu.make_async_copy(w_hbm.at[:, pl.ds(wide, inner)], w_ref, local_sem.at[0]),
        pltpu.make_async_copy(value_hbm, value_ref, local_sem.at[1]),
        pltpu.make_async_copy(res_hbm.at[:, column(me)], res_ref, local_sem.at[2]),
    ]
    for copy in loads:
        copy.start()
    far_ref[...] = jnp.zeros_like(far_ref)
    state_halo[...] = jnp.zeros_like(state_halo)
    signal_halo[...] = jnp.zeros_like(signal_halo)
    rows_barrier(me, n)
    line = LineReduce(me, n, lambda d: part_ref.at[:, column(d)], right_box, left_box,
                      line_groups(sems[8:12]))
    loads[0].wait()
    line.step(0)
    for copy in loads[1:]:
        copy.wait()
    scale = row_columns(stat_ref[0:1, :])
    gates = notes_ref.shape[0] - 8
    cross = row_columns(notes_ref[gates : gates + 1, :])
    back_part(dout_ref, w_ref, mixer_ref, value_ref, act_ref, run_exp_ref, link_ref, gain_ref,
              scale, cross, packed_ref, heads_ref, zgrad_ref, gated_ref, direct_ref, sums_ref,
              inner=inner, nstate=nstate, di_all=di_all)
    states = StatePush(direct_ref, far_ref, groups[0], True)
    states.start()
    line.step(1)
    weights.product(dout_ref, gated_ref, 0, False)
    weights.to_sibling(0, inner)
    weights.product(mixed_t_ref, zgrad_ref, inner)
    weights.to_sibling(inner, inner)
    run_t = run_ref[...].T
    for h in range(heads):
        run_t_ref[h] = run_t[h : h + 1, :]
    intra_back_part(heads_ref, act_ref, scaled_ref, run_t_ref, run_exp_ref, seg_col_ref, seg_row_ref,
                    dscaled_ref, dstate_ref, drun_ref, scores_ref, dscores_ref,
                    inner=inner, nstate=nstate, per=per, block=128)
    line.step(2)
    weights.pair(0, main_ref)
    states.wait_recv()
    state_back_part(heads_ref, act_ref, step_ref, run_ref, run_exp_ref, link_ref, end_ref, value_ref,
                    taps_ref, same_ref, dstate_ref, state_ref, far_ref, rows_ref, dtaps_ref,
                    leaving_ref, kept_ref, dact_ref.at[:, pl.ds(0, 2 * nstate)],
                    inner=inner, nstate=nstate, per=per)
    body = lambda d: pl.ds(pl.multiple_of(HALO + d * own, 16), own)
    reduces, gathers = [], []
    place, count = ctx_place()
    sends, gets = place > 0, place < count - 1
    before = ctx_peer(jnp.maximum(place - 1, 0))
    state_copy = push(rows_ref.at[pl.ds(0, HALO)], state_halo, groups[2], 0, before)
    signal_copy = push(ext_ref.at[pl.ds(0, HALO), pl.ds(inner, inner)], signal_halo, groups[2], 1, before)
    pl.when(sends)(state_copy.start)

    weights.pair(1, main_ref)

    def middle():
        pl.when(gets)(state_copy.wait_recv)
        rows_ref[tokens:, :] = rows_ref[tokens:, :] + state_halo[...]
        for d in range(1, n):
            peer = lax.rem(me + d, n)
            reduces.append(push(rows_ref.at[body(peer)], rows_box.at[d - 1], groups[1], d - 1, peer))
            reduces[-1].start()

    def between():
        pl.when(sends)(signal_copy.start)
        total = rows_ref[body(me), :].astype(f32)
        for copy in reduces:
            copy.wait_recv()
        for d in range(1, n):
            total = total + rows_box[d - 1].astype(f32)
        sum_box[body(me), :] = total.astype(bf16)
        for d in range(1, n):
            peer = lax.rem(me + d, n)
            gathers.append(push(sum_box.at[body(me)], sum_box.at[body(me)], groups[3], d - 1, peer))
            gathers[-1].start()

    signal_back_part(heads_ref, act_ref, step_ref, value_ref, taps_ref, same_ref, bias_ref, decay_ref,
                     skip_ref, mixer_ref, inner_ref, dscaled_ref, drun_ref, leaving_ref, kept_ref,
                     zgrad_ref, rows_ref, ext_ref, dtaps_ref, small_ref, dact_ref, middle, between,
                     inner=inner, nstate=nstate, per=per)
    grad_ref[...] = ext_ref[HALO:, :]
    pl.when(gets)(signal_copy.wait_recv)
    grad_ref[tokens - HALO :, inner : 2 * inner] = (
        ext_ref[tokens:, inner : 2 * inner] + signal_halo[...]
    )
    for t in range(3, n):
        line.step(t)
    out_ref[...] = (line.total() + res_ref[...].astype(f32)).astype(bf16)
    for copy in gathers:
        copy.wait_recv()
    state_all_ref[...] = sum_box[HALO:, :]
    weights.wait_send()
    states.wait_send()
    line.wait_send()
    pl.when(sends)(state_copy.wait_send)
    pl.when(sends)(signal_copy.wait_send)
    for copy in reduces + gathers:
        copy.wait_send()


def rear(vmem_args, part, value, weights, residual, inner, nstate, per, heads, di_all):
    n = lax.axis_size("tensor")
    others = lax.axis_size(CTX) - 1
    ext, wide = value.shape
    tokens = ext - HALO
    depth = residual.shape[1]
    quarter = depth // n
    boxes, main = weight_boxes(depth, 2 * inner, 2, False)
    shape = jax.ShapeDtypeStruct
    outs = [
        shape((tokens, wide), bf16), main, shape((CONV, inner + 2 * nstate), f32),
        shape((8, inner), f32), shape((8, LANES), f32), shape((tokens, 2 * nstate), bf16),
        shape((tokens, quarter), bf16),
    ]
    dma = pltpu.SemaphoreType.DMA
    return pl.pallas_call(
        partial(rear_kernel, inner=inner, nstate=nstate, per=per, heads=heads, di_all=di_all, n=n,
                boxes=len(boxes) - 1),
        in_specs=[VMEM] * len(vmem_args) + [HBM] * 4,
        out_specs=[VMEM] * len(outs),
        out_shape=outs,
        scratch_shapes=[
            pltpu.VMEM((tokens, inner), bf16),
            pltpu.VMEM((ext, wide), f32), pltpu.VMEM((depth, inner), bf16),
            pltpu.VMEM((tokens, quarter), bf16), pltpu.VMEM((heads, 1, tokens), f32),
            pltpu.VMEM((tokens, inner), f32), pltpu.VMEM((tokens, inner), bf16),
            pltpu.VMEM((inner + 16, nstate), bf16), pltpu.VMEM((tokens, inner), f32),
            pltpu.VMEM((tokens, 2 * nstate), f32), pltpu.VMEM((tokens, LANES), f32),
            pltpu.VMEM((tokens, tokens), f32), pltpu.VMEM((tokens, tokens), f32),
            pltpu.VMEM((tokens, inner), f32), pltpu.VMEM((8, LANES), f32),
            pltpu.VMEM((ext, 2 * nstate), bf16), pltpu.VMEM((tokens, inner), f32),
            pltpu.VMEM((others, inner + 16, nstate), bf16),
            pltpu.VMEM((tokens, depth), bf16),
            pltpu.VMEM((n, tokens, quarter), bf16), pltpu.VMEM((n, tokens, quarter), bf16),
            pltpu.VMEM((n - 1, tokens // n, 2 * nstate), bf16),
            pltpu.VMEM((ext, 2 * nstate), bf16), pltpu.VMEM((ext, wide), bf16),
            pltpu.VMEM((HALO, 2 * nstate), bf16), pltpu.VMEM((HALO, inner), bf16),
            dma((4,)),
        ] + boxes + [
            dma((others,)), dma((others,)), dma((n - 1,)), dma((n - 1,)), dma((2,)), dma((2,)),
            dma((n - 1,)), dma((n - 1,)),
        ] + line_sems(n),
        compiler_params=pltpu.CompilerParams(
            vmem_limit_bytes=63 << 20, collective_id=5, has_side_effects=True
        ),
        cost_estimate=cost(50),
        name="rear",
    )(*vmem_args, part, value, weights, residual)


def swiglu(first, second):
    sig = sigmoid(first)
    act = first * sig
    return act, sig * (1.0 + first * (1.0 - sig)), (act * second).astype(bf16)


def experts_kernel(res_ref, cot_ref, gain_ref, chosen_ref, router_ref, w_ref, shared_hbm,
                   gates_ref, dgate_t_ref, out_hbm, dmix_hbm, mix_t_hbm, dw_hbm,
                   mix_ref, mix_t_ref, dgate_ref, total_ref, grads_ref, down_ref, hidden_ref, dval_ref,
                   grad_ref, shared_ref, first_ref, second_ref, result_ref, local_sem, *remote,
                   tile, senders, core):
    step = pl.program_id(0)
    last = step == pl.num_programs(0) - 1
    rows, depth = mix_ref.shape
    place = row_place()
    far_send, far_receive, near_send, near_receive, keep_sem, *remote = remote
    gather = RowGather(shared_hbm, shared_ref, ((far_send, far_receive), (near_send, near_receive)))
    own_copy = pltpu.make_async_copy(shared_hbm, shared_ref.at[place], local_sem.at[0])
    mix_copy = pltpu.make_async_copy(mix_t_ref, mix_t_hbm, local_sem.at[1])
    if core == 2:
        inbox, shared_in, send, receive, pair_sem = remote
        me = lax.axis_index("core")
        slot = lax.rem(step + me, 2)
        pair_copy = lambda k: push(grad_ref.at[1], inbox.at[k], (send, receive), k, {"core": 1 - me})
        keep_copy = lambda k: pltpu.make_async_copy(
            inbox.at[k], dw_hbm.at[k, pl.ds(0, 3 * depth)], pair_sem.at[k]
        )
    else:
        slot = 0

    @pl.when(step == 0)
    def _():
        own_copy.start()
        barrier = pltpu.get_barrier_semaphore()
        cy, chips = lax.axis_size("cy"), lax.axis_size(CHIPS)
        chip = lax.axis_index("shard") * cy + lax.axis_index("cy")
        for d in range(1, chips):
            peer = lax.rem(chip + d, chips)
            pl.semaphore_signal(barrier, inc=1, device_id={"shard": peer // cy, "cy": lax.rem(peer, cy)},
                                device_id_type=MESH)
        if core == 2:
            pl.semaphore_signal(barrier, inc=1, device_id={"core": 1 - me}, device_id_type=MESH)
        pl.semaphore_wait(barrier, chips - 1 + core - 1)
        gather.start()
        res = res_ref[...].astype(f32)
        scale = lax.rsqrt(jnp.mean(res * res, axis=1, keepdims=True) + epsilon)
        mix = (res * scale * gain_ref[...]).astype(bf16)
        mix_ref[...] = mix
        mix_t_ref[...] = mix.T
        mix_copy.start()
        chosen = chosen_ref[...] > 0.0
        logits = dot_rows(mix, router_ref[...])
        top = jnp.max(jnp.where(chosen, logits, -1e30), axis=1, keepdims=True)
        weight = jnp.where(chosen, jnp.exp(jnp.where(chosen, logits - top, 0.0)), 0.0)
        gates_ref[...] = weight / jnp.sum(weight, axis=1, keepdims=True)
        total_ref[...] = jnp.zeros_like(total_ref)
        grads_ref[...] = jnp.zeros_like(grads_ref)
        dgate_ref[...] = jnp.zeros_like(dgate_ref)
        own_copy.wait()

    if core == 2:
        @pl.when((step >= 2) & (step < senders) & (slot == 1))
        def _():
            pair_copy((step - 2) // 2).wait_send()

    @pl.when(step < senders)
    def _():
        pair_grads(
            step, slot, mix_ref, mix_t_ref, cot_ref, gates_ref, w_ref, dgate_ref, total_ref, grads_ref,
            down_ref, hidden_ref, dval_ref, grad_ref, tile
        )

    @pl.when(step == 1)
    def _():
        gather.relay()
        mix_copy.wait()

    @pl.when(step == 2)
    def _():
        gather.finish()

    if core == 2:
        @pl.when((step < senders) & (slot == 1))
        def _():
            pair_copy(step // 2).start()

        @pl.when((step >= 1) & (slot == 1))
        def _():
            at = (step - 1) // 2
            pair_copy(at).wait_recv()
            inbox[at] = grad_ref[0] + inbox[at]
            keep_copy(at).start()

        @pl.when(last)
        def _():
            pair_copy(senders // 2 - 1).wait_send()
    else:
        @pl.when(step < senders)
        def _():
            copy = pltpu.make_async_copy(
                grad_ref.at[0], dw_hbm.at[step, pl.ds(0, 3 * depth)], local_sem.at[3]
            )
            copy.start()
            copy.wait()

    @pl.when(last)
    def _():
        wide = w_ref.shape[2]
        hid = wide // 2
        wrows = depth // senders
        for p in range(2):
            first_ref[p] = shared_ref[:, p * wrows : (p + 1) * wrows, :].reshape(depth, wide)
        second_ref[...] = shared_ref[:, 2 * wrows :, :].reshape(depth, wide)
        raw = dot_rows(cot_ref[...], second_ref[...])
        for p in range(2):
            value = dot_rows(mix_ref[...], first_ref[p])
            act, slope, hidden = swiglu(value[:, :hid], value[:, hid:])
            dh = raw[:, p * hid : (p + 1) * hid]
            dval_ref[p, :, :hid] = (dh * value[:, hid:] * slope).astype(bf16)
            dval_ref[p, :, hid:] = (dh * act).astype(bf16)
            hidden_ref[:, p * hid : (p + 1) * hid] = hidden
        result_ref[...] = (
            total_ref[...] + dot_outer(hidden_ref[...], second_ref[...])
        ).astype(bf16)
        out_copy = pltpu.make_async_copy(result_ref, out_hbm, local_sem.at[2])
        out_copy.start()
        gates = gates_ref[...]
        dgate = dgate_ref[...]
        inside = jnp.sum(gates * dgate, axis=1, keepdims=True)
        dlogits = (gates * (dgate - inside)).astype(bf16)
        dmix = grads_ref[...] + dot_outer(dlogits, router_ref[...])
        for p in range(2):
            dmix = dmix + dot_outer(dval_ref[p], first_ref[p])
        dgate_t_ref[...] = dgate.T[: dgate_t_ref.shape[0], :]
        for k in range(3):
            if k < 2:
                grad = dot_rows(mix_t_ref[...], dval_ref[k]).astype(bf16)
            else:
                grad = dot_inner(cot_ref[...], hidden_ref[...]).astype(bf16)
            for j in range(senders):
                at = (3 * ((j % core) * (senders // core) + j // core) + k) * wrows
                grad_ref[0, at : at + wrows, :] = grad[j * wrows : (j + 1) * wrows]
        span = 3 * depth // core
        part = 3 * wrows
        if core == 2:
            mine = pl.ds(pl.multiple_of(me * span, 16), span)
            theirs = pl.ds(pl.multiple_of((1 - me) * span, 16), span)
            shared_copy = push(grad_ref.at[0, theirs], shared_in, (send, receive), senders // 2,
                               {"core": 1 - me})
            shared_copy.start()
        mix_ref[...] = dmix.astype(bf16)
        dmix_copy = pltpu.make_async_copy(mix_ref, dmix_hbm, local_sem.at[4])
        dmix_copy.start()
        copies = [out_copy, dmix_copy]
        source = grad_ref.at[0]
        if core == 2:
            shared_copy.wait_recv()
            shared_in[...] = shared_in[...] + grad_ref[0, mine, :]
            source = shared_in
        kept = senders // core
        for j in range(kept):
            copies.append(pltpu.make_async_copy(
                source.at[pl.ds(j * part, part)], dw_hbm.at[j, pl.ds(3 * depth, part)], keep_sem.at[j]
            ))
            copies[-1].start()
        for copy in copies:
            copy.wait()
        if core == 2:
            for k in range(kept):
                keep_copy(k).wait()
            shared_copy.wait_send()


def pair_grads(step, slot, mix_ref, mix_t_ref, cot_ref, gates_ref, w_ref, dgate_ref, total_ref, grads_ref,
               down_ref, hidden_ref, dval_ref, grad_ref, tile):
    rows, depth = mix_ref.shape
    wide = w_ref.shape[2]
    hid = wide // 2
    chunks = depth // wide
    deep = depth + depth // 2
    for p in range(2):
        for c in range(chunks):
            down_ref[p * hid : (p + 1) * hid, c * wide : (c + 1) * wide] = (
                w_ref[0, p * deep + depth + c * hid : p * deep + depth + (c + 1) * hid, :]
            )
    down = down_ref[...]

    def part(i, _):
        at = pl.ds(pl.multiple_of(i * tile, tile), tile)
        mix = mix_ref[at, :]
        raw = dot_outer(cot_ref[at, :], down)
        gates = gates_ref[at, :]
        lane = col_iota(gates.shape)
        dmix, noted = None, jnp.zeros_like(gates)
        for p in range(2):
            here = lane == 2 * step + p
            gate = jnp.sum(jnp.where(here, gates, 0.0), axis=1, keepdims=True)
            weights = w_ref[0, p * deep : p * deep + depth, :]
            value = dot_rows(mix, weights)
            act, slope, hidden = swiglu(value[:, :hid], value[:, hid:])
            hidden = hidden.astype(f32)
            dh = raw[:, p * hid : (p + 1) * hid]
            noted = noted + jnp.where(here, jnp.sum(hidden * dh, axis=1, keepdims=True), 0.0)
            dh = gate * dh
            dval_ref[p, at, :hid] = (dh * value[:, hid:] * slope).astype(bf16)
            dval_ref[p, at, hid:] = (dh * act).astype(bf16)
            hidden_ref[at, p * hid : (p + 1) * hid] = (gate * hidden).astype(bf16)
            term = dot_outer(dval_ref[p, at, :], weights)
            dmix = term if dmix is None else dmix + term
        dgate_ref[at, :] += noted
        total_ref[at, :] += dot_rows(hidden_ref[at, :], down)
        grads_ref[at, :] += dmix
        return 0

    lax.fori_loop(0, rows // tile, part, 0)
    for c in range(chunks):
        grad = dot_inner(hidden_ref[...], cot_ref[:, c * wide : (c + 1) * wide]).astype(bf16)
        for p in range(2):
            first = p * deep + depth + c * hid
            grad_ref[slot, first : first + hid, :] = grad[p * hid : (p + 1) * hid]
    for p in range(2):
        grad_ref[slot, p * deep : p * deep + depth, :] = (
            dot_rows(mix_t_ref[...], dval_ref[p]).astype(bf16)
        )


def experts(residual, cot, gain, chosen, weights, router_at, experts_w, shared):
    senders, deep, wide = experts_w.shape
    rows, depth = residual.shape
    core, chips = lax.axis_size("core"), lax.axis_size(CHIPS)
    kept = senders // core
    kinds = 2 * senders + -2 * senders % 8
    shape = jax.ShapeDtypeStruct
    dma = pltpu.SemaphoreType.DMA
    once = lambda a: pl.BlockSpec(a.shape, lambda i: (0,) * a.ndim, pipeline_mode=pl.Buffered(1))
    outs = [shape((rows, LANES), f32), shape((kinds, rows), f32)]
    remote = []
    if core == 2:
        remote = [pltpu.VMEM((kept, deep, wide), bf16), pltpu.VMEM((deep // 2, wide), bf16),
                  dma((kept + 1,)), dma((kept + 1,)), dma((kept,))]
    return pl.pallas_call(
        partial(experts_kernel, tile=rows, senders=senders, core=core),
        grid=(senders + 1,),
        in_specs=[once(residual), once(cot), once(gain), once(chosen),
                  pl.BlockSpec((depth, LANES), lambda i: (0, router_at // LANES)),
                  pl.BlockSpec((1, deep, wide), lambda i: (jnp.minimum(i, senders - 1), 0, 0)), HBM],
        out_specs=[whole(o) for o in outs] + [HBM] * 4,
        out_shape=outs + [
            shape((rows, depth), bf16), shape((rows, depth), bf16), shape((depth, rows), bf16),
            shape((kept, deep + shared.shape[0], wide), bf16),
        ],
        scratch_shapes=[
            pltpu.VMEM((rows, depth), bf16), pltpu.VMEM((depth, rows), bf16), pltpu.VMEM((rows, LANES), f32),
            pltpu.VMEM((rows, depth), f32), pltpu.VMEM((rows, depth), f32),
            pltpu.VMEM((wide, depth), bf16), pltpu.VMEM((rows, wide), bf16),
            pltpu.VMEM((2, rows, wide), bf16), pltpu.VMEM((core, deep, wide), bf16),
            pltpu.VMEM((senders,) + shared.shape, bf16), pltpu.VMEM((2, depth, wide), bf16),
            pltpu.VMEM((depth, wide), bf16), pltpu.VMEM((rows, depth), bf16), dma((5,)),
            dma((max(chips - 1, 1),)), dma((max(chips - 1, 1),)), dma((chips,)), dma((chips,)),
            dma((kept,)),
        ] + remote,
        compiler_params=pltpu.CompilerParams(
            vmem_limit_bytes=63 << 20, collective_id=4, has_side_effects=True
        ),
        cost_estimate=cost(7 * senders),
        name="experts",
    )(residual, cot, gain, chosen, weights, experts_w, shared)


def local(
    block_input, gain_input, proj_main, proj_state, proj_step, conv_main, conv_state, step_bias,
    decay_log, skip_gain, gain_gate, proj_out, gain_mix, router_weight, shared_gates, shared_down,
    expert_gates, expert_down, segments, routes, cotangent,
):
    tokens, quarter = block_input.shape
    heads = step_bias.shape[0]
    inner = conv_main.shape[1]
    nstate = conv_state.shape[1] // 2
    per = inner // heads
    tensors = lax.axis_size("tensor")
    zi = lax.axis_index("tensor")
    senders = lax.axis_size(ROWS)
    depth = quarter * tensors
    di_all = inner * tensors
    own = tokens // tensors
    column = zi * quarter
    row0 = zi * own
    wrows = proj_main.shape[0]
    hid = expert_gates.shape[3]
    local_experts = expert_gates.shape[0]
    experts_all = local_experts * senders
    shared_here = shared_down.shape[1]
    router_pad = -experts_all % LANES

    main_wide = 2 * inner + 2 * nstate + LANES
    router_at = main_wide + inner
    weights = gather_rows(
        jnp.concatenate(
            [proj_main[:, 0], proj_main[:, 1], proj_state,
             jnp.pad(proj_step, ((0, 0), (0, LANES - heads))), proj_out,
             jnp.pad(router_weight, ((0, 0), (0, router_pad)))], axis=1
        )
    )
    pair_down = expert_down.reshape(local_experts, hid, depth // (2 * hid), 2 * hid)
    pair = jnp.concatenate(
        [expert_gates.reshape(local_experts, depth, 2 * hid),
         pair_down.transpose(0, 2, 1, 3).reshape(local_experts, -1, 2 * hid)], axis=1
    )
    shared_pair = shared_gates.reshape(wrows, 2, 2, shared_here // 2).transpose(2, 0, 1, 3)
    experts_w = gather_rows(pair.reshape(1, -1, 2 * hid))
    shared_local = jnp.concatenate([shared_pair.reshape(-1, shared_here), shared_down], axis=0)

    seg_row = segments[0]
    halo_seg = shifted(seg_row[tokens - CONV + 1 :], CTX, 1)
    gains = jnp.concatenate(
        [gain_input[None], gain_mix[None], jnp.zeros((14, quarter), bf16)], axis=0
    )
    mixed_ext, mixed_t, got, gain_rows = intake(block_input, gains)
    gain_row, gain_mid = gain_rows[0:1], gain_rows[1:2]

    segments_ext = jnp.concatenate([halo_seg, seg_row], axis=0)
    same = jnp.stack(
        [segments_ext[offset : offset + tokens] == seg_row for offset in range(CONV)]
    ).astype(f32)
    same = jnp.broadcast_to(same[:, :, None], (CONV, tokens, LANES))
    taps = jnp.concatenate([conv_main, conv_state], axis=1).astype(f32)
    lanes = lambda v: jnp.pad(v, (0, LANES - heads))[None]
    bias = lanes(step_bias)
    decay = lanes(decay_log)
    skip = jnp.repeat(skip_gain, per)[None]
    link = (seg_row == halo_seg[-1]).astype(f32)[:, None]
    at_end = (seg_row == seg_row[-1]).astype(f32)[:, None]
    seg_col = seg_row[:, None]
    seg_line = seg_row[None]
    gain_gate_f = gain_gate.astype(f32)[None, :]
    (value, act, scaled, step, running, run_exp, within, mixer, state_in, packed, residual, scale_rows,
     own_part, cot_full) = front(
        mixed_ext, taps, same, bias, decay, at_end, link, seg_col, seg_line, skip, gain_gate_f, got,
        cotangent, weights, inner, nstate, per, heads, di_all
    )

    chosen = jnp.any(
        routes[:, :, None] == jnp.arange(LANES, dtype=jnp.int32)[None, None, :], axis=1
    ).astype(f32)
    gates, dgate, out_part, dmix_part, mix_t, dw = experts(
        residual, cot_full, gain_mid, chosen, weights, router_at, experts_w, shared_local
    )
    expert_rows = scatter_chips(dw.reshape(-1, 2 * hid))
    dmixer, notes, gains_mid = turn_step(
        dmix_part, dgate, residual, cot_full, own_part, gain_mid
    )

    value_grad, rear_main, dtaps, sums, small_sums, state_all, output = rear(
        (dmixer, scale_rows, notes, mixer, within, act, scaled, step, running, run_exp, state_in, taps,
         same, bias, decay, skip, gain_gate_f, at_end, link, seg_col, seg_line, packed[inner:],
         mixed_t),
        out_part, value, weights, residual, inner, nstate, per, heads, di_all
    )
    first = 2 * inner
    last = first + 2 * nstate
    rear_main, expert_rows = lax.optimization_barrier((rear_main, expert_rows))
    rear_main = scatter_chips(rear_main)

    early = jnp.concatenate(
        [dtaps[:, :inner], sums[:2], jnp.pad(small_sums[:2], ((0, 0), (0, inner - LANES)))], axis=0
    )
    state_taps = jnp.pad(dtaps[:, inner:], ((0, 8 - CONV), (0, 0)))
    grad_input, early, late, main = last_step(
        (value_grad, got, dmixer, gain_row, gains_mid, state_taps, early, mixed_t, mix_t, state_all,
         gates, notes),
        weights, inner, last,
    )
    if lax.axis_size("core") != 2:
        main = scatter_chips(main)
    (output, grad_input, grad_gain_in, grad_main, grad_state, grad_step, grad_conv, grad_conv_state,
     grad_bias, grad_decay, grad_skip, grad_gate, grad_proj_out, grad_gain_mid, grad_router, grad_shared,
     grad_shared_down, grad_gates, grad_down) = emit(
        (output, grad_input, early, late, rear_main, main, expert_rows), inner, nstate, per, heads, experts_all, hid
    )
    return (
        output,
        grad_input,
        grad_gain_in.reshape(quarter),
        grad_main,
        grad_state,
        grad_step.T,
        grad_conv,
        grad_conv_state,
        grad_bias[0],
        grad_decay[0],
        grad_skip[0],
        grad_gate.reshape(inner),
        grad_proj_out,
        grad_gain_mid.reshape(quarter),
        grad_router.T,
        grad_shared,
        grad_shared_down,
        grad_gates.reshape(expert_gates.shape),
        grad_down,
    )


def solution(mesh):
    shard, ctx, tensor = (mesh.shape[name] for name in ("shard", "ctx", "tensor"))
    core = 2 if shard * ctx == 8 else 1
    split = jax.sharding.Mesh(
        mesh.devices.reshape(shard, ctx // core, core, tensor), ("shard", "cy", "core", "tensor")
    )
    return jax.shard_map(
        local,
        mesh=split,
        in_specs=(
            P(ROWS, "tensor"),
            P("tensor"),
            P(ROWS, None, "tensor"),
            P(ROWS, None),
            P(ROWS, "tensor"),
            P(None, "tensor"),
            P(),
            P("tensor"),
            P("tensor"),
            P("tensor"),
            P("tensor"),
            P(ROWS, "tensor"),
            P("tensor"),
            P(ROWS, None),
            P(ROWS, None, "tensor"),
            P(ROWS, "tensor"),
            P(ROWS, None, None, "tensor"),
            P(ROWS, "tensor", None),
            P("shard", CTX),
            P(ROWS, None),
            P(ROWS, "tensor"),
        ),
        out_specs=(
            P(ROWS, "tensor"),
            P(ROWS, "tensor"),
            P("tensor"),
            P(ROWS, None, "tensor"),
            P(ROWS, None),
            P(ROWS, "tensor"),
            P(None, "tensor"),
            P(),
            P("tensor"),
            P("tensor"),
            P("tensor"),
            P("tensor"),
            P(ROWS, "tensor"),
            P("tensor"),
            P(ROWS, None),
            P(ROWS, None, "tensor"),
            P(ROWS, "tensor"),
            P(ROWS, None, None, "tensor"),
            P(ROWS, "tensor", None),
        ),
        check_vma=False,
    )
```

```python
from functools import partial

import jax
import jax.numpy as jnp
from jax import lax
from jax.experimental import pallas as pl
from jax.experimental.pallas import tpu as pltpu
from jax.sharding import PartitionSpec as P

CONV = 4
HALO = 16
LANES = 128
LANES = 128
LANES = 128


epsilon = 1e-05
highest = lax.Precision.HIGHEST
CTX = ("cy", "core")
CHIPS = ("shard", "cy")
ROWS = ("shard", "cy", "core")
f32 = jnp.float32
MESH = pl.DeviceIdType.MESH
bf16 = jnp.bfloat16
BIG = pltpu.CompilerParams(vmem_limit_bytes=60 << 20)


def cost(micros):
    return pl.CostEstimate(flops=micros * 900_000_000, transcendentals=0, bytes_accessed=1 << 20)
BIG = pltpu.CompilerParams(vmem_limit_bytes=60 << 20)


def cost(micros):
    return pl.CostEstimate(flops=micros * 900_000_000, transcendentals=0, bytes_accessed=1 << 20)
BIG = pltpu.CompilerParams(vmem_limit_bytes=60 << 20)


def cost(micros):
    return pl.CostEstimate(flops=micros * 900_000_000, transcendentals=0, bytes_accessed=1 << 20)


def shifted(value, axis, steps):
    count = lax.axis_size(axis)
    leading, last = (max(0, -steps), min(count, count - steps))
    return lax.ppermute(value, axis, [(source, source + steps) for source in range(leading, last)])


def dot_rows(left, right, precision=None):
    return jnp.dot(left, right, preferred_element_type=f32, precision=precision)


def dot_inner(left, right):
    return lax.dot_general(left, right, (((0,), (0,)), ((), ())), preferred_element_type=f32)


def dot_outer(left, right):
    return lax.dot_general(left, right, (((1,), (1,)), ((), ())), preferred_element_type=f32)


def sigmoid(value):
    return 1.0 / (1.0 + jnp.exp(-value))


def gather_rows(value):
    return lax.all_gather(value, ROWS, axis=0, tiled=True)


def scatter_rows(value):
    return lax.psum_scatter(value, ROWS, scatter_dimension=0, tiled=True)


def scatter_chips(value):
    axes = CHIPS if lax.axis_size("core") == 2 else ROWS
    return lax.psum_scatter(value, axes, scatter_dimension=0, tiled=True)


def exchange(blocks):
    return lax.all_to_all(blocks, "tensor", split_axis=0, concat_axis=0, tiled=True)


def spread(block):
    count = lax.axis_size("tensor")
    return exchange(jnp.broadcast_to(block[None], (count,) + block.shape))


def spread_small(block):
    count, index = lax.axis_size("tensor"), lax.axis_index("tensor")
    width = block.shape[1]
    full = jnp.zeros((block.shape[0], count * width), block.dtype)
    for away in range(count):
        moved = block if away == 0 else lax.ppermute(
            block, "tensor", [(i, (i + away) % count) for i in range(count)]
        )
        origin = lax.rem(index - away + count, count)
        full = lax.dynamic_update_slice_in_dim(full, moved, origin * width, 1)
    return full


def halves(value):
    high = value.astype(bf16)
    return high, (value - high.astype(f32)).astype(bf16)


def far_states(packed, reverse):
    count = lax.axis_size(CTX)
    return jnp.stack([
        shifted(packed, CTX, -away if reverse else away) for away in range(1, count)
    ])


def row_iota(shape):
    return lax.broadcasted_iota(jnp.int32, shape, 0)


def col_iota(shape):
    return lax.broadcasted_iota(jnp.int32, shape, 1)


def expander(lanes, width, per):
    low = row_iota((lanes, width)) * per
    at = col_iota((lanes, width))
    return ((at >= low) & (at < low + per)).astype(f32)


def head_fold(width, lanes, per):
    low = col_iota((width, lanes)) * per
    at = row_iota((width, lanes))
    return ((at >= low) & (at < low + per)).astype(f32)


def pack_state(state, through):
    high, low = halves(through)
    row = row_iota((16, LANES))
    tail = jnp.where(row == 0, high.astype(f32), jnp.where(row == 1, low.astype(f32), 0.0))
    return jnp.concatenate([state, tail], axis=0).astype(bf16)


def join_states(far_ref, inner, per):
    spread_heads = head_fold(inner, LANES, per)
    total = None
    for k in reversed(range(far_ref.shape[0])):
        state = far_ref[k, :inner, :].astype(f32)
        if total is not None:
            through = far_ref[k, inner : inner + 16, :].astype(f32)
            through = through[0:1] + through[1:2]
            state = state + jnp.sum(spread_heads * through, axis=1, keepdims=True) * total
        total = state
    return total


def thirds(value):
    high = value.astype(bf16)
    rest = value - high.astype(f32)
    middle = rest.astype(bf16)
    return high, middle, (rest - middle.astype(f32)).astype(bf16)


def spread_lanes(value, grow):
    ones = grow.astype(bf16)
    return sum(dot_rows(part, ones) for part in thirds(value))


def left_sums(zero_one, value):
    return sum(dot_rows(zero_one, part) for part in thirds(value))


def fold_heads(value, folds):
    high, low = halves(value)
    return dot_rows(high, folds) + dot_rows(low, folds)


def conv_pre(value_ref, column, taps_ref, taps_column, same_ref, tokens):
    rows = value_ref[:, pl.ds(column, LANES)]
    total = None
    for offset in range(CONV):
        first = HALO - CONV + 1 + offset
        term = rows[first : first + tokens] * (
            same_ref[offset] * taps_ref[offset : offset + 1, pl.ds(taps_column, LANES)]
        )
        total = term if total is None else total + term
    return rows, total


def enter_part(mixed_ref, w_ref, taps_ref, same_ref, bias_ref, decay_ref, end_ref, link_ref,
                 value_ref, act_ref, scaled_ref, step_ref, run_ref, run_exp_ref,
                 state_ref, *, inner, nstate, per):
    tokens = act_ref.shape[0]
    width = 2 * inner + 2 * nstate + LANES
    tile = 384

    def matmul(i, _):
        columns = pl.ds(pl.multiple_of(i * tile, LANES), tile)
        value_ref[:, columns] = dot_rows(mixed_ref[...], w_ref[:, columns])
        return 0

    lax.fori_loop(0, width // tile, matmul, 0)

    def conv(i, _):
        at = pl.multiple_of(i * LANES, LANES)
        _, total = conv_pre(value_ref, inner + at, taps_ref, at, same_ref, tokens)
        act_ref[:, pl.ds(at, LANES)] = (total * sigmoid(total)).astype(bf16)
        return 0

    lax.fori_loop(0, (inner + 2 * nstate) // LANES, conv, 0)
    raw = value_ref[HALO:, 2 * inner + 2 * nstate :] + bias_ref[...]
    step = jnp.maximum(raw, 0.0) + jnp.log1p(jnp.exp(-jnp.abs(raw)))
    log_decay = step * -jnp.exp(decay_ref[...])
    tri = (row_iota((tokens, tokens)) >= col_iota((tokens, tokens))).astype(bf16)
    running = left_sums(tri, log_decay)
    step_ref[...] = step
    run_ref[...] = running
    grow = expander(LANES, inner, per)
    run_exp_ref[...] = spread_lanes(running, grow)
    signal = act_ref[:, :inner].astype(f32)
    scaled_ref[...] = (signal * spread_lanes(step, grow)).astype(bf16)
    toward = step * jnp.exp(running[tokens - 1 :] - running) * end_ref[...]
    pushed = (signal * spread_lanes(toward, grow)).astype(bf16)
    through = jnp.exp(running[tokens - 1 :]) * link_ref[tokens - 1 :]
    state_ref[...] = pack_state(dot_inner(pushed, act_ref[:, inner : inner + nstate]), through)


def whole(a):
    return pl.BlockSpec(a.shape, lambda i: (0,) * len(a.shape))


def columns(a, width, at=0):
    assert at % width == 0
    return pl.BlockSpec((a.shape[0], width), lambda i: (0, at // width))


def masked_scores(query, keys, seg_col_ref, seg_row_ref, start, stop):
    shape = (stop - start, stop)
    allowed = (row_iota(shape) + start >= col_iota(shape)) & (
        seg_col_ref[start:stop, :1] == seg_row_ref[:, :stop]
    )
    return jnp.where(allowed, dot_outer(query[start:stop], keys[:stop]), 0.0)


def intra_part(act_ref, scaled_ref, run_t_ref, run_exp_ref, seg_col_ref, seg_row_ref,
                 inner_ref, scores_ref, *, inner, nstate, per, block):
    tokens = act_ref.shape[0]
    keys = act_ref[:, inner : inner + nstate]
    query = act_ref[:, inner + nstate :]
    for start in range(0, tokens, block):
        stop = start + block
        scores_ref[start:stop, :stop] = masked_scores(
            query, keys, seg_col_ref, seg_row_ref, start, stop
        )

    def pair(i, _):
        columns = pl.ds(pl.multiple_of(i * LANES, LANES), LANES)
        scaled = scaled_ref[:, columns]
        lane = col_iota(scaled.shape)
        run = run_exp_ref[:, columns]
        for start in range(0, tokens, block):
            stop = start + block
            total = None
            for h in range(LANES // per):
                mine = (lane >= h * per) & (lane < (h + 1) * per)
                vals = jnp.where(mine, scaled, jnp.zeros_like(scaled))[:stop]
                row = run_t_ref[i * (LANES // per) + h, :, :stop]
                decay = jnp.exp(jnp.minimum(run[start:stop, h * per : h * per + 1] - row, 0.0))
                weight = (decay * scores_ref[start:stop, :stop]).astype(bf16)
                term = dot_rows(weight, vals)
                total = term if total is None else total + term
            inner_ref[start:stop, columns] = total
        return 0

    lax.fori_loop(0, inner // LANES, pair, 0)


def row_sums(value):
    folded = value[:, :LANES]
    for at in range(LANES, value.shape[1], LANES):
        folded = folded + value[:, at : at + LANES]
    ones = jnp.ones((8, LANES), bf16)
    high, low = halves(folded)
    return dot_outer(ones, high) + dot_outer(ones, low)


def as_column(row):
    n = row.shape[1]
    eye = row_iota((n, n)) == col_iota((n, n))
    return jnp.sum(jnp.where(eye, row, 0.0), axis=1, keepdims=True)


def tensor_barrier(me, n):
    barrier = pltpu.get_barrier_semaphore()
    for d in range(1, n):
        pl.semaphore_signal(
            barrier, inc=1, device_id={"tensor": lax.rem(me + d, n)}, device_id_type=MESH
        )
    pl.semaphore_wait(barrier, n - 1)


def push(source, target, sems, slot, peer):
    send, receive = sems
    return pltpu.make_async_remote_copy(
        src_ref=source, dst_ref=target, send_sem=send.at[slot], recv_sem=receive.at[slot],
        device_id=peer if isinstance(peer, dict) else {"tensor": peer}, device_id_type=MESH,
    )


def ctx_place():
    core = lax.axis_size("core")
    return lax.axis_index("cy") * core + lax.axis_index("core"), lax.axis_size("cy") * core


def ctx_peer(place):
    core = lax.axis_size("core")
    return {"cy": place // core, "core": lax.rem(place, core)}


def front_barrier(me, n):
    barrier = pltpu.get_barrier_semaphore()
    place, count = ctx_place()
    for d in range(1, n):
        pl.semaphore_signal(
            barrier, inc=1, device_id={"tensor": lax.rem(me + d, n)}, device_id_type=MESH
        )
    for d in range(1, count):
        pl.semaphore_signal(
            barrier, inc=1, device_id=ctx_peer(lax.rem(place + d, count)), device_id_type=MESH
        )
    pl.semaphore_wait(barrier, n - 1 + count - 1)


def rows_barrier(me, n):
    barrier = line_barrier(me, n)
    place, count = row_place(), lax.axis_size(ROWS)
    for d in range(1, count):
        pl.semaphore_signal(barrier, inc=1, device_id=row_peer(lax.rem(place + d, count)),
                            device_id_type=MESH)
    pl.semaphore_wait(barrier, n - 1 + count - 1)


class RowGather:
    def __init__(self, source, full, sems):
        self.cy, self.core = lax.axis_size("cy"), lax.axis_size("core")
        self.chips = lax.axis_size(CHIPS)
        me = lax.axis_index("core")
        chip = lax.axis_index("shard") * self.cy + lax.axis_index("cy")
        slot = lambda c: c * self.core + me
        self.far, self.near = [], []
        for d in range(1, self.chips):
            peer = lax.rem(chip + d, self.chips)
            self.far.append(push(source, full.at[slot(chip)], sems[0], d - 1,
                                 {"shard": peer // self.cy, "cy": lax.rem(peer, self.cy)}))
        if self.core == 2:
            for d in range(self.chips):
                origin = lax.rem(chip - d + self.chips, self.chips)
                self.near.append(push(source if d == 0 else full.at[slot(origin)], full.at[slot(origin)],
                                      sems[1], d, {"core": 1 - me}))

    def start(self):
        for copy in self.far + self.near[:1]:
            copy.start()

    def relay(self):
        for d, copy in enumerate(self.far):
            copy.wait_recv()
            if self.near:
                self.near[d + 1].start()

    def finish(self):
        for copy in self.near:
            copy.wait()
        for copy in self.far:
            copy.wait_send()


class WeightSum:
    def __init__(self, stage, boxes):
        self.stage, self.boxes = stage, boxes
        self.depth = stage.shape[0]
        self.core, self.cy = lax.axis_index("core"), lax.axis_size("cy")
        self.chip = lax.axis_index("shard") * self.cy + lax.axis_index("cy")
        self.chips = boxes[0].shape[0] if boxes else 0
        self.paired = boxes[1:3] if len(boxes) == 3 else boxes[3:5]
        self.owner = boxes[0].shape[1] if boxes else 0
        self.siblings, self.mains, self.units = [], [], []

    def rows(self, k):
        return pl.ds(pl.multiple_of(k * self.owner, 16), self.owner)

    def product(self, lhs_ref, rhs, at, transposed=True):
        span = rhs.shape[1]
        tall = self.depth // 2

        def part(m, _):
            here = pl.ds(pl.multiple_of(m * tall, tall), tall)
            if transposed:
                value = dot_rows(lhs_ref[here, :], rhs[...])
            else:
                value = dot_inner(lhs_ref[:, here], rhs[...])
            self.stage[here, at : at + span] = value.astype(bf16)
            return 0

        lax.fori_loop(0, 2, part, 0)

    def to_sibling(self, at, span):
        unit = len(self.units)
        self.units.append((at, span))
        copies = []
        for j in range(self.chips):
            copies.append(push(
                self.stage.at[self.rows(2 * j + 1 - self.core), pl.ds(at, span)],
                self.boxes[0].at[j, :, pl.ds(at, span)], self.paired, unit * self.chips + j,
                {"core": 1 - self.core},
            ))
            copies[-1].start()
        self.siblings.append(copies)

    def to_chips(self, unit):
        if not self.chips:
            return
        sib_in, sum_ref, main_in = self.boxes[:3]
        at, span = self.units[unit]
        for j, copy in enumerate(self.siblings[unit]):
            copy.wait_recv()
            sum_ref[j * self.owner : (j + 1) * self.owner, at : at + span] = (
                self.stage[self.rows(2 * j + self.core), at : at + span] + sib_in[j, :, at : at + span]
            )
        for d in range(1, self.chips):
            peer = lax.rem(self.chip + d, self.chips)
            self.mains.append(push(
                sum_ref.at[self.rows(peer), pl.ds(at, span)], main_in.at[d - 1, :, pl.ds(at, span)],
                self.boxes[5:7], unit * (self.chips - 1) + d - 1,
                {"shard": peer // self.cy, "cy": lax.rem(peer, self.cy)},
            ))
            self.mains[-1].start()

    def pair(self, unit, out_ref):
        at, span = self.units[unit]
        if not self.chips:
            out_ref[:, at : at + span] = self.stage[:, at : at + span]
            return
        for j, copy in enumerate(self.siblings[unit]):
            copy.wait_recv()
            out_ref[j * self.owner : (j + 1) * self.owner, at : at + span] = (
                self.stage[self.rows(2 * j + self.core), at : at + span]
                + self.boxes[0][j, :, at : at + span]
            )

    def wait_send(self):
        for copies in self.siblings:
            for copy in copies:
                copy.wait_send()

    def finish(self, out_ref):
        if not self.chips:
            out_ref[...] = self.stage[...]
            return
        _, sum_ref, main_in = self.boxes[:3]
        main_in[self.chips - 1] = sum_ref[self.rows(self.chip), :]
        for copy in self.mains:
            copy.wait_recv()
        out_ref[...] = in_order(main_in, self.chip, self.chips)
        self.wait_send()
        for copy in self.mains:
            copy.wait_send()


def weight_boxes(depth, width, units, between_chips=True):
    dma = pltpu.SemaphoreType.DMA
    if lax.axis_size("core") != 2:
        return [pltpu.VMEM((depth, width), bf16)], jax.ShapeDtypeStruct((depth, width), bf16)
    chips = lax.axis_size(CHIPS)
    owner = depth // (2 * chips)
    if not between_chips:
        return [
            pltpu.VMEM((depth, width), bf16), pltpu.VMEM((chips, owner, width), bf16),
            dma((units * chips,)), dma((units * chips,)),
        ], jax.ShapeDtypeStruct((chips * owner, width), bf16)
    return [
        pltpu.VMEM((depth, width), bf16), pltpu.VMEM((chips, owner, width), bf16),
        pltpu.VMEM((chips * owner, width), bf16), pltpu.VMEM((chips, owner, width), bf16),
        dma((units * chips,)), dma((units * chips,)), dma((units * (chips - 1),)),
        dma((units * (chips - 1),)),
    ], jax.ShapeDtypeStruct((owner, width), f32)


class StatePush:
    def __init__(self, source, far_ref, sems, reverse):
        place, count = ctx_place()
        sign = -1 if reverse else 1
        self.copies = []
        for d in range(1, count):
            to, origin = place + sign * d, place - sign * d
            copy = push(source, far_ref.at[d - 1], sems, d - 1,
                        ctx_peer(lax.rem(to + count, count)))
            self.copies.append((copy, (to >= 0) & (to < count), (origin >= 0) & (origin < count)))

    def start(self):
        for copy, sends, _ in self.copies:
            pl.when(sends)(copy.start)

    def wait_recv(self):
        for copy, _, gets in self.copies:
            pl.when(gets)(copy.wait_recv)

    def wait_send(self):
        for copy, sends, _ in self.copies:
            pl.when(sends)(copy.wait_send)


class LineReduce:
    def __init__(self, me, n, blocks, right, left, sems):
        self.me, self.n, self.blocks, self.right, self.left = me, n, blocks, right, left
        self.right_sems, self.left_sems = sems
        self.keep = lambda d: jnp.minimum(jnp.maximum(d, 0), n - 1)

    def rightward(self, d):
        return push(self.blocks(d), self.right.at[d], self.right_sems, d,
                    jnp.minimum(self.me + 1, self.n - 1))

    def leftward(self, d):
        return push(self.blocks(d), self.left.at[d], self.left_sems, d, jnp.maximum(self.me - 1, 0))

    def step(self, t):
        me, n = self.me, self.n
        ways = []
        if t < n:
            ways.append((n - 1 - t + me, me >= 1, lambda d: d > me, t >= me, self.rightward, self.right))
            ways.append((t - (n - 1 - me), me <= n - 2, lambda d: d < me, t >= n - 1 - me,
                         self.leftward, self.left))
        for d, gets, passes, ready, copy_of, box in ways:
            at = self.keep(d)
            copy = copy_of(at)

            @pl.when(gets & ready)
            def _():
                copy.wait_recv()

            @pl.when(gets & ready & passes(d))
            def _():
                view = self.blocks(at)
                view[...] = view[...] + box[at]

            @pl.when(ready & passes(d))
            def _():
                copy.start()

    def total(self):
        me, n = self.me, self.n
        value = self.blocks(me)[...].astype(f32)
        value = value + jnp.where(me >= 1, self.right[me].astype(f32), 0.0)
        return value + jnp.where(me <= n - 2, self.left[me].astype(f32), 0.0)

    def wait_send(self):
        for d in range(self.n):
            pl.when(self.me < d)(self.rightward(d).wait_send)
            pl.when(self.me > d)(self.leftward(d).wait_send)


class LineGather:
    def __init__(self, me, n, blocks, sems):
        self.me, self.n, self.blocks = me, n, blocks
        self.right_sems, self.left_sems = sems

    def rightward(self, d):
        return push(self.blocks(d), self.blocks(d), self.right_sems, d,
                    jnp.minimum(self.me + 1, self.n - 1))

    def leftward(self, d):
        return push(self.blocks(d), self.blocks(d), self.left_sems, d, jnp.maximum(self.me - 1, 0))

    def step(self, t):
        me, n = self.me, self.n
        from_left, from_right = me - t, me + t
        right = self.rightward(jnp.maximum(from_left, 0))
        left = self.leftward(jnp.minimum(from_right, n - 1))
        if t > 0:
            pl.when(from_left >= 0)(right.wait_recv)
        pl.when((from_left >= 0) & (me <= n - 2))(right.start)
        if t > 0:
            pl.when(from_right <= n - 1)(left.wait_recv)
        pl.when((from_right <= n - 1) & (me >= 1))(left.start)

    def wait_send(self):
        for d in range(self.n):
            pl.when((self.me >= d) & (self.me <= self.n - 2))(self.rightward(d).wait_send)
            pl.when((self.me <= d) & (self.me >= 1))(self.leftward(d).wait_send)


def line_sems(n):
    return [pltpu.SemaphoreType.DMA((n,))] * 4


def line_groups(sems):
    return (sems[0], sems[1]), (sems[2], sems[3])


def line_barrier(me, n):
    barrier = pltpu.get_barrier_semaphore()
    for d in range(1, n):
        pl.semaphore_signal(
            barrier, inc=1, device_id={"tensor": lax.rem(me + d, n)}, device_id_type=MESH
        )
    return barrier


def intake_kernel(x_ref, gains_ref, mixed_ref, mixed_t_ref, full_ref, gain_out,
                  x_box, gains_box, halo_box, *sems, n):
    me = lax.axis_index("tensor")
    place, count = ctx_place()
    rows, quarter = x_ref.shape
    column = lambda d: pl.ds(pl.multiple_of(d * quarter, LANES), quarter)
    gain_sems, halo_sems = (sems[0], sems[1]), (sems[2], sems[3])
    halo_box[...] = jnp.zeros_like(halo_box)
    x_box[:, column(me)] = x_ref[...]
    gains_box[:, column(me)] = gains_ref[...]
    barrier = line_barrier(me, n)
    for away in (1, count - 1):
        for z in range(n):
            pl.semaphore_signal(
                barrier, inc=1, device_id={**ctx_peer(lax.rem(place + away, count)), "tensor": z},
                device_id_type=MESH,
            )
    pl.semaphore_wait(barrier, n - 1 + 2 * n)
    x_line = LineGather(me, n, lambda d: x_box.at[:, column(d)], line_groups(sems[4:8]))
    x_line.step(0)
    gains = [push(gains_box.at[:, column(me)], gains_box.at[:, column(me)], gain_sems, d - 1,
                  lax.rem(me + d, n)) for d in range(1, n)]
    for copy in gains:
        copy.start()
    sends, gets = place < count - 1, place > 0
    halos = []
    for d in range(n):
        peer = {**ctx_peer(jnp.minimum(place + 1, count - 1)), "tensor": lax.rem(me + d, n)}
        halos.append(push(x_ref.at[rows - HALO :], halo_box.at[:, column(me)], halo_sems, d, peer))
        pl.when(sends)(halos[-1].start)
    for t in range(1, n):
        x_line.step(t)
    for copy in gains:
        copy.wait_recv()
    for copy in halos:
        pl.when(gets)(copy.wait_recv)
    gain = gains_box[0:1, :].astype(f32)
    gain_out[...] = gains_box[...].astype(f32)

    def normed(x):
        x = x.astype(f32)
        scale = lax.rsqrt(jnp.mean(x * x, axis=1, keepdims=True) + epsilon)
        return (x * scale * gain).astype(bf16)

    mixed_ref[:HALO, :] = normed(halo_box[...])
    full_ref[...] = x_box[...]
    mixed_ref[HALO:, :] = normed(x_box[...])
    mixed_t_ref[...] = mixed_ref[HALO:, :].T
    for copy in gains:
        copy.wait_send()
    for copy in halos:
        pl.when(sends)(copy.wait_send)
    x_line.wait_send()


def intake(x, gains):
    n = lax.axis_size("tensor")
    rows, quarter = x.shape
    depth = n * quarter
    shape = jax.ShapeDtypeStruct
    dma = pltpu.SemaphoreType.DMA
    return pl.pallas_call(
        partial(intake_kernel, n=n),
        in_specs=[VMEM] * 2,
        out_specs=[VMEM] * 4,
        out_shape=[shape((rows + HALO, depth), bf16), shape((depth, rows), bf16),
                   shape((rows, depth), bf16), shape((16, depth), f32)],
        scratch_shapes=[
            pltpu.VMEM((rows, depth), bf16),
            pltpu.VMEM((16, depth), bf16), pltpu.VMEM((HALO, depth), bf16),
            dma((n - 1,)), dma((n - 1,)), dma((n,)), dma((n,)),
        ] + line_sems(n),
        compiler_params=pltpu.CompilerParams(
            vmem_limit_bytes=60 << 20, collective_id=7, has_side_effects=True
        ),
        cost_estimate=cost(50),
        name="intake",
    )(x, gains)


def row_columns(row):
    return jnp.concatenate(
        [as_column(row[:, at : at + LANES]) for at in range(0, row.shape[1], LANES)], axis=0
    )


def front_kernel(mixed_ref, taps_ref, same_ref, bias_ref, decay_ref, end_ref, link_ref, seg_col_ref,
                 seg_row_ref, skip_ref, gain_ref, x_ref, cot_ref, mid_ref, chosen_ref, w_ref,
                 value_ref, act_ref, scaled_ref, step_ref, run_ref, run_exp_ref, inner_ref, mixer_ref,
                 state_ref, packed_ref, res_ref, stat_ref, own_ref, cot_full_ref, mix_ref, mix_t_ref, gates_ref,
                 wm_ref, wo_ref, run_t_ref, scores_ref, part_ref, square_ref, lifted_ref, far_ref,
                 right_box, left_box, square_box, res_box, stat_box, cot_box, router_ref, local_sem, *sems,
                 inner, nstate, per, heads, di_all, n):
    me = lax.axis_index("tensor")
    rows, depth = x_ref.shape
    own = rows // n
    groups = [(sems[2 * i], sems[2 * i + 1]) for i in range(3)]
    block_at = lambda d: pl.ds(pl.multiple_of(d * own, own), own)
    half = own // 2
    half_at = lambda d, h: pl.ds(pl.multiple_of(d * own + h * half, half), half)
    lines_at = lambda k: line_groups(sems[6 + 4 * k : 10 + 4 * k])
    mine = pl.ds(pl.multiple_of(me * own, own), own)
    wide = wm_ref.shape[1]
    loads = [
        pltpu.make_async_copy(w_ref.at[:, pl.ds(0, wide)], wm_ref, local_sem.at[0]),
        pltpu.make_async_copy(w_ref.at[:, pl.ds(wide, inner)], wo_ref, local_sem.at[1]),
        pltpu.make_async_copy(w_ref.at[:, pl.ds(wide + inner, LANES)], router_ref, local_sem.at[2]),
    ]
    for copy in loads:
        copy.start()
    far_ref[...] = jnp.zeros_like(far_ref)
    quarter = cot_ref.shape[1]
    column = pl.ds(pl.multiple_of(me * quarter, LANES), quarter)
    cot_box[:, column] = cot_ref[...]
    front_barrier(me, n)
    cots = LineGather(
        me, n, lambda d: cot_box.at[:, pl.ds(pl.multiple_of(d * quarter, LANES), quarter)],
        lines_at(0),
    )
    cots.step(0)
    loads[0].wait()
    enter_part(mixed_ref, wm_ref, taps_ref, same_ref, bias_ref, decay_ref, end_ref, link_ref,
               value_ref, act_ref, scaled_ref, step_ref, run_ref, run_exp_ref, packed_ref,
               inner=inner, nstate=nstate, per=per)
    states = StatePush(packed_ref, far_ref, groups[0], False)
    states.start()
    cots.step(1)
    run_t = run_ref[...].T
    for h in range(heads):
        run_t_ref[h] = run_t[h : h + 1, :]
    intra_part(act_ref, scaled_ref, run_t_ref, run_exp_ref, seg_col_ref, seg_row_ref, inner_ref,
               scores_ref, inner=inner, nstate=nstate, per=per, block=128)
    cots.step(2)
    states.wait_recv()
    state = join_states(far_ref, inner, per)
    state_ref[...] = state
    carried = dot_outer(act_ref[:, inner + nstate :], state.astype(bf16)) * (
        jnp.exp(run_exp_ref[...]) * link_ref[...]
    )
    mixer = inner_ref[...] + carried + skip_ref[...] * act_ref[:, :inner].astype(f32)
    mixer_ref[...] = mixer
    z = value_ref[HALO:, :inner]
    gated = mixer * (z * sigmoid(z))
    square_ref[...] = row_sums(gated * gated)
    lifted_ref[...] = (gated * gain_ref[...]).astype(bf16)
    loads[1].wait()
    for t in range(3, n):
        cots.step(t)
    squares, stats = [], []
    for d in range(1, n):
        peer = lax.rem(me + d, n)
        squares.append(push(square_ref.at[:, block_at(peer)], square_box.at[d - 1], groups[1], d - 1, peer))
        squares[-1].start()
    lines = [
        LineReduce(me, n, lambda d, h=h: part_ref.at[d, pl.ds(h * half, half)], right_box.at[h],
                   left_box.at[h], lines_at(1 + h)) for h in range(2)
    ]
    gathers = [LineGather(me, n, lambda d, h=h: res_box.at[half_at(d, h)], lines_at(3 + h))
               for h in range(2)]
    for k in range(n):
        d = jnp.where(2 * me < n, n - 1 - k, k)
        part_ref[d] = dot_outer(lifted_ref[block_at(d), :], wo_ref[...]).astype(bf16)
        if k == 0:
            for line in lines:
                line.step(0)
    square = square_ref[:, mine]
    for copy in squares:
        copy.wait_recv()
    for d in range(1, n):
        square = square + square_box[d - 1]
    scale = lax.rsqrt(square / di_all + epsilon)
    stat_box[:, mine] = scale
    for d in range(1, n):
        stats.append(push(stat_box.at[:, mine], stat_box.at[:, mine], groups[2], d - 1,
                          lax.rem(me + d, n)))
        stats[-1].start()
    scale = as_column(scale[:1])
    for t in range(1, n - 1):
        for line in lines:
            line.step(t)
    for h in range(2):
        lines[h].step(n - 1)
        total = lines[h].total()
        own_ref[h * half : (h + 1) * half, :] = total
        here = half_at(me, h)
        res_box[here, :] = (
            x_ref[here, :].astype(f32) + total * scale[h * half : (h + 1) * half]
        ).astype(bf16)
        gathers[h].step(0)
    for t in range(1, n):
        for gather in gathers:
            gather.step(t)
    cot_full_ref[...] = cot_box[...]
    states.wait_send()
    cots.wait_send()
    for line in lines + gathers:
        line.wait_send()
    for copy in squares:
        copy.wait_send()
    for copy in stats:
        copy.wait()
    res_ref[...] = res_box[...]
    stat_ref[...] = stat_box[...]
    res = res_box[...].astype(f32)
    mix = (
        res * lax.rsqrt(jnp.mean(res * res, axis=1, keepdims=True) + epsilon) * mid_ref[...]
    ).astype(bf16)
    mix_ref[...] = mix
    mix_t_ref[...] = mix.T
    loads[2].wait()
    chosen = chosen_ref[...] > 0.0
    logits = dot_rows(mix, router_ref[...])
    top = jnp.max(jnp.where(chosen, logits, -1e30), axis=1, keepdims=True)
    weight = jnp.where(chosen, jnp.exp(jnp.where(chosen, logits - top, 0.0)), 0.0)
    gates_ref[...] = weight / jnp.sum(weight, axis=1, keepdims=True)


def pairs(count, n):
    return [pltpu.SemaphoreType.DMA((n - 1,))] * (2 * count)


VMEM = pl.BlockSpec(memory_space=pltpu.VMEM)
HBM = pl.BlockSpec(memory_space=pl.ANY)


def front(mixed_ext, taps, same, bias, decay, at_end, link, seg_col, seg_row, skip, gain, x, cot, mid,
          chosen, weights, inner, nstate, per, heads, di_all):
    n = lax.axis_size("tensor")
    others = lax.axis_size(CTX) - 1
    tokens, depth = x.shape
    ext = tokens + HALO
    own = tokens // n
    wide = 2 * inner + 2 * nstate + LANES
    shape = jax.ShapeDtypeStruct
    outs = [
        shape((ext, wide), f32), shape((tokens, inner + 2 * nstate), bf16),
        shape((tokens, inner), bf16), shape((tokens, LANES), f32), shape((tokens, LANES), f32),
        shape((tokens, inner), f32), shape((tokens, inner), f32), shape((tokens, inner), f32),
        shape((inner, nstate), f32), shape((inner + 16, nstate), bf16),
        shape((tokens, depth), bf16), shape((8, tokens), f32), shape((own, depth), f32),
        shape((tokens, depth), bf16), shape((tokens, depth), bf16), shape((depth, tokens), bf16),
        shape((tokens, LANES), f32),
    ]
    dma = pltpu.SemaphoreType.DMA
    return pl.pallas_call(
        partial(front_kernel, inner=inner, nstate=nstate, per=per, heads=heads, di_all=di_all, n=n),
        in_specs=[VMEM] * 15 + [HBM],
        out_specs=[VMEM] * 17,
        out_shape=outs,
        scratch_shapes=[
            pltpu.VMEM((depth, wide), bf16), pltpu.VMEM((depth, inner), bf16),
            pltpu.VMEM((heads, 1, tokens), f32), pltpu.VMEM((tokens, tokens), f32),
            pltpu.VMEM((n, own, depth), bf16), pltpu.VMEM((8, tokens), f32),
            pltpu.VMEM((tokens, inner), bf16), pltpu.VMEM((others, inner + 16, nstate), bf16),
            pltpu.VMEM((2, n, own // 2, depth), bf16), pltpu.VMEM((2, n, own // 2, depth), bf16),
            pltpu.VMEM((n - 1, 8, own), f32),
            pltpu.VMEM((tokens, depth), bf16), pltpu.VMEM((8, tokens), f32),
            pltpu.VMEM((tokens, depth), bf16), pltpu.VMEM((depth, LANES), bf16), dma((3,)),
            dma((others,)), dma((others,)),
        ] + pairs(2, n) + line_sems(n) * 5,
        compiler_params=pltpu.CompilerParams(
            vmem_limit_bytes=63 << 20, collective_id=1, has_side_effects=True
        ),
        cost_estimate=cost(100),
        name="front",
    )(mixed_ext, taps, same, bias, decay, at_end, link, seg_col, seg_row, skip, gain, x, cot, mid,
      chosen, weights)


def turn_kernel(dmix_hbm, dgate_ref, res_ref, cot_ref, own_ref, gain_ref,
                dres_ref, notes_ref, gains_ref,
                dmix_ref, right_box, left_box, gate_box, dres_box, notes_box, load_sem, *sems, n):
    me = lax.axis_index("tensor")
    rows, depth = res_ref.shape
    own = rows // n
    groups = [(sems[2 * i], sems[2 * i + 1]) for i in range(2)]
    block_at = lambda d: pl.ds(pl.multiple_of(d * own, own), own)
    mine = block_at(me)
    load = pltpu.make_async_copy(dmix_hbm, dmix_ref, load_sem)
    load.start()
    tensor_barrier(me, n)
    load.wait()
    half = own // 2
    half_at = lambda d, h: pl.ds(pl.multiple_of(d * own + h * half, half), half)
    lines_at = lambda k: line_groups(sems[4 + 4 * k : 8 + 4 * k])
    lines = [LineReduce(me, n, lambda d, h=h: dmix_ref.at[half_at(d, h)], right_box.at[h],
                        left_box.at[h], lines_at(h)) for h in range(2)]
    gathers = [LineGather(me, n, lambda d, h=h: dres_box.at[half_at(d, h)], lines_at(2 + h))
               for h in range(2)]
    for line in lines:
        line.step(0)
    first, second = [], []
    for d in range(1, n):
        peer = lax.rem(me + d, n)
        first.append(push(dgate_ref.at[:, block_at(peer)], gate_box.at[d - 1], groups[0], d - 1, peer))
        first[-1].start()
    res = res_ref[mine, :].astype(f32)
    scale = lax.rsqrt(jnp.mean(res * res, axis=1, keepdims=True) + epsilon)
    normed = res * scale
    for t in range(1, n - 1):
        for line in lines:
            line.step(t)
    gain_sum = None
    for h in range(2):
        lines[h].step(n - 1)
        dmix = lines[h].total()
        part = slice(h * half, (h + 1) * half)
        here = half_at(me, h)
        lifted = dmix * gain_ref[...]
        inside = jnp.mean(lifted * normed[part], axis=1, keepdims=True)
        dres_box[here, :] = (
            cot_ref[here, :].astype(f32) + scale[part] * (lifted - normed[part] * inside)
        ).astype(bf16)
        gathers[h].step(0)
        term = jnp.sum(dmix * normed[part], axis=0, keepdims=True)
        gain_sum = term if gain_sum is None else gain_sum + term
    gains_ref[...] = jnp.broadcast_to(gain_sum, gains_ref.shape)
    dgate = dgate_ref[:, mine]
    for copy in first:
        copy.wait_recv()
    for d in range(1, n):
        dgate = dgate + gate_box[d - 1]
    gates = dgate.shape[0]
    notes_box[:gates, mine] = dgate
    notes_box[gates:, mine] = row_sums(dres_box[mine, :].astype(f32) * own_ref[...])
    for d in range(1, n):
        peer = lax.rem(me + d, n)
        second.append(push(notes_box.at[:, mine], notes_box.at[:, mine], groups[1], d - 1, peer))
        second[-1].start()
    for t in range(1, n):
        for gather in gathers:
            gather.step(t)
    for line in lines + gathers:
        line.wait_send()
    for copy in first:
        copy.wait_send()
    for copy in second:
        copy.wait()
    dres_ref[...] = dres_box[...]
    notes_ref[...] = notes_box[...]


def turn_step(dmix, dgate, residual, cot, own_part, gain):
    n = lax.axis_size("tensor")
    tokens, depth = dmix.shape
    own = tokens // n
    shape = jax.ShapeDtypeStruct
    return pl.pallas_call(
        partial(turn_kernel, n=n),
        in_specs=[HBM] + [VMEM] * 5,
        out_specs=[VMEM] * 3,
        out_shape=[shape((tokens, depth), bf16), shape((dgate.shape[0] + 8, tokens), f32),
                   shape((8, depth), f32)],
        scratch_shapes=[
            pltpu.VMEM((tokens, depth), bf16),
            pltpu.VMEM((2, n, own // 2, depth), bf16), pltpu.VMEM((2, n, own // 2, depth), bf16),
            pltpu.VMEM((n - 1, dgate.shape[0], own), f32),
            pltpu.VMEM((tokens, depth), bf16), pltpu.VMEM((dgate.shape[0] + 8, tokens), f32),
            pltpu.SemaphoreType.DMA,
        ] + pairs(2, n) + line_sems(n) * 4,
        compiler_params=pltpu.CompilerParams(
            vmem_limit_bytes=60 << 20, collective_id=2, has_side_effects=True
        ),
        cost_estimate=cost(60),
        name="turn_step",
    )(dmix, dgate, residual, cot, own_part, gain)


def in_order(box, me, count):
    total = None
    for source in range(count):
        term = box[lax.rem(me - source + 2 * count - 1, count)].astype(f32)
        total = term if total is None else total + term
    return total


def row_place():
    cy, core = lax.axis_size("cy"), lax.axis_size("core")
    return (lax.axis_index("shard") * cy + lax.axis_index("cy")) * core + lax.axis_index("core")


def row_peer(place):
    cy, core = lax.axis_size("cy"), lax.axis_size("core")
    return {"shard": place // (cy * core), "cy": lax.rem(place // core, cy), "core": lax.rem(place, core)}


def last_kernel(grad_ref, x_ref, dres_ref, gain_ref, mid_ref, state_ref, early_ref, mixed_t_ref, mix_t_ref,
                state_all_ref, gates_ref, notes_ref, w_hbm,
                out_ref, early_out, late_out, main_out,
                w_ref, blocks_ref, right_box, left_box, cross_box, cross_in, gains_box, gains_in, state_in,
                early_in, late_ref, late_in, load_sem, stage_ref, *sems, n, count, boxes, inner, last):
    weights = WeightSum(stage_ref, sems[:boxes])
    sems = sems[boxes:]
    me = lax.axis_index("tensor")
    place = row_place()
    rows, depth = x_ref.shape
    quarter = depth // n
    wide = w_ref.shape[1]
    groups = [(sems[2 * i], sems[2 * i + 1]) for i in range(3)]
    row_groups = [(sems[6 + 2 * i], sems[7 + 2 * i]) for i in range(2)]
    load = pltpu.make_async_copy(w_hbm.at[:, pl.ds(0, wide)], w_ref, load_sem)
    load.start()
    rows_barrier(me, n)
    copies, states, lates = [], [], []
    x = x_ref[...].astype(f32)
    scale = lax.rsqrt(jnp.mean(x * x, axis=1, keepdims=True) + epsilon)
    load.wait()
    half = rows // 2
    lines = [
        LineReduce(me, n, lambda d, h=h: blocks_ref.at[d, pl.ds(h * half, half)], right_box.at[h],
                   left_box.at[h], line_groups(sems[10 + 4 * h : 14 + 4 * h])) for h in range(2)
    ]
    cross = jnp.zeros((8, rows), f32)
    for k in range(n):
        d = jnp.where(2 * me < n, n - 1 - k, k)
        theirs = pl.ds(pl.multiple_of(d * quarter, LANES), quarter)
        w = w_ref[theirs, :]
        block = dot_outer(grad_ref[...], w)
        blocks_ref[d] = block.astype(bf16)
        if k == 0:
            for line in lines:
                line.step(0)
        normed = x_ref[:, theirs].astype(f32) * scale
        cross = cross + row_sums(block * normed * gain_ref[:, theirs])
        gains_box[d] = jnp.where(
            row_iota((8, quarter)) == 0, jnp.sum(block * normed, axis=0, keepdims=True),
            mid_ref[:, theirs],
        )
    cross_box[...] = cross
    sums = []
    for d in range(1, n):
        peer = lax.rem(me + d, n)
        sums.append(push(gains_box.at[peer], gains_in.at[d - 1], groups[0], d - 1, peer))
        sums.append(push(cross_box, cross_in.at[d - 1], groups[1], d - 1, peer))
        states.append(push(state_ref, state_in.at[d - 1], groups[2], d - 1, peer))
    for d in range(1, count):
        copies.append(push(early_ref, early_in.at[d - 1], row_groups[0], d - 1,
                           row_peer(lax.rem(place + d, count))))
    for copy in sums + states + copies:
        copy.start()

    gates = gates_ref[...]
    kinds = notes_ref.shape[0] - 8
    moved = jnp.concatenate(
        [notes_ref[:kinds, :], jnp.zeros((LANES - kinds, gates.shape[0]), f32)], axis=0
    ).T
    inside = jnp.sum(gates * moved, axis=1, keepdims=True)
    first = 2 * inner
    weights.product(mixed_t_ref, grad_ref.at[:, pl.ds(inner, inner)], 0)
    weights.to_sibling(0, inner)
    for line in lines:
        line.step(1)
    weights.product(mixed_t_ref, state_all_ref, inner)
    weights.product(mixed_t_ref, grad_ref.at[:, pl.ds(last, LANES)], inner + last - first)
    weights.product(mix_t_ref, (gates * (moved - inside)).astype(bf16), inner + wide - first)
    weights.to_sibling(inner, wide - first + LANES)
    weights.to_chips(0)
    for copy in sums + states:
        copy.wait_recv()
    gains = gains_box[me]
    for d in range(1, n):
        gains = gains + gains_in[d - 1]
        cross = cross + cross_in[d - 1]
    state_in[n - 1] = state_ref[...]
    late_ref[:, :quarter] = gains
    late_ref[:, quarter:] = in_order(state_in, me, n)
    for d in range(1, count):
        lates.append(push(late_ref, late_in.at[d - 1], row_groups[1], d - 1,
                          row_peer(lax.rem(place + d, count))))
        lates[-1].start()
    for t in range(2, n - 1):
        for line in lines:
            line.step(t)
    weights.to_chips(1)
    here = pl.ds(pl.multiple_of(me * quarter, LANES), quarter)
    inside = row_columns(cross[:1]) / depth
    for h in range(2):
        lines[h].step(n - 1)
        part = slice(h * half, (h + 1) * half)
        out_ref[part, :] = dres_ref[part, here].astype(f32) + scale[part] * (
            lines[h].total() * gain_ref[:, here]
            - x_ref[part, here].astype(f32) * scale[part] * inside[part]
        )
    for copy in copies + lates:
        copy.wait_recv()
    early_in[count - 1] = early_ref[...]
    late_in[count - 1] = late_ref[...]
    early_out[...] = in_order(early_in, place, count)
    late_out[...] = in_order(late_in, place, count)
    weights.finish(main_out)
    for copy in copies + states + lates + sums:
        copy.wait_send()
    for line in lines:
        line.wait_send()


def last_step(vmem_args, weights, inner, last):
    value_grad, x, early, state = (vmem_args[i] for i in (0, 1, 6, 5))
    n, count = lax.axis_size("tensor"), lax.axis_size(ROWS)
    tokens, depth = x.shape
    quarter = depth // n
    wide = value_grad.shape[1]
    late = quarter + state.shape[1]
    shape = jax.ShapeDtypeStruct
    dma = pltpu.SemaphoreType.DMA
    boxes, main = weight_boxes(depth, wide - inner + LANES, 2)
    return pl.pallas_call(
        partial(last_kernel, n=n, count=count, boxes=len(boxes) - 1, inner=inner, last=last),
        in_specs=[VMEM] * len(vmem_args) + [HBM],
        out_specs=[VMEM] * 4,
        out_shape=[shape((tokens, quarter), f32), shape(early.shape, f32), shape((8, late), f32), main],
        scratch_shapes=[
            pltpu.VMEM((depth, wide), bf16), pltpu.VMEM((n, tokens, quarter), bf16),
            pltpu.VMEM((2, n, tokens // 2, quarter), bf16), pltpu.VMEM((2, n, tokens // 2, quarter), bf16),
            pltpu.VMEM((8, tokens), f32), pltpu.VMEM((n - 1, 8, tokens), f32),
            pltpu.VMEM((n, 8, quarter), f32), pltpu.VMEM((n - 1, 8, quarter), f32),
            pltpu.VMEM((n,) + state.shape, f32), pltpu.VMEM((count,) + early.shape, f32),
            pltpu.VMEM((8, late), f32), pltpu.VMEM((count, 8, late), f32), dma,
        ] + boxes + pairs(3, n) + [dma((count - 1,))] * 4 + line_sems(n) * 2,
        compiler_params=pltpu.CompilerParams(
            vmem_limit_bytes=62 << 20, collective_id=3, has_side_effects=True
        ),
        cost_estimate=cost(60),
        name="last_step",
    )(*vmem_args, weights)


def emit_kernel(out_ref, grad_ref, early_ref, late_ref, rear_ref, main_ref, pair_ref, *outs, per):
    (out, grad, gain_in, pair_out, state_out, step_out, conv, conv_state, bias, decay, skip, gate, proj,
     gain_mid, router, shared_up, shared_down, gates, down) = outs
    out[...] = out_ref[...]
    grad[...] = grad_ref[...]
    taps, inner = conv.shape
    heads = bias.shape[1]
    quarter = grad.shape[1]
    conv[...] = early_ref[:taps]
    conv_state[...] = late_ref[:taps, quarter:]
    for i in range(inner // LANES):
        gate[i : i + 1, :] = early_ref[taps : taps + 1, i * LANES : (i + 1) * LANES]
    for i in range(quarter // LANES):
        columns = slice(i * LANES, (i + 1) * LANES)
        gain_in[i : i + 1, :] = late_ref[0:1, columns]
        gain_mid[i : i + 1, :] = late_ref[1:2, columns]
    skips = jnp.broadcast_to(early_ref[taps + 1 : taps + 2], (8, inner))
    skip[...] = fold_heads(skips, head_fold(inner, LANES, per).astype(bf16))[:1, :heads]
    bias[...] = early_ref[taps + 2 : taps + 3, :heads]
    decay[...] = early_ref[taps + 3 : taps + 4, :heads]
    last = inner + state_out.shape[1]
    wide = last + LANES
    proj[...] = rear_ref[:, :inner].astype(f32)
    pair_out[:, 0, :] = rear_ref[:, inner:].astype(f32)
    pair_out[:, 1, :] = main_ref[:, :inner].astype(f32)
    state_out[...] = main_ref[:, inner:last].astype(f32)
    step_out[...] = main_ref[:, last:wide].astype(f32).T[:heads, :]
    router[...] = main_ref[:, wide:].astype(f32).T[: router.shape[0], :]
    hid, depth = down.shape[1:]
    wides = 2 * hid
    deep = depth + depth // 2
    for p in range(2):
        top = pair_ref[p * deep : p * deep + depth, :].astype(f32)
        gates[p * depth : (p + 1) * depth, 0, :] = top[:, :hid]
        gates[p * depth : (p + 1) * depth, 1, :] = top[:, hid:]
        for c in range(depth // wides):
            at = p * deep + depth + c * hid
            down[p, :, c * wides : (c + 1) * wides] = pair_ref[at : at + hid, :].astype(f32)
    wrows = shared_down.shape[0]
    part = shared_down.shape[1] // 2
    for p in range(2):
        top = pair_ref[2 * deep + p * wrows : 2 * deep + (p + 1) * wrows, :].astype(f32)
        shared_up[:, 0, p * part : (p + 1) * part] = top[:, :part]
        shared_up[:, 1, p * part : (p + 1) * part] = top[:, part:]
    shared_down[...] = pair_ref[2 * deep + 2 * wrows :, :].astype(f32)


def emit(args, inner, nstate, per, heads, kinds, hid):
    out, grad, _, _, _, main, pair = args
    tokens, quarter = grad.shape
    wrows = main.shape[0]
    depth = pair.shape[0] // 3 - wrows
    wide = pair.shape[1]
    flat = lambda *size: jax.ShapeDtypeStruct(size, f32)
    outs = [
        jax.ShapeDtypeStruct(out.shape, bf16), flat(tokens, quarter), flat(quarter // LANES, LANES),
        flat(wrows, 2, inner), flat(wrows, 2 * nstate), flat(heads, wrows), flat(CONV, inner),
        flat(CONV, 2 * nstate), flat(1, heads), flat(1, heads), flat(1, heads),
        flat(inner // LANES, LANES), flat(wrows, inner), flat(quarter // LANES, LANES), flat(kinds, wrows),
        flat(wrows, 2, wide), flat(wrows, wide), flat(2 * depth, 2, hid), flat(2, hid, depth),
    ]
    return pl.pallas_call(
        partial(emit_kernel, per=per),
        in_specs=[VMEM] * 7,
        out_specs=[VMEM] * len(outs),
        out_shape=outs,
        compiler_params=BIG,
        cost_estimate=cost(8),
        name="emit",
    )(*args)


def back_part(dout_ref, w_ref, mixer_ref, value_ref, act_ref, run_exp_ref, link_ref, gain_ref,
                scale, cross, through_ref, heads_ref, zgrad_ref, gated_ref, direct_ref, sums_ref,
                *, inner, nstate, di_all):
    mixer = mixer_ref[...]
    z = value_ref[HALO:, :inner]
    sig = sigmoid(z)
    act = z * sig
    gated = mixer * act
    grad = dot_rows(dout_ref[...], w_ref[...])
    gated_ref[...] = (gated * scale * gain_ref[...]).astype(bf16)
    sums_ref[0:1, :] = jnp.sum(grad * gated * scale, axis=0, keepdims=True)
    gated_grad = scale * (grad * gain_ref[...]) - gated * (scale * scale * scale * cross / di_all)
    zgrad_ref[...] = (gated_grad * mixer * (sig * (1.0 + z * (1.0 - sig)))).astype(bf16)
    heads = gated_grad * act
    heads_ref[...] = heads
    sums_ref[1:2, :] = jnp.sum(heads * act_ref[:, :inner].astype(f32), axis=0, keepdims=True)
    sums_ref[2:, :] = jnp.zeros((6, inner), f32)
    carried = (heads * (jnp.exp(run_exp_ref[...]) * link_ref[...])).astype(bf16)
    direct_ref[:inner, :] = dot_inner(carried, act_ref[:, inner + nstate :]).astype(bf16)
    direct_ref[inner:, :] = through_ref[inner:, :]


def intra_back_part(heads_ref, act_ref, scaled_ref, run_t_ref, run_exp_ref, seg_col_ref,
                      seg_row_ref, dscaled_ref, dstate_ref, drun_ref, scores_ref, dscores_ref, *, inner, nstate, per, block):
    tokens = act_ref.shape[0]
    keys = act_ref[:, inner : inner + nstate]
    query = act_ref[:, inner + nstate :]
    for start in range(0, tokens, block):
        stop = start + block
        scores_ref[start:stop, :stop] = masked_scores(
            query, keys, seg_col_ref, seg_row_ref, start, stop
        )
    dscores_ref[...] = jnp.zeros_like(dscores_ref)
    drun_ref[...] = jnp.zeros_like(drun_ref)

    def pair(i, _):
        columns = pl.ds(pl.multiple_of(i * LANES, LANES), LANES)
        scaled = scaled_ref[:, columns]
        heads = heads_ref[:, columns].astype(bf16)
        lane = col_iota(scaled.shape)
        run = run_exp_ref[:, columns]
        dscaled_ref[:, columns] = jnp.zeros((tokens, LANES), f32)
        for h in range(LANES // per):
            head = i * (LANES // per) + h
            mine = (lane >= h * per) & (lane < (h + 1) * per)
            vals = jnp.where(mine, scaled, jnp.zeros_like(scaled))
            grads = jnp.where(mine, heads, jnp.zeros_like(heads))
            pick = (col_iota((block, LANES)) == head).astype(bf16)
            for start in range(0, tokens, block):
                stop = start + block
                row = run_t_ref[head, :, :stop]
                decay = jnp.exp(jnp.minimum(run[start:stop, h * per : h * per + 1] - row, 0.0))
                weight = decay * scores_ref[start:stop, :stop]
                dweight = dot_outer(grads[start:stop], vals[:stop])
                dscores_ref[start:stop, :stop] += dweight * decay
                flow = (dweight * weight).astype(bf16)
                dscaled_ref[:stop, columns] += dot_inner(weight.astype(bf16), grads[start:stop])
                picks = jnp.broadcast_to(pick[:1], (stop, LANES))
                drun_ref[start:stop, :] += dot_rows(flow, picks)
                drun_ref[:stop, :] -= dot_inner(flow, pick)
        return 0

    lax.fori_loop(0, inner // LANES, pair, 0)
    dkeys = jnp.zeros((tokens, nstate), f32)
    dstate_ref[:, :nstate] = dkeys
    for start in range(0, tokens, block):
        stop = start + block
        shape = (block, stop)
        allowed = (row_iota(shape) + start >= col_iota(shape)) & (
            seg_col_ref[start:stop, :1] == seg_row_ref[:, :stop]
        )
        grad = jnp.where(allowed, dscores_ref[start:stop, :stop], 0.0).astype(bf16)
        dstate_ref[start:stop, nstate:] = dot_rows(grad, keys[:stop])
        dstate_ref[:stop, :nstate] += dot_inner(grad, query[start:stop])


def conv_back(value_ref, column, taps_ref, same_ref, dact, at, dtaps_ref, tokens):
    ext = tokens + HALO
    rows, total = conv_pre(value_ref, column, taps_ref, at, same_ref, tokens)
    sig = sigmoid(total)
    dpre = dact * (sig * (1.0 + total * (1.0 - sig)))
    drows = None
    for offset in range(CONV):
        first = HALO - CONV + 1 + offset
        kept = dpre * same_ref[offset]
        dtaps_ref[offset : offset + 1, pl.ds(at, LANES)] = jnp.sum(
            kept * rows[first : first + tokens], axis=0, keepdims=True
        )
        term = kept * taps_ref[offset : offset + 1, pl.ds(at, LANES)]
        after = ext - first - tokens
        pieces = [jnp.zeros((first, LANES), f32), term]
        if after:
            pieces.append(jnp.zeros((after, LANES), f32))
        term = jnp.concatenate(pieces, axis=0)
        drows = term if drows is None else drows + term
    return drows


def state_back_part(heads_ref, act_ref, step_ref, run_ref, run_exp_ref, link_ref, end_ref,
                      value_ref, taps_ref, same_ref, dstate_ref, in_ref, far_ref,
                      rows_ref, dtaps_ref, leaving_ref, kept_ref, dact_ref, *, inner, nstate, per):
    tokens = act_ref.shape[0]
    keys = act_ref[:, inner : inner + nstate]
    signal = act_ref[:, :inner].astype(f32)
    grow = expander(LANES, inner, per)
    running = run_ref[...]
    state_grad = join_states(far_ref, inner, per)
    lifted = (heads_ref[...] * (jnp.exp(run_exp_ref[...]) * link_ref[...])).astype(bf16)
    dact_ref[:, nstate:] = dot_rows(lifted, in_ref[...].astype(bf16)) + dstate_ref[:, nstate:]
    toward = jnp.exp(running[tokens - 1 :] - running) * end_ref[...]
    toward_exp = spread_lanes(toward, grow)
    pushed = (signal * spread_lanes(step_ref[...] * toward, grow)).astype(bf16)
    leaving_ref[...] = dot_outer(keys, state_grad.astype(bf16)) * toward_exp
    dact_ref[:, :nstate] = dot_rows(pushed, state_grad.astype(bf16)) + dstate_ref[:, :nstate]
    kept = jnp.sum(in_ref[...] * state_grad, axis=1, keepdims=True)
    kept = jnp.sum(head_fold(inner, LANES, per) * kept, axis=0, keepdims=True)
    kept = kept * jnp.exp(running[tokens - 1 :]) * link_ref[tokens - 1 :]
    kept_ref[...] = jnp.broadcast_to(kept, kept_ref.shape)

    def conv(i, _):
        at = pl.multiple_of(i * LANES, LANES)
        drows = conv_back(value_ref, 2 * inner + at, taps_ref, same_ref, dact_ref[:, pl.ds(at, LANES)],
                          inner + at, dtaps_ref, tokens)
        rows_ref[:, pl.ds(at, LANES)] = drows.astype(bf16)
        return 0

    lax.fori_loop(0, 2 * nstate // LANES, conv, 0)


def signal_back_part(heads_ref, act_ref, step_ref, value_ref, taps_ref, same_ref, bias_ref,
                       decay_ref, skip_ref, mixer_ref, inner_ref, dscaled_ref, drun_ref, leaving_ref,
                       kept_ref, zgrad_ref, state_ref,
                       grad_ref, dtaps_ref, small_ref, dact_ref, middle, between, *, inner, nstate, per):
    tokens = act_ref.shape[0]
    signal = act_ref[:, :inner].astype(f32)
    grow = expander(LANES, inner, per)
    folds = head_fold(inner, LANES, per).astype(bf16)
    step = step_ref[...]
    heads = heads_ref[...]
    leaving = leaving_ref[...]
    step_exp = spread_lanes(step, grow)
    dscaled = dscaled_ref[...] + leaving
    dact_ref[...] = dscaled * step_exp + skip_ref[...] * heads

    def conv(i, _):
        at = pl.multiple_of(i * LANES, LANES)
        drows = conv_back(value_ref, inner + at, taps_ref, same_ref, dact_ref[:, pl.ds(at, LANES)], at,
                          dtaps_ref, tokens)
        grad_ref[:, pl.ds(inner + at, LANES)] = drows.astype(bf16)
        return 0

    half = inner // LANES // 2
    lax.fori_loop(0, half, conv, 0)
    middle()
    lax.fori_loop(half, inner // LANES, conv, 0)
    between()
    carried = mixer_ref[...] - inner_ref[...] - skip_ref[...] * signal
    tri = (row_iota((tokens, tokens)) <= col_iota((tokens, tokens))).astype(bf16)
    strict = (row_iota((tokens, tokens)) > col_iota((tokens, tokens))).astype(bf16)
    back_sum = drun_ref[...] + fold_heads(heads * carried, folds)
    front_sum = fold_heads(signal * step_exp * leaving, folds)
    dlog = left_sums(tri, back_sum) + left_sums(strict, front_sum) + kept_ref[0:1, :]
    rate = -jnp.exp(decay_ref[...])
    dstep = dlog * rate + fold_heads(dscaled * signal, folds)
    draw = dstep * sigmoid(value_ref[HALO:, 2 * inner + 2 * nstate :] + bias_ref[...])
    small_ref[0:1, :] = jnp.sum(draw, axis=0, keepdims=True)
    small_ref[1:2, :] = jnp.sum(dlog * step, axis=0, keepdims=True) * rate
    small_ref[2:, :] = jnp.zeros((6, LANES), f32)
    state_at = 2 * inner
    step_at = state_at + 2 * nstate
    grad_ref[:HALO, :inner] = jnp.zeros((HALO, inner), bf16)
    grad_ref[HALO:, :inner] = zgrad_ref[...]
    grad_ref[:, state_at:step_at] = state_ref[...]
    grad_ref[:HALO, step_at:] = jnp.zeros((HALO, LANES), bf16)
    used = col_iota((tokens, LANES)) < inner // per
    grad_ref[HALO:, step_at:] = jnp.where(used, draw, 0.0).astype(bf16)


def rear_kernel(dout_ref, stat_ref, notes_ref, mixer_ref, inner_ref, act_ref, scaled_ref, step_ref,
                run_ref, run_exp_ref, state_ref, taps_ref, same_ref, bias_ref, decay_ref, skip_ref,
                gain_ref, end_ref, link_ref, seg_col_ref, seg_row_ref, packed_ref, mixed_t_ref,
                part_hbm, value_hbm, w_hbm, res_hbm,
                grad_ref, main_ref, early_ref, taps_out, state_all_ref, out_ref,
                dtaps_ref, sums_ref, small_ref, gated_ref, value_ref, w_ref, res_ref, run_t_ref, heads_ref, zgrad_ref, direct_ref, dscaled_ref,
                dstate_ref, drun_ref, scores_ref, dscores_ref, leaving_ref, kept_ref, rows_ref, dact_ref,
                far_ref, part_ref, right_box, left_box, rows_box, sum_box, ext_ref, state_halo, signal_halo,
                local_sem, stage_ref, *sems,
                inner, nstate, per, heads, di_all, n, boxes):
    me = lax.axis_index("tensor")
    weights = WeightSum(stage_ref, sems[:boxes])
    sems = sems[boxes:]
    tokens = act_ref.shape[0]
    quarter = part_ref.shape[1] // n
    own = tokens // n
    wide = value_ref.shape[1]
    groups = [(sems[2 * i], sems[2 * i + 1]) for i in range(4)]
    column = lambda k: pl.ds(pl.multiple_of(k * quarter, LANES), quarter)
    loads = [
        pltpu.make_async_copy(part_hbm, part_ref, local_sem.at[3]),
        pltpu.make_async_copy(w_hbm.at[:, pl.ds(wide, inner)], w_ref, local_sem.at[0]),
        pltpu.make_async_copy(value_hbm, value_ref, local_sem.at[1]),
        pltpu.make_async_copy(res_hbm.at[:, column(me)], res_ref, local_sem.at[2]),
    ]
    for copy in loads:
        copy.start()
    far_ref[...] = jnp.zeros_like(far_ref)
    state_halo[...] = jnp.zeros_like(state_halo)
    signal_halo[...] = jnp.zeros_like(signal_halo)
    rows_barrier(me, n)
    line = LineReduce(me, n, lambda d: part_ref.at[:, column(d)], right_box, left_box,
                      line_groups(sems[8:12]))
    loads[0].wait()
    line.step(0)
    for copy in loads[1:]:
        copy.wait()
    scale = row_columns(stat_ref[0:1, :])
    gates = notes_ref.shape[0] - 8
    cross = row_columns(notes_ref[gates : gates + 1, :])
    back_part(dout_ref, w_ref, mixer_ref, value_ref, act_ref, run_exp_ref, link_ref, gain_ref,
              scale, cross, packed_ref, heads_ref, zgrad_ref, gated_ref, direct_ref, sums_ref,
              inner=inner, nstate=nstate, di_all=di_all)
    states = StatePush(direct_ref, far_ref, groups[0], True)
    states.start()
    weights.product(dout_ref, gated_ref, 0, False)
    weights.to_sibling(0, inner)
    weights.product(mixed_t_ref, zgrad_ref, inner)
    weights.to_sibling(inner, inner)
    line.step(1)
    run_t = run_ref[...].T
    for h in range(heads):
        run_t_ref[h] = run_t[h : h + 1, :]
    intra_back_part(heads_ref, act_ref, scaled_ref, run_t_ref, run_exp_ref, seg_col_ref, seg_row_ref,
                    dscaled_ref, dstate_ref, drun_ref, scores_ref, dscores_ref,
                    inner=inner, nstate=nstate, per=per, block=128)
    line.step(2)
    weights.pair(0, main_ref)
    states.wait_recv()
    state_back_part(heads_ref, act_ref, step_ref, run_ref, run_exp_ref, link_ref, end_ref, value_ref,
                    taps_ref, same_ref, dstate_ref, state_ref, far_ref, rows_ref, dtaps_ref,
                    leaving_ref, kept_ref, dact_ref.at[:, pl.ds(0, 2 * nstate)],
                    inner=inner, nstate=nstate, per=per)
    body = lambda d: pl.ds(pl.multiple_of(HALO + d * own, 16), own)
    reduces, gathers = [], []
    place, count = ctx_place()
    sends, gets = place > 0, place < count - 1
    before = ctx_peer(jnp.maximum(place - 1, 0))
    state_copy = push(rows_ref.at[pl.ds(0, HALO)], state_halo, groups[2], 0, before)
    signal_copy = push(ext_ref.at[pl.ds(0, HALO), pl.ds(inner, inner)], signal_halo, groups[2], 1, before)
    pl.when(sends)(state_copy.start)

    weights.pair(1, main_ref)

    def middle():
        pl.when(gets)(state_copy.wait_recv)
        rows_ref[tokens:, :] = rows_ref[tokens:, :] + state_halo[...]
        for d in range(1, n):
            peer = lax.rem(me + d, n)
            reduces.append(push(rows_ref.at[body(peer)], rows_box.at[d - 1], groups[1], d - 1, peer))
            reduces[-1].start()

    def between():
        pl.when(sends)(signal_copy.start)
        total = rows_ref[body(me), :].astype(f32)
        for copy in reduces:
            copy.wait_recv()
        for d in range(1, n):
            total = total + rows_box[d - 1].astype(f32)
        sum_box[body(me), :] = total.astype(bf16)
        for d in range(1, n):
            peer = lax.rem(me + d, n)
            gathers.append(push(sum_box.at[body(me)], sum_box.at[body(me)], groups[3], d - 1, peer))
            gathers[-1].start()

    signal_back_part(heads_ref, act_ref, step_ref, value_ref, taps_ref, same_ref, bias_ref, decay_ref,
                     skip_ref, mixer_ref, inner_ref, dscaled_ref, drun_ref, leaving_ref, kept_ref,
                     zgrad_ref, rows_ref, ext_ref, dtaps_ref, small_ref, dact_ref, middle, between,
                     inner=inner, nstate=nstate, per=per)
    early_ref[:CONV, :] = dtaps_ref[:, :inner]
    early_ref[CONV : CONV + 2, :] = sums_ref[:2, :]
    early_ref[CONV + 2 :, :] = jnp.zeros((2, inner), f32)
    early_ref[CONV + 2 :, :LANES] = small_ref[:2, :]
    taps_out[:CONV, :] = dtaps_ref[:, inner:]
    taps_out[CONV:, :] = jnp.zeros((8 - CONV, 2 * nstate), f32)
    grad_ref[...] = ext_ref[HALO:, :]
    pl.when(gets)(signal_copy.wait_recv)
    grad_ref[tokens - HALO :, inner : 2 * inner] = (
        ext_ref[tokens:, inner : 2 * inner] + signal_halo[...]
    )
    for t in range(3, n):
        line.step(t)
    out_ref[...] = (line.total() + res_ref[...].astype(f32)).astype(bf16)
    for copy in gathers:
        copy.wait_recv()
    state_all_ref[...] = sum_box[HALO:, :]
    weights.wait_send()
    states.wait_send()
    line.wait_send()
    pl.when(sends)(state_copy.wait_send)
    pl.when(sends)(signal_copy.wait_send)
    for copy in reduces + gathers:
        copy.wait_send()


def rear(vmem_args, part, value, weights, residual, inner, nstate, per, heads, di_all):
    n = lax.axis_size("tensor")
    others = lax.axis_size(CTX) - 1
    ext, wide = value.shape
    tokens = ext - HALO
    depth = residual.shape[1]
    quarter = depth // n
    boxes, main = weight_boxes(depth, 2 * inner, 2, False)
    shape = jax.ShapeDtypeStruct
    outs = [
        shape((tokens, wide), bf16), main, shape((8, inner), f32), shape((8, 2 * nstate), f32),
        shape((tokens, 2 * nstate), bf16),
        shape((tokens, quarter), bf16),
    ]
    dma = pltpu.SemaphoreType.DMA
    return pl.pallas_call(
        partial(rear_kernel, inner=inner, nstate=nstate, per=per, heads=heads, di_all=di_all, n=n,
                boxes=len(boxes) - 1),
        in_specs=[VMEM] * len(vmem_args) + [HBM] * 4,
        out_specs=[VMEM] * len(outs),
        out_shape=outs,
        scratch_shapes=[
            pltpu.VMEM((CONV, inner + 2 * nstate), f32), pltpu.VMEM((8, inner), f32),
            pltpu.VMEM((8, LANES), f32), pltpu.VMEM((tokens, inner), bf16),
            pltpu.VMEM((ext, wide), f32), pltpu.VMEM((depth, inner), bf16),
            pltpu.VMEM((tokens, quarter), bf16), pltpu.VMEM((heads, 1, tokens), f32),
            pltpu.VMEM((tokens, inner), f32), pltpu.VMEM((tokens, inner), bf16),
            pltpu.VMEM((inner + 16, nstate), bf16), pltpu.VMEM((tokens, inner), f32),
            pltpu.VMEM((tokens, 2 * nstate), f32), pltpu.VMEM((tokens, LANES), f32),
            pltpu.VMEM((tokens, tokens), f32), pltpu.VMEM((tokens, tokens), f32),
            pltpu.VMEM((tokens, inner), f32), pltpu.VMEM((8, LANES), f32),
            pltpu.VMEM((ext, 2 * nstate), bf16), pltpu.VMEM((tokens, inner), f32),
            pltpu.VMEM((others, inner + 16, nstate), bf16),
            pltpu.VMEM((tokens, depth), bf16),
            pltpu.VMEM((n, tokens, quarter), bf16), pltpu.VMEM((n, tokens, quarter), bf16),
            pltpu.VMEM((n - 1, tokens // n, 2 * nstate), bf16),
            pltpu.VMEM((ext, 2 * nstate), bf16), pltpu.VMEM((ext, wide), bf16),
            pltpu.VMEM((HALO, 2 * nstate), bf16), pltpu.VMEM((HALO, inner), bf16),
            dma((4,)),
        ] + boxes + [
            dma((others,)), dma((others,)), dma((n - 1,)), dma((n - 1,)), dma((2,)), dma((2,)),
            dma((n - 1,)), dma((n - 1,)),
        ] + line_sems(n),
        compiler_params=pltpu.CompilerParams(
            vmem_limit_bytes=63 << 20, collective_id=5, has_side_effects=True
        ),
        cost_estimate=cost(50),
        name="rear",
    )(*vmem_args, part, value, weights, residual)


def swiglu(first, second):
    sig = sigmoid(first)
    act = first * sig
    return act, sig * (1.0 + first * (1.0 - sig)), (act * second).astype(bf16)


def experts_kernel(mix_ref, mix_t_ref, cot_ref, gates_ref, router_ref, w_ref, shared_hbm,
                   dgate_t_ref, out_hbm, dmix_hbm, dw_hbm, dgate_ref, total_ref, grads_ref, down_ref, hidden_ref, dval_ref,
                   grad_ref, shared_ref, first_ref, second_ref, result_ref, extra_ref, local_sem, *remote,
                   tile, senders, core):
    step = pl.program_id(0)
    last = step == pl.num_programs(0) - 1
    rows, depth = mix_ref.shape
    place = row_place()
    far_send, far_receive, near_send, near_receive, keep_sem, *remote = remote
    gather = RowGather(shared_hbm, shared_ref, ((far_send, far_receive), (near_send, near_receive)))
    own_copy = pltpu.make_async_copy(shared_hbm, shared_ref.at[place], local_sem.at[0])
    if core == 2:
        inbox, shared_in, send, receive, pair_sem = remote
        me = lax.axis_index("core")
        slot = lax.rem(step + me, 2)
        pair_copy = lambda k: push(grad_ref.at[1], inbox.at[k], (send, receive), k, {"core": 1 - me})
        span = 3 * depth // 2
        mine = pl.ds(pl.multiple_of(me * span, 16), span)
        theirs = pl.ds(pl.multiple_of((1 - me) * span, 16), span)
        shared_copy = push(extra_ref.at[theirs], shared_in, (send, receive), senders // 2,
                           {"core": 1 - me})
        keep_copy = lambda k: pltpu.make_async_copy(
            inbox.at[k], dw_hbm.at[k, pl.ds(0, 3 * depth)], pair_sem.at[k]
        )
    else:
        slot = 0

    @pl.when(step == 0)
    def _():
        own_copy.start()
        barrier = pltpu.get_barrier_semaphore()
        cy, chips = lax.axis_size("cy"), lax.axis_size(CHIPS)
        chip = lax.axis_index("shard") * cy + lax.axis_index("cy")
        for d in range(1, chips):
            peer = lax.rem(chip + d, chips)
            pl.semaphore_signal(barrier, inc=1, device_id={"shard": peer // cy, "cy": lax.rem(peer, cy)},
                                device_id_type=MESH)
        if core == 2:
            pl.semaphore_signal(barrier, inc=1, device_id={"core": 1 - me}, device_id_type=MESH)
        pl.semaphore_wait(barrier, chips - 1 + core - 1)
        gather.start()
        total_ref[...] = jnp.zeros_like(total_ref)
        grads_ref[...] = jnp.zeros_like(grads_ref)
        dgate_ref[...] = jnp.zeros_like(dgate_ref)
        own_copy.wait()

    if core == 2:
        @pl.when((step >= 2) & (step < senders) & (slot == 1))
        def _():
            pair_copy((step - 2) // 2).wait_send()

    kept_at = lambda k: 2 * lax.rem(k, 2)
    buffer = jnp.where(slot == 1, 1, kept_at(step // 2)) if core == 2 else 0

    @pl.when(step < senders)
    def _():
        pair_grads(
            step, buffer, mix_ref, mix_t_ref, cot_ref, gates_ref, w_ref, dgate_ref, total_ref, grads_ref,
            down_ref, hidden_ref, dval_ref, grad_ref, tile
        )

    @pl.when(step == 1)
    def _():
        gather.relay()

    @pl.when(step == 2)
    def _():
        gather.finish()

    if core == 2:
        @pl.when((step < senders) & (slot == 1))
        def _():
            pair_copy(step // 2).start()

        def add_sibling(at):
            pair_copy(at).wait_recv()
            inbox[at] = grad_ref[kept_at(at)] + inbox[at]
            keep_copy(at).start()

        @pl.when((step >= 2) & (slot == 0))
        def _():
            add_sibling((step - 2) // 2)

        @pl.when(last)
        def _():
            pair_copy(senders // 2 - 1).wait_send()
    else:
        @pl.when(step < senders)
        def _():
            copy = pltpu.make_async_copy(
                grad_ref.at[0], dw_hbm.at[step, pl.ds(0, 3 * depth)], local_sem.at[3]
            )
            copy.start()
            copy.wait()

    @pl.when(step == 3)
    def _():
        wide = w_ref.shape[2]
        hid = wide // 2
        wrows = depth // senders
        for p in range(2):
            first_ref[p] = shared_ref[:, p * wrows : (p + 1) * wrows, :].reshape(depth, wide)
        second_ref[...] = shared_ref[:, 2 * wrows :, :].reshape(depth, wide)
        raw = dot_rows(cot_ref[...], second_ref[...])
        for p in range(2):
            value = dot_rows(mix_ref[...], first_ref[p])
            act, slope, hidden = swiglu(value[:, :hid], value[:, hid:])
            dh = raw[:, p * hid : (p + 1) * hid]
            dval_ref[p, :, :hid] = (dh * value[:, hid:] * slope).astype(bf16)
            dval_ref[p, :, hid:] = (dh * act).astype(bf16)
            hidden_ref[:, p * hid : (p + 1) * hid] = hidden
        total_ref[...] += dot_outer(hidden_ref[...], second_ref[...])
        grads_ref[...] += dot_outer(dval_ref[0], first_ref[0]) + dot_outer(dval_ref[1], first_ref[1])
        for k in range(3):
            if k < 2:
                grad = dot_rows(mix_t_ref[...], dval_ref[k]).astype(bf16)
            else:
                grad = dot_inner(cot_ref[...], hidden_ref[...]).astype(bf16)
            for j in range(senders):
                at = (3 * ((j % core) * (senders // core) + j // core) + k) * wrows
                extra_ref[at : at + wrows, :] = grad[j * wrows : (j + 1) * wrows]
        if core == 2:
            shared_copy.start()

    @pl.when(last)
    def _():
        result_ref[...] = total_ref[...].astype(bf16)
        out_copy = pltpu.make_async_copy(result_ref, out_hbm, local_sem.at[2])
        out_copy.start()
        copies = [out_copy]
        part = 3 * (depth // senders)
        source = extra_ref
        if core == 2:
            shared_copy.wait_recv()
            shared_in[...] = shared_in[...] + extra_ref[mine, :]
            source = shared_in
        kept = senders // core
        for j in range(kept):
            copies.append(pltpu.make_async_copy(
                source.at[pl.ds(j * part, part)], dw_hbm.at[j, pl.ds(3 * depth, part)], keep_sem.at[j]
            ))
            copies[-1].start()
        gates = gates_ref[...]
        dgate = dgate_ref[...]
        inside = jnp.sum(gates * dgate, axis=1, keepdims=True)
        dlogits = (gates * (dgate - inside)).astype(bf16)
        out_copy.wait()
        result_ref[...] = (grads_ref[...] + dot_outer(dlogits, router_ref[...])).astype(bf16)
        dmix_copy = pltpu.make_async_copy(result_ref, dmix_hbm, local_sem.at[4])
        dmix_copy.start()
        dgate_t_ref[...] = dgate.T[: dgate_t_ref.shape[0], :]
        if core == 2:
            pl.when(slot == 1)(lambda: add_sibling(senders // 2 - 1))
        for copy in copies[1:] + [dmix_copy]:
            copy.wait()
        if core == 2:
            for k in range(kept):
                keep_copy(k).wait()
            shared_copy.wait_send()


def pair_grads(step, slot, mix_ref, mix_t_ref, cot_ref, gates_ref, w_ref, dgate_ref, total_ref, grads_ref,
               down_ref, hidden_ref, dval_ref, grad_ref, tile):
    rows, depth = mix_ref.shape
    wide = w_ref.shape[2]
    hid = wide // 2
    chunks = depth // wide
    deep = depth + depth // 2
    for p in range(2):
        for c in range(chunks):
            down_ref[p * hid : (p + 1) * hid, c * wide : (c + 1) * wide] = (
                w_ref[0, p * deep + depth + c * hid : p * deep + depth + (c + 1) * hid, :]
            )
    down = down_ref[...]

    def part(i, _):
        at = pl.ds(pl.multiple_of(i * tile, tile), tile)
        mix = mix_ref[at, :]
        raw = dot_outer(cot_ref[at, :], down)
        gates = gates_ref[at, :]
        lane = col_iota(gates.shape)
        dmix, noted = None, jnp.zeros_like(gates)
        for p in range(2):
            here = lane == 2 * step + p
            gate = jnp.sum(jnp.where(here, gates, 0.0), axis=1, keepdims=True)
            weights = w_ref[0, p * deep : p * deep + depth, :]
            value = dot_rows(mix, weights)
            act, slope, hidden = swiglu(value[:, :hid], value[:, hid:])
            hidden = hidden.astype(f32)
            dh = raw[:, p * hid : (p + 1) * hid]
            noted = noted + jnp.where(here, jnp.sum(hidden * dh, axis=1, keepdims=True), 0.0)
            dh = gate * dh
            dval_ref[p, at, :hid] = (dh * value[:, hid:] * slope).astype(bf16)
            dval_ref[p, at, hid:] = (dh * act).astype(bf16)
            hidden_ref[at, p * hid : (p + 1) * hid] = (gate * hidden).astype(bf16)
            term = dot_outer(dval_ref[p, at, :], weights)
            dmix = term if dmix is None else dmix + term
        dgate_ref[at, :] += noted
        total_ref[at, :] += dot_rows(hidden_ref[at, :], down)
        grads_ref[at, :] += dmix
        return 0

    lax.fori_loop(0, rows // tile, part, 0)
    hidden_t = hidden_ref[...].T
    for c in range(chunks):
        grad = dot_rows(hidden_t, cot_ref[:, c * wide : (c + 1) * wide]).astype(bf16)
        for p in range(2):
            first = p * deep + depth + c * hid
            grad_ref[slot, first : first + hid, :] = grad[p * hid : (p + 1) * hid]
    for p in range(2):
        grad_ref[slot, p * deep : p * deep + depth, :] = (
            dot_rows(mix_t_ref[...], dval_ref[p]).astype(bf16)
        )


def experts(mix, mix_t, cot, gates, weights, router_at, experts_w, shared):
    senders, deep, wide = experts_w.shape
    rows, depth = mix.shape
    core, chips = lax.axis_size("core"), lax.axis_size(CHIPS)
    kept = senders // core
    kinds = 2 * senders + -2 * senders % 8
    shape = jax.ShapeDtypeStruct
    dma = pltpu.SemaphoreType.DMA
    once = lambda a: pl.BlockSpec(a.shape, lambda i: (0,) * a.ndim, pipeline_mode=pl.Buffered(1))
    outs = [shape((kinds, rows), f32)]
    remote = []
    if core == 2:
        remote = [pltpu.VMEM((kept, deep, wide), bf16), pltpu.VMEM((deep // 2, wide), bf16),
                  dma((kept + 1,)), dma((kept + 1,)), dma((kept,))]
    return pl.pallas_call(
        partial(experts_kernel, tile=rows, senders=senders, core=core),
        grid=(senders + 1,),
        in_specs=[once(mix), once(mix_t), once(cot), once(gates),
                  pl.BlockSpec((depth, LANES), lambda i: (0, router_at // LANES)),
                  pl.BlockSpec((1, deep, wide), lambda i: (jnp.minimum(i, senders - 1), 0, 0)), HBM],
        out_specs=[whole(o) for o in outs] + [HBM] * 3,
        out_shape=outs + [
            shape((rows, depth), bf16), shape((rows, depth), bf16),
            shape((kept, deep + shared.shape[0], wide), bf16),
        ],
        scratch_shapes=[
            pltpu.VMEM((rows, LANES), f32),
            pltpu.VMEM((rows, depth), f32), pltpu.VMEM((rows, depth), f32),
            pltpu.VMEM((wide, depth), bf16), pltpu.VMEM((rows, wide), bf16),
            pltpu.VMEM((2, rows, wide), bf16), pltpu.VMEM((2 * core - 1, deep, wide), bf16),
            pltpu.VMEM((senders,) + shared.shape, bf16), pltpu.VMEM((2, depth, wide), bf16),
            pltpu.VMEM((depth, wide), bf16), pltpu.VMEM((rows, depth), bf16), pltpu.VMEM((deep, wide), bf16), dma((5,)),
            dma((max(chips - 1, 1),)), dma((max(chips - 1, 1),)), dma((chips,)), dma((chips,)),
            dma((kept,)),
        ] + remote,
        compiler_params=pltpu.CompilerParams(
            vmem_limit_bytes=63 << 20, collective_id=4, has_side_effects=True
        ),
        cost_estimate=cost(7 * senders),
        name="experts",
    )(mix, mix_t, cot, gates, weights, experts_w, shared)


def local(
    block_input, gain_input, proj_main, proj_state, proj_step, conv_main, conv_state, step_bias,
    decay_log, skip_gain, gain_gate, proj_out, gain_mix, router_weight, shared_gates, shared_down,
    expert_gates, expert_down, segments, routes, cotangent,
):
    tokens, quarter = block_input.shape
    heads = step_bias.shape[0]
    inner = conv_main.shape[1]
    nstate = conv_state.shape[1] // 2
    per = inner // heads
    tensors = lax.axis_size("tensor")
    zi = lax.axis_index("tensor")
    senders = lax.axis_size(ROWS)
    depth = quarter * tensors
    di_all = inner * tensors
    own = tokens // tensors
    column = zi * quarter
    row0 = zi * own
    wrows = proj_main.shape[0]
    hid = expert_gates.shape[3]
    local_experts = expert_gates.shape[0]
    experts_all = local_experts * senders
    shared_here = shared_down.shape[1]
    router_pad = -experts_all % LANES

    main_wide = 2 * inner + 2 * nstate + LANES
    router_at = main_wide + inner
    weights = gather_rows(
        jnp.concatenate(
            [proj_main[:, 0], proj_main[:, 1], proj_state,
             jnp.pad(proj_step, ((0, 0), (0, LANES - heads))), proj_out,
             jnp.pad(router_weight, ((0, 0), (0, router_pad)))], axis=1
        )
    )
    pair_down = expert_down.reshape(local_experts, hid, depth // (2 * hid), 2 * hid)
    pair = jnp.concatenate(
        [expert_gates.reshape(local_experts, depth, 2 * hid),
         pair_down.transpose(0, 2, 1, 3).reshape(local_experts, -1, 2 * hid)], axis=1
    )
    shared_pair = shared_gates.reshape(wrows, 2, 2, shared_here // 2).transpose(2, 0, 1, 3)
    experts_w = gather_rows(pair.reshape(1, -1, 2 * hid))
    shared_local = jnp.concatenate([shared_pair.reshape(-1, shared_here), shared_down], axis=0)

    seg_row = segments[0]
    halo_seg = shifted(seg_row[tokens - CONV + 1 :], CTX, 1)
    gains = jnp.concatenate(
        [gain_input[None], gain_mix[None], jnp.zeros((14, quarter), bf16)], axis=0
    )
    mixed_ext, mixed_t, got, gain_rows = intake(block_input, gains)
    gain_row, gain_mid = gain_rows[0:1], gain_rows[1:2]

    segments_ext = jnp.concatenate([halo_seg, seg_row], axis=0)
    same = jnp.stack(
        [segments_ext[offset : offset + tokens] == seg_row for offset in range(CONV)]
    ).astype(f32)
    same = jnp.broadcast_to(same[:, :, None], (CONV, tokens, LANES))
    taps = jnp.concatenate([conv_main, conv_state], axis=1).astype(f32)
    lanes = lambda v: jnp.pad(v, (0, LANES - heads))[None]
    bias = lanes(step_bias)
    decay = lanes(decay_log)
    skip = jnp.repeat(skip_gain, per)[None]
    link = (seg_row == halo_seg[-1]).astype(f32)[:, None]
    at_end = (seg_row == seg_row[-1]).astype(f32)[:, None]
    seg_col = seg_row[:, None]
    seg_line = seg_row[None]
    chosen = jnp.any(
        routes[:, :, None] == jnp.arange(LANES, dtype=jnp.int32)[None, None, :], axis=1
    ).astype(f32)
    gain_gate_f = gain_gate.astype(f32)[None, :]
    (value, act, scaled, step, running, run_exp, within, mixer, state_in, packed, residual, scale_rows,
     own_part, cot_full, mix, mix_t, gates) = front(
        mixed_ext, taps, same, bias, decay, at_end, link, seg_col, seg_line, skip, gain_gate_f, got,
        cotangent, gain_mid, chosen, weights, inner, nstate, per, heads, di_all
    )

    dgate, out_part, dmix_part, dw = experts(
        mix, mix_t, cot_full, gates, weights, router_at, experts_w, shared_local
    )
    expert_rows = scatter_chips(dw.reshape(-1, 2 * hid))
    dmixer, notes, gains_mid = turn_step(
        dmix_part, dgate, residual, cot_full, own_part, gain_mid
    )

    value_grad, rear_main, early, state_taps, state_all, output = rear(
        (dmixer, scale_rows, notes, mixer, within, act, scaled, step, running, run_exp, state_in, taps,
         same, bias, decay, skip, gain_gate_f, at_end, link, seg_col, seg_line, packed,
         mixed_t),
        out_part, value, weights, residual, inner, nstate, per, heads, di_all
    )
    first = 2 * inner
    last = first + 2 * nstate
    rear_main, expert_rows = lax.optimization_barrier((rear_main, expert_rows))
    rear_main = scatter_chips(rear_main)

    grad_input, early, late, main = last_step(
        (value_grad, got, dmixer, gain_row, gains_mid, state_taps, early, mixed_t, mix_t, state_all,
         gates, notes),
        weights, inner, last,
    )
    if lax.axis_size("core") != 2:
        main = scatter_chips(main)
    (output, grad_input, grad_gain_in, grad_main, grad_state, grad_step, grad_conv, grad_conv_state,
     grad_bias, grad_decay, grad_skip, grad_gate, grad_proj_out, grad_gain_mid, grad_router, grad_shared,
     grad_shared_down, grad_gates, grad_down) = emit(
        (output, grad_input, early, late, rear_main, main, expert_rows), inner, nstate, per, heads, experts_all, hid
    )
    return (
        output,
        grad_input,
        grad_gain_in.reshape(quarter),
        grad_main,
        grad_state,
        grad_step.T,
        grad_conv,
        grad_conv_state,
        grad_bias[0],
        grad_decay[0],
        grad_skip[0],
        grad_gate.reshape(inner),
        grad_proj_out,
        grad_gain_mid.reshape(quarter),
        grad_router.T,
        grad_shared,
        grad_shared_down,
        grad_gates.reshape(expert_gates.shape),
        grad_down,
    )


def solution(mesh):
    shard, ctx, tensor = (mesh.shape[name] for name in ("shard", "ctx", "tensor"))
    core = 2 if shard * ctx == 8 else 1
    split = jax.sharding.Mesh(
        mesh.devices.reshape(shard, ctx // core, core, tensor), ("shard", "cy", "core", "tensor")
    )
    return jax.shard_map(
        local,
        mesh=split,
        in_specs=(
            P(ROWS, "tensor"),
            P("tensor"),
            P(ROWS, None, "tensor"),
            P(ROWS, None),
            P(ROWS, "tensor"),
            P(None, "tensor"),
            P(),
            P("tensor"),
            P("tensor"),
            P("tensor"),
            P("tensor"),
            P(ROWS, "tensor"),
            P("tensor"),
            P(ROWS, None),
            P(ROWS, None, "tensor"),
            P(ROWS, "tensor"),
            P(ROWS, None, None, "tensor"),
            P(ROWS, "tensor", None),
            P("shard", CTX),
            P(ROWS, None),
            P(ROWS, "tensor"),
        ),
        out_specs=(
            P(ROWS, "tensor"),
            P(ROWS, "tensor"),
            P("tensor"),
            P(ROWS, None, "tensor"),
            P(ROWS, None),
            P(ROWS, "tensor"),
            P(None, "tensor"),
            P(),
            P("tensor"),
            P("tensor"),
            P("tensor"),
            P("tensor"),
            P(ROWS, "tensor"),
            P("tensor"),
            P(ROWS, None),
            P(ROWS, None, "tensor"),
            P(ROWS, "tensor"),
            P(ROWS, None, None, "tensor"),
            P(ROWS, "tensor", None),
        ),
        check_vma=False,
    )
```

```python
from functools import partial

import jax
import jax.numpy as jnp
from jax import lax
from jax.experimental import pallas as pl
from jax.experimental.pallas import tpu as pltpu
from jax.sharding import PartitionSpec as P

CONV = 4
HALO = 16
LANES = 128
LANES = 128
LANES = 128


epsilon = 1e-05
highest = lax.Precision.HIGHEST
CTX = ("cy", "core")
CHIPS = ("shard", "cy")
ROWS = ("shard", "cy", "core")
f32 = jnp.float32
MESH = pl.DeviceIdType.MESH
bf16 = jnp.bfloat16
BIG = pltpu.CompilerParams(vmem_limit_bytes=60 << 20)


def cost(micros):
    return pl.CostEstimate(flops=micros * 900_000_000, transcendentals=0, bytes_accessed=1 << 20)
BIG = pltpu.CompilerParams(vmem_limit_bytes=60 << 20)


def cost(micros):
    return pl.CostEstimate(flops=micros * 900_000_000, transcendentals=0, bytes_accessed=1 << 20)
BIG = pltpu.CompilerParams(vmem_limit_bytes=60 << 20)


def cost(micros):
    return pl.CostEstimate(flops=micros * 900_000_000, transcendentals=0, bytes_accessed=1 << 20)


def shifted(value, axis, steps):
    count = lax.axis_size(axis)
    leading, last = (max(0, -steps), min(count, count - steps))
    return lax.ppermute(value, axis, [(source, source + steps) for source in range(leading, last)])


def dot_rows(left, right, precision=None):
    return jnp.dot(left, right, preferred_element_type=f32, precision=precision)


def dot_inner(left, right):
    return lax.dot_general(left, right, (((0,), (0,)), ((), ())), preferred_element_type=f32)


def dot_outer(left, right):
    return lax.dot_general(left, right, (((1,), (1,)), ((), ())), preferred_element_type=f32)


def sigmoid(value):
    return 1.0 / (1.0 + jnp.exp(-value))


def gather_rows(value):
    return lax.all_gather(value, ROWS, axis=0, tiled=True)


def scatter_rows(value):
    return lax.psum_scatter(value, ROWS, scatter_dimension=0, tiled=True)


def scatter_chips(value):
    axes = CHIPS if lax.axis_size("core") == 2 else ROWS
    return lax.psum_scatter(value, axes, scatter_dimension=0, tiled=True)


def exchange(blocks):
    return lax.all_to_all(blocks, "tensor", split_axis=0, concat_axis=0, tiled=True)


def spread(block):
    count = lax.axis_size("tensor")
    return exchange(jnp.broadcast_to(block[None], (count,) + block.shape))


def spread_small(block):
    count, index = lax.axis_size("tensor"), lax.axis_index("tensor")
    width = block.shape[1]
    full = jnp.zeros((block.shape[0], count * width), block.dtype)
    for away in range(count):
        moved = block if away == 0 else lax.ppermute(
            block, "tensor", [(i, (i + away) % count) for i in range(count)]
        )
        origin = lax.rem(index - away + count, count)
        full = lax.dynamic_update_slice_in_dim(full, moved, origin * width, 1)
    return full


def halves(value):
    high = value.astype(bf16)
    return high, (value - high.astype(f32)).astype(bf16)


def far_states(packed, reverse):
    count = lax.axis_size(CTX)
    return jnp.stack([
        shifted(packed, CTX, -away if reverse else away) for away in range(1, count)
    ])


def row_iota(shape):
    return lax.broadcasted_iota(jnp.int32, shape, 0)


def col_iota(shape):
    return lax.broadcasted_iota(jnp.int32, shape, 1)


def expander(lanes, width, per):
    low = row_iota((lanes, width)) * per
    at = col_iota((lanes, width))
    return ((at >= low) & (at < low + per)).astype(f32)


def head_fold(width, lanes, per):
    low = col_iota((width, lanes)) * per
    at = row_iota((width, lanes))
    return ((at >= low) & (at < low + per)).astype(f32)


def pack_state(state, through):
    high, low = halves(through)
    row = row_iota((16, LANES))
    tail = jnp.where(row == 0, high.astype(f32), jnp.where(row == 1, low.astype(f32), 0.0))
    return jnp.concatenate([state, tail], axis=0).astype(bf16)


def join_states(far_ref, inner, per):
    spread_heads = head_fold(inner, LANES, per)
    total = None
    for k in reversed(range(far_ref.shape[0])):
        state = far_ref[k, :inner, :].astype(f32)
        if total is not None:
            through = far_ref[k, inner : inner + 16, :].astype(f32)
            through = through[0:1] + through[1:2]
            state = state + jnp.sum(spread_heads * through, axis=1, keepdims=True) * total
        total = state
    return total


def thirds(value):
    high = value.astype(bf16)
    rest = value - high.astype(f32)
    middle = rest.astype(bf16)
    return high, middle, (rest - middle.astype(f32)).astype(bf16)


def spread_lanes(value, grow):
    ones = grow.astype(bf16)
    return sum(dot_rows(part, ones) for part in thirds(value))


def left_sums(zero_one, value):
    return sum(dot_rows(zero_one, part) for part in thirds(value))


def fold_heads(value, folds):
    high, low = halves(value)
    return dot_rows(high, folds) + dot_rows(low, folds)


def conv_pre(value_ref, column, taps_ref, taps_column, same_ref, tokens):
    rows = value_ref[:, pl.ds(column, LANES)]
    total = None
    for offset in range(CONV):
        first = HALO - CONV + 1 + offset
        term = rows[first : first + tokens] * (
            same_ref[offset] * taps_ref[offset : offset + 1, pl.ds(taps_column, LANES)]
        )
        total = term if total is None else total + term
    return rows, total


def enter_part(mixed_ref, w_ref, taps_ref, same_ref, bias_ref, decay_ref, end_ref, link_ref,
                 value_ref, act_ref, scaled_ref, step_ref, run_ref, run_exp_ref,
                 state_ref, *, inner, nstate, per):
    tokens = act_ref.shape[0]
    width = 2 * inner + 2 * nstate + LANES
    tile = 384

    def matmul(i, _):
        columns = pl.ds(pl.multiple_of(i * tile, LANES), tile)
        value_ref[:, columns] = dot_rows(mixed_ref[...], w_ref[:, columns])
        return 0

    lax.fori_loop(0, width // tile, matmul, 0)

    def conv(i, _):
        at = pl.multiple_of(i * LANES, LANES)
        _, total = conv_pre(value_ref, inner + at, taps_ref, at, same_ref, tokens)
        act_ref[:, pl.ds(at, LANES)] = (total * sigmoid(total)).astype(bf16)
        return 0

    lax.fori_loop(0, (inner + 2 * nstate) // LANES, conv, 0)
    raw = value_ref[HALO:, 2 * inner + 2 * nstate :] + bias_ref[...]
    step = jnp.maximum(raw, 0.0) + jnp.log1p(jnp.exp(-jnp.abs(raw)))
    log_decay = step * -jnp.exp(decay_ref[...])
    tri = (row_iota((tokens, tokens)) >= col_iota((tokens, tokens))).astype(bf16)
    running = left_sums(tri, log_decay)
    step_ref[...] = step
    run_ref[...] = running
    grow = expander(LANES, inner, per)
    run_exp_ref[...] = spread_lanes(running, grow)
    signal = act_ref[:, :inner].astype(f32)
    scaled_ref[...] = (signal * spread_lanes(step, grow)).astype(bf16)
    toward = step * jnp.exp(running[tokens - 1 :] - running) * end_ref[...]
    pushed = (signal * spread_lanes(toward, grow)).astype(bf16)
    through = jnp.exp(running[tokens - 1 :]) * link_ref[tokens - 1 :]
    state_ref[...] = pack_state(dot_inner(pushed, act_ref[:, inner : inner + nstate]), through)


def whole(a):
    return pl.BlockSpec(a.shape, lambda i: (0,) * len(a.shape))


def columns(a, width, at=0):
    assert at % width == 0
    return pl.BlockSpec((a.shape[0], width), lambda i: (0, at // width))


def masked_scores(query, keys, seg_col_ref, seg_row_ref, start, stop):
    shape = (stop - start, stop)
    allowed = (row_iota(shape) + start >= col_iota(shape)) & (
        seg_col_ref[start:stop, :1] == seg_row_ref[:, :stop]
    )
    return jnp.where(allowed, dot_outer(query[start:stop], keys[:stop]), 0.0)


def intra_part(act_ref, scaled_ref, run_t_ref, run_exp_ref, seg_col_ref, seg_row_ref,
                 inner_ref, scores_ref, *, inner, nstate, per, block):
    tokens = act_ref.shape[0]
    keys = act_ref[:, inner : inner + nstate]
    query = act_ref[:, inner + nstate :]
    for start in range(0, tokens, block):
        stop = start + block
        scores_ref[start:stop, :stop] = masked_scores(
            query, keys, seg_col_ref, seg_row_ref, start, stop
        )

    def pair(i, _):
        columns = pl.ds(pl.multiple_of(i * LANES, LANES), LANES)
        scaled = scaled_ref[:, columns]
        lane = col_iota(scaled.shape)
        run = run_exp_ref[:, columns]
        for start in range(0, tokens, block):
            stop = start + block
            total = None
            for h in range(LANES // per):
                mine = (lane >= h * per) & (lane < (h + 1) * per)
                vals = jnp.where(mine, scaled, jnp.zeros_like(scaled))[:stop]
                row = run_t_ref[i * (LANES // per) + h, :, :stop]
                decay = jnp.exp(jnp.minimum(run[start:stop, h * per : h * per + 1] - row, 0.0))
                weight = (decay * scores_ref[start:stop, :stop]).astype(bf16)
                term = dot_rows(weight, vals)
                total = term if total is None else total + term
            inner_ref[start:stop, columns] = total
        return 0

    lax.fori_loop(0, inner // LANES, pair, 0)


def row_sums(value):
    folded = value[:, :LANES]
    for at in range(LANES, value.shape[1], LANES):
        folded = folded + value[:, at : at + LANES]
    ones = jnp.ones((8, LANES), bf16)
    high, low = halves(folded)
    return dot_outer(ones, high) + dot_outer(ones, low)


def as_column(row):
    n = row.shape[1]
    eye = row_iota((n, n)) == col_iota((n, n))
    return jnp.sum(jnp.where(eye, row, 0.0), axis=1, keepdims=True)


def tensor_barrier(me, n):
    barrier = pltpu.get_barrier_semaphore()
    for d in range(1, n):
        pl.semaphore_signal(
            barrier, inc=1, device_id={"tensor": lax.rem(me + d, n)}, device_id_type=MESH
        )
    pl.semaphore_wait(barrier, n - 1)


def push(source, target, sems, slot, peer):
    send, receive = sems
    return pltpu.make_async_remote_copy(
        src_ref=source, dst_ref=target, send_sem=send.at[slot], recv_sem=receive.at[slot],
        device_id=peer if isinstance(peer, dict) else {"tensor": peer}, device_id_type=MESH,
    )


def ctx_place():
    core = lax.axis_size("core")
    return lax.axis_index("cy") * core + lax.axis_index("core"), lax.axis_size("cy") * core


def ctx_peer(place):
    core = lax.axis_size("core")
    return {"cy": place // core, "core": lax.rem(place, core)}


def front_barrier(me, n):
    barrier = pltpu.get_barrier_semaphore()
    place, count = ctx_place()
    for d in range(1, n):
        pl.semaphore_signal(
            barrier, inc=1, device_id={"tensor": lax.rem(me + d, n)}, device_id_type=MESH
        )
    for d in range(1, count):
        pl.semaphore_signal(
            barrier, inc=1, device_id=ctx_peer(lax.rem(place + d, count)), device_id_type=MESH
        )
    pl.semaphore_wait(barrier, n - 1 + count - 1)


def rows_barrier(me, n):
    barrier = line_barrier(me, n)
    place, count = row_place(), lax.axis_size(ROWS)
    for d in range(1, count):
        pl.semaphore_signal(barrier, inc=1, device_id=row_peer(lax.rem(place + d, count)),
                            device_id_type=MESH)
    pl.semaphore_wait(barrier, n - 1 + count - 1)


class RowGather:
    def __init__(self, source, full, sems):
        self.cy, self.core = lax.axis_size("cy"), lax.axis_size("core")
        self.chips = lax.axis_size(CHIPS)
        me = lax.axis_index("core")
        chip = lax.axis_index("shard") * self.cy + lax.axis_index("cy")
        slot = lambda c: c * self.core + me
        self.far, self.near = [], []
        for d in range(1, self.chips):
            peer = lax.rem(chip + d, self.chips)
            self.far.append(push(source, full.at[slot(chip)], sems[0], d - 1,
                                 {"shard": peer // self.cy, "cy": lax.rem(peer, self.cy)}))
        if self.core == 2:
            for d in range(self.chips):
                origin = lax.rem(chip - d + self.chips, self.chips)
                self.near.append(push(source if d == 0 else full.at[slot(origin)], full.at[slot(origin)],
                                      sems[1], d, {"core": 1 - me}))

    def start(self):
        for copy in self.far + self.near[:1]:
            copy.start()

    def relay(self):
        for d, copy in enumerate(self.far):
            copy.wait_recv()
            if self.near:
                self.near[d + 1].start()

    def finish(self):
        for copy in self.near:
            copy.wait()
        for copy in self.far:
            copy.wait_send()


class WeightSum:
    def __init__(self, stage, boxes):
        self.stage, self.boxes = stage, boxes
        self.depth = stage.shape[0]
        self.core, self.cy = lax.axis_index("core"), lax.axis_size("cy")
        self.chip = lax.axis_index("shard") * self.cy + lax.axis_index("cy")
        self.chips = boxes[0].shape[0] if boxes else 0
        self.paired = boxes[1:3] if len(boxes) == 3 else boxes[3:5]
        self.owner = boxes[0].shape[1] if boxes else 0
        self.siblings, self.mains, self.units = [], [], []

    def rows(self, k):
        return pl.ds(pl.multiple_of(k * self.owner, 16), self.owner)

    def product(self, lhs_ref, rhs, at, transposed=True):
        span = rhs.shape[1]
        tall = self.depth // 2

        def part(m, _):
            here = pl.ds(pl.multiple_of(m * tall, tall), tall)
            if transposed:
                value = dot_rows(lhs_ref[here, :], rhs[...])
            else:
                value = dot_inner(lhs_ref[:, here], rhs[...])
            self.stage[here, at : at + span] = value.astype(bf16)
            return 0

        lax.fori_loop(0, 2, part, 0)

    def to_sibling(self, at, span):
        unit = len(self.units)
        self.units.append((at, span))
        copies = []
        for j in range(self.chips):
            copies.append(push(
                self.stage.at[self.rows(2 * j + 1 - self.core), pl.ds(at, span)],
                self.boxes[0].at[j, :, pl.ds(at, span)], self.paired, unit * self.chips + j,
                {"core": 1 - self.core},
            ))
            copies[-1].start()
        self.siblings.append(copies)

    def to_chips(self, unit):
        if not self.chips:
            return
        sib_in, sum_ref, main_in = self.boxes[:3]
        at, span = self.units[unit]
        for j, copy in enumerate(self.siblings[unit]):
            copy.wait_recv()
            sum_ref[j * self.owner : (j + 1) * self.owner, at : at + span] = (
                self.stage[self.rows(2 * j + self.core), at : at + span] + sib_in[j, :, at : at + span]
            )
        for d in range(1, self.chips):
            peer = lax.rem(self.chip + d, self.chips)
            self.mains.append(push(
                sum_ref.at[self.rows(peer), pl.ds(at, span)], main_in.at[d - 1, :, pl.ds(at, span)],
                self.boxes[5:7], unit * (self.chips - 1) + d - 1,
                {"shard": peer // self.cy, "cy": lax.rem(peer, self.cy)},
            ))
            self.mains[-1].start()

    def pair(self, unit, out_ref):
        at, span = self.units[unit]
        if not self.chips:
            out_ref[:, at : at + span] = self.stage[:, at : at + span]
            return
        for j, copy in enumerate(self.siblings[unit]):
            copy.wait_recv()
            out_ref[j * self.owner : (j + 1) * self.owner, at : at + span] = (
                self.stage[self.rows(2 * j + self.core), at : at + span]
                + self.boxes[0][j, :, at : at + span]
            )

    def wait_send(self):
        for copies in self.siblings:
            for copy in copies:
                copy.wait_send()

    def finish(self, out_ref):
        if not self.chips:
            out_ref[...] = self.stage[...]
            return
        _, sum_ref, main_in = self.boxes[:3]
        main_in[self.chips - 1] = sum_ref[self.rows(self.chip), :]
        for copy in self.mains:
            copy.wait_recv()
        out_ref[...] = in_order(main_in, self.chip, self.chips)
        self.wait_send()
        for copy in self.mains:
            copy.wait_send()


def weight_boxes(depth, width, units, between_chips=True):
    dma = pltpu.SemaphoreType.DMA
    if lax.axis_size("core") != 2:
        return [pltpu.VMEM((depth, width), bf16)], jax.ShapeDtypeStruct((depth, width), bf16)
    chips = lax.axis_size(CHIPS)
    owner = depth // (2 * chips)
    if not between_chips:
        return [
            pltpu.VMEM((depth, width), bf16), pltpu.VMEM((chips, owner, width), bf16),
            dma((units * chips,)), dma((units * chips,)),
        ], jax.ShapeDtypeStruct((chips * owner, width), bf16)
    return [
        pltpu.VMEM((depth, width), bf16), pltpu.VMEM((chips, owner, width), bf16),
        pltpu.VMEM((chips * owner, width), bf16), pltpu.VMEM((chips, owner, width), bf16),
        dma((units * chips,)), dma((units * chips,)), dma((units * (chips - 1),)),
        dma((units * (chips - 1),)),
    ], jax.ShapeDtypeStruct((owner, width), f32)


class StatePush:
    def __init__(self, source, far_ref, sems, reverse):
        place, count = ctx_place()
        sign = -1 if reverse else 1
        self.copies = []
        for d in range(1, count):
            to, origin = place + sign * d, place - sign * d
            copy = push(source, far_ref.at[d - 1], sems, d - 1,
                        ctx_peer(lax.rem(to + count, count)))
            self.copies.append((copy, (to >= 0) & (to < count), (origin >= 0) & (origin < count)))

    def start(self):
        for copy, sends, _ in self.copies:
            pl.when(sends)(copy.start)

    def wait_recv(self):
        for copy, _, gets in self.copies:
            pl.when(gets)(copy.wait_recv)

    def wait_send(self):
        for copy, sends, _ in self.copies:
            pl.when(sends)(copy.wait_send)


class LineReduce:
    def __init__(self, me, n, blocks, right, left, sems):
        self.me, self.n, self.blocks, self.right, self.left = me, n, blocks, right, left
        self.right_sems, self.left_sems = sems
        self.keep = lambda d: jnp.minimum(jnp.maximum(d, 0), n - 1)

    def rightward(self, d):
        return push(self.blocks(d), self.right.at[d], self.right_sems, d,
                    jnp.minimum(self.me + 1, self.n - 1))

    def leftward(self, d):
        return push(self.blocks(d), self.left.at[d], self.left_sems, d, jnp.maximum(self.me - 1, 0))

    def step(self, t):
        me, n = self.me, self.n
        ways = []
        if t < n:
            ways.append((n - 1 - t + me, me >= 1, lambda d: d > me, t >= me, self.rightward, self.right))
            ways.append((t - (n - 1 - me), me <= n - 2, lambda d: d < me, t >= n - 1 - me,
                         self.leftward, self.left))
        for d, gets, passes, ready, copy_of, box in ways:
            at = self.keep(d)
            copy = copy_of(at)

            @pl.when(gets & ready)
            def _():
                copy.wait_recv()

            @pl.when(gets & ready & passes(d))
            def _():
                view = self.blocks(at)
                view[...] = view[...] + box[at]

            @pl.when(ready & passes(d))
            def _():
                copy.start()

    def total(self):
        me, n = self.me, self.n
        value = self.blocks(me)[...].astype(f32)
        value = value + jnp.where(me >= 1, self.right[me].astype(f32), 0.0)
        return value + jnp.where(me <= n - 2, self.left[me].astype(f32), 0.0)

    def wait_send(self):
        for d in range(self.n):
            pl.when(self.me < d)(self.rightward(d).wait_send)
            pl.when(self.me > d)(self.leftward(d).wait_send)


class LineGather:
    def __init__(self, me, n, blocks, sems):
        self.me, self.n, self.blocks = me, n, blocks
        self.right_sems, self.left_sems = sems

    def rightward(self, d):
        return push(self.blocks(d), self.blocks(d), self.right_sems, d,
                    jnp.minimum(self.me + 1, self.n - 1))

    def leftward(self, d):
        return push(self.blocks(d), self.blocks(d), self.left_sems, d, jnp.maximum(self.me - 1, 0))

    def step(self, t):
        me, n = self.me, self.n
        from_left, from_right = me - t, me + t
        right = self.rightward(jnp.maximum(from_left, 0))
        left = self.leftward(jnp.minimum(from_right, n - 1))
        if t > 0:
            pl.when(from_left >= 0)(right.wait_recv)
        pl.when((from_left >= 0) & (me <= n - 2))(right.start)
        if t > 0:
            pl.when(from_right <= n - 1)(left.wait_recv)
        pl.when((from_right <= n - 1) & (me >= 1))(left.start)

    def wait_send(self):
        for d in range(self.n):
            pl.when((self.me >= d) & (self.me <= self.n - 2))(self.rightward(d).wait_send)
            pl.when((self.me <= d) & (self.me >= 1))(self.leftward(d).wait_send)


def line_sems(n):
    return [pltpu.SemaphoreType.DMA((n,))] * 4


def line_groups(sems):
    return (sems[0], sems[1]), (sems[2], sems[3])


def line_barrier(me, n):
    barrier = pltpu.get_barrier_semaphore()
    for d in range(1, n):
        pl.semaphore_signal(
            barrier, inc=1, device_id={"tensor": lax.rem(me + d, n)}, device_id_type=MESH
        )
    return barrier


def intake_kernel(x_ref, gains_ref, mixed_ref, mixed_t_ref, full_ref, gain_out,
                  x_box, gains_box, halo_box, *sems, n):
    me = lax.axis_index("tensor")
    place, count = ctx_place()
    rows, quarter = x_ref.shape
    column = lambda d: pl.ds(pl.multiple_of(d * quarter, LANES), quarter)
    gain_sems, halo_sems = (sems[0], sems[1]), (sems[2], sems[3])
    halo_box[...] = jnp.zeros_like(halo_box)
    x_box[:, column(me)] = x_ref[...]
    gains_box[:, column(me)] = gains_ref[...]
    barrier = line_barrier(me, n)
    for away in (1, count - 1):
        for z in range(n):
            pl.semaphore_signal(
                barrier, inc=1, device_id={**ctx_peer(lax.rem(place + away, count)), "tensor": z},
                device_id_type=MESH,
            )
    pl.semaphore_wait(barrier, n - 1 + 2 * n)
    x_line = LineGather(me, n, lambda d: x_box.at[:, column(d)], line_groups(sems[4:8]))
    x_line.step(0)
    gains = [push(gains_box.at[:, column(me)], gains_box.at[:, column(me)], gain_sems, d - 1,
                  lax.rem(me + d, n)) for d in range(1, n)]
    for copy in gains:
        copy.start()
    sends, gets = place < count - 1, place > 0
    halos = []
    for d in range(n):
        peer = {**ctx_peer(jnp.minimum(place + 1, count - 1)), "tensor": lax.rem(me + d, n)}
        halos.append(push(x_ref.at[rows - HALO :], halo_box.at[:, column(me)], halo_sems, d, peer))
        pl.when(sends)(halos[-1].start)
    for t in range(1, n):
        x_line.step(t)
    for copy in gains:
        copy.wait_recv()
    for copy in halos:
        pl.when(gets)(copy.wait_recv)
    gain = gains_box[0:1, :].astype(f32)
    gain_out[...] = gains_box[...].astype(f32)

    def normed(x):
        x = x.astype(f32)
        scale = lax.rsqrt(jnp.mean(x * x, axis=1, keepdims=True) + epsilon)
        return (x * scale * gain).astype(bf16)

    mixed_ref[:HALO, :] = normed(halo_box[...])
    full_ref[...] = x_box[...]
    mixed_ref[HALO:, :] = normed(x_box[...])
    mixed_t_ref[...] = mixed_ref[HALO:, :].T
    for copy in gains:
        copy.wait_send()
    for copy in halos:
        pl.when(sends)(copy.wait_send)
    x_line.wait_send()


def intake(x, gains):
    n = lax.axis_size("tensor")
    rows, quarter = x.shape
    depth = n * quarter
    shape = jax.ShapeDtypeStruct
    dma = pltpu.SemaphoreType.DMA
    return pl.pallas_call(
        partial(intake_kernel, n=n),
        in_specs=[VMEM] * 2,
        out_specs=[VMEM] * 4,
        out_shape=[shape((rows + HALO, depth), bf16), shape((depth, rows), bf16),
                   shape((rows, depth), bf16), shape((16, depth), f32)],
        scratch_shapes=[
            pltpu.VMEM((rows, depth), bf16),
            pltpu.VMEM((16, depth), bf16), pltpu.VMEM((HALO, depth), bf16),
            dma((n - 1,)), dma((n - 1,)), dma((n,)), dma((n,)),
        ] + line_sems(n),
        compiler_params=pltpu.CompilerParams(
            vmem_limit_bytes=60 << 20, collective_id=7, has_side_effects=True
        ),
        cost_estimate=cost(50),
        name="intake",
    )(x, gains)


def row_columns(row):
    return jnp.concatenate(
        [as_column(row[:, at : at + LANES]) for at in range(0, row.shape[1], LANES)], axis=0
    )


def front_kernel(mixed_ref, taps_ref, same_ref, bias_ref, decay_ref, end_ref, link_ref, seg_col_ref,
                 seg_row_ref, skip_ref, gain_ref, x_ref, cot_ref, mid_ref, chosen_ref, w_ref,
                 value_ref, act_ref, scaled_ref, step_ref, run_ref, run_exp_ref, inner_ref, mixer_ref,
                 state_ref, packed_ref, res_ref, stat_ref, own_ref, cot_full_ref, mix_ref, mix_t_ref, gates_ref,
                 wm_ref, wo_ref, run_t_ref, scores_ref, part_ref, square_ref, lifted_ref, far_ref,
                 right_box, left_box, square_box, res_box, stat_box, cot_box, router_ref, local_sem, *sems,
                 inner, nstate, per, heads, di_all, n):
    me = lax.axis_index("tensor")
    rows, depth = x_ref.shape
    own = rows // n
    groups = [(sems[2 * i], sems[2 * i + 1]) for i in range(3)]
    block_at = lambda d: pl.ds(pl.multiple_of(d * own, own), own)
    half = own // 2
    half_at = lambda d, h: pl.ds(pl.multiple_of(d * own + h * half, half), half)
    lines_at = lambda k: line_groups(sems[6 + 4 * k : 10 + 4 * k])
    mine = pl.ds(pl.multiple_of(me * own, own), own)
    wide = wm_ref.shape[1]
    loads = [
        pltpu.make_async_copy(w_ref.at[:, pl.ds(0, wide)], wm_ref, local_sem.at[0]),
        pltpu.make_async_copy(w_ref.at[:, pl.ds(wide, inner)], wo_ref, local_sem.at[1]),
        pltpu.make_async_copy(w_ref.at[:, pl.ds(wide + inner, LANES)], router_ref, local_sem.at[2]),
    ]
    for copy in loads:
        copy.start()
    far_ref[...] = jnp.zeros_like(far_ref)
    quarter = cot_ref.shape[1]
    column = pl.ds(pl.multiple_of(me * quarter, LANES), quarter)
    cot_box[:, column] = cot_ref[...]
    front_barrier(me, n)
    cots = LineGather(
        me, n, lambda d: cot_box.at[:, pl.ds(pl.multiple_of(d * quarter, LANES), quarter)],
        lines_at(0),
    )
    cots.step(0)
    loads[0].wait()
    enter_part(mixed_ref, wm_ref, taps_ref, same_ref, bias_ref, decay_ref, end_ref, link_ref,
               value_ref, act_ref, scaled_ref, step_ref, run_ref, run_exp_ref, packed_ref,
               inner=inner, nstate=nstate, per=per)
    states = StatePush(packed_ref, far_ref, groups[0], False)
    states.start()
    cots.step(1)
    run_t = run_ref[...].T
    for h in range(heads):
        run_t_ref[h] = run_t[h : h + 1, :]
    intra_part(act_ref, scaled_ref, run_t_ref, run_exp_ref, seg_col_ref, seg_row_ref, inner_ref,
               scores_ref, inner=inner, nstate=nstate, per=per, block=128)
    cots.step(2)
    states.wait_recv()
    state = join_states(far_ref, inner, per)
    state_ref[...] = state
    carried = dot_outer(act_ref[:, inner + nstate :], state.astype(bf16)) * (
        jnp.exp(run_exp_ref[...]) * link_ref[...]
    )
    mixer = inner_ref[...] + carried + skip_ref[...] * act_ref[:, :inner].astype(f32)
    mixer_ref[...] = mixer
    z = value_ref[HALO:, :inner]
    gated = mixer * (z * sigmoid(z))
    square_ref[...] = row_sums(gated * gated)
    lifted_ref[...] = (gated * gain_ref[...]).astype(bf16)
    loads[1].wait()
    for t in range(3, n):
        cots.step(t)
    squares, stats = [], []
    for d in range(1, n):
        peer = lax.rem(me + d, n)
        squares.append(push(square_ref.at[:, block_at(peer)], square_box.at[d - 1], groups[1], d - 1, peer))
        squares[-1].start()
    lines = [
        LineReduce(me, n, lambda d, h=h: part_ref.at[d, pl.ds(h * half, half)], right_box.at[h],
                   left_box.at[h], lines_at(1 + h)) for h in range(2)
    ]
    gathers = [LineGather(me, n, lambda d, h=h: res_box.at[half_at(d, h)], lines_at(3 + h))
               for h in range(2)]
    for k in range(n):
        d = jnp.where(2 * me < n, n - 1 - k, k)
        part_ref[d] = dot_outer(lifted_ref[block_at(d), :], wo_ref[...]).astype(bf16)
        if k == 0:
            for line in lines:
                line.step(0)
    square = square_ref[:, mine]
    for copy in squares:
        copy.wait_recv()
    for d in range(1, n):
        square = square + square_box[d - 1]
    scale = lax.rsqrt(square / di_all + epsilon)
    stat_box[:, mine] = scale
    for d in range(1, n):
        stats.append(push(stat_box.at[:, mine], stat_box.at[:, mine], groups[2], d - 1,
                          lax.rem(me + d, n)))
        stats[-1].start()
    scale = as_column(scale[:1])
    for t in range(1, n - 1):
        for line in lines:
            line.step(t)
    for h in range(2):
        lines[h].step(n - 1)
        total = lines[h].total()
        own_ref[h * half : (h + 1) * half, :] = total
        here = half_at(me, h)
        res_box[here, :] = (
            x_ref[here, :].astype(f32) + total * scale[h * half : (h + 1) * half]
        ).astype(bf16)
        gathers[h].step(0)
    for t in range(1, n):
        for gather in gathers:
            gather.step(t)
    cot_full_ref[...] = cot_box[...]
    states.wait_send()
    cots.wait_send()
    for line in lines + gathers:
        line.wait_send()
    for copy in squares:
        copy.wait_send()
    for copy in stats:
        copy.wait()
    res_ref[...] = res_box[...]
    stat_ref[...] = stat_box[...]
    res = res_box[...].astype(f32)
    mix = (
        res * lax.rsqrt(jnp.mean(res * res, axis=1, keepdims=True) + epsilon) * mid_ref[...]
    ).astype(bf16)
    mix_ref[...] = mix
    mix_t_ref[...] = mix.T
    loads[2].wait()
    chosen = chosen_ref[...] > 0.0
    logits = dot_rows(mix, router_ref[...])
    top = jnp.max(jnp.where(chosen, logits, -1e30), axis=1, keepdims=True)
    weight = jnp.where(chosen, jnp.exp(jnp.where(chosen, logits - top, 0.0)), 0.0)
    gates_ref[...] = weight / jnp.sum(weight, axis=1, keepdims=True)


def pairs(count, n):
    return [pltpu.SemaphoreType.DMA((n - 1,))] * (2 * count)


VMEM = pl.BlockSpec(memory_space=pltpu.VMEM)
HBM = pl.BlockSpec(memory_space=pl.ANY)


def front(mixed_ext, taps, same, bias, decay, at_end, link, seg_col, seg_row, skip, gain, x, cot, mid,
          chosen, weights, inner, nstate, per, heads, di_all):
    n = lax.axis_size("tensor")
    others = lax.axis_size(CTX) - 1
    tokens, depth = x.shape
    ext = tokens + HALO
    own = tokens // n
    wide = 2 * inner + 2 * nstate + LANES
    shape = jax.ShapeDtypeStruct
    outs = [
        shape((ext, wide), f32), shape((tokens, inner + 2 * nstate), bf16),
        shape((tokens, inner), bf16), shape((tokens, LANES), f32), shape((tokens, LANES), f32),
        shape((tokens, inner), f32), shape((tokens, inner), f32), shape((tokens, inner), f32),
        shape((inner, nstate), f32), shape((inner + 16, nstate), bf16),
        shape((tokens, depth), bf16), shape((8, tokens), f32), shape((own, depth), f32),
        shape((tokens, depth), bf16), shape((tokens, depth), bf16), shape((depth, tokens), bf16),
        shape((tokens, LANES), f32),
    ]
    dma = pltpu.SemaphoreType.DMA
    return pl.pallas_call(
        partial(front_kernel, inner=inner, nstate=nstate, per=per, heads=heads, di_all=di_all, n=n),
        in_specs=[VMEM] * 15 + [HBM],
        out_specs=[VMEM] * 17,
        out_shape=outs,
        scratch_shapes=[
            pltpu.VMEM((depth, wide), bf16), pltpu.VMEM((depth, inner), bf16),
            pltpu.VMEM((heads, 1, tokens), f32), pltpu.VMEM((tokens, tokens), f32),
            pltpu.VMEM((n, own, depth), bf16), pltpu.VMEM((8, tokens), f32),
            pltpu.VMEM((tokens, inner), bf16), pltpu.VMEM((others, inner + 16, nstate), bf16),
            pltpu.VMEM((2, n, own // 2, depth), bf16), pltpu.VMEM((2, n, own // 2, depth), bf16),
            pltpu.VMEM((n - 1, 8, own), f32),
            pltpu.VMEM((tokens, depth), bf16), pltpu.VMEM((8, tokens), f32),
            pltpu.VMEM((tokens, depth), bf16), pltpu.VMEM((depth, LANES), bf16), dma((3,)),
            dma((others,)), dma((others,)),
        ] + pairs(2, n) + line_sems(n) * 5,
        compiler_params=pltpu.CompilerParams(
            vmem_limit_bytes=63 << 20, collective_id=1, has_side_effects=True
        ),
        cost_estimate=cost(100),
        name="front",
    )(mixed_ext, taps, same, bias, decay, at_end, link, seg_col, seg_row, skip, gain, x, cot, mid,
      chosen, weights)


def turn_kernel(dmix_hbm, dgate_ref, res_ref, cot_ref, own_ref, gain_ref,
                dres_ref, notes_ref, gains_ref,
                dmix_ref, right_box, left_box, gate_box, dres_box, notes_box, load_sem, *sems, n):
    me = lax.axis_index("tensor")
    rows, depth = res_ref.shape
    own = rows // n
    groups = [(sems[2 * i], sems[2 * i + 1]) for i in range(2)]
    block_at = lambda d: pl.ds(pl.multiple_of(d * own, own), own)
    mine = block_at(me)
    load = pltpu.make_async_copy(dmix_hbm, dmix_ref, load_sem)
    load.start()
    tensor_barrier(me, n)
    load.wait()
    half = own // 2
    half_at = lambda d, h: pl.ds(pl.multiple_of(d * own + h * half, half), half)
    lines_at = lambda k: line_groups(sems[4 + 4 * k : 8 + 4 * k])
    lines = [LineReduce(me, n, lambda d, h=h: dmix_ref.at[half_at(d, h)], right_box.at[h],
                        left_box.at[h], lines_at(h)) for h in range(2)]
    gathers = [LineGather(me, n, lambda d, h=h: dres_box.at[half_at(d, h)], lines_at(2 + h))
               for h in range(2)]
    for line in lines:
        line.step(0)
    first, second = [], []
    for d in range(1, n):
        peer = lax.rem(me + d, n)
        first.append(push(dgate_ref.at[:, block_at(peer)], gate_box.at[d - 1], groups[0], d - 1, peer))
        first[-1].start()
    res = res_ref[mine, :].astype(f32)
    scale = lax.rsqrt(jnp.mean(res * res, axis=1, keepdims=True) + epsilon)
    normed = res * scale
    for t in range(1, n - 1):
        for line in lines:
            line.step(t)
    gain_sum = None
    for h in range(2):
        lines[h].step(n - 1)
        dmix = lines[h].total()
        part = slice(h * half, (h + 1) * half)
        here = half_at(me, h)
        lifted = dmix * gain_ref[...]
        inside = jnp.mean(lifted * normed[part], axis=1, keepdims=True)
        dres_box[here, :] = (
            cot_ref[here, :].astype(f32) + scale[part] * (lifted - normed[part] * inside)
        ).astype(bf16)
        gathers[h].step(0)
        term = jnp.sum(dmix * normed[part], axis=0, keepdims=True)
        gain_sum = term if gain_sum is None else gain_sum + term
    gains_ref[...] = jnp.broadcast_to(gain_sum, gains_ref.shape)
    dgate = dgate_ref[:, mine]
    for copy in first:
        copy.wait_recv()
    for d in range(1, n):
        dgate = dgate + gate_box[d - 1]
    gates = dgate.shape[0]
    notes_box[:gates, mine] = dgate
    notes_box[gates:, mine] = row_sums(dres_box[mine, :].astype(f32) * own_ref[...])
    for d in range(1, n):
        peer = lax.rem(me + d, n)
        second.append(push(notes_box.at[:, mine], notes_box.at[:, mine], groups[1], d - 1, peer))
        second[-1].start()
    for t in range(1, n):
        for gather in gathers:
            gather.step(t)
    for line in lines + gathers:
        line.wait_send()
    for copy in first:
        copy.wait_send()
    for copy in second:
        copy.wait()
    dres_ref[...] = dres_box[...]
    notes_ref[...] = notes_box[...]


def turn_step(dmix, dgate, residual, cot, own_part, gain):
    n = lax.axis_size("tensor")
    tokens, depth = dmix.shape
    own = tokens // n
    shape = jax.ShapeDtypeStruct
    return pl.pallas_call(
        partial(turn_kernel, n=n),
        in_specs=[HBM] + [VMEM] * 5,
        out_specs=[VMEM] * 3,
        out_shape=[shape((tokens, depth), bf16), shape((dgate.shape[0] + 8, tokens), f32),
                   shape((8, depth), f32)],
        scratch_shapes=[
            pltpu.VMEM((tokens, depth), bf16),
            pltpu.VMEM((2, n, own // 2, depth), bf16), pltpu.VMEM((2, n, own // 2, depth), bf16),
            pltpu.VMEM((n - 1, dgate.shape[0], own), f32),
            pltpu.VMEM((tokens, depth), bf16), pltpu.VMEM((dgate.shape[0] + 8, tokens), f32),
            pltpu.SemaphoreType.DMA,
        ] + pairs(2, n) + line_sems(n) * 4,
        compiler_params=pltpu.CompilerParams(
            vmem_limit_bytes=60 << 20, collective_id=2, has_side_effects=True
        ),
        cost_estimate=cost(60),
        name="turn_step",
    )(dmix, dgate, residual, cot, own_part, gain)


def in_order(box, me, count):
    total = None
    for source in range(count):
        term = box[lax.rem(me - source + 2 * count - 1, count)].astype(f32)
        total = term if total is None else total + term
    return total


def row_place():
    cy, core = lax.axis_size("cy"), lax.axis_size("core")
    return (lax.axis_index("shard") * cy + lax.axis_index("cy")) * core + lax.axis_index("core")


def row_peer(place):
    cy, core = lax.axis_size("cy"), lax.axis_size("core")
    return {"shard": place // (cy * core), "cy": lax.rem(place // core, cy), "core": lax.rem(place, core)}


def last_kernel(grad_ref, x_ref, dres_ref, gain_ref, mid_ref, state_ref, early_ref, mixed_t_ref, mix_t_ref,
                state_all_ref, gates_ref, notes_ref, w_hbm,
                out_ref, early_out, late_out, main_out,
                w_ref, blocks_ref, right_box, left_box, cross_box, cross_in, gains_box, gains_in, state_in,
                early_in, late_ref, late_in, load_sem, stage_ref, *sems, n, count, boxes, inner, last):
    weights = WeightSum(stage_ref, sems[:boxes])
    sems = sems[boxes:]
    me = lax.axis_index("tensor")
    place = row_place()
    rows, depth = x_ref.shape
    quarter = depth // n
    wide = w_ref.shape[1]
    groups = [(sems[2 * i], sems[2 * i + 1]) for i in range(3)]
    row_groups = [(sems[6 + 2 * i], sems[7 + 2 * i]) for i in range(2)]
    load = pltpu.make_async_copy(w_hbm.at[:, pl.ds(0, wide)], w_ref, load_sem)
    load.start()
    rows_barrier(me, n)
    copies, states, lates = [], [], []
    x = x_ref[...].astype(f32)
    scale = lax.rsqrt(jnp.mean(x * x, axis=1, keepdims=True) + epsilon)
    load.wait()
    half = rows // 2
    lines = [
        LineReduce(me, n, lambda d, h=h: blocks_ref.at[d, pl.ds(h * half, half)], right_box.at[h],
                   left_box.at[h], line_groups(sems[10 + 4 * h : 14 + 4 * h])) for h in range(2)
    ]
    cross = jnp.zeros((8, rows), f32)
    for k in range(n):
        d = jnp.where(2 * me < n, n - 1 - k, k)
        theirs = pl.ds(pl.multiple_of(d * quarter, LANES), quarter)
        w = w_ref[theirs, :]
        block = dot_outer(grad_ref[...], w)
        blocks_ref[d] = block.astype(bf16)
        if k == 0:
            for line in lines:
                line.step(0)
            weights.product(mixed_t_ref, grad_ref.at[:, pl.ds(inner, inner)], 0)
            weights.to_sibling(0, inner)
        normed = x_ref[:, theirs].astype(f32) * scale
        cross = cross + row_sums(block * normed * gain_ref[:, theirs])
        gains_box[d] = jnp.where(
            row_iota((8, quarter)) == 0, jnp.sum(block * normed, axis=0, keepdims=True),
            mid_ref[:, theirs],
        )
    weights.to_chips(0)
    cross_box[...] = cross
    sums = []
    for d in range(1, n):
        peer = lax.rem(me + d, n)
        sums.append(push(gains_box.at[peer], gains_in.at[d - 1], groups[0], d - 1, peer))
        sums.append(push(cross_box, cross_in.at[d - 1], groups[1], d - 1, peer))
        states.append(push(state_ref, state_in.at[d - 1], groups[2], d - 1, peer))
    for d in range(1, count):
        copies.append(push(early_ref, early_in.at[d - 1], row_groups[0], d - 1,
                           row_peer(lax.rem(place + d, count))))
    for copy in sums + states + copies:
        copy.start()

    gates = gates_ref[...]
    kinds = notes_ref.shape[0] - 8
    moved = jnp.concatenate(
        [notes_ref[:kinds, :], jnp.zeros((LANES - kinds, gates.shape[0]), f32)], axis=0
    ).T
    inside = jnp.sum(gates * moved, axis=1, keepdims=True)
    first = 2 * inner
    for line in lines:
        line.step(1)
    weights.product(mixed_t_ref, state_all_ref, inner)
    weights.product(mixed_t_ref, grad_ref.at[:, pl.ds(last, LANES)], inner + last - first)
    weights.product(mix_t_ref, (gates * (moved - inside)).astype(bf16), inner + wide - first)
    weights.to_sibling(inner, wide - first + LANES)
    for copy in sums + states:
        copy.wait_recv()
    gains = gains_box[me]
    for d in range(1, n):
        gains = gains + gains_in[d - 1]
        cross = cross + cross_in[d - 1]
    state_in[n - 1] = state_ref[...]
    late_ref[:, :quarter] = gains
    late_ref[:, quarter:] = in_order(state_in, me, n)
    for d in range(1, count):
        lates.append(push(late_ref, late_in.at[d - 1], row_groups[1], d - 1,
                          row_peer(lax.rem(place + d, count))))
        lates[-1].start()
    for t in range(2, n - 1):
        for line in lines:
            line.step(t)
    weights.to_chips(1)
    here = pl.ds(pl.multiple_of(me * quarter, LANES), quarter)
    inside = row_columns(cross[:1]) / depth
    for h in range(2):
        lines[h].step(n - 1)
        part = slice(h * half, (h + 1) * half)
        out_ref[part, :] = dres_ref[part, here].astype(f32) + scale[part] * (
            lines[h].total() * gain_ref[:, here]
            - x_ref[part, here].astype(f32) * scale[part] * inside[part]
        )
    for copy in copies + lates:
        copy.wait_recv()
    early_in[count - 1] = early_ref[...]
    late_in[count - 1] = late_ref[...]
    early_out[...] = in_order(early_in, place, count)
    late_out[...] = in_order(late_in, place, count)
    weights.finish(main_out)
    for copy in copies + states + lates + sums:
        copy.wait_send()
    for line in lines:
        line.wait_send()


def last_step(vmem_args, weights, inner, last):
    value_grad, x, early, state = (vmem_args[i] for i in (0, 1, 6, 5))
    n, count = lax.axis_size("tensor"), lax.axis_size(ROWS)
    tokens, depth = x.shape
    quarter = depth // n
    wide = value_grad.shape[1]
    late = quarter + state.shape[1]
    shape = jax.ShapeDtypeStruct
    dma = pltpu.SemaphoreType.DMA
    boxes, main = weight_boxes(depth, wide - inner + LANES, 2)
    return pl.pallas_call(
        partial(last_kernel, n=n, count=count, boxes=len(boxes) - 1, inner=inner, last=last),
        in_specs=[VMEM] * len(vmem_args) + [HBM],
        out_specs=[VMEM] * 4,
        out_shape=[shape((tokens, quarter), f32), shape(early.shape, f32), shape((8, late), f32), main],
        scratch_shapes=[
            pltpu.VMEM((depth, wide), bf16), pltpu.VMEM((n, tokens, quarter), bf16),
            pltpu.VMEM((2, n, tokens // 2, quarter), bf16), pltpu.VMEM((2, n, tokens // 2, quarter), bf16),
            pltpu.VMEM((8, tokens), f32), pltpu.VMEM((n - 1, 8, tokens), f32),
            pltpu.VMEM((n, 8, quarter), f32), pltpu.VMEM((n - 1, 8, quarter), f32),
            pltpu.VMEM((n,) + state.shape, f32), pltpu.VMEM((count,) + early.shape, f32),
            pltpu.VMEM((8, late), f32), pltpu.VMEM((count, 8, late), f32), dma,
        ] + boxes + pairs(3, n) + [dma((count - 1,))] * 4 + line_sems(n) * 2,
        compiler_params=pltpu.CompilerParams(
            vmem_limit_bytes=62 << 20, collective_id=3, has_side_effects=True
        ),
        cost_estimate=cost(60),
        name="last_step",
    )(*vmem_args, weights)


def emit_kernel(out_ref, grad_ref, early_ref, late_ref, rear_ref, main_ref, *outs, per):
    (out, grad, gain_in, pair_out, state_out, step_out, conv, conv_state, bias, decay, skip, gate, proj,
     gain_mid, router) = outs
    out[...] = out_ref[...]
    grad[...] = grad_ref[...]
    taps, inner = conv.shape
    heads = bias.shape[1]
    quarter = grad.shape[1]
    conv[...] = early_ref[:taps]
    conv_state[...] = late_ref[:taps, quarter:]
    for i in range(inner // LANES):
        gate[i : i + 1, :] = early_ref[taps : taps + 1, i * LANES : (i + 1) * LANES]
    for i in range(quarter // LANES):
        columns = slice(i * LANES, (i + 1) * LANES)
        gain_in[i : i + 1, :] = late_ref[0:1, columns]
        gain_mid[i : i + 1, :] = late_ref[1:2, columns]
    skips = jnp.broadcast_to(early_ref[taps + 1 : taps + 2], (8, inner))
    skip[...] = fold_heads(skips, head_fold(inner, LANES, per).astype(bf16))[:1, :heads]
    bias[...] = early_ref[taps + 2 : taps + 3, :heads]
    decay[...] = early_ref[taps + 3 : taps + 4, :heads]
    last = inner + state_out.shape[1]
    wide = last + LANES
    proj[...] = rear_ref[:, :inner].astype(f32)
    pair_out[:, 0, :] = rear_ref[:, inner:].astype(f32)
    pair_out[:, 1, :] = main_ref[:, :inner].astype(f32)
    state_out[...] = main_ref[:, inner:last].astype(f32)
    step_out[...] = main_ref[:, last:wide].astype(f32).T[:heads, :]
    router[...] = main_ref[:, wide:].astype(f32).T[: router.shape[0], :]


def emit_experts_kernel(pair_ref, shared_up, shared_down, gates, down):
    hid, depth = down.shape[1:]
    wides = 2 * hid
    deep = depth + depth // 2
    for p in range(2):
        top = pair_ref[p * deep : p * deep + depth, :].astype(f32)
        gates[p * depth : (p + 1) * depth, 0, :] = top[:, :hid]
        gates[p * depth : (p + 1) * depth, 1, :] = top[:, hid:]
        for c in range(depth // wides):
            at = p * deep + depth + c * hid
            down[p, :, c * wides : (c + 1) * wides] = pair_ref[at : at + hid, :].astype(f32)
    wrows = shared_down.shape[0]
    part = shared_down.shape[1] // 2
    for p in range(2):
        top = pair_ref[2 * deep + p * wrows : 2 * deep + (p + 1) * wrows, :].astype(f32)
        shared_up[:, 0, p * part : (p + 1) * part] = top[:, :part]
        shared_up[:, 1, p * part : (p + 1) * part] = top[:, part:]
    shared_down[...] = pair_ref[2 * deep + 2 * wrows :, :].astype(f32)


def emit(args, inner, nstate, per, heads, kinds):
    out, grad, _, _, _, main = args
    tokens, quarter = grad.shape
    wrows = main.shape[0]
    flat = lambda *size: jax.ShapeDtypeStruct(size, f32)
    outs = [
        jax.ShapeDtypeStruct(out.shape, bf16), flat(tokens, quarter), flat(quarter // LANES, LANES),
        flat(wrows, 2, inner), flat(wrows, 2 * nstate), flat(heads, wrows), flat(CONV, inner),
        flat(CONV, 2 * nstate), flat(1, heads), flat(1, heads), flat(1, heads),
        flat(inner // LANES, LANES), flat(wrows, inner), flat(quarter // LANES, LANES), flat(kinds, wrows),
    ]
    return pl.pallas_call(
        partial(emit_kernel, per=per),
        in_specs=[VMEM] * 6,
        out_specs=[VMEM] * len(outs),
        out_shape=outs,
        compiler_params=BIG,
        cost_estimate=cost(4),
        name="emit",
    )(*args)


def emit_experts(pair, wrows, hid):
    depth = pair.shape[0] // 3 - wrows
    wide = pair.shape[1]
    flat = lambda *size: jax.ShapeDtypeStruct(size, f32)
    outs = [flat(wrows, 2, wide), flat(wrows, wide), flat(2 * depth, 2, hid), flat(2, hid, depth)]
    return pl.pallas_call(
        emit_experts_kernel,
        in_specs=[VMEM],
        out_specs=[VMEM] * len(outs),
        out_shape=outs,
        compiler_params=BIG,
        cost_estimate=cost(5),
        name="emit_experts",
    )(pair)


def back_part(dout_ref, w_ref, mixer_ref, value_ref, act_ref, run_exp_ref, link_ref, gain_ref,
                scale, cross, through_ref, heads_ref, zgrad_ref, gated_ref, direct_ref, sums_ref,
                *, inner, nstate, di_all):
    mixer = mixer_ref[...]
    z = value_ref[HALO:, :inner]
    sig = sigmoid(z)
    act = z * sig
    gated = mixer * act
    grad = dot_rows(dout_ref[...], w_ref[...])
    gated_ref[...] = (gated * scale * gain_ref[...]).astype(bf16)
    sums_ref[0:1, :] = jnp.sum(grad * gated * scale, axis=0, keepdims=True)
    gated_grad = scale * (grad * gain_ref[...]) - gated * (scale * scale * scale * cross / di_all)
    zgrad_ref[...] = (gated_grad * mixer * (sig * (1.0 + z * (1.0 - sig)))).astype(bf16)
    heads = gated_grad * act
    heads_ref[...] = heads
    sums_ref[1:2, :] = jnp.sum(heads * act_ref[:, :inner].astype(f32), axis=0, keepdims=True)
    sums_ref[2:, :] = jnp.zeros((6, inner), f32)
    carried = (heads * (jnp.exp(run_exp_ref[...]) * link_ref[...])).astype(bf16)
    direct_ref[:inner, :] = dot_inner(carried, act_ref[:, inner + nstate :]).astype(bf16)
    direct_ref[inner:, :] = through_ref[inner:, :]


def intra_back_part(heads_ref, act_ref, scaled_ref, run_t_ref, run_exp_ref, seg_col_ref,
                      seg_row_ref, dscaled_ref, dstate_ref, drun_ref, scores_ref, dscores_ref, *, inner, nstate, per, block):
    tokens = act_ref.shape[0]
    keys = act_ref[:, inner : inner + nstate]
    query = act_ref[:, inner + nstate :]
    for start in range(0, tokens, block):
        stop = start + block
        scores_ref[start:stop, :stop] = masked_scores(
            query, keys, seg_col_ref, seg_row_ref, start, stop
        )
    dscores_ref[...] = jnp.zeros_like(dscores_ref)
    drun_ref[...] = jnp.zeros_like(drun_ref)

    def pair(i, _):
        columns = pl.ds(pl.multiple_of(i * LANES, LANES), LANES)
        scaled = scaled_ref[:, columns]
        heads = heads_ref[:, columns].astype(bf16)
        lane = col_iota(scaled.shape)
        run = run_exp_ref[:, columns]
        dscaled_ref[:, columns] = jnp.zeros((tokens, LANES), f32)
        for h in range(LANES // per):
            head = i * (LANES // per) + h
            mine = (lane >= h * per) & (lane < (h + 1) * per)
            vals = jnp.where(mine, scaled, jnp.zeros_like(scaled))
            grads = jnp.where(mine, heads, jnp.zeros_like(heads))
            pick = (col_iota((block, LANES)) == head).astype(bf16)
            for start in range(0, tokens, block):
                stop = start + block
                row = run_t_ref[head, :, :stop]
                decay = jnp.exp(jnp.minimum(run[start:stop, h * per : h * per + 1] - row, 0.0))
                weight = decay * scores_ref[start:stop, :stop]
                dweight = dot_outer(grads[start:stop], vals[:stop])
                dscores_ref[start:stop, :stop] += dweight * decay
                flow = (dweight * weight).astype(bf16)
                dscaled_ref[:stop, columns] += dot_inner(weight.astype(bf16), grads[start:stop])
                picks = jnp.broadcast_to(pick[:1], (stop, LANES))
                drun_ref[start:stop, :] += dot_rows(flow, picks)
                drun_ref[:stop, :] -= dot_inner(flow, pick)
        return 0

    lax.fori_loop(0, inner // LANES, pair, 0)
    dkeys = jnp.zeros((tokens, nstate), f32)
    dstate_ref[:, :nstate] = dkeys
    for start in range(0, tokens, block):
        stop = start + block
        shape = (block, stop)
        allowed = (row_iota(shape) + start >= col_iota(shape)) & (
            seg_col_ref[start:stop, :1] == seg_row_ref[:, :stop]
        )
        grad = jnp.where(allowed, dscores_ref[start:stop, :stop], 0.0).astype(bf16)
        dstate_ref[start:stop, nstate:] = dot_rows(grad, keys[:stop])
        dstate_ref[:stop, :nstate] += dot_inner(grad, query[start:stop])


def conv_back(value_ref, column, taps_ref, same_ref, dact, at, dtaps_ref, tokens):
    ext = tokens + HALO
    rows, total = conv_pre(value_ref, column, taps_ref, at, same_ref, tokens)
    sig = sigmoid(total)
    dpre = dact * (sig * (1.0 + total * (1.0 - sig)))
    drows = None
    for offset in range(CONV):
        first = HALO - CONV + 1 + offset
        kept = dpre * same_ref[offset]
        dtaps_ref[offset : offset + 1, pl.ds(at, LANES)] = jnp.sum(
            kept * rows[first : first + tokens], axis=0, keepdims=True
        )
        term = kept * taps_ref[offset : offset + 1, pl.ds(at, LANES)]
        after = ext - first - tokens
        pieces = [jnp.zeros((first, LANES), f32), term]
        if after:
            pieces.append(jnp.zeros((after, LANES), f32))
        term = jnp.concatenate(pieces, axis=0)
        drows = term if drows is None else drows + term
    return drows


def state_back_part(heads_ref, act_ref, step_ref, run_ref, run_exp_ref, link_ref, end_ref,
                      value_ref, taps_ref, same_ref, dstate_ref, in_ref, far_ref,
                      rows_ref, dtaps_ref, leaving_ref, kept_ref, dact_ref, *, inner, nstate, per):
    tokens = act_ref.shape[0]
    keys = act_ref[:, inner : inner + nstate]
    signal = act_ref[:, :inner].astype(f32)
    grow = expander(LANES, inner, per)
    running = run_ref[...]
    state_grad = join_states(far_ref, inner, per)
    lifted = (heads_ref[...] * (jnp.exp(run_exp_ref[...]) * link_ref[...])).astype(bf16)
    dact_ref[:, nstate:] = dot_rows(lifted, in_ref[...].astype(bf16)) + dstate_ref[:, nstate:]
    toward = jnp.exp(running[tokens - 1 :] - running) * end_ref[...]
    toward_exp = spread_lanes(toward, grow)
    pushed = (signal * spread_lanes(step_ref[...] * toward, grow)).astype(bf16)
    leaving_ref[...] = dot_outer(keys, state_grad.astype(bf16)) * toward_exp
    dact_ref[:, :nstate] = dot_rows(pushed, state_grad.astype(bf16)) + dstate_ref[:, :nstate]
    kept = jnp.sum(in_ref[...] * state_grad, axis=1, keepdims=True)
    kept = jnp.sum(head_fold(inner, LANES, per) * kept, axis=0, keepdims=True)
    kept = kept * jnp.exp(running[tokens - 1 :]) * link_ref[tokens - 1 :]
    kept_ref[...] = jnp.broadcast_to(kept, kept_ref.shape)

    def conv(i, _):
        at = pl.multiple_of(i * LANES, LANES)
        drows = conv_back(value_ref, 2 * inner + at, taps_ref, same_ref, dact_ref[:, pl.ds(at, LANES)],
                          inner + at, dtaps_ref, tokens)
        rows_ref[:, pl.ds(at, LANES)] = drows.astype(bf16)
        return 0

    lax.fori_loop(0, 2 * nstate // LANES, conv, 0)


def signal_back_part(heads_ref, act_ref, step_ref, value_ref, taps_ref, same_ref, bias_ref,
                       decay_ref, skip_ref, mixer_ref, inner_ref, dscaled_ref, drun_ref, leaving_ref,
                       kept_ref, zgrad_ref, state_ref,
                       grad_ref, dtaps_ref, small_ref, dact_ref, middle, between, *, inner, nstate, per):
    tokens = act_ref.shape[0]
    signal = act_ref[:, :inner].astype(f32)
    grow = expander(LANES, inner, per)
    folds = head_fold(inner, LANES, per).astype(bf16)
    step = step_ref[...]
    heads = heads_ref[...]
    leaving = leaving_ref[...]
    step_exp = spread_lanes(step, grow)
    dscaled = dscaled_ref[...] + leaving
    dact_ref[...] = dscaled * step_exp + skip_ref[...] * heads

    def conv(i, _):
        at = pl.multiple_of(i * LANES, LANES)
        drows = conv_back(value_ref, inner + at, taps_ref, same_ref, dact_ref[:, pl.ds(at, LANES)], at,
                          dtaps_ref, tokens)
        grad_ref[:, pl.ds(inner + at, LANES)] = drows.astype(bf16)
        return 0

    half = inner // LANES // 2
    lax.fori_loop(0, half, conv, 0)
    middle()
    lax.fori_loop(half, inner // LANES, conv, 0)
    between()
    carried = mixer_ref[...] - inner_ref[...] - skip_ref[...] * signal
    tri = (row_iota((tokens, tokens)) <= col_iota((tokens, tokens))).astype(bf16)
    strict = (row_iota((tokens, tokens)) > col_iota((tokens, tokens))).astype(bf16)
    back_sum = drun_ref[...] + fold_heads(heads * carried, folds)
    front_sum = fold_heads(signal * step_exp * leaving, folds)
    dlog = left_sums(tri, back_sum) + left_sums(strict, front_sum) + kept_ref[0:1, :]
    rate = -jnp.exp(decay_ref[...])
    dstep = dlog * rate + fold_heads(dscaled * signal, folds)
    draw = dstep * sigmoid(value_ref[HALO:, 2 * inner + 2 * nstate :] + bias_ref[...])
    small_ref[0:1, :] = jnp.sum(draw, axis=0, keepdims=True)
    small_ref[1:2, :] = jnp.sum(dlog * step, axis=0, keepdims=True) * rate
    small_ref[2:, :] = jnp.zeros((6, LANES), f32)
    state_at = 2 * inner
    step_at = state_at + 2 * nstate
    grad_ref[:HALO, :inner] = jnp.zeros((HALO, inner), bf16)
    grad_ref[HALO:, :inner] = zgrad_ref[...]
    grad_ref[:, state_at:step_at] = state_ref[...]
    grad_ref[:HALO, step_at:] = jnp.zeros((HALO, LANES), bf16)
    used = col_iota((tokens, LANES)) < inner // per
    grad_ref[HALO:, step_at:] = jnp.where(used, draw, 0.0).astype(bf16)


def rear_kernel(dout_ref, stat_ref, notes_ref, mixer_ref, inner_ref, act_ref, scaled_ref, step_ref,
                run_ref, run_exp_ref, state_ref, taps_ref, same_ref, bias_ref, decay_ref, skip_ref,
                gain_ref, end_ref, link_ref, seg_col_ref, seg_row_ref, packed_ref, mixed_t_ref,
                part_hbm, value_hbm, w_hbm, res_hbm,
                grad_ref, main_ref, early_ref, taps_out, state_all_ref, out_ref,
                dtaps_ref, sums_ref, small_ref, gated_ref, value_ref, w_ref, res_ref, run_t_ref, heads_ref, zgrad_ref, direct_ref, dscaled_ref,
                dstate_ref, drun_ref, scores_ref, dscores_ref, leaving_ref, kept_ref, rows_ref, dact_ref,
                far_ref, part_ref, right_box, left_box, rows_box, sum_box, ext_ref, state_halo, signal_halo,
                local_sem, stage_ref, *sems,
                inner, nstate, per, heads, di_all, n, boxes):
    me = lax.axis_index("tensor")
    weights = WeightSum(stage_ref, sems[:boxes])
    sems = sems[boxes:]
    tokens = act_ref.shape[0]
    quarter = part_ref.shape[1] // n
    own = tokens // n
    wide = value_ref.shape[1]
    groups = [(sems[2 * i], sems[2 * i + 1]) for i in range(4)]
    column = lambda k: pl.ds(pl.multiple_of(k * quarter, LANES), quarter)
    loads = [
        pltpu.make_async_copy(part_hbm, part_ref, local_sem.at[3]),
        pltpu.make_async_copy(w_hbm.at[:, pl.ds(wide, inner)], w_ref, local_sem.at[0]),
        pltpu.make_async_copy(value_hbm, value_ref, local_sem.at[1]),
        pltpu.make_async_copy(res_hbm.at[:, column(me)], res_ref, local_sem.at[2]),
    ]
    for copy in loads:
        copy.start()
    far_ref[...] = jnp.zeros_like(far_ref)
    state_halo[...] = jnp.zeros_like(state_halo)
    signal_halo[...] = jnp.zeros_like(signal_halo)
    rows_barrier(me, n)
    line = LineReduce(me, n, lambda d: part_ref.at[:, column(d)], right_box, left_box,
                      line_groups(sems[8:12]))
    loads[0].wait()
    line.step(0)
    for copy in loads[1:]:
        copy.wait()
    scale = row_columns(stat_ref[0:1, :])
    gates = notes_ref.shape[0] - 8
    cross = row_columns(notes_ref[gates : gates + 1, :])
    back_part(dout_ref, w_ref, mixer_ref, value_ref, act_ref, run_exp_ref, link_ref, gain_ref,
              scale, cross, packed_ref, heads_ref, zgrad_ref, gated_ref, direct_ref, sums_ref,
              inner=inner, nstate=nstate, di_all=di_all)
    states = StatePush(direct_ref, far_ref, groups[0], True)
    states.start()
    weights.product(dout_ref, gated_ref, 0, False)
    weights.to_sibling(0, inner)
    weights.product(mixed_t_ref, zgrad_ref, inner)
    weights.to_sibling(inner, inner)
    line.step(1)
    run_t = run_ref[...].T
    for h in range(heads):
        run_t_ref[h] = run_t[h : h + 1, :]
    intra_back_part(heads_ref, act_ref, scaled_ref, run_t_ref, run_exp_ref, seg_col_ref, seg_row_ref,
                    dscaled_ref, dstate_ref, drun_ref, scores_ref, dscores_ref,
                    inner=inner, nstate=nstate, per=per, block=128)
    line.step(2)
    weights.pair(0, main_ref)
    states.wait_recv()
    state_back_part(heads_ref, act_ref, step_ref, run_ref, run_exp_ref, link_ref, end_ref, value_ref,
                    taps_ref, same_ref, dstate_ref, state_ref, far_ref, rows_ref, dtaps_ref,
                    leaving_ref, kept_ref, dact_ref.at[:, pl.ds(0, 2 * nstate)],
                    inner=inner, nstate=nstate, per=per)
    body = lambda d: pl.ds(pl.multiple_of(HALO + d * own, 16), own)
    reduces, gathers = [], []
    place, count = ctx_place()
    sends, gets = place > 0, place < count - 1
    before = ctx_peer(jnp.maximum(place - 1, 0))
    state_copy = push(rows_ref.at[pl.ds(0, HALO)], state_halo, groups[2], 0, before)
    signal_copy = push(ext_ref.at[pl.ds(0, HALO), pl.ds(inner, inner)], signal_halo, groups[2], 1, before)
    pl.when(sends)(state_copy.start)

    weights.pair(1, main_ref)

    def middle():
        pl.when(gets)(state_copy.wait_recv)
        rows_ref[tokens:, :] = rows_ref[tokens:, :] + state_halo[...]
        for d in range(1, n):
            peer = lax.rem(me + d, n)
            reduces.append(push(rows_ref.at[body(peer)], rows_box.at[d - 1], groups[1], d - 1, peer))
            reduces[-1].start()

    def between():
        pl.when(sends)(signal_copy.start)
        total = rows_ref[body(me), :].astype(f32)
        for copy in reduces:
            copy.wait_recv()
        for d in range(1, n):
            total = total + rows_box[d - 1].astype(f32)
        sum_box[body(me), :] = total.astype(bf16)
        for d in range(1, n):
            peer = lax.rem(me + d, n)
            gathers.append(push(sum_box.at[body(me)], sum_box.at[body(me)], groups[3], d - 1, peer))
            gathers[-1].start()

    signal_back_part(heads_ref, act_ref, step_ref, value_ref, taps_ref, same_ref, bias_ref, decay_ref,
                     skip_ref, mixer_ref, inner_ref, dscaled_ref, drun_ref, leaving_ref, kept_ref,
                     zgrad_ref, rows_ref, ext_ref, dtaps_ref, small_ref, dact_ref, middle, between,
                     inner=inner, nstate=nstate, per=per)
    early_ref[:CONV, :] = dtaps_ref[:, :inner]
    early_ref[CONV : CONV + 2, :] = sums_ref[:2, :]
    early_ref[CONV + 2 :, :] = jnp.zeros((2, inner), f32)
    early_ref[CONV + 2 :, :LANES] = small_ref[:2, :]
    taps_out[:CONV, :] = dtaps_ref[:, inner:]
    taps_out[CONV:, :] = jnp.zeros((8 - CONV, 2 * nstate), f32)
    grad_ref[...] = ext_ref[HALO:, :]
    pl.when(gets)(signal_copy.wait_recv)
    grad_ref[tokens - HALO :, inner : 2 * inner] = (
        ext_ref[tokens:, inner : 2 * inner] + signal_halo[...]
    )
    for t in range(3, n):
        line.step(t)
    out_ref[...] = (line.total() + res_ref[...].astype(f32)).astype(bf16)
    for copy in gathers:
        copy.wait_recv()
    state_all_ref[...] = sum_box[HALO:, :]
    weights.wait_send()
    states.wait_send()
    line.wait_send()
    pl.when(sends)(state_copy.wait_send)
    pl.when(sends)(signal_copy.wait_send)
    for copy in reduces + gathers:
        copy.wait_send()


def rear(vmem_args, part, value, weights, residual, inner, nstate, per, heads, di_all):
    n = lax.axis_size("tensor")
    others = lax.axis_size(CTX) - 1
    ext, wide = value.shape
    tokens = ext - HALO
    depth = residual.shape[1]
    quarter = depth // n
    boxes, main = weight_boxes(depth, 2 * inner, 2, False)
    shape = jax.ShapeDtypeStruct
    outs = [
        shape((tokens, wide), bf16), main, shape((8, inner), f32), shape((8, 2 * nstate), f32),
        shape((tokens, 2 * nstate), bf16),
        shape((tokens, quarter), bf16),
    ]
    dma = pltpu.SemaphoreType.DMA
    return pl.pallas_call(
        partial(rear_kernel, inner=inner, nstate=nstate, per=per, heads=heads, di_all=di_all, n=n,
                boxes=len(boxes) - 1),
        in_specs=[VMEM] * len(vmem_args) + [HBM] * 4,
        out_specs=[VMEM] * len(outs),
        out_shape=outs,
        scratch_shapes=[
            pltpu.VMEM((CONV, inner + 2 * nstate), f32), pltpu.VMEM((8, inner), f32),
            pltpu.VMEM((8, LANES), f32), pltpu.VMEM((tokens, inner), bf16),
            pltpu.VMEM((ext, wide), f32), pltpu.VMEM((depth, inner), bf16),
            pltpu.VMEM((tokens, quarter), bf16), pltpu.VMEM((heads, 1, tokens), f32),
            pltpu.VMEM((tokens, inner), f32), pltpu.VMEM((tokens, inner), bf16),
            pltpu.VMEM((inner + 16, nstate), bf16), pltpu.VMEM((tokens, inner), f32),
            pltpu.VMEM((tokens, 2 * nstate), f32), pltpu.VMEM((tokens, LANES), f32),
            pltpu.VMEM((tokens, tokens), f32), pltpu.VMEM((tokens, tokens), f32),
            pltpu.VMEM((tokens, inner), f32), pltpu.VMEM((8, LANES), f32),
            pltpu.VMEM((ext, 2 * nstate), bf16), pltpu.VMEM((tokens, inner), f32),
            pltpu.VMEM((others, inner + 16, nstate), bf16),
            pltpu.VMEM((tokens, depth), bf16),
            pltpu.VMEM((n, tokens, quarter), bf16), pltpu.VMEM((n, tokens, quarter), bf16),
            pltpu.VMEM((n - 1, tokens // n, 2 * nstate), bf16),
            pltpu.VMEM((ext, 2 * nstate), bf16), pltpu.VMEM((ext, wide), bf16),
            pltpu.VMEM((HALO, 2 * nstate), bf16), pltpu.VMEM((HALO, inner), bf16),
            dma((4,)),
        ] + boxes + [
            dma((others,)), dma((others,)), dma((n - 1,)), dma((n - 1,)), dma((2,)), dma((2,)),
            dma((n - 1,)), dma((n - 1,)),
        ] + line_sems(n),
        compiler_params=pltpu.CompilerParams(
            vmem_limit_bytes=63 << 20, collective_id=5, has_side_effects=True
        ),
        cost_estimate=cost(50),
        name="rear",
    )(*vmem_args, part, value, weights, residual)


def swiglu(first, second):
    sig = sigmoid(first)
    act = first * sig
    return act, sig * (1.0 + first * (1.0 - sig)), (act * second).astype(bf16)


def experts_kernel(mix_ref, mix_t_ref, cot_ref, gates_ref, router_ref, w_ref, shared_hbm,
                   dgate_t_ref, out_hbm, dmix_hbm, dw_hbm, dgate_ref, total_ref, grads_ref, down_ref, hidden_ref, dval_ref,
                   grad_ref, shared_ref, first_ref, second_ref, result_ref, extra_ref, local_sem, *remote,
                   tile, senders, core):
    step = pl.program_id(0)
    last = step == pl.num_programs(0) - 1
    rows, depth = mix_ref.shape
    place = row_place()
    far_send, far_receive, near_send, near_receive, keep_sem, *remote = remote
    gather = RowGather(shared_hbm, shared_ref, ((far_send, far_receive), (near_send, near_receive)))
    own_copy = pltpu.make_async_copy(shared_hbm, shared_ref.at[place], local_sem.at[0])
    if core == 2:
        inbox, shared_in, send, receive, pair_sem = remote
        me = lax.axis_index("core")
        slot = lax.rem(step + me, 2)
        pair_copy = lambda k: push(grad_ref.at[1], inbox.at[k], (send, receive), k, {"core": 1 - me})
        span = 3 * depth // 2
        mine = pl.ds(pl.multiple_of(me * span, 16), span)
        theirs = pl.ds(pl.multiple_of((1 - me) * span, 16), span)
        shared_copy = push(extra_ref.at[theirs], shared_in, (send, receive), senders // 2,
                           {"core": 1 - me})
        keep_copy = lambda k: pltpu.make_async_copy(
            inbox.at[k], dw_hbm.at[k, pl.ds(0, 3 * depth)], pair_sem.at[k]
        )
    else:
        slot = 0

    @pl.when(step == 0)
    def _():
        own_copy.start()
        barrier = pltpu.get_barrier_semaphore()
        cy, chips = lax.axis_size("cy"), lax.axis_size(CHIPS)
        chip = lax.axis_index("shard") * cy + lax.axis_index("cy")
        for d in range(1, chips):
            peer = lax.rem(chip + d, chips)
            pl.semaphore_signal(barrier, inc=1, device_id={"shard": peer // cy, "cy": lax.rem(peer, cy)},
                                device_id_type=MESH)
        if core == 2:
            pl.semaphore_signal(barrier, inc=1, device_id={"core": 1 - me}, device_id_type=MESH)
        pl.semaphore_wait(barrier, chips - 1 + core - 1)
        gather.start()
        total_ref[...] = jnp.zeros_like(total_ref)
        grads_ref[...] = jnp.zeros_like(grads_ref)
        dgate_ref[...] = jnp.zeros_like(dgate_ref)
        own_copy.wait()

    if core == 2:
        @pl.when((step >= 2) & (step < senders) & (slot == 1))
        def _():
            pair_copy((step - 2) // 2).wait_send()

    kept_at = lambda k: 2 * lax.rem(k, 2)
    buffer = jnp.where(slot == 1, 1, kept_at(step // 2)) if core == 2 else 0

    @pl.when(step < senders)
    def _():
        pair_grads(
            step, buffer, mix_ref, mix_t_ref, cot_ref, gates_ref, w_ref, dgate_ref, total_ref, grads_ref,
            down_ref, hidden_ref, dval_ref, grad_ref, tile
        )

    @pl.when(step == 1)
    def _():
        gather.relay()

    @pl.when(step == 2)
    def _():
        gather.finish()

    if core == 2:
        @pl.when((step < senders) & (slot == 1))
        def _():
            pair_copy(step // 2).start()

        def add_sibling(at):
            pair_copy(at).wait_recv()
            inbox[at] = grad_ref[kept_at(at)] + inbox[at]
            keep_copy(at).start()

        @pl.when((step >= 2) & (slot == 0))
        def _():
            add_sibling((step - 2) // 2)

        @pl.when(last)
        def _():
            pair_copy(senders // 2 - 1).wait_send()
    else:
        @pl.when(step < senders)
        def _():
            copy = pltpu.make_async_copy(
                grad_ref.at[0], dw_hbm.at[step, pl.ds(0, 3 * depth)], local_sem.at[3]
            )
            copy.start()
            copy.wait()

    @pl.when(step == 3)
    def _():
        wide = w_ref.shape[2]
        hid = wide // 2
        wrows = depth // senders
        for p in range(2):
            first_ref[p] = shared_ref[:, p * wrows : (p + 1) * wrows, :].reshape(depth, wide)
        second_ref[...] = shared_ref[:, 2 * wrows :, :].reshape(depth, wide)
        raw = dot_rows(cot_ref[...], second_ref[...])
        for p in range(2):
            value = dot_rows(mix_ref[...], first_ref[p])
            act, slope, hidden = swiglu(value[:, :hid], value[:, hid:])
            dh = raw[:, p * hid : (p + 1) * hid]
            dval_ref[p, :, :hid] = (dh * value[:, hid:] * slope).astype(bf16)
            dval_ref[p, :, hid:] = (dh * act).astype(bf16)
            hidden_ref[:, p * hid : (p + 1) * hid] = hidden
        total_ref[...] += dot_outer(hidden_ref[...], second_ref[...])
        grads_ref[...] += dot_outer(dval_ref[0], first_ref[0]) + dot_outer(dval_ref[1], first_ref[1])
        for k in range(3):
            if k < 2:
                grad = dot_rows(mix_t_ref[...], dval_ref[k]).astype(bf16)
            else:
                grad = dot_inner(cot_ref[...], hidden_ref[...]).astype(bf16)
            for j in range(senders):
                at = (3 * ((j % core) * (senders // core) + j // core) + k) * wrows
                extra_ref[at : at + wrows, :] = grad[j * wrows : (j + 1) * wrows]
        if core == 2:
            shared_copy.start()

    @pl.when(last)
    def _():
        result_ref[...] = total_ref[...].astype(bf16)
        out_copy = pltpu.make_async_copy(result_ref, out_hbm, local_sem.at[2])
        out_copy.start()
        copies = [out_copy]
        part = 3 * (depth // senders)
        source = extra_ref
        if core == 2:
            shared_copy.wait_recv()
            shared_in[...] = shared_in[...] + extra_ref[mine, :]
            source = shared_in
        kept = senders // core
        for j in range(kept):
            copies.append(pltpu.make_async_copy(
                source.at[pl.ds(j * part, part)], dw_hbm.at[j, pl.ds(3 * depth, part)], keep_sem.at[j]
            ))
            copies[-1].start()
        gates = gates_ref[...]
        dgate = dgate_ref[...]
        inside = jnp.sum(gates * dgate, axis=1, keepdims=True)
        dlogits = (gates * (dgate - inside)).astype(bf16)
        out_copy.wait()
        result_ref[...] = (grads_ref[...] + dot_outer(dlogits, router_ref[...])).astype(bf16)
        dmix_copy = pltpu.make_async_copy(result_ref, dmix_hbm, local_sem.at[4])
        dmix_copy.start()
        dgate_t_ref[...] = dgate.T[: dgate_t_ref.shape[0], :]
        if core == 2:
            pl.when(slot == 1)(lambda: add_sibling(senders // 2 - 1))
        for copy in copies[1:] + [dmix_copy]:
            copy.wait()
        if core == 2:
            for k in range(kept):
                keep_copy(k).wait()
            shared_copy.wait_send()


def pair_grads(step, slot, mix_ref, mix_t_ref, cot_ref, gates_ref, w_ref, dgate_ref, total_ref, grads_ref,
               down_ref, hidden_ref, dval_ref, grad_ref, tile):
    rows, depth = mix_ref.shape
    wide = w_ref.shape[2]
    hid = wide // 2
    chunks = depth // wide
    deep = depth + depth // 2
    for p in range(2):
        for c in range(chunks):
            down_ref[p * hid : (p + 1) * hid, c * wide : (c + 1) * wide] = (
                w_ref[0, p * deep + depth + c * hid : p * deep + depth + (c + 1) * hid, :]
            )
    down = down_ref[...]

    def part(i, _):
        at = pl.ds(pl.multiple_of(i * tile, tile), tile)
        mix = mix_ref[at, :]
        raw = dot_outer(cot_ref[at, :], down)
        gates = gates_ref[at, :]
        lane = col_iota(gates.shape)
        dmix, noted = None, jnp.zeros_like(gates)
        for p in range(2):
            here = lane == 2 * step + p
            gate = jnp.sum(jnp.where(here, gates, 0.0), axis=1, keepdims=True)
            weights = w_ref[0, p * deep : p * deep + depth, :]
            value = dot_rows(mix, weights)
            act, slope, hidden = swiglu(value[:, :hid], value[:, hid:])
            hidden = hidden.astype(f32)
            dh = raw[:, p * hid : (p + 1) * hid]
            noted = noted + jnp.where(here, jnp.sum(hidden * dh, axis=1, keepdims=True), 0.0)
            dh = gate * dh
            dval_ref[p, at, :hid] = (dh * value[:, hid:] * slope).astype(bf16)
            dval_ref[p, at, hid:] = (dh * act).astype(bf16)
            hidden_ref[at, p * hid : (p + 1) * hid] = (gate * hidden).astype(bf16)
            term = dot_outer(dval_ref[p, at, :], weights)
            dmix = term if dmix is None else dmix + term
        dgate_ref[at, :] += noted
        total_ref[at, :] += dot_rows(hidden_ref[at, :], down)
        grads_ref[at, :] += dmix
        return 0

    lax.fori_loop(0, rows // tile, part, 0)
    hidden_t = hidden_ref[...].T
    for c in range(chunks):
        grad = dot_rows(hidden_t, cot_ref[:, c * wide : (c + 1) * wide]).astype(bf16)
        for p in range(2):
            first = p * deep + depth + c * hid
            grad_ref[slot, first : first + hid, :] = grad[p * hid : (p + 1) * hid]
    for p in range(2):
        grad_ref[slot, p * deep : p * deep + depth, :] = (
            dot_rows(mix_t_ref[...], dval_ref[p]).astype(bf16)
        )


def experts(mix, mix_t, cot, gates, weights, router_at, experts_w, shared):
    senders, deep, wide = experts_w.shape
    rows, depth = mix.shape
    core, chips = lax.axis_size("core"), lax.axis_size(CHIPS)
    kept = senders // core
    kinds = 2 * senders + -2 * senders % 8
    shape = jax.ShapeDtypeStruct
    dma = pltpu.SemaphoreType.DMA
    once = lambda a: pl.BlockSpec(a.shape, lambda i: (0,) * a.ndim, pipeline_mode=pl.Buffered(1))
    outs = [shape((kinds, rows), f32)]
    remote = []
    if core == 2:
        remote = [pltpu.VMEM((kept, deep, wide), bf16), pltpu.VMEM((deep // 2, wide), bf16),
                  dma((kept + 1,)), dma((kept + 1,)), dma((kept,))]
    return pl.pallas_call(
        partial(experts_kernel, tile=rows, senders=senders, core=core),
        grid=(senders + 1,),
        in_specs=[once(mix), once(mix_t), once(cot), once(gates),
                  pl.BlockSpec((depth, LANES), lambda i: (0, router_at // LANES)),
                  pl.BlockSpec((1, deep, wide), lambda i: (jnp.minimum(i, senders - 1), 0, 0)), HBM],
        out_specs=[whole(o) for o in outs] + [HBM] * 3,
        out_shape=outs + [
            shape((rows, depth), bf16), shape((rows, depth), bf16),
            shape((kept, deep + shared.shape[0], wide), bf16),
        ],
        scratch_shapes=[
            pltpu.VMEM((rows, LANES), f32),
            pltpu.VMEM((rows, depth), f32), pltpu.VMEM((rows, depth), f32),
            pltpu.VMEM((wide, depth), bf16), pltpu.VMEM((rows, wide), bf16),
            pltpu.VMEM((2, rows, wide), bf16), pltpu.VMEM((2 * core - 1, deep, wide), bf16),
            pltpu.VMEM((senders,) + shared.shape, bf16), pltpu.VMEM((2, depth, wide), bf16),
            pltpu.VMEM((depth, wide), bf16), pltpu.VMEM((rows, depth), bf16), pltpu.VMEM((deep, wide), bf16), dma((5,)),
            dma((max(chips - 1, 1),)), dma((max(chips - 1, 1),)), dma((chips,)), dma((chips,)),
            dma((kept,)),
        ] + remote,
        compiler_params=pltpu.CompilerParams(
            vmem_limit_bytes=63 << 20, collective_id=4, has_side_effects=True
        ),
        cost_estimate=cost(7 * senders),
        name="experts",
    )(mix, mix_t, cot, gates, weights, experts_w, shared)


def local(
    block_input, gain_input, proj_main, proj_state, proj_step, conv_main, conv_state, step_bias,
    decay_log, skip_gain, gain_gate, proj_out, gain_mix, router_weight, shared_gates, shared_down,
    expert_gates, expert_down, segments, routes, cotangent,
):
    tokens, quarter = block_input.shape
    heads = step_bias.shape[0]
    inner = conv_main.shape[1]
    nstate = conv_state.shape[1] // 2
    per = inner // heads
    tensors = lax.axis_size("tensor")
    zi = lax.axis_index("tensor")
    senders = lax.axis_size(ROWS)
    depth = quarter * tensors
    di_all = inner * tensors
    own = tokens // tensors
    column = zi * quarter
    row0 = zi * own
    wrows = proj_main.shape[0]
    hid = expert_gates.shape[3]
    local_experts = expert_gates.shape[0]
    experts_all = local_experts * senders
    shared_here = shared_down.shape[1]
    router_pad = -experts_all % LANES

    main_wide = 2 * inner + 2 * nstate + LANES
    router_at = main_wide + inner
    weights = gather_rows(
        jnp.concatenate(
            [proj_main[:, 0], proj_main[:, 1], proj_state,
             jnp.pad(proj_step, ((0, 0), (0, LANES - heads))), proj_out,
             jnp.pad(router_weight, ((0, 0), (0, router_pad)))], axis=1
        )
    )
    pair_down = expert_down.reshape(local_experts, hid, depth // (2 * hid), 2 * hid)
    pair = jnp.concatenate(
        [expert_gates.reshape(local_experts, depth, 2 * hid),
         pair_down.transpose(0, 2, 1, 3).reshape(local_experts, -1, 2 * hid)], axis=1
    )
    shared_pair = shared_gates.reshape(wrows, 2, 2, shared_here // 2).transpose(2, 0, 1, 3)
    experts_w = gather_rows(pair.reshape(1, -1, 2 * hid))
    shared_local = jnp.concatenate([shared_pair.reshape(-1, shared_here), shared_down], axis=0)

    seg_row = segments[0]
    halo_seg = shifted(seg_row[tokens - CONV + 1 :], CTX, 1)
    gains = jnp.concatenate(
        [gain_input[None], gain_mix[None], jnp.zeros((14, quarter), bf16)], axis=0
    )
    mixed_ext, mixed_t, got, gain_rows = intake(block_input, gains)
    gain_row, gain_mid = gain_rows[0:1], gain_rows[1:2]

    segments_ext = jnp.concatenate([halo_seg, seg_row], axis=0)
    same = jnp.stack(
        [segments_ext[offset : offset + tokens] == seg_row for offset in range(CONV)]
    ).astype(f32)
    same = jnp.broadcast_to(same[:, :, None], (CONV, tokens, LANES))
    taps = jnp.concatenate([conv_main, conv_state], axis=1).astype(f32)
    lanes = lambda v: jnp.pad(v, (0, LANES - heads))[None]
    bias = lanes(step_bias)
    decay = lanes(decay_log)
    skip = jnp.repeat(skip_gain, per)[None]
    link = (seg_row == halo_seg[-1]).astype(f32)[:, None]
    at_end = (seg_row == seg_row[-1]).astype(f32)[:, None]
    seg_col = seg_row[:, None]
    seg_line = seg_row[None]
    chosen = jnp.any(
        routes[:, :, None] == jnp.arange(LANES, dtype=jnp.int32)[None, None, :], axis=1
    ).astype(f32)
    gain_gate_f = gain_gate.astype(f32)[None, :]
    (value, act, scaled, step, running, run_exp, within, mixer, state_in, packed, residual, scale_rows,
     own_part, cot_full, mix, mix_t, gates) = front(
        mixed_ext, taps, same, bias, decay, at_end, link, seg_col, seg_line, skip, gain_gate_f, got,
        cotangent, gain_mid, chosen, weights, inner, nstate, per, heads, di_all
    )

    dgate, out_part, dmix_part, dw = experts(
        mix, mix_t, cot_full, gates, weights, router_at, experts_w, shared_local
    )
    expert_rows = scatter_chips(dw.reshape(-1, 2 * hid))
    dmixer, notes, gains_mid = turn_step(
        dmix_part, dgate, residual, cot_full, own_part, gain_mid
    )

    value_grad, rear_main, early, state_taps, state_all, output = rear(
        (dmixer, scale_rows, notes, mixer, within, act, scaled, step, running, run_exp, state_in, taps,
         same, bias, decay, skip, gain_gate_f, at_end, link, seg_col, seg_line, packed,
         mixed_t),
        out_part, value, weights, residual, inner, nstate, per, heads, di_all
    )
    first = 2 * inner
    last = first + 2 * nstate
    rear_main, expert_rows = lax.optimization_barrier((rear_main, expert_rows))
    rear_main = scatter_chips(rear_main)

    grad_input, early, late, main = last_step(
        (value_grad, got, dmixer, gain_row, gains_mid, state_taps, early, mixed_t, mix_t, state_all,
         gates, notes),
        weights, inner, last,
    )
    if lax.axis_size("core") != 2:
        main = scatter_chips(main)
    expert_rows, main = lax.optimization_barrier((expert_rows, main))
    grad_shared, grad_shared_down, grad_gates, grad_down = emit_experts(expert_rows, wrows, hid)
    (output, grad_input, grad_gain_in, grad_main, grad_state, grad_step, grad_conv, grad_conv_state,
     grad_bias, grad_decay, grad_skip, grad_gate, grad_proj_out, grad_gain_mid, grad_router) = emit(
        (output, grad_input, early, late, rear_main, main), inner, nstate, per, heads, experts_all
    )
    return (
        output,
        grad_input,
        grad_gain_in.reshape(quarter),
        grad_main,
        grad_state,
        grad_step.T,
        grad_conv,
        grad_conv_state,
        grad_bias[0],
        grad_decay[0],
        grad_skip[0],
        grad_gate.reshape(inner),
        grad_proj_out,
        grad_gain_mid.reshape(quarter),
        grad_router.T,
        grad_shared,
        grad_shared_down,
        grad_gates.reshape(expert_gates.shape),
        grad_down,
    )


def solution(mesh):
    shard, ctx, tensor = (mesh.shape[name] for name in ("shard", "ctx", "tensor"))
    core = 2 if shard * ctx == 8 else 1
    split = jax.sharding.Mesh(
        mesh.devices.reshape(shard, ctx // core, core, tensor), ("shard", "cy", "core", "tensor")
    )
    return jax.shard_map(
        local,
        mesh=split,
        in_specs=(
            P(ROWS, "tensor"),
            P("tensor"),
            P(ROWS, None, "tensor"),
            P(ROWS, None),
            P(ROWS, "tensor"),
            P(None, "tensor"),
            P(),
            P("tensor"),
            P("tensor"),
            P("tensor"),
            P("tensor"),
            P(ROWS, "tensor"),
            P("tensor"),
            P(ROWS, None),
            P(ROWS, None, "tensor"),
            P(ROWS, "tensor"),
            P(ROWS, None, None, "tensor"),
            P(ROWS, "tensor", None),
            P("shard", CTX),
            P(ROWS, None),
            P(ROWS, "tensor"),
        ),
        out_specs=(
            P(ROWS, "tensor"),
            P(ROWS, "tensor"),
            P("tensor"),
            P(ROWS, None, "tensor"),
            P(ROWS, None),
            P(ROWS, "tensor"),
            P(None, "tensor"),
            P(),
            P("tensor"),
            P("tensor"),
            P("tensor"),
            P("tensor"),
            P(ROWS, "tensor"),
            P("tensor"),
            P(ROWS, None),
            P(ROWS, None, "tensor"),
            P(ROWS, "tensor"),
            P(ROWS, None, None, "tensor"),
            P(ROWS, "tensor", None),
        ),
        check_vma=False,
    )
```

```python
from functools import partial

import jax
import jax.numpy as jnp
from jax import lax
from jax.experimental import pallas as pl
from jax.experimental.pallas import tpu as pltpu
from jax.sharding import PartitionSpec as P

CONV = 4
HALO = 16
LANES = 128
LANES = 128
LANES = 128


epsilon = 1e-05
highest = lax.Precision.HIGHEST
CTX = ("cy", "core")
CHIPS = ("shard", "cy")
ROWS = ("shard", "cy", "core")
f32 = jnp.float32
MESH = pl.DeviceIdType.MESH
bf16 = jnp.bfloat16
BIG = pltpu.CompilerParams(vmem_limit_bytes=60 << 20)


def cost(micros):
    return pl.CostEstimate(flops=micros * 900_000_000, transcendentals=0, bytes_accessed=1 << 20)
BIG = pltpu.CompilerParams(vmem_limit_bytes=60 << 20)


def cost(micros):
    return pl.CostEstimate(flops=micros * 900_000_000, transcendentals=0, bytes_accessed=1 << 20)
BIG = pltpu.CompilerParams(vmem_limit_bytes=60 << 20)


def cost(micros):
    return pl.CostEstimate(flops=micros * 900_000_000, transcendentals=0, bytes_accessed=1 << 20)


def shifted(value, axis, steps):
    count = lax.axis_size(axis)
    leading, last = (max(0, -steps), min(count, count - steps))
    return lax.ppermute(value, axis, [(source, source + steps) for source in range(leading, last)])


def dot_rows(left, right, precision=None):
    return jnp.dot(left, right, preferred_element_type=f32, precision=precision)


def dot_inner(left, right):
    return lax.dot_general(left, right, (((0,), (0,)), ((), ())), preferred_element_type=f32)


def dot_outer(left, right):
    return lax.dot_general(left, right, (((1,), (1,)), ((), ())), preferred_element_type=f32)


def sigmoid(value):
    return 1.0 / (1.0 + jnp.exp(-value))


def gather_rows(value):
    return lax.all_gather(value, ROWS, axis=0, tiled=True)


def scatter_rows(value):
    return lax.psum_scatter(value, ROWS, scatter_dimension=0, tiled=True)


def scatter_chips(value):
    axes = CHIPS if lax.axis_size("core") == 2 else ROWS
    return lax.psum_scatter(value, axes, scatter_dimension=0, tiled=True)


def exchange(blocks):
    return lax.all_to_all(blocks, "tensor", split_axis=0, concat_axis=0, tiled=True)


def spread(block):
    count = lax.axis_size("tensor")
    return exchange(jnp.broadcast_to(block[None], (count,) + block.shape))


def spread_small(block):
    count, index = lax.axis_size("tensor"), lax.axis_index("tensor")
    width = block.shape[1]
    full = jnp.zeros((block.shape[0], count * width), block.dtype)
    for away in range(count):
        moved = block if away == 0 else lax.ppermute(
            block, "tensor", [(i, (i + away) % count) for i in range(count)]
        )
        origin = lax.rem(index - away + count, count)
        full = lax.dynamic_update_slice_in_dim(full, moved, origin * width, 1)
    return full


def halves(value):
    high = value.astype(bf16)
    return high, (value - high.astype(f32)).astype(bf16)


def far_states(packed, reverse):
    count = lax.axis_size(CTX)
    return jnp.stack([
        shifted(packed, CTX, -away if reverse else away) for away in range(1, count)
    ])


def row_iota(shape):
    return lax.broadcasted_iota(jnp.int32, shape, 0)


def col_iota(shape):
    return lax.broadcasted_iota(jnp.int32, shape, 1)


def expander(lanes, width, per):
    low = row_iota((lanes, width)) * per
    at = col_iota((lanes, width))
    return ((at >= low) & (at < low + per)).astype(f32)


def head_fold(width, lanes, per):
    low = col_iota((width, lanes)) * per
    at = row_iota((width, lanes))
    return ((at >= low) & (at < low + per)).astype(f32)


def pack_state(state, through):
    high, low = halves(through)
    row = row_iota((16, LANES))
    tail = jnp.where(row == 0, high.astype(f32), jnp.where(row == 1, low.astype(f32), 0.0))
    return jnp.concatenate([state, tail], axis=0).astype(bf16)


def join_states(far_ref, inner, per):
    spread_heads = head_fold(inner, LANES, per)
    total = None
    for k in reversed(range(far_ref.shape[0])):
        state = far_ref[k, :inner, :].astype(f32)
        if total is not None:
            through = far_ref[k, inner : inner + 16, :].astype(f32)
            through = through[0:1] + through[1:2]
            state = state + jnp.sum(spread_heads * through, axis=1, keepdims=True) * total
        total = state
    return total


def thirds(value):
    high = value.astype(bf16)
    rest = value - high.astype(f32)
    middle = rest.astype(bf16)
    return high, middle, (rest - middle.astype(f32)).astype(bf16)


def spread_lanes(value, grow):
    ones = grow.astype(bf16)
    return sum(dot_rows(part, ones) for part in thirds(value))


def left_sums(zero_one, value):
    return sum(dot_rows(zero_one, part) for part in thirds(value))


def fold_heads(value, folds):
    high, low = halves(value)
    return dot_rows(high, folds) + dot_rows(low, folds)


def conv_pre(value_ref, column, taps_ref, taps_column, same_ref, tokens):
    rows = value_ref[:, pl.ds(column, LANES)]
    total = None
    for offset in range(CONV):
        first = HALO - CONV + 1 + offset
        term = rows[first : first + tokens] * (
            same_ref[offset] * taps_ref[offset : offset + 1, pl.ds(taps_column, LANES)]
        )
        total = term if total is None else total + term
    return rows, total


def enter_part(mixed_ref, w_ref, taps_ref, same_ref, bias_ref, decay_ref, end_ref, link_ref,
                 value_ref, act_ref, scaled_ref, step_ref, run_ref, run_exp_ref,
                 state_ref, *, inner, nstate, per):
    tokens = act_ref.shape[0]
    width = 2 * inner + 2 * nstate + LANES
    tile = 384

    def matmul(i, _):
        columns = pl.ds(pl.multiple_of(i * tile, LANES), tile)
        value_ref[:, columns] = dot_rows(mixed_ref[...], w_ref[:, columns])
        return 0

    lax.fori_loop(0, width // tile, matmul, 0)

    def conv(i, _):
        at = pl.multiple_of(i * LANES, LANES)
        _, total = conv_pre(value_ref, inner + at, taps_ref, at, same_ref, tokens)
        act_ref[:, pl.ds(at, LANES)] = (total * sigmoid(total)).astype(bf16)
        return 0

    lax.fori_loop(0, (inner + 2 * nstate) // LANES, conv, 0)
    raw = value_ref[HALO:, 2 * inner + 2 * nstate :] + bias_ref[...]
    step = jnp.maximum(raw, 0.0) + jnp.log1p(jnp.exp(-jnp.abs(raw)))
    log_decay = step * -jnp.exp(decay_ref[...])
    tri = (row_iota((tokens, tokens)) >= col_iota((tokens, tokens))).astype(bf16)
    running = left_sums(tri, log_decay)
    step_ref[...] = step
    run_ref[...] = running
    grow = expander(LANES, inner, per)
    run_exp_ref[...] = spread_lanes(running, grow)
    signal = act_ref[:, :inner].astype(f32)
    scaled_ref[...] = (signal * spread_lanes(step, grow)).astype(bf16)
    toward = step * jnp.exp(running[tokens - 1 :] - running) * end_ref[...]
    pushed = (signal * spread_lanes(toward, grow)).astype(bf16)
    through = jnp.exp(running[tokens - 1 :]) * link_ref[tokens - 1 :]
    state_ref[...] = pack_state(dot_inner(pushed, act_ref[:, inner : inner + nstate]), through)


def whole(a):
    return pl.BlockSpec(a.shape, lambda i: (0,) * len(a.shape))


def columns(a, width, at=0):
    assert at % width == 0
    return pl.BlockSpec((a.shape[0], width), lambda i: (0, at // width))


def masked_scores(query, keys, seg_col_ref, seg_row_ref, start, stop):
    shape = (stop - start, stop)
    allowed = (row_iota(shape) + start >= col_iota(shape)) & (
        seg_col_ref[start:stop, :1] == seg_row_ref[:, :stop]
    )
    return jnp.where(allowed, dot_outer(query[start:stop], keys[:stop]), 0.0)


def intra_part(act_ref, scaled_ref, run_t_ref, run_exp_ref, seg_col_ref, seg_row_ref,
                 inner_ref, scores_ref, *, inner, nstate, per, block):
    tokens = act_ref.shape[0]
    keys = act_ref[:, inner : inner + nstate]
    query = act_ref[:, inner + nstate :]
    for start in range(0, tokens, block):
        stop = start + block
        scores_ref[start:stop, :stop] = masked_scores(
            query, keys, seg_col_ref, seg_row_ref, start, stop
        )

    def pair(i, _):
        columns = pl.ds(pl.multiple_of(i * LANES, LANES), LANES)
        scaled = scaled_ref[:, columns]
        lane = col_iota(scaled.shape)
        run = run_exp_ref[:, columns]
        for start in range(0, tokens, block):
            stop = start + block
            total = None
            for h in range(LANES // per):
                mine = (lane >= h * per) & (lane < (h + 1) * per)
                vals = jnp.where(mine, scaled, jnp.zeros_like(scaled))[:stop]
                row = run_t_ref[i * (LANES // per) + h, :, :stop]
                decay = jnp.exp(jnp.minimum(run[start:stop, h * per : h * per + 1] - row, 0.0))
                weight = (decay * scores_ref[start:stop, :stop]).astype(bf16)
                term = dot_rows(weight, vals)
                total = term if total is None else total + term
            inner_ref[start:stop, columns] = total
        return 0

    lax.fori_loop(0, inner // LANES, pair, 0)


def row_sums(value):
    folded = value[:, :LANES]
    for at in range(LANES, value.shape[1], LANES):
        folded = folded + value[:, at : at + LANES]
    ones = jnp.ones((8, LANES), bf16)
    high, low = halves(folded)
    return dot_outer(ones, high) + dot_outer(ones, low)


def as_column(row):
    n = row.shape[1]
    eye = row_iota((n, n)) == col_iota((n, n))
    return jnp.sum(jnp.where(eye, row, 0.0), axis=1, keepdims=True)


def tensor_barrier(me, n):
    barrier = pltpu.get_barrier_semaphore()
    for d in range(1, n):
        pl.semaphore_signal(
            barrier, inc=1, device_id={"tensor": lax.rem(me + d, n)}, device_id_type=MESH
        )
    pl.semaphore_wait(barrier, n - 1)


def push(source, target, sems, slot, peer):
    send, receive = sems
    return pltpu.make_async_remote_copy(
        src_ref=source, dst_ref=target, send_sem=send.at[slot], recv_sem=receive.at[slot],
        device_id=peer if isinstance(peer, dict) else {"tensor": peer}, device_id_type=MESH,
    )


def ctx_place():
    core = lax.axis_size("core")
    return lax.axis_index("cy") * core + lax.axis_index("core"), lax.axis_size("cy") * core


def ctx_peer(place):
    core = lax.axis_size("core")
    return {"cy": place // core, "core": lax.rem(place, core)}


def front_barrier(me, n):
    barrier = pltpu.get_barrier_semaphore()
    place, count = ctx_place()
    for d in range(1, n):
        pl.semaphore_signal(
            barrier, inc=1, device_id={"tensor": lax.rem(me + d, n)}, device_id_type=MESH
        )
    for d in range(1, count):
        pl.semaphore_signal(
            barrier, inc=1, device_id=ctx_peer(lax.rem(place + d, count)), device_id_type=MESH
        )
    pl.semaphore_wait(barrier, n - 1 + count - 1)


def rows_barrier(me, n, meanwhile=lambda: None):
    barrier = line_barrier(me, n)
    place, count = row_place(), lax.axis_size(ROWS)
    for d in range(1, count):
        pl.semaphore_signal(barrier, inc=1, device_id=row_peer(lax.rem(place + d, count)),
                            device_id_type=MESH)
    result = meanwhile()
    pl.semaphore_wait(barrier, n - 1 + count - 1)
    return result


class RowGather:
    def __init__(self, source, full, sems):
        self.cy, self.core = lax.axis_size("cy"), lax.axis_size("core")
        self.chips = lax.axis_size(CHIPS)
        me = lax.axis_index("core")
        chip = lax.axis_index("shard") * self.cy + lax.axis_index("cy")
        slot = lambda c: c * self.core + me
        self.far, self.near = [], []
        for d in range(1, self.chips):
            peer = lax.rem(chip + d, self.chips)
            self.far.append(push(source, full.at[slot(chip)], sems[0], d - 1,
                                 {"shard": peer // self.cy, "cy": lax.rem(peer, self.cy)}))
        if self.core == 2:
            for d in range(self.chips):
                origin = lax.rem(chip - d + self.chips, self.chips)
                self.near.append(push(source if d == 0 else full.at[slot(origin)], full.at[slot(origin)],
                                      sems[1], d, {"core": 1 - me}))

    def start(self):
        for copy in self.far + self.near[:1]:
            copy.start()

    def relay(self):
        for d, copy in enumerate(self.far):
            copy.wait_recv()
            if self.near:
                self.near[d + 1].start()

    def finish(self):
        for copy in self.near:
            copy.wait()
        for copy in self.far:
            copy.wait_send()


class WeightSum:
    def __init__(self, stage, boxes):
        self.stage, self.boxes = stage, boxes
        self.depth = stage.shape[0]
        self.core, self.cy = lax.axis_index("core"), lax.axis_size("cy")
        self.chip = lax.axis_index("shard") * self.cy + lax.axis_index("cy")
        self.chips = boxes[0].shape[0] if boxes else 0
        self.paired = boxes[1:3] if len(boxes) == 3 else boxes[3:5]
        self.owner = boxes[0].shape[1] if boxes else 0
        self.siblings, self.mains, self.units = [], [], []

    def rows(self, k):
        return pl.ds(pl.multiple_of(k * self.owner, 16), self.owner)

    def product(self, lhs_ref, rhs, at, transposed=True):
        span = rhs.shape[1]
        tall = self.depth // 2

        def part(m, _):
            here = pl.ds(pl.multiple_of(m * tall, tall), tall)
            if transposed:
                value = dot_rows(lhs_ref[here, :], rhs[...])
            else:
                value = dot_inner(lhs_ref[:, here], rhs[...])
            self.stage[here, at : at + span] = value.astype(bf16)
            return 0

        lax.fori_loop(0, 2, part, 0)

    def to_sibling(self, at, span):
        unit = len(self.units)
        self.units.append((at, span))
        copies = []
        for j in range(self.chips):
            copies.append(push(
                self.stage.at[self.rows(2 * j + 1 - self.core), pl.ds(at, span)],
                self.boxes[0].at[j, :, pl.ds(at, span)], self.paired, unit * self.chips + j,
                {"core": 1 - self.core},
            ))
            copies[-1].start()
        self.siblings.append(copies)

    def to_chips(self, unit):
        if not self.chips:
            return
        sib_in, sum_ref, main_in = self.boxes[:3]
        at, span = self.units[unit]
        for j, copy in enumerate(self.siblings[unit]):
            copy.wait_recv()
            sum_ref[j * self.owner : (j + 1) * self.owner, at : at + span] = (
                self.stage[self.rows(2 * j + self.core), at : at + span] + sib_in[j, :, at : at + span]
            )
        for d in range(1, self.chips):
            peer = lax.rem(self.chip + d, self.chips)
            self.mains.append(push(
                sum_ref.at[self.rows(peer), pl.ds(at, span)], main_in.at[d - 1, :, pl.ds(at, span)],
                self.boxes[5:7], unit * (self.chips - 1) + d - 1,
                {"shard": peer // self.cy, "cy": lax.rem(peer, self.cy)},
            ))
            self.mains[-1].start()

    def pair(self, unit, out_ref):
        at, span = self.units[unit]
        if not self.chips:
            out_ref[:, at : at + span] = self.stage[:, at : at + span]
            return
        for j, copy in enumerate(self.siblings[unit]):
            copy.wait_recv()
            out_ref[j * self.owner : (j + 1) * self.owner, at : at + span] = (
                self.stage[self.rows(2 * j + self.core), at : at + span]
                + self.boxes[0][j, :, at : at + span]
            )

    def wait_send(self):
        for copies in self.siblings:
            for copy in copies:
                copy.wait_send()

    def finish(self, out_ref):
        if not self.chips:
            out_ref[...] = self.stage[...]
            return
        _, sum_ref, main_in = self.boxes[:3]
        main_in[self.chips - 1] = sum_ref[self.rows(self.chip), :]
        for copy in self.mains:
            copy.wait_recv()
        out_ref[...] = in_order(main_in, self.chip, self.chips)
        self.wait_send()
        for copy in self.mains:
            copy.wait_send()


def weight_boxes(depth, width, units, between_chips=True):
    dma = pltpu.SemaphoreType.DMA
    if lax.axis_size("core") != 2:
        return [pltpu.VMEM((depth, width), bf16)], jax.ShapeDtypeStruct((depth, width), bf16)
    chips = lax.axis_size(CHIPS)
    owner = depth // (2 * chips)
    if not between_chips:
        return [
            pltpu.VMEM((depth, width), bf16), pltpu.VMEM((chips, owner, width), bf16),
            dma((units * chips,)), dma((units * chips,)),
        ], jax.ShapeDtypeStruct((chips * owner, width), bf16)
    return [
        pltpu.VMEM((depth, width), bf16), pltpu.VMEM((chips, owner, width), bf16),
        pltpu.VMEM((chips * owner, width), bf16), pltpu.VMEM((chips, owner, width), bf16),
        dma((units * chips,)), dma((units * chips,)), dma((units * (chips - 1),)),
        dma((units * (chips - 1),)),
    ], jax.ShapeDtypeStruct((owner, width), f32)


class StatePush:
    def __init__(self, source, far_ref, sems, reverse):
        place, count = ctx_place()
        sign = -1 if reverse else 1
        self.copies = []
        for d in range(1, count):
            to, origin = place + sign * d, place - sign * d
            copy = push(source, far_ref.at[d - 1], sems, d - 1,
                        ctx_peer(lax.rem(to + count, count)))
            self.copies.append((copy, (to >= 0) & (to < count), (origin >= 0) & (origin < count)))

    def start(self):
        for copy, sends, _ in self.copies:
            pl.when(sends)(copy.start)

    def wait_recv(self):
        for copy, _, gets in self.copies:
            pl.when(gets)(copy.wait_recv)

    def wait_send(self):
        for copy, sends, _ in self.copies:
            pl.when(sends)(copy.wait_send)


class LineReduce:
    def __init__(self, me, n, blocks, right, left, sems):
        self.me, self.n, self.blocks, self.right, self.left = me, n, blocks, right, left
        self.right_sems, self.left_sems = sems
        self.keep = lambda d: jnp.minimum(jnp.maximum(d, 0), n - 1)

    def rightward(self, d):
        return push(self.blocks(d), self.right.at[d], self.right_sems, d,
                    jnp.minimum(self.me + 1, self.n - 1))

    def leftward(self, d):
        return push(self.blocks(d), self.left.at[d], self.left_sems, d, jnp.maximum(self.me - 1, 0))

    def step(self, t):
        me, n = self.me, self.n
        ways = []
        if t < n:
            ways.append((n - 1 - t + me, me >= 1, lambda d: d > me, t >= me, self.rightward, self.right))
            ways.append((t - (n - 1 - me), me <= n - 2, lambda d: d < me, t >= n - 1 - me,
                         self.leftward, self.left))
        for d, gets, passes, ready, copy_of, box in ways:
            at = self.keep(d)
            copy = copy_of(at)

            @pl.when(gets & ready)
            def _():
                copy.wait_recv()

            @pl.when(gets & ready & passes(d))
            def _():
                view = self.blocks(at)
                view[...] = view[...] + box[at]

            @pl.when(ready & passes(d))
            def _():
                copy.start()

    def total(self):
        me, n = self.me, self.n
        value = self.blocks(me)[...].astype(f32)
        value = value + jnp.where(me >= 1, self.right[me].astype(f32), 0.0)
        return value + jnp.where(me <= n - 2, self.left[me].astype(f32), 0.0)

    def wait_send(self):
        for d in range(self.n):
            pl.when(self.me < d)(self.rightward(d).wait_send)
            pl.when(self.me > d)(self.leftward(d).wait_send)


class LineGather:
    def __init__(self, me, n, blocks, sems):
        self.me, self.n, self.blocks = me, n, blocks
        self.right_sems, self.left_sems = sems

    def rightward(self, d):
        return push(self.blocks(d), self.blocks(d), self.right_sems, d,
                    jnp.minimum(self.me + 1, self.n - 1))

    def leftward(self, d):
        return push(self.blocks(d), self.blocks(d), self.left_sems, d, jnp.maximum(self.me - 1, 0))

    def step(self, t):
        me, n = self.me, self.n
        from_left, from_right = me - t, me + t
        right = self.rightward(jnp.maximum(from_left, 0))
        left = self.leftward(jnp.minimum(from_right, n - 1))
        if t > 0:
            pl.when(from_left >= 0)(right.wait_recv)
        pl.when((from_left >= 0) & (me <= n - 2))(right.start)
        if t > 0:
            pl.when(from_right <= n - 1)(left.wait_recv)
        pl.when((from_right <= n - 1) & (me >= 1))(left.start)

    def wait_send(self):
        for d in range(self.n):
            pl.when((self.me >= d) & (self.me <= self.n - 2))(self.rightward(d).wait_send)
            pl.when((self.me <= d) & (self.me >= 1))(self.leftward(d).wait_send)


def line_sems(n):
    return [pltpu.SemaphoreType.DMA((n,))] * 4


def line_groups(sems):
    return (sems[0], sems[1]), (sems[2], sems[3])


def line_barrier(me, n):
    barrier = pltpu.get_barrier_semaphore()
    for d in range(1, n):
        pl.semaphore_signal(
            barrier, inc=1, device_id={"tensor": lax.rem(me + d, n)}, device_id_type=MESH
        )
    return barrier


def intake_kernel(x_ref, gains_ref, mixed_ref, mixed_t_ref, full_ref, gain_out,
                  x_box, gains_box, halo_box, *sems, n):
    me = lax.axis_index("tensor")
    place, count = ctx_place()
    rows, quarter = x_ref.shape
    column = lambda d: pl.ds(pl.multiple_of(d * quarter, LANES), quarter)
    gain_sems, halo_sems = (sems[0], sems[1]), (sems[2], sems[3])
    halo_box[...] = jnp.zeros_like(halo_box)
    x_box[:, column(me)] = x_ref[...]
    gains_box[:, column(me)] = gains_ref[...]
    barrier = line_barrier(me, n)
    for away in (1, count - 1):
        for z in range(n):
            pl.semaphore_signal(
                barrier, inc=1, device_id={**ctx_peer(lax.rem(place + away, count)), "tensor": z},
                device_id_type=MESH,
            )
    pl.semaphore_wait(barrier, n - 1 + 2 * n)
    x_line = LineGather(me, n, lambda d: x_box.at[:, column(d)], line_groups(sems[4:8]))
    x_line.step(0)
    gains = [push(gains_box.at[:, column(me)], gains_box.at[:, column(me)], gain_sems, d - 1,
                  lax.rem(me + d, n)) for d in range(1, n)]
    for copy in gains:
        copy.start()
    sends, gets = place < count - 1, place > 0
    halos = []
    for d in range(n):
        peer = {**ctx_peer(jnp.minimum(place + 1, count - 1)), "tensor": lax.rem(me + d, n)}
        halos.append(push(x_ref.at[rows - HALO :], halo_box.at[:, column(me)], halo_sems, d, peer))
        pl.when(sends)(halos[-1].start)
    for t in range(1, n):
        x_line.step(t)
    for copy in gains:
        copy.wait_recv()
    for copy in halos:
        pl.when(gets)(copy.wait_recv)
    gain = gains_box[0:1, :].astype(f32)
    gain_out[...] = gains_box[...].astype(f32)

    def normed(x):
        x = x.astype(f32)
        scale = lax.rsqrt(jnp.mean(x * x, axis=1, keepdims=True) + epsilon)
        return (x * scale * gain).astype(bf16)

    mixed_ref[:HALO, :] = normed(halo_box[...])
    full_ref[...] = x_box[...]
    mixed_ref[HALO:, :] = normed(x_box[...])
    mixed_t_ref[...] = mixed_ref[HALO:, :].T
    for copy in gains:
        copy.wait_send()
    for copy in halos:
        pl.when(sends)(copy.wait_send)
    x_line.wait_send()


def intake(x, gains):
    n = lax.axis_size("tensor")
    rows, quarter = x.shape
    depth = n * quarter
    shape = jax.ShapeDtypeStruct
    dma = pltpu.SemaphoreType.DMA
    return pl.pallas_call(
        partial(intake_kernel, n=n),
        in_specs=[VMEM] * 2,
        out_specs=[VMEM] * 4,
        out_shape=[shape((rows + HALO, depth), bf16), shape((depth, rows), bf16),
                   shape((rows, depth), bf16), shape((16, depth), f32)],
        scratch_shapes=[
            pltpu.VMEM((rows, depth), bf16),
            pltpu.VMEM((16, depth), bf16), pltpu.VMEM((HALO, depth), bf16),
            dma((n - 1,)), dma((n - 1,)), dma((n,)), dma((n,)),
        ] + line_sems(n),
        compiler_params=pltpu.CompilerParams(
            vmem_limit_bytes=60 << 20, collective_id=7, has_side_effects=True
        ),
        cost_estimate=cost(50),
        name="intake",
    )(x, gains)


def row_columns(row):
    return jnp.concatenate(
        [as_column(row[:, at : at + LANES]) for at in range(0, row.shape[1], LANES)], axis=0
    )


def front_kernel(mixed_ref, taps_ref, same_ref, bias_ref, decay_ref, end_ref, link_ref, seg_col_ref,
                 seg_row_ref, skip_ref, gain_ref, x_ref, cot_ref, mid_ref, chosen_ref, w_ref,
                 value_ref, act_ref, scaled_ref, step_ref, run_ref, run_exp_ref, inner_ref, mixer_ref,
                 state_ref, packed_ref, res_ref, stat_ref, own_ref, cot_full_ref, mix_ref, mix_t_ref, gates_ref,
                 wm_ref, wo_ref, run_t_ref, scores_ref, part_ref, square_ref, lifted_ref, far_ref,
                 right_box, left_box, square_box, res_box, stat_box, cot_box, router_ref, local_sem, *sems,
                 inner, nstate, per, heads, di_all, n):
    me = lax.axis_index("tensor")
    rows, depth = x_ref.shape
    own = rows // n
    groups = [(sems[2 * i], sems[2 * i + 1]) for i in range(3)]
    block_at = lambda d: pl.ds(pl.multiple_of(d * own, own), own)
    half = own // 2
    half_at = lambda d, h: pl.ds(pl.multiple_of(d * own + h * half, half), half)
    lines_at = lambda k: line_groups(sems[6 + 4 * k : 10 + 4 * k])
    mine = pl.ds(pl.multiple_of(me * own, own), own)
    wide = wm_ref.shape[1]
    loads = [
        pltpu.make_async_copy(w_ref.at[:, pl.ds(0, wide)], wm_ref, local_sem.at[0]),
        pltpu.make_async_copy(w_ref.at[:, pl.ds(wide, inner)], wo_ref, local_sem.at[1]),
        pltpu.make_async_copy(w_ref.at[:, pl.ds(wide + inner, LANES)], router_ref, local_sem.at[2]),
    ]
    for copy in loads:
        copy.start()
    far_ref[...] = jnp.zeros_like(far_ref)
    quarter = cot_ref.shape[1]
    column = pl.ds(pl.multiple_of(me * quarter, LANES), quarter)
    cot_box[:, column] = cot_ref[...]
    front_barrier(me, n)
    cots = LineGather(
        me, n, lambda d: cot_box.at[:, pl.ds(pl.multiple_of(d * quarter, LANES), quarter)],
        lines_at(0),
    )
    cots.step(0)
    loads[0].wait()
    enter_part(mixed_ref, wm_ref, taps_ref, same_ref, bias_ref, decay_ref, end_ref, link_ref,
               value_ref, act_ref, scaled_ref, step_ref, run_ref, run_exp_ref, packed_ref,
               inner=inner, nstate=nstate, per=per)
    states = StatePush(packed_ref, far_ref, groups[0], False)
    states.start()
    cots.step(1)
    run_t = run_ref[...].T
    for h in range(heads):
        run_t_ref[h] = run_t[h : h + 1, :]
    intra_part(act_ref, scaled_ref, run_t_ref, run_exp_ref, seg_col_ref, seg_row_ref, inner_ref,
               scores_ref, inner=inner, nstate=nstate, per=per, block=128)
    cots.step(2)
    states.wait_recv()
    state = join_states(far_ref, inner, per)
    state_ref[...] = state
    carried = dot_outer(act_ref[:, inner + nstate :], state.astype(bf16)) * (
        jnp.exp(run_exp_ref[...]) * link_ref[...]
    )
    mixer = inner_ref[...] + carried + skip_ref[...] * act_ref[:, :inner].astype(f32)
    mixer_ref[...] = mixer
    z = value_ref[HALO:, :inner]
    gated = mixer * (z * sigmoid(z))
    square_ref[...] = row_sums(gated * gated)
    lifted_ref[...] = (gated * gain_ref[...]).astype(bf16)
    loads[1].wait()
    for t in range(3, n):
        cots.step(t)
    squares, stats = [], []
    for d in range(1, n):
        peer = lax.rem(me + d, n)
        squares.append(push(square_ref.at[:, block_at(peer)], square_box.at[d - 1], groups[1], d - 1, peer))
        squares[-1].start()
    lines = [
        LineReduce(me, n, lambda d, h=h: part_ref.at[d, pl.ds(h * half, half)], right_box.at[h],
                   left_box.at[h], lines_at(1 + h)) for h in range(2)
    ]
    gathers = [LineGather(me, n, lambda d, h=h: res_box.at[half_at(d, h)], lines_at(3 + h))
               for h in range(2)]
    for k in range(n):
        d = jnp.where(2 * me < n, n - 1 - k, k)
        part_ref[d] = dot_outer(lifted_ref[block_at(d), :], wo_ref[...]).astype(bf16)
        if k == 0:
            for line in lines:
                line.step(0)
    square = square_ref[:, mine]
    for copy in squares:
        copy.wait_recv()
    for d in range(1, n):
        square = square + square_box[d - 1]
    scale = lax.rsqrt(square / di_all + epsilon)
    stat_box[:, mine] = scale
    for d in range(1, n):
        stats.append(push(stat_box.at[:, mine], stat_box.at[:, mine], groups[2], d - 1,
                          lax.rem(me + d, n)))
        stats[-1].start()
    scale = as_column(scale[:1])
    for t in range(1, n - 1):
        for line in lines:
            line.step(t)
    for h in range(2):
        lines[h].step(n - 1)
        total = lines[h].total()
        own_ref[h * half : (h + 1) * half, :] = total
        here = half_at(me, h)
        res_box[here, :] = (
            x_ref[here, :].astype(f32) + total * scale[h * half : (h + 1) * half]
        ).astype(bf16)
        gathers[h].step(0)
    for t in range(1, n):
        for gather in gathers:
            gather.step(t)
    cot_full_ref[...] = cot_box[...]
    states.wait_send()
    cots.wait_send()
    for line in lines + gathers:
        line.wait_send()
    for copy in squares:
        copy.wait_send()
    for copy in stats:
        copy.wait()
    res_ref[...] = res_box[...]
    stat_ref[...] = stat_box[...]
    res = res_box[...].astype(f32)
    mix = (
        res * lax.rsqrt(jnp.mean(res * res, axis=1, keepdims=True) + epsilon) * mid_ref[...]
    ).astype(bf16)
    mix_ref[...] = mix
    mix_t_ref[...] = mix.T
    loads[2].wait()
    chosen = chosen_ref[...] > 0.0
    logits = dot_rows(mix, router_ref[...])
    top = jnp.max(jnp.where(chosen, logits, -1e30), axis=1, keepdims=True)
    weight = jnp.where(chosen, jnp.exp(jnp.where(chosen, logits - top, 0.0)), 0.0)
    gates_ref[...] = weight / jnp.sum(weight, axis=1, keepdims=True)


def pairs(count, n):
    return [pltpu.SemaphoreType.DMA((n - 1,))] * (2 * count)


VMEM = pl.BlockSpec(memory_space=pltpu.VMEM)
HBM = pl.BlockSpec(memory_space=pl.ANY)


def front(mixed_ext, taps, same, bias, decay, at_end, link, seg_col, seg_row, skip, gain, x, cot, mid,
          chosen, weights, inner, nstate, per, heads, di_all):
    n = lax.axis_size("tensor")
    others = lax.axis_size(CTX) - 1
    tokens, depth = x.shape
    ext = tokens + HALO
    own = tokens // n
    wide = 2 * inner + 2 * nstate + LANES
    shape = jax.ShapeDtypeStruct
    outs = [
        shape((ext, wide), f32), shape((tokens, inner + 2 * nstate), bf16),
        shape((tokens, inner), bf16), shape((tokens, LANES), f32), shape((tokens, LANES), f32),
        shape((tokens, inner), f32), shape((tokens, inner), f32), shape((tokens, inner), f32),
        shape((inner, nstate), f32), shape((inner + 16, nstate), bf16),
        shape((tokens, depth), bf16), shape((8, tokens), f32), shape((own, depth), f32),
        shape((tokens, depth), bf16), shape((tokens, depth), bf16), shape((depth, tokens), bf16),
        shape((tokens, LANES), f32),
    ]
    dma = pltpu.SemaphoreType.DMA
    return pl.pallas_call(
        partial(front_kernel, inner=inner, nstate=nstate, per=per, heads=heads, di_all=di_all, n=n),
        in_specs=[VMEM] * 15 + [HBM],
        out_specs=[VMEM] * 17,
        out_shape=outs,
        scratch_shapes=[
            pltpu.VMEM((depth, wide), bf16), pltpu.VMEM((depth, inner), bf16),
            pltpu.VMEM((heads, 1, tokens), f32), pltpu.VMEM((tokens, tokens), f32),
            pltpu.VMEM((n, own, depth), bf16), pltpu.VMEM((8, tokens), f32),
            pltpu.VMEM((tokens, inner), bf16), pltpu.VMEM((others, inner + 16, nstate), bf16),
            pltpu.VMEM((2, n, own // 2, depth), bf16), pltpu.VMEM((2, n, own // 2, depth), bf16),
            pltpu.VMEM((n - 1, 8, own), f32),
            pltpu.VMEM((tokens, depth), bf16), pltpu.VMEM((8, tokens), f32),
            pltpu.VMEM((tokens, depth), bf16), pltpu.VMEM((depth, LANES), bf16), dma((3,)),
            dma((others,)), dma((others,)),
        ] + pairs(2, n) + line_sems(n) * 5,
        compiler_params=pltpu.CompilerParams(
            vmem_limit_bytes=63 << 20, collective_id=1, has_side_effects=True
        ),
        cost_estimate=cost(100),
        name="front",
    )(mixed_ext, taps, same, bias, decay, at_end, link, seg_col, seg_row, skip, gain, x, cot, mid,
      chosen, weights)


def turn_kernel(dmix_hbm, dgate_ref, res_ref, cot_ref, own_ref, gain_ref,
                dres_ref, notes_ref, gains_ref,
                dmix_ref, right_box, left_box, gate_box, dres_box, notes_box, load_sem, *sems, n):
    me = lax.axis_index("tensor")
    rows, depth = res_ref.shape
    own = rows // n
    groups = [(sems[2 * i], sems[2 * i + 1]) for i in range(2)]
    block_at = lambda d: pl.ds(pl.multiple_of(d * own, own), own)
    mine = block_at(me)
    load = pltpu.make_async_copy(dmix_hbm, dmix_ref, load_sem)
    load.start()
    tensor_barrier(me, n)
    load.wait()
    half = own // 2
    half_at = lambda d, h: pl.ds(pl.multiple_of(d * own + h * half, half), half)
    lines_at = lambda k: line_groups(sems[4 + 4 * k : 8 + 4 * k])
    lines = [LineReduce(me, n, lambda d, h=h: dmix_ref.at[half_at(d, h)], right_box.at[h],
                        left_box.at[h], lines_at(h)) for h in range(2)]
    gathers = [LineGather(me, n, lambda d, h=h: dres_box.at[half_at(d, h)], lines_at(2 + h))
               for h in range(2)]
    for line in lines:
        line.step(0)
    first, second = [], []
    for d in range(1, n):
        peer = lax.rem(me + d, n)
        first.append(push(dgate_ref.at[:, block_at(peer)], gate_box.at[d - 1], groups[0], d - 1, peer))
        first[-1].start()
    res = res_ref[mine, :].astype(f32)
    scale = lax.rsqrt(jnp.mean(res * res, axis=1, keepdims=True) + epsilon)
    normed = res * scale
    for t in range(1, n - 1):
        for line in lines:
            line.step(t)
    gain_sum = None
    for h in range(2):
        lines[h].step(n - 1)
        dmix = lines[h].total()
        part = slice(h * half, (h + 1) * half)
        here = half_at(me, h)
        lifted = dmix * gain_ref[...]
        inside = jnp.mean(lifted * normed[part], axis=1, keepdims=True)
        dres_box[here, :] = (
            cot_ref[here, :].astype(f32) + scale[part] * (lifted - normed[part] * inside)
        ).astype(bf16)
        gathers[h].step(0)
        term = jnp.sum(dmix * normed[part], axis=0, keepdims=True)
        gain_sum = term if gain_sum is None else gain_sum + term
    gains_ref[...] = jnp.broadcast_to(gain_sum, gains_ref.shape)
    dgate = dgate_ref[:, mine]
    for copy in first:
        copy.wait_recv()
    for d in range(1, n):
        dgate = dgate + gate_box[d - 1]
    gates = dgate.shape[0]
    notes_box[:gates, mine] = dgate
    notes_box[gates:, mine] = row_sums(dres_box[mine, :].astype(f32) * own_ref[...])
    for d in range(1, n):
        peer = lax.rem(me + d, n)
        second.append(push(notes_box.at[:, mine], notes_box.at[:, mine], groups[1], d - 1, peer))
        second[-1].start()
    for t in range(1, n):
        for gather in gathers:
            gather.step(t)
    for line in lines + gathers:
        line.wait_send()
    for copy in first:
        copy.wait_send()
    for copy in second:
        copy.wait()
    dres_ref[...] = dres_box[...]
    notes_ref[...] = notes_box[...]


def turn_step(dmix, dgate, residual, cot, own_part, gain):
    n = lax.axis_size("tensor")
    tokens, depth = dmix.shape
    own = tokens // n
    shape = jax.ShapeDtypeStruct
    return pl.pallas_call(
        partial(turn_kernel, n=n),
        in_specs=[HBM] + [VMEM] * 5,
        out_specs=[VMEM] * 3,
        out_shape=[shape((tokens, depth), bf16), shape((dgate.shape[0] + 8, tokens), f32),
                   shape((8, depth), f32)],
        scratch_shapes=[
            pltpu.VMEM((tokens, depth), bf16),
            pltpu.VMEM((2, n, own // 2, depth), bf16), pltpu.VMEM((2, n, own // 2, depth), bf16),
            pltpu.VMEM((n - 1, dgate.shape[0], own), f32),
            pltpu.VMEM((tokens, depth), bf16), pltpu.VMEM((dgate.shape[0] + 8, tokens), f32),
            pltpu.SemaphoreType.DMA,
        ] + pairs(2, n) + line_sems(n) * 4,
        compiler_params=pltpu.CompilerParams(
            vmem_limit_bytes=60 << 20, collective_id=2, has_side_effects=True
        ),
        cost_estimate=cost(60),
        name="turn_step",
    )(dmix, dgate, residual, cot, own_part, gain)


def in_order(box, me, count):
    total = None
    for source in range(count):
        term = box[lax.rem(me - source + 2 * count - 1, count)].astype(f32)
        total = term if total is None else total + term
    return total


def row_place():
    cy, core = lax.axis_size("cy"), lax.axis_size("core")
    return (lax.axis_index("shard") * cy + lax.axis_index("cy")) * core + lax.axis_index("core")


def row_peer(place):
    cy, core = lax.axis_size("cy"), lax.axis_size("core")
    return {"shard": place // (cy * core), "cy": lax.rem(place // core, cy), "core": lax.rem(place, core)}


def last_kernel(grad_ref, x_ref, dres_ref, gain_ref, mid_ref, state_ref, early_ref, mixed_t_ref, mix_t_ref,
                state_all_ref, gates_ref, notes_ref, w_hbm,
                out_ref, early_out, late_out, main_out,
                w_ref, blocks_ref, right_box, left_box, cross_box, cross_in, gains_box, gains_in, state_in,
                early_in, late_ref, late_in, load_sem, stage_ref, *sems, n, count, boxes, inner, last):
    weights = WeightSum(stage_ref, sems[:boxes])
    sems = sems[boxes:]
    me = lax.axis_index("tensor")
    place = row_place()
    rows, depth = x_ref.shape
    quarter = depth // n
    wide = w_ref.shape[1]
    groups = [(sems[2 * i], sems[2 * i + 1]) for i in range(3)]
    row_groups = [(sems[6 + 2 * i], sems[7 + 2 * i]) for i in range(2)]
    load = pltpu.make_async_copy(w_hbm.at[:, pl.ds(0, wide)], w_ref, load_sem)
    load.start()

    def row_scale():
        x = x_ref[...].astype(f32)
        return lax.rsqrt(jnp.mean(x * x, axis=1, keepdims=True) + epsilon)

    scale = rows_barrier(me, n, row_scale)
    copies, states, lates = [], [], []
    load.wait()
    half = rows // 2
    lines = [
        LineReduce(me, n, lambda d, h=h: blocks_ref.at[d, pl.ds(h * half, half)], right_box.at[h],
                   left_box.at[h], line_groups(sems[10 + 4 * h : 14 + 4 * h])) for h in range(2)
    ]
    cross = jnp.zeros((8, rows), f32)
    for k in range(n):
        d = jnp.where(2 * me < n, n - 1 - k, k)
        theirs = pl.ds(pl.multiple_of(d * quarter, LANES), quarter)
        w = w_ref[theirs, :]
        block = dot_outer(grad_ref[...], w)
        blocks_ref[d] = block.astype(bf16)
        if k == 0:
            for line in lines:
                line.step(0)
            weights.product(mixed_t_ref, grad_ref.at[:, pl.ds(inner, inner)], 0)
            weights.to_sibling(0, inner)
        normed = x_ref[:, theirs].astype(f32) * scale
        cross = cross + row_sums(block * normed * gain_ref[:, theirs])
        gains_box[d] = jnp.where(
            row_iota((8, quarter)) == 0, jnp.sum(block * normed, axis=0, keepdims=True),
            mid_ref[:, theirs],
        )
    weights.to_chips(0)
    cross_box[...] = cross
    sums = []
    for d in range(1, n):
        peer = lax.rem(me + d, n)
        sums.append(push(gains_box.at[peer], gains_in.at[d - 1], groups[0], d - 1, peer))
        sums.append(push(cross_box, cross_in.at[d - 1], groups[1], d - 1, peer))
        states.append(push(state_ref, state_in.at[d - 1], groups[2], d - 1, peer))
    for d in range(1, count):
        copies.append(push(early_ref, early_in.at[d - 1], row_groups[0], d - 1,
                           row_peer(lax.rem(place + d, count))))
    for copy in sums + states + copies:
        copy.start()

    gates = gates_ref[...]
    kinds = notes_ref.shape[0] - 8
    moved = jnp.concatenate(
        [notes_ref[:kinds, :], jnp.zeros((LANES - kinds, gates.shape[0]), f32)], axis=0
    ).T
    inside = jnp.sum(gates * moved, axis=1, keepdims=True)
    first = 2 * inner
    for line in lines:
        line.step(1)
    weights.product(mixed_t_ref, state_all_ref, inner)
    weights.product(mixed_t_ref, grad_ref.at[:, pl.ds(last, LANES)], inner + last - first)
    weights.product(mix_t_ref, (gates * (moved - inside)).astype(bf16), inner + wide - first)
    weights.to_sibling(inner, wide - first + LANES)
    for copy in sums + states:
        copy.wait_recv()
    gains = gains_box[me]
    for d in range(1, n):
        gains = gains + gains_in[d - 1]
        cross = cross + cross_in[d - 1]
    state_in[n - 1] = state_ref[...]
    late_ref[:, :quarter] = gains
    late_ref[:, quarter:] = in_order(state_in, me, n)
    for d in range(1, count):
        lates.append(push(late_ref, late_in.at[d - 1], row_groups[1], d - 1,
                          row_peer(lax.rem(place + d, count))))
        lates[-1].start()
    for t in range(2, n - 1):
        for line in lines:
            line.step(t)
    weights.to_chips(1)
    here = pl.ds(pl.multiple_of(me * quarter, LANES), quarter)
    inside = row_columns(cross[:1]) / depth
    for h in range(2):
        lines[h].step(n - 1)
        part = slice(h * half, (h + 1) * half)
        out_ref[part, :] = dres_ref[part, here].astype(f32) + scale[part] * (
            lines[h].total() * gain_ref[:, here]
            - x_ref[part, here].astype(f32) * scale[part] * inside[part]
        )
    for copy in copies + lates:
        copy.wait_recv()
    early_in[count - 1] = early_ref[...]
    late_in[count - 1] = late_ref[...]
    early_out[...] = in_order(early_in, place, count)
    late_out[...] = in_order(late_in, place, count)
    weights.finish(main_out)
    for copy in copies + states + lates + sums:
        copy.wait_send()
    for line in lines:
        line.wait_send()


def last_step(vmem_args, weights, inner, last):
    value_grad, x, early, state = (vmem_args[i] for i in (0, 1, 6, 5))
    n, count = lax.axis_size("tensor"), lax.axis_size(ROWS)
    tokens, depth = x.shape
    quarter = depth // n
    wide = value_grad.shape[1]
    late = quarter + state.shape[1]
    shape = jax.ShapeDtypeStruct
    dma = pltpu.SemaphoreType.DMA
    boxes, main = weight_boxes(depth, wide - inner + LANES, 2)
    return pl.pallas_call(
        partial(last_kernel, n=n, count=count, boxes=len(boxes) - 1, inner=inner, last=last),
        in_specs=[VMEM] * len(vmem_args) + [HBM],
        out_specs=[VMEM] * 4,
        out_shape=[shape((tokens, quarter), f32), shape(early.shape, f32), shape((8, late), f32), main],
        scratch_shapes=[
            pltpu.VMEM((depth, wide), bf16), pltpu.VMEM((n, tokens, quarter), bf16),
            pltpu.VMEM((2, n, tokens // 2, quarter), bf16), pltpu.VMEM((2, n, tokens // 2, quarter), bf16),
            pltpu.VMEM((8, tokens), f32), pltpu.VMEM((n - 1, 8, tokens), f32),
            pltpu.VMEM((n, 8, quarter), f32), pltpu.VMEM((n - 1, 8, quarter), f32),
            pltpu.VMEM((n,) + state.shape, f32), pltpu.VMEM((count,) + early.shape, f32),
            pltpu.VMEM((8, late), f32), pltpu.VMEM((count, 8, late), f32), dma,
        ] + boxes + pairs(3, n) + [dma((count - 1,))] * 4 + line_sems(n) * 2,
        compiler_params=pltpu.CompilerParams(
            vmem_limit_bytes=62 << 20, collective_id=3, has_side_effects=True
        ),
        cost_estimate=cost(60),
        name="last_step",
    )(*vmem_args, weights)


def emit_kernel(out_ref, grad_ref, early_ref, late_ref, rear_ref, main_ref, *outs, per):
    (out, grad, gain_in, pair_out, state_out, step_out, conv, conv_state, bias, decay, skip, gate, proj,
     gain_mid, router) = outs
    out[...] = out_ref[...]
    grad[...] = grad_ref[...]
    taps, inner = conv.shape
    heads = bias.shape[1]
    quarter = grad.shape[1]
    conv[...] = early_ref[:taps]
    conv_state[...] = late_ref[:taps, quarter:]
    for i in range(inner // LANES):
        gate[i : i + 1, :] = early_ref[taps : taps + 1, i * LANES : (i + 1) * LANES]
    for i in range(quarter // LANES):
        columns = slice(i * LANES, (i + 1) * LANES)
        gain_in[i : i + 1, :] = late_ref[0:1, columns]
        gain_mid[i : i + 1, :] = late_ref[1:2, columns]
    skips = jnp.broadcast_to(early_ref[taps + 1 : taps + 2], (8, inner))
    skip[...] = fold_heads(skips, head_fold(inner, LANES, per).astype(bf16))[:1, :heads]
    bias[...] = early_ref[taps + 2 : taps + 3, :heads]
    decay[...] = early_ref[taps + 3 : taps + 4, :heads]
    last = inner + state_out.shape[1]
    wide = last + LANES
    proj[...] = rear_ref[:, :inner].astype(f32)
    pair_out[:, 0, :] = rear_ref[:, inner:].astype(f32)
    pair_out[:, 1, :] = main_ref[:, :inner].astype(f32)
    state_out[...] = main_ref[:, inner:last].astype(f32)
    step_out[...] = main_ref[:, last:wide].astype(f32).T[:heads, :]
    router[...] = main_ref[:, wide:].astype(f32).T[: router.shape[0], :]


def emit_experts_kernel(pair_ref, shared_up, shared_down, gates, down):
    hid, depth = down.shape[1:]
    wides = 2 * hid
    deep = depth + depth // 2
    for p in range(2):
        top = pair_ref[p * deep : p * deep + depth, :].astype(f32)
        gates[p * depth : (p + 1) * depth, 0, :] = top[:, :hid]
        gates[p * depth : (p + 1) * depth, 1, :] = top[:, hid:]
        for c in range(depth // wides):
            at = p * deep + depth + c * hid
            down[p, :, c * wides : (c + 1) * wides] = pair_ref[at : at + hid, :].astype(f32)
    wrows = shared_down.shape[0]
    part = shared_down.shape[1] // 2
    for p in range(2):
        top = pair_ref[2 * deep + p * wrows : 2 * deep + (p + 1) * wrows, :].astype(f32)
        shared_up[:, 0, p * part : (p + 1) * part] = top[:, :part]
        shared_up[:, 1, p * part : (p + 1) * part] = top[:, part:]
    shared_down[...] = pair_ref[2 * deep + 2 * wrows :, :].astype(f32)


def emit(args, inner, nstate, per, heads, kinds):
    out, grad, _, _, _, main = args
    tokens, quarter = grad.shape
    wrows = main.shape[0]
    flat = lambda *size: jax.ShapeDtypeStruct(size, f32)
    outs = [
        jax.ShapeDtypeStruct(out.shape, bf16), flat(tokens, quarter), flat(quarter // LANES, LANES),
        flat(wrows, 2, inner), flat(wrows, 2 * nstate), flat(heads, wrows), flat(CONV, inner),
        flat(CONV, 2 * nstate), flat(1, heads), flat(1, heads), flat(1, heads),
        flat(inner // LANES, LANES), flat(wrows, inner), flat(quarter // LANES, LANES), flat(kinds, wrows),
    ]
    return pl.pallas_call(
        partial(emit_kernel, per=per),
        in_specs=[VMEM] * 6,
        out_specs=[VMEM] * len(outs),
        out_shape=outs,
        compiler_params=BIG,
        cost_estimate=cost(4),
        name="emit",
    )(*args)


def emit_experts(pair, wrows, hid):
    depth = pair.shape[0] // 3 - wrows
    wide = pair.shape[1]
    flat = lambda *size: jax.ShapeDtypeStruct(size, f32)
    outs = [flat(wrows, 2, wide), flat(wrows, wide), flat(2 * depth, 2, hid), flat(2, hid, depth)]
    return pl.pallas_call(
        emit_experts_kernel,
        in_specs=[VMEM],
        out_specs=[VMEM] * len(outs),
        out_shape=outs,
        compiler_params=BIG,
        cost_estimate=cost(5),
        name="emit_experts",
    )(pair)


def back_part(dout_ref, w_ref, mixer_ref, value_ref, act_ref, run_exp_ref, link_ref, gain_ref,
                scale, cross, through_ref, heads_ref, zgrad_ref, gated_ref, direct_ref, sums_ref,
                *, inner, nstate, di_all):
    mixer = mixer_ref[...]
    z = value_ref[HALO:, :inner]
    sig = sigmoid(z)
    act = z * sig
    gated = mixer * act
    grad = dot_rows(dout_ref[...], w_ref[...])
    gated_ref[...] = (gated * scale * gain_ref[...]).astype(bf16)
    sums_ref[0:1, :] = jnp.sum(grad * gated * scale, axis=0, keepdims=True)
    gated_grad = scale * (grad * gain_ref[...]) - gated * (scale * scale * scale * cross / di_all)
    zgrad_ref[...] = (gated_grad * mixer * (sig * (1.0 + z * (1.0 - sig)))).astype(bf16)
    heads = gated_grad * act
    heads_ref[...] = heads
    sums_ref[1:2, :] = jnp.sum(heads * act_ref[:, :inner].astype(f32), axis=0, keepdims=True)
    sums_ref[2:, :] = jnp.zeros((6, inner), f32)
    carried = (heads * (jnp.exp(run_exp_ref[...]) * link_ref[...])).astype(bf16)
    direct_ref[:inner, :] = dot_inner(carried, act_ref[:, inner + nstate :]).astype(bf16)
    direct_ref[inner:, :] = through_ref[inner:, :]


def intra_back_part(heads_ref, act_ref, scaled_ref, run_t_ref, run_exp_ref, seg_col_ref,
                      seg_row_ref, dscaled_ref, dstate_ref, drun_ref, scores_ref, dscores_ref, *, inner, nstate, per, block):
    tokens = act_ref.shape[0]
    keys = act_ref[:, inner : inner + nstate]
    query = act_ref[:, inner + nstate :]
    for start in range(0, tokens, block):
        stop = start + block
        scores_ref[start:stop, :stop] = masked_scores(
            query, keys, seg_col_ref, seg_row_ref, start, stop
        )
    dscores_ref[...] = jnp.zeros_like(dscores_ref)
    drun_ref[...] = jnp.zeros_like(drun_ref)

    def pair(i, _):
        columns = pl.ds(pl.multiple_of(i * LANES, LANES), LANES)
        scaled = scaled_ref[:, columns]
        heads = heads_ref[:, columns].astype(bf16)
        lane = col_iota(scaled.shape)
        run = run_exp_ref[:, columns]
        dscaled_ref[:, columns] = jnp.zeros((tokens, LANES), f32)
        for h in range(LANES // per):
            head = i * (LANES // per) + h
            mine = (lane >= h * per) & (lane < (h + 1) * per)
            vals = jnp.where(mine, scaled, jnp.zeros_like(scaled))
            grads = jnp.where(mine, heads, jnp.zeros_like(heads))
            pick = (col_iota((block, LANES)) == head).astype(bf16)
            for start in range(0, tokens, block):
                stop = start + block
                row = run_t_ref[head, :, :stop]
                decay = jnp.exp(jnp.minimum(run[start:stop, h * per : h * per + 1] - row, 0.0))
                weight = decay * scores_ref[start:stop, :stop]
                dweight = dot_outer(grads[start:stop], vals[:stop])
                dscores_ref[start:stop, :stop] += dweight * decay
                flow = (dweight * weight).astype(bf16)
                dscaled_ref[:stop, columns] += dot_inner(weight.astype(bf16), grads[start:stop])
                picks = jnp.broadcast_to(pick[:1], (stop, LANES))
                drun_ref[start:stop, :] += dot_rows(flow, picks)
                drun_ref[:stop, :] -= dot_inner(flow, pick)
        return 0

    lax.fori_loop(0, inner // LANES, pair, 0)
    dkeys = jnp.zeros((tokens, nstate), f32)
    dstate_ref[:, :nstate] = dkeys
    for start in range(0, tokens, block):
        stop = start + block
        shape = (block, stop)
        allowed = (row_iota(shape) + start >= col_iota(shape)) & (
            seg_col_ref[start:stop, :1] == seg_row_ref[:, :stop]
        )
        grad = jnp.where(allowed, dscores_ref[start:stop, :stop], 0.0).astype(bf16)
        dstate_ref[start:stop, nstate:] = dot_rows(grad, keys[:stop])
        dstate_ref[:stop, :nstate] += dot_inner(grad, query[start:stop])


def conv_back(value_ref, column, taps_ref, same_ref, dact, at, dtaps_ref, tokens):
    ext = tokens + HALO
    rows, total = conv_pre(value_ref, column, taps_ref, at, same_ref, tokens)
    sig = sigmoid(total)
    dpre = dact * (sig * (1.0 + total * (1.0 - sig)))
    drows = None
    for offset in range(CONV):
        first = HALO - CONV + 1 + offset
        kept = dpre * same_ref[offset]
        dtaps_ref[offset : offset + 1, pl.ds(at, LANES)] = jnp.sum(
            kept * rows[first : first + tokens], axis=0, keepdims=True
        )
        term = kept * taps_ref[offset : offset + 1, pl.ds(at, LANES)]
        after = ext - first - tokens
        pieces = [jnp.zeros((first, LANES), f32), term]
        if after:
            pieces.append(jnp.zeros((after, LANES), f32))
        term = jnp.concatenate(pieces, axis=0)
        drows = term if drows is None else drows + term
    return drows


def state_back_part(heads_ref, act_ref, step_ref, run_ref, run_exp_ref, link_ref, end_ref,
                      value_ref, taps_ref, same_ref, dstate_ref, in_ref, far_ref,
                      rows_ref, dtaps_ref, leaving_ref, kept_ref, dact_ref, *, inner, nstate, per):
    tokens = act_ref.shape[0]
    keys = act_ref[:, inner : inner + nstate]
    signal = act_ref[:, :inner].astype(f32)
    grow = expander(LANES, inner, per)
    running = run_ref[...]
    state_grad = join_states(far_ref, inner, per)
    lifted = (heads_ref[...] * (jnp.exp(run_exp_ref[...]) * link_ref[...])).astype(bf16)
    dact_ref[:, nstate:] = dot_rows(lifted, in_ref[...].astype(bf16)) + dstate_ref[:, nstate:]
    toward = jnp.exp(running[tokens - 1 :] - running) * end_ref[...]
    toward_exp = spread_lanes(toward, grow)
    pushed = (signal * spread_lanes(step_ref[...] * toward, grow)).astype(bf16)
    leaving_ref[...] = dot_outer(keys, state_grad.astype(bf16)) * toward_exp
    dact_ref[:, :nstate] = dot_rows(pushed, state_grad.astype(bf16)) + dstate_ref[:, :nstate]
    kept = jnp.sum(in_ref[...] * state_grad, axis=1, keepdims=True)
    kept = jnp.sum(head_fold(inner, LANES, per) * kept, axis=0, keepdims=True)
    kept = kept * jnp.exp(running[tokens - 1 :]) * link_ref[tokens - 1 :]
    kept_ref[...] = jnp.broadcast_to(kept, kept_ref.shape)

    def conv(i, _):
        at = pl.multiple_of(i * LANES, LANES)
        drows = conv_back(value_ref, 2 * inner + at, taps_ref, same_ref, dact_ref[:, pl.ds(at, LANES)],
                          inner + at, dtaps_ref, tokens)
        rows_ref[:, pl.ds(at, LANES)] = drows.astype(bf16)
        return 0

    lax.fori_loop(0, 2 * nstate // LANES, conv, 0)


def signal_back_part(heads_ref, act_ref, step_ref, value_ref, taps_ref, same_ref, bias_ref,
                       decay_ref, skip_ref, mixer_ref, inner_ref, dscaled_ref, drun_ref, leaving_ref,
                       kept_ref, zgrad_ref, state_ref,
                       grad_ref, dtaps_ref, small_ref, dact_ref, middle, between, *, inner, nstate, per):
    tokens = act_ref.shape[0]
    signal = act_ref[:, :inner].astype(f32)
    grow = expander(LANES, inner, per)
    folds = head_fold(inner, LANES, per).astype(bf16)
    step = step_ref[...]
    heads = heads_ref[...]
    leaving = leaving_ref[...]
    step_exp = spread_lanes(step, grow)
    dscaled = dscaled_ref[...] + leaving
    dact_ref[...] = dscaled * step_exp + skip_ref[...] * heads

    def conv(i, _):
        at = pl.multiple_of(i * LANES, LANES)
        drows = conv_back(value_ref, inner + at, taps_ref, same_ref, dact_ref[:, pl.ds(at, LANES)], at,
                          dtaps_ref, tokens)
        grad_ref[:, pl.ds(inner + at, LANES)] = drows.astype(bf16)
        return 0

    half = inner // LANES // 2
    lax.fori_loop(0, half, conv, 0)
    middle()
    lax.fori_loop(half, inner // LANES, conv, 0)
    between()
    carried = mixer_ref[...] - inner_ref[...] - skip_ref[...] * signal
    tri = (row_iota((tokens, tokens)) <= col_iota((tokens, tokens))).astype(bf16)
    strict = (row_iota((tokens, tokens)) > col_iota((tokens, tokens))).astype(bf16)
    back_sum = drun_ref[...] + fold_heads(heads * carried, folds)
    front_sum = fold_heads(signal * step_exp * leaving, folds)
    dlog = left_sums(tri, back_sum) + left_sums(strict, front_sum) + kept_ref[0:1, :]
    rate = -jnp.exp(decay_ref[...])
    dstep = dlog * rate + fold_heads(dscaled * signal, folds)
    draw = dstep * sigmoid(value_ref[HALO:, 2 * inner + 2 * nstate :] + bias_ref[...])
    small_ref[0:1, :] = jnp.sum(draw, axis=0, keepdims=True)
    small_ref[1:2, :] = jnp.sum(dlog * step, axis=0, keepdims=True) * rate
    small_ref[2:, :] = jnp.zeros((6, LANES), f32)
    state_at = 2 * inner
    step_at = state_at + 2 * nstate
    grad_ref[:HALO, :inner] = jnp.zeros((HALO, inner), bf16)
    grad_ref[HALO:, :inner] = zgrad_ref[...]
    grad_ref[:, state_at:step_at] = state_ref[...]
    grad_ref[:HALO, step_at:] = jnp.zeros((HALO, LANES), bf16)
    used = col_iota((tokens, LANES)) < inner // per
    grad_ref[HALO:, step_at:] = jnp.where(used, draw, 0.0).astype(bf16)


def rear_kernel(dout_ref, stat_ref, notes_ref, mixer_ref, inner_ref, act_ref, scaled_ref, step_ref,
                run_ref, run_exp_ref, state_ref, taps_ref, same_ref, bias_ref, decay_ref, skip_ref,
                gain_ref, end_ref, link_ref, seg_col_ref, seg_row_ref, packed_ref, mixed_t_ref,
                part_hbm, value_hbm, w_hbm, res_hbm,
                grad_ref, main_ref, early_ref, taps_out, state_all_ref, out_ref,
                dtaps_ref, sums_ref, small_ref, gated_ref, value_ref, w_ref, res_ref, run_t_ref, heads_ref, zgrad_ref, direct_ref, dscaled_ref,
                dstate_ref, drun_ref, scores_ref, dscores_ref, leaving_ref, kept_ref, rows_ref, dact_ref,
                far_ref, part_ref, right_box, left_box, rows_box, sum_box, ext_ref, state_halo, signal_halo,
                local_sem, stage_ref, *sems,
                inner, nstate, per, heads, di_all, n, boxes):
    me = lax.axis_index("tensor")
    weights = WeightSum(stage_ref, sems[:boxes])
    sems = sems[boxes:]
    tokens = act_ref.shape[0]
    quarter = part_ref.shape[1] // n
    own = tokens // n
    wide = value_ref.shape[1]
    groups = [(sems[2 * i], sems[2 * i + 1]) for i in range(4)]
    column = lambda k: pl.ds(pl.multiple_of(k * quarter, LANES), quarter)
    loads = [
        pltpu.make_async_copy(part_hbm, part_ref, local_sem.at[3]),
        pltpu.make_async_copy(w_hbm.at[:, pl.ds(wide, inner)], w_ref, local_sem.at[0]),
        pltpu.make_async_copy(value_hbm, value_ref, local_sem.at[1]),
        pltpu.make_async_copy(res_hbm.at[:, column(me)], res_ref, local_sem.at[2]),
    ]
    for copy in loads:
        copy.start()
    far_ref[...] = jnp.zeros_like(far_ref)
    state_halo[...] = jnp.zeros_like(state_halo)
    signal_halo[...] = jnp.zeros_like(signal_halo)

    def prepare():
        run_t = run_ref[...].T
        for h in range(heads):
            run_t_ref[h] = run_t[h : h + 1, :]
        gates = notes_ref.shape[0] - 8
        return row_columns(stat_ref[0:1, :]), row_columns(notes_ref[gates : gates + 1, :])

    scale, cross = rows_barrier(me, n, prepare)
    line = LineReduce(me, n, lambda d: part_ref.at[:, column(d)], right_box, left_box,
                      line_groups(sems[8:12]))
    loads[0].wait()
    line.step(0)
    for copy in loads[1:]:
        copy.wait()
    back_part(dout_ref, w_ref, mixer_ref, value_ref, act_ref, run_exp_ref, link_ref, gain_ref,
              scale, cross, packed_ref, heads_ref, zgrad_ref, gated_ref, direct_ref, sums_ref,
              inner=inner, nstate=nstate, di_all=di_all)
    states = StatePush(direct_ref, far_ref, groups[0], True)
    states.start()
    weights.product(dout_ref, gated_ref, 0, False)
    weights.to_sibling(0, inner)
    weights.product(mixed_t_ref, zgrad_ref, inner)
    weights.to_sibling(inner, inner)
    line.step(1)
    intra_back_part(heads_ref, act_ref, scaled_ref, run_t_ref, run_exp_ref, seg_col_ref, seg_row_ref,
                    dscaled_ref, dstate_ref, drun_ref, scores_ref, dscores_ref,
                    inner=inner, nstate=nstate, per=per, block=128)
    line.step(2)
    weights.pair(0, main_ref)
    states.wait_recv()
    state_back_part(heads_ref, act_ref, step_ref, run_ref, run_exp_ref, link_ref, end_ref, value_ref,
                    taps_ref, same_ref, dstate_ref, state_ref, far_ref, rows_ref, dtaps_ref,
                    leaving_ref, kept_ref, dact_ref.at[:, pl.ds(0, 2 * nstate)],
                    inner=inner, nstate=nstate, per=per)
    body = lambda d: pl.ds(pl.multiple_of(HALO + d * own, 16), own)
    reduces, gathers = [], []
    place, count = ctx_place()
    sends, gets = place > 0, place < count - 1
    before = ctx_peer(jnp.maximum(place - 1, 0))
    state_copy = push(rows_ref.at[pl.ds(0, HALO)], state_halo, groups[2], 0, before)
    signal_copy = push(ext_ref.at[pl.ds(0, HALO), pl.ds(inner, inner)], signal_halo, groups[2], 1, before)
    pl.when(sends)(state_copy.start)

    weights.pair(1, main_ref)

    def middle():
        pl.when(gets)(state_copy.wait_recv)
        rows_ref[tokens:, :] = rows_ref[tokens:, :] + state_halo[...]
        for d in range(1, n):
            peer = lax.rem(me + d, n)
            reduces.append(push(rows_ref.at[body(peer)], rows_box.at[d - 1], groups[1], d - 1, peer))
            reduces[-1].start()

    def between():
        pl.when(sends)(signal_copy.start)
        total = rows_ref[body(me), :].astype(f32)
        for copy in reduces:
            copy.wait_recv()
        for d in range(1, n):
            total = total + rows_box[d - 1].astype(f32)
        sum_box[body(me), :] = total.astype(bf16)
        for d in range(1, n):
            peer = lax.rem(me + d, n)
            gathers.append(push(sum_box.at[body(me)], sum_box.at[body(me)], groups[3], d - 1, peer))
            gathers[-1].start()

    signal_back_part(heads_ref, act_ref, step_ref, value_ref, taps_ref, same_ref, bias_ref, decay_ref,
                     skip_ref, mixer_ref, inner_ref, dscaled_ref, drun_ref, leaving_ref, kept_ref,
                     zgrad_ref, rows_ref, ext_ref, dtaps_ref, small_ref, dact_ref, middle, between,
                     inner=inner, nstate=nstate, per=per)
    early_ref[:CONV, :] = dtaps_ref[:, :inner]
    early_ref[CONV : CONV + 2, :] = sums_ref[:2, :]
    early_ref[CONV + 2 :, :] = jnp.zeros((2, inner), f32)
    early_ref[CONV + 2 :, :LANES] = small_ref[:2, :]
    taps_out[:CONV, :] = dtaps_ref[:, inner:]
    taps_out[CONV:, :] = jnp.zeros((8 - CONV, 2 * nstate), f32)
    grad_ref[...] = ext_ref[HALO:, :]
    pl.when(gets)(signal_copy.wait_recv)
    grad_ref[tokens - HALO :, inner : 2 * inner] = (
        ext_ref[tokens:, inner : 2 * inner] + signal_halo[...]
    )
    for t in range(3, n):
        line.step(t)
    out_ref[...] = (line.total() + res_ref[...].astype(f32)).astype(bf16)
    for copy in gathers:
        copy.wait_recv()
    state_all_ref[...] = sum_box[HALO:, :]
    weights.wait_send()
    states.wait_send()
    line.wait_send()
    pl.when(sends)(state_copy.wait_send)
    pl.when(sends)(signal_copy.wait_send)
    for copy in reduces + gathers:
        copy.wait_send()


def rear(vmem_args, part, value, weights, residual, inner, nstate, per, heads, di_all):
    n = lax.axis_size("tensor")
    others = lax.axis_size(CTX) - 1
    ext, wide = value.shape
    tokens = ext - HALO
    depth = residual.shape[1]
    quarter = depth // n
    boxes, main = weight_boxes(depth, 2 * inner, 2, False)
    shape = jax.ShapeDtypeStruct
    outs = [
        shape((tokens, wide), bf16), main, shape((8, inner), f32), shape((8, 2 * nstate), f32),
        shape((tokens, 2 * nstate), bf16),
        shape((tokens, quarter), bf16),
    ]
    dma = pltpu.SemaphoreType.DMA
    return pl.pallas_call(
        partial(rear_kernel, inner=inner, nstate=nstate, per=per, heads=heads, di_all=di_all, n=n,
                boxes=len(boxes) - 1),
        in_specs=[VMEM] * len(vmem_args) + [HBM] * 4,
        out_specs=[VMEM] * len(outs),
        out_shape=outs,
        scratch_shapes=[
            pltpu.VMEM((CONV, inner + 2 * nstate), f32), pltpu.VMEM((8, inner), f32),
            pltpu.VMEM((8, LANES), f32), pltpu.VMEM((tokens, inner), bf16),
            pltpu.VMEM((ext, wide), f32), pltpu.VMEM((depth, inner), bf16),
            pltpu.VMEM((tokens, quarter), bf16), pltpu.VMEM((heads, 1, tokens), f32),
            pltpu.VMEM((tokens, inner), f32), pltpu.VMEM((tokens, inner), bf16),
            pltpu.VMEM((inner + 16, nstate), bf16), pltpu.VMEM((tokens, inner), f32),
            pltpu.VMEM((tokens, 2 * nstate), f32), pltpu.VMEM((tokens, LANES), f32),
            pltpu.VMEM((tokens, tokens), f32), pltpu.VMEM((tokens, tokens), f32),
            pltpu.VMEM((tokens, inner), f32), pltpu.VMEM((8, LANES), f32),
            pltpu.VMEM((ext, 2 * nstate), bf16), pltpu.VMEM((tokens, inner), f32),
            pltpu.VMEM((others, inner + 16, nstate), bf16),
            pltpu.VMEM((tokens, depth), bf16),
            pltpu.VMEM((n, tokens, quarter), bf16), pltpu.VMEM((n, tokens, quarter), bf16),
            pltpu.VMEM((n - 1, tokens // n, 2 * nstate), bf16),
            pltpu.VMEM((ext, 2 * nstate), bf16), pltpu.VMEM((ext, wide), bf16),
            pltpu.VMEM((HALO, 2 * nstate), bf16), pltpu.VMEM((HALO, inner), bf16),
            dma((4,)),
        ] + boxes + [
            dma((others,)), dma((others,)), dma((n - 1,)), dma((n - 1,)), dma((2,)), dma((2,)),
            dma((n - 1,)), dma((n - 1,)),
        ] + line_sems(n),
        compiler_params=pltpu.CompilerParams(
            vmem_limit_bytes=63 << 20, collective_id=5, has_side_effects=True
        ),
        cost_estimate=cost(50),
        name="rear",
    )(*vmem_args, part, value, weights, residual)


def swiglu(first, second):
    sig = sigmoid(first)
    act = first * sig
    return act, sig * (1.0 + first * (1.0 - sig)), (act * second).astype(bf16)


def experts_kernel(mix_ref, mix_t_ref, cot_ref, gates_ref, router_ref, w_ref, shared_hbm,
                   dgate_t_ref, out_hbm, dmix_hbm, dw_hbm, dgate_ref, total_ref, grads_ref, down_ref, hidden_ref, dval_ref,
                   grad_ref, shared_ref, first_ref, second_ref, result_ref, extra_ref, local_sem, *remote,
                   tile, senders, core):
    step = pl.program_id(0)
    last = step == pl.num_programs(0) - 1
    rows, depth = mix_ref.shape
    place = row_place()
    far_send, far_receive, near_send, near_receive, keep_sem, *remote = remote
    gather = RowGather(shared_hbm, shared_ref, ((far_send, far_receive), (near_send, near_receive)))
    own_copy = pltpu.make_async_copy(shared_hbm, shared_ref.at[place], local_sem.at[0])
    if core == 2:
        inbox, shared_in, send, receive, pair_sem = remote
        me = lax.axis_index("core")
        slot = lax.rem(step + me, 2)
        pair_copy = lambda k: push(grad_ref.at[1], inbox.at[k], (send, receive), k, {"core": 1 - me})
        span = 3 * depth // 2
        mine = pl.ds(pl.multiple_of(me * span, 16), span)
        theirs = pl.ds(pl.multiple_of((1 - me) * span, 16), span)
        shared_copy = push(extra_ref.at[theirs], shared_in, (send, receive), senders // 2,
                           {"core": 1 - me})
        keep_copy = lambda k: pltpu.make_async_copy(
            inbox.at[k], dw_hbm.at[k, pl.ds(0, 3 * depth)], pair_sem.at[k]
        )
    else:
        slot = 0

    @pl.when(step == 0)
    def _():
        own_copy.start()
        barrier = pltpu.get_barrier_semaphore()
        cy, chips = lax.axis_size("cy"), lax.axis_size(CHIPS)
        chip = lax.axis_index("shard") * cy + lax.axis_index("cy")
        for d in range(1, chips):
            peer = lax.rem(chip + d, chips)
            pl.semaphore_signal(barrier, inc=1, device_id={"shard": peer // cy, "cy": lax.rem(peer, cy)},
                                device_id_type=MESH)
        if core == 2:
            pl.semaphore_signal(barrier, inc=1, device_id={"core": 1 - me}, device_id_type=MESH)
        pl.semaphore_wait(barrier, chips - 1 + core - 1)
        gather.start()
        total_ref[...] = jnp.zeros_like(total_ref)
        grads_ref[...] = jnp.zeros_like(grads_ref)
        dgate_ref[...] = jnp.zeros_like(dgate_ref)
        own_copy.wait()

    if core == 2:
        @pl.when((step >= 2) & (step < senders) & (slot == 1))
        def _():
            pair_copy((step - 2) // 2).wait_send()

    kept_at = lambda k: 2 * lax.rem(k, 2)
    buffer = jnp.where(slot == 1, 1, kept_at(step // 2)) if core == 2 else 0

    @pl.when(step < senders)
    def _():
        pair_grads(
            step, buffer, mix_ref, mix_t_ref, cot_ref, gates_ref, w_ref, dgate_ref, total_ref, grads_ref,
            down_ref, hidden_ref, dval_ref, grad_ref, tile
        )

    @pl.when(step == 1)
    def _():
        gather.relay()

    @pl.when(step == 2)
    def _():
        gather.finish()

    if core == 2:
        @pl.when((step < senders) & (slot == 1))
        def _():
            pair_copy(step // 2).start()

        def add_sibling(at):
            pair_copy(at).wait_recv()
            inbox[at] = grad_ref[kept_at(at)] + inbox[at]
            keep_copy(at).start()

        @pl.when((step >= 2) & (slot == 0))
        def _():
            add_sibling((step - 2) // 2)

        @pl.when(last)
        def _():
            pair_copy(senders // 2 - 1).wait_send()
    else:
        @pl.when(step < senders)
        def _():
            copy = pltpu.make_async_copy(
                grad_ref.at[0], dw_hbm.at[step, pl.ds(0, 3 * depth)], local_sem.at[3]
            )
            copy.start()
            copy.wait()

    @pl.when(step == 3)
    def _():
        wide = w_ref.shape[2]
        hid = wide // 2
        wrows = depth // senders
        for p in range(2):
            first_ref[p] = shared_ref[:, p * wrows : (p + 1) * wrows, :].reshape(depth, wide)
        second_ref[...] = shared_ref[:, 2 * wrows :, :].reshape(depth, wide)
        raw = dot_rows(cot_ref[...], second_ref[...])
        for p in range(2):
            value = dot_rows(mix_ref[...], first_ref[p])
            act, slope, hidden = swiglu(value[:, :hid], value[:, hid:])
            dh = raw[:, p * hid : (p + 1) * hid]
            dval_ref[p, :, :hid] = (dh * value[:, hid:] * slope).astype(bf16)
            dval_ref[p, :, hid:] = (dh * act).astype(bf16)
            hidden_ref[:, p * hid : (p + 1) * hid] = hidden
        total_ref[...] += dot_outer(hidden_ref[...], second_ref[...])
        grads_ref[...] += dot_outer(dval_ref[0], first_ref[0]) + dot_outer(dval_ref[1], first_ref[1])
        for k in range(3):
            if k < 2:
                grad = dot_rows(mix_t_ref[...], dval_ref[k]).astype(bf16)
            else:
                grad = dot_inner(cot_ref[...], hidden_ref[...]).astype(bf16)
            for j in range(senders):
                at = (3 * ((j % core) * (senders // core) + j // core) + k) * wrows
                extra_ref[at : at + wrows, :] = grad[j * wrows : (j + 1) * wrows]
        if core == 2:
            shared_copy.start()

    @pl.when(last)
    def _():
        result_ref[...] = total_ref[...].astype(bf16)
        out_copy = pltpu.make_async_copy(result_ref, out_hbm, local_sem.at[2])
        out_copy.start()
        copies = [out_copy]
        part = 3 * (depth // senders)
        source = extra_ref
        if core == 2:
            shared_copy.wait_recv()
            shared_in[...] = shared_in[...] + extra_ref[mine, :]
            source = shared_in
        kept = senders // core
        for j in range(kept):
            copies.append(pltpu.make_async_copy(
                source.at[pl.ds(j * part, part)], dw_hbm.at[j, pl.ds(3 * depth, part)], keep_sem.at[j]
            ))
            copies[-1].start()
        gates = gates_ref[...]
        dgate = dgate_ref[...]
        inside = jnp.sum(gates * dgate, axis=1, keepdims=True)
        dlogits = (gates * (dgate - inside)).astype(bf16)
        out_copy.wait()
        result_ref[...] = (grads_ref[...] + dot_outer(dlogits, router_ref[...])).astype(bf16)
        dmix_copy = pltpu.make_async_copy(result_ref, dmix_hbm, local_sem.at[4])
        dmix_copy.start()
        dgate_t_ref[...] = dgate.T[: dgate_t_ref.shape[0], :]
        if core == 2:
            pl.when(slot == 1)(lambda: add_sibling(senders // 2 - 1))
        for copy in copies[1:] + [dmix_copy]:
            copy.wait()
        if core == 2:
            for k in range(kept):
                keep_copy(k).wait()
            shared_copy.wait_send()


def pair_grads(step, slot, mix_ref, mix_t_ref, cot_ref, gates_ref, w_ref, dgate_ref, total_ref, grads_ref,
               down_ref, hidden_ref, dval_ref, grad_ref, tile):
    rows, depth = mix_ref.shape
    wide = w_ref.shape[2]
    hid = wide // 2
    chunks = depth // wide
    deep = depth + depth // 2
    for p in range(2):
        for c in range(chunks):
            down_ref[p * hid : (p + 1) * hid, c * wide : (c + 1) * wide] = (
                w_ref[0, p * deep + depth + c * hid : p * deep + depth + (c + 1) * hid, :]
            )
    down = down_ref[...]

    def part(i, _):
        at = pl.ds(pl.multiple_of(i * tile, tile), tile)
        mix = mix_ref[at, :]
        raw = dot_outer(cot_ref[at, :], down)
        gates = gates_ref[at, :]
        lane = col_iota(gates.shape)
        dmix, noted = None, jnp.zeros_like(gates)
        for p in range(2):
            here = lane == 2 * step + p
            gate = jnp.sum(jnp.where(here, gates, 0.0), axis=1, keepdims=True)
            weights = w_ref[0, p * deep : p * deep + depth, :]
            value = dot_rows(mix, weights)
            act, slope, hidden = swiglu(value[:, :hid], value[:, hid:])
            hidden = hidden.astype(f32)
            dh = raw[:, p * hid : (p + 1) * hid]
            noted = noted + jnp.where(here, jnp.sum(hidden * dh, axis=1, keepdims=True), 0.0)
            dh = gate * dh
            dval_ref[p, at, :hid] = (dh * value[:, hid:] * slope).astype(bf16)
            dval_ref[p, at, hid:] = (dh * act).astype(bf16)
            hidden_ref[at, p * hid : (p + 1) * hid] = (gate * hidden).astype(bf16)
            term = dot_outer(dval_ref[p, at, :], weights)
            dmix = term if dmix is None else dmix + term
        dgate_ref[at, :] += noted
        total_ref[at, :] += dot_rows(hidden_ref[at, :], down)
        grads_ref[at, :] += dmix
        return 0

    lax.fori_loop(0, rows // tile, part, 0)
    hidden_t = hidden_ref[...].T
    for c in range(chunks):
        grad = dot_rows(hidden_t, cot_ref[:, c * wide : (c + 1) * wide]).astype(bf16)
        for p in range(2):
            first = p * deep + depth + c * hid
            grad_ref[slot, first : first + hid, :] = grad[p * hid : (p + 1) * hid]
    for p in range(2):
        grad_ref[slot, p * deep : p * deep + depth, :] = (
            dot_rows(mix_t_ref[...], dval_ref[p]).astype(bf16)
        )


def experts(mix, mix_t, cot, gates, weights, router_at, experts_w, shared):
    senders, deep, wide = experts_w.shape
    rows, depth = mix.shape
    core, chips = lax.axis_size("core"), lax.axis_size(CHIPS)
    kept = senders // core
    kinds = 2 * senders + -2 * senders % 8
    shape = jax.ShapeDtypeStruct
    dma = pltpu.SemaphoreType.DMA
    once = lambda a: pl.BlockSpec(a.shape, lambda i: (0,) * a.ndim, pipeline_mode=pl.Buffered(1))
    outs = [shape((kinds, rows), f32)]
    remote = []
    if core == 2:
        remote = [pltpu.VMEM((kept, deep, wide), bf16), pltpu.VMEM((deep // 2, wide), bf16),
                  dma((kept + 1,)), dma((kept + 1,)), dma((kept,))]
    return pl.pallas_call(
        partial(experts_kernel, tile=rows, senders=senders, core=core),
        grid=(senders + 1,),
        in_specs=[once(mix), once(mix_t), once(cot), once(gates),
                  pl.BlockSpec((depth, LANES), lambda i: (0, router_at // LANES)),
                  pl.BlockSpec((1, deep, wide), lambda i: (jnp.minimum(i, senders - 1), 0, 0)), HBM],
        out_specs=[whole(o) for o in outs] + [HBM] * 3,
        out_shape=outs + [
            shape((rows, depth), bf16), shape((rows, depth), bf16),
            shape((kept, deep + shared.shape[0], wide), bf16),
        ],
        scratch_shapes=[
            pltpu.VMEM((rows, LANES), f32),
            pltpu.VMEM((rows, depth), f32), pltpu.VMEM((rows, depth), f32),
            pltpu.VMEM((wide, depth), bf16), pltpu.VMEM((rows, wide), bf16),
            pltpu.VMEM((2, rows, wide), bf16), pltpu.VMEM((2 * core - 1, deep, wide), bf16),
            pltpu.VMEM((senders,) + shared.shape, bf16), pltpu.VMEM((2, depth, wide), bf16),
            pltpu.VMEM((depth, wide), bf16), pltpu.VMEM((rows, depth), bf16), pltpu.VMEM((deep, wide), bf16), dma((5,)),
            dma((max(chips - 1, 1),)), dma((max(chips - 1, 1),)), dma((chips,)), dma((chips,)),
            dma((kept,)),
        ] + remote,
        compiler_params=pltpu.CompilerParams(
            vmem_limit_bytes=63 << 20, collective_id=4, has_side_effects=True
        ),
        cost_estimate=cost(7 * senders),
        name="experts",
    )(mix, mix_t, cot, gates, weights, experts_w, shared)


def local(
    block_input, gain_input, proj_main, proj_state, proj_step, conv_main, conv_state, step_bias,
    decay_log, skip_gain, gain_gate, proj_out, gain_mix, router_weight, shared_gates, shared_down,
    expert_gates, expert_down, segments, routes, cotangent,
):
    tokens, quarter = block_input.shape
    heads = step_bias.shape[0]
    inner = conv_main.shape[1]
    nstate = conv_state.shape[1] // 2
    per = inner // heads
    tensors = lax.axis_size("tensor")
    zi = lax.axis_index("tensor")
    senders = lax.axis_size(ROWS)
    depth = quarter * tensors
    di_all = inner * tensors
    own = tokens // tensors
    column = zi * quarter
    row0 = zi * own
    wrows = proj_main.shape[0]
    hid = expert_gates.shape[3]
    local_experts = expert_gates.shape[0]
    experts_all = local_experts * senders
    shared_here = shared_down.shape[1]
    router_pad = -experts_all % LANES

    main_wide = 2 * inner + 2 * nstate + LANES
    router_at = main_wide + inner
    weights = gather_rows(
        jnp.concatenate(
            [proj_main[:, 0], proj_main[:, 1], proj_state,
             jnp.pad(proj_step, ((0, 0), (0, LANES - heads))), proj_out,
             jnp.pad(router_weight, ((0, 0), (0, router_pad)))], axis=1
        )
    )
    pair_down = expert_down.reshape(local_experts, hid, depth // (2 * hid), 2 * hid)
    pair = jnp.concatenate(
        [expert_gates.reshape(local_experts, depth, 2 * hid),
         pair_down.transpose(0, 2, 1, 3).reshape(local_experts, -1, 2 * hid)], axis=1
    )
    shared_pair = shared_gates.reshape(wrows, 2, 2, shared_here // 2).transpose(2, 0, 1, 3)
    experts_w = gather_rows(pair.reshape(1, -1, 2 * hid))
    shared_local = jnp.concatenate([shared_pair.reshape(-1, shared_here), shared_down], axis=0)

    seg_row = segments[0]
    halo_seg = shifted(seg_row[tokens - CONV + 1 :], CTX, 1)
    gains = jnp.concatenate(
        [gain_input[None], gain_mix[None], jnp.zeros((14, quarter), bf16)], axis=0
    )
    mixed_ext, mixed_t, got, gain_rows = intake(block_input, gains)
    gain_row, gain_mid = gain_rows[0:1], gain_rows[1:2]

    segments_ext = jnp.concatenate([halo_seg, seg_row], axis=0)
    same = jnp.stack(
        [segments_ext[offset : offset + tokens] == seg_row for offset in range(CONV)]
    ).astype(f32)
    same = jnp.broadcast_to(same[:, :, None], (CONV, tokens, LANES))
    taps = jnp.concatenate([conv_main, conv_state], axis=1).astype(f32)
    lanes = lambda v: jnp.pad(v, (0, LANES - heads))[None]
    bias = lanes(step_bias)
    decay = lanes(decay_log)
    skip = jnp.repeat(skip_gain, per)[None]
    link = (seg_row == halo_seg[-1]).astype(f32)[:, None]
    at_end = (seg_row == seg_row[-1]).astype(f32)[:, None]
    seg_col = seg_row[:, None]
    seg_line = seg_row[None]
    chosen = jnp.any(
        routes[:, :, None] == jnp.arange(LANES, dtype=jnp.int32)[None, None, :], axis=1
    ).astype(f32)
    gain_gate_f = gain_gate.astype(f32)[None, :]
    (value, act, scaled, step, running, run_exp, within, mixer, state_in, packed, residual, scale_rows,
     own_part, cot_full, mix, mix_t, gates) = front(
        mixed_ext, taps, same, bias, decay, at_end, link, seg_col, seg_line, skip, gain_gate_f, got,
        cotangent, gain_mid, chosen, weights, inner, nstate, per, heads, di_all
    )

    dgate, out_part, dmix_part, dw = experts(
        mix, mix_t, cot_full, gates, weights, router_at, experts_w, shared_local
    )
    expert_rows = scatter_chips(dw.reshape(-1, 2 * hid))
    dmixer, notes, gains_mid = turn_step(
        dmix_part, dgate, residual, cot_full, own_part, gain_mid
    )

    value_grad, rear_main, early, state_taps, state_all, output = rear(
        (dmixer, scale_rows, notes, mixer, within, act, scaled, step, running, run_exp, state_in, taps,
         same, bias, decay, skip, gain_gate_f, at_end, link, seg_col, seg_line, packed,
         mixed_t),
        out_part, value, weights, residual, inner, nstate, per, heads, di_all
    )
    first = 2 * inner
    last = first + 2 * nstate
    rear_main, expert_rows = lax.optimization_barrier((rear_main, expert_rows))
    rear_main = scatter_chips(rear_main)

    grad_input, early, late, main = last_step(
        (value_grad, got, dmixer, gain_row, gains_mid, state_taps, early, mixed_t, mix_t, state_all,
         gates, notes),
        weights, inner, last,
    )
    if lax.axis_size("core") != 2:
        main = scatter_chips(main)
    expert_rows, main = lax.optimization_barrier((expert_rows, main))
    grad_shared, grad_shared_down, grad_gates, grad_down = emit_experts(expert_rows, wrows, hid)
    (output, grad_input, grad_gain_in, grad_main, grad_state, grad_step, grad_conv, grad_conv_state,
     grad_bias, grad_decay, grad_skip, grad_gate, grad_proj_out, grad_gain_mid, grad_router) = emit(
        (output, grad_input, early, late, rear_main, main), inner, nstate, per, heads, experts_all
    )
    return (
        output,
        grad_input,
        grad_gain_in.reshape(quarter),
        grad_main,
        grad_state,
        grad_step.T,
        grad_conv,
        grad_conv_state,
        grad_bias[0],
        grad_decay[0],
        grad_skip[0],
        grad_gate.reshape(inner),
        grad_proj_out,
        grad_gain_mid.reshape(quarter),
        grad_router.T,
        grad_shared,
        grad_shared_down,
        grad_gates.reshape(expert_gates.shape),
        grad_down,
    )


def solution(mesh):
    shard, ctx, tensor = (mesh.shape[name] for name in ("shard", "ctx", "tensor"))
    core = 2 if shard * ctx == 8 else 1
    split = jax.sharding.Mesh(
        mesh.devices.reshape(shard, ctx // core, core, tensor), ("shard", "cy", "core", "tensor")
    )
    return jax.shard_map(
        local,
        mesh=split,
        in_specs=(
            P(ROWS, "tensor"),
            P("tensor"),
            P(ROWS, None, "tensor"),
            P(ROWS, None),
            P(ROWS, "tensor"),
            P(None, "tensor"),
            P(),
            P("tensor"),
            P("tensor"),
            P("tensor"),
            P("tensor"),
            P(ROWS, "tensor"),
            P("tensor"),
            P(ROWS, None),
            P(ROWS, None, "tensor"),
            P(ROWS, "tensor"),
            P(ROWS, None, None, "tensor"),
            P(ROWS, "tensor", None),
            P("shard", CTX),
            P(ROWS, None),
            P(ROWS, "tensor"),
        ),
        out_specs=(
            P(ROWS, "tensor"),
            P(ROWS, "tensor"),
            P("tensor"),
            P(ROWS, None, "tensor"),
            P(ROWS, None),
            P(ROWS, "tensor"),
            P(None, "tensor"),
            P(),
            P("tensor"),
            P("tensor"),
            P("tensor"),
            P("tensor"),
            P(ROWS, "tensor"),
            P("tensor"),
            P(ROWS, None),
            P(ROWS, None, "tensor"),
            P(ROWS, "tensor"),
            P(ROWS, None, None, "tensor"),
            P(ROWS, "tensor", None),
        ),
        check_vma=False,
    )
```
